32 devices in a mesh: blk: 4 (over z), seq: 2 (over y), shard: 4 (over x, core).
Axes of the slice: x: 2, y: 2, z: 4, core: 2. Of those that a mesh axis runs over, the one named last changes fastest.
Arguments:
- tokens: bfloat16 [8, 2048, 768], P(('seq', 'shard'), 'blk'), may hold values from -6 to 6
- segments: int32 [8, 2048], P(('seq', 'shard')), may hold values from 0 to 2047, as said below
- live_mask: int32 [8, 2048], P(('seq', 'shard')), may hold values from 0 to 1, as said below
- query_weight: bfloat16 [768, 768], P(('seq', 'shard')), may hold values from -0.21875 to 0.21875
- key_weight: bfloat16 [768, 768], P(('seq', 'shard')), may hold values from -0.21875 to 0.21875
- value_weight: bfloat16 [768, 768], P(('seq', 'shard')), may hold values from -0.21875 to 0.21875
- out_weight: bfloat16 [768, 768], P(('seq', 'shard')), may hold values from -6 to 6
- query_bias: bfloat16 [768], P(('seq', 'shard')), may hold values from -1 to 1
- value_bias: bfloat16 [768], P(('seq', 'shard')), may hold values from -1 to 1
- out_bias: bfloat16 [768], P(('seq', 'shard')), may hold values from -1 to 1
- first_gain: bfloat16 [768], P(('seq', 'shard')), may hold values from 0.5 to 1.5
- first_shift: bfloat16 [768], P(('seq', 'shard')), may hold values from -1 to 1
- up_weight: bfloat16 [768, 3072], P(('seq', 'shard')), may hold values from -0.21875 to 0.21875
- up_bias: bfloat16 [3072], P(('seq', 'shard')), may hold values from -1 to 1
- down_weight: bfloat16 [3072, 768], P(('seq', 'shard')), may hold values from -0.109375 to 0.109375
- down_bias: bfloat16 [768], P(('seq', 'shard')), may hold values from -1 to 1
- second_gain: bfloat16 [768], P(('seq', 'shard')), may hold values from 0.5 to 1.5
- second_shift: bfloat16 [768], P(('seq', 'shard')), may hold values from -1 to 1
- cotangent: bfloat16 [8, 2048, 768], P(('seq', 'shard'), 'blk'), may hold values from -6 to 6
Outputs:
- layer_out: bfloat16 [8, 2048, 768], P(('seq', 'shard'), 'blk')
- token_grad: bfloat16 [8, 2048, 768], P(('seq', 'shard'), 'blk')
- query_weight_grad: float32 [768, 768], P(('seq', 'shard'))
- key_weight_grad: float32 [768, 768], P(('seq', 'shard'))
- value_weight_grad: float32 [768, 768], P(('seq', 'shard'))
- out_weight_grad: float32 [768, 768], P(('seq', 'shard'))
- query_bias_grad: float32 [768], P(('seq', 'shard'))
- value_bias_grad: float32 [768], P(('seq', 'shard'))
- out_bias_grad: float32 [768], P(('seq', 'shard'))
- first_gain_grad: float32 [768], P(('seq', 'shard'))
- first_shift_grad: float32 [768], P(('seq', 'shard'))
- up_weight_grad: float32 [768, 3072], P(('seq', 'shard'))
- up_bias_grad: float32 [3072], P(('seq', 'shard'))
- down_weight_grad: float32 [3072, 768], P(('seq', 'shard'))
- down_bias_grad: float32 [768], P(('seq', 'shard'))
- second_gain_grad: float32 [768], P(('seq', 'shard'))
- second_shift_grad: float32 [768], P(('seq', 'shard'))
The draws below stay inside these ranges and needn't reach their ends.
Inputs may be any that keep to these rules, and one draw needn't show every extreme that they name: `segments`: ids never fall along a sequence and start at 0; in at least one sequence one document begins within the first 512 tokens and ends within the last 512; the padding tokens form the sequence's last document, with id 2048 - 1. `live_mask`: each sequence ends with 1 to 256 padding tokens, marked 0; all others are 1.
All inputs are finite; a program needn't handle non-finite values.
Results may differ from the reference program's by a relative error of at most 0.02.
Values may be sent and summed in bfloat16 or wider, within the bound.
A program may use at most 128 MiB of HBM per device.

```python
import jax
import jax.numpy as jnp
from jax import lax

D = 768
FF = 3072
HEADS = 12
HEAD_DIM = 64
TOK_DEV = 512
SEQLEN = 2048
SEQS = 8
N_BLK = 4


def sequence_layout(key):
    pick_key, often_key, split_key = jax.random.split(jax.random.fold_in(key, 11), 3)
    keys = jax.random.split(split_key, SEQS)
    chosen = jax.random.randint(pick_key, (), 0, SEQS)
    often = jax.random.randint(often_key, (SEQS,), 0, 4) == 0
    spanning = (jnp.arange(SEQS, dtype=jnp.int32) == chosen) | often
    top_power = SEQLEN.bit_length() - 1
    count = SEQLEN // 4

    def single(sequence_key, is_long):
        first_key, last_key, pad_key, cut_key, power_key, extra_key = jax.random.split(sequence_key, 6)
        first = jax.random.randint(first_key, (), 1, TOK_DEV)
        final = jax.random.randint(last_key, (), SEQLEN - TOK_DEV, SEQLEN - TOK_DEV // 2)
        padding = jax.random.randint(pad_key, (), 1, TOK_DEV // 2 + 1)
        pad_start = SEQLEN - padding
        places = jnp.arange(SEQLEN, dtype=jnp.int32)
        cuts = jax.random.randint(cut_key, (SEQLEN,), 0, 48) == 0
        outside = (places < first) | (places > final) & (places < pad_start)
        long_flags = cuts & outside | (places == first) | (places == final + 1)
        powers = jax.random.randint(power_key, (count,), 2, top_power + 1)
        base = jnp.left_shift(jnp.ones((count,), jnp.int32), powers).astype(jnp.int32)
        extra = jax.random.randint(extra_key, (count,), 0, base)
        bounds = jnp.cumsum(base + extra).astype(jnp.int32)
        short_flags = jnp.any(places[:, None] == bounds[None, :], axis=1)
        flags = jnp.where(is_long, long_flags, short_flags) & (places > 0)
        doc_ids = jnp.cumsum(flags.astype(jnp.int32)).astype(jnp.int32)
        doc_ids = jnp.where(places >= pad_start, SEQLEN - 1, doc_ids).astype(jnp.int32)
        live_all = (places < pad_start).astype(jnp.int32)
        return (doc_ids, live_all)
    return jax.vmap(single)(keys, spanning)


def draw_segments(key, part):
    return sequence_layout(key)[0]


def draw_live_mask(key, part):
    return sequence_layout(key)[1]


def spiked(drawn, own_key, source, target, parts, factor):
    def block_of(dim):
        return (jnp.arange(drawn.shape[dim]) // (drawn.shape[dim] // parts)).reshape((-1,) + (1,) * (drawn.ndim - 1 - dim))

    one_side = jax.random.permutation(own_key, parts)[block_of(target)]
    second = (block_of(target) + parts // 2) % parts
    return jnp.where((block_of(source) == one_side) | (block_of(source) == second), factor * drawn, drawn)


def block_scale(key, shape, pieces, smallest, largest):
    level, own = 1.0, jax.random.fold_in(key, 6)
    for dim, parts in pieces:
        heights = jnp.exp(jax.random.uniform(jax.random.fold_in(own, dim), (parts,), jnp.float32, smallest / len(pieces), largest / len(pieces)))
        level = level * jnp.repeat(heights, shape[dim] // parts).reshape([-1 if axis == dim else 1 for axis in range(len(shape))])
    return level


def centred(own_key, dims, scale, bound, cuts=(), kind=jnp.bfloat16):
    array = scale * jax.random.normal(own_key, dims, jnp.float32)
    if cuts:
        array = array * block_scale(own_key, dims, cuts, -0.22, 0.18)
    return jnp.clip(array, -bound, bound).astype(kind)


def heavy_noise(own_key, shape, scale, limit, shards, heavy, held_as=jnp.bfloat16):
    values = scale * jax.random.normal(own_key, shape, jnp.float32)
    if shards:
        values = values * block_scale(own_key, shape, shards, -0.22, 0.18)
    return jnp.clip(spiked(values, jax.random.fold_in(own_key, 3), *heavy), -limit, limit).astype(held_as)


def setup_inputs(seed: int = 0) -> dict:
    seeds = jax.random.split(jax.random.key(seed), 20)
    tokens = heavy_noise(seeds[0], (SEQS, SEQLEN, D), 1.0, 6.0, ((0, 8), (1, 4)), (0, 2, 8, 2.0))
    segments = draw_segments(jax.random.fold_in(seeds[19], 71), 0)
    live_mask = draw_live_mask(jax.random.fold_in(seeds[19], 71), 0)
    query_weight = centred(seeds[3], (D, D), D ** -0.5, 0.21875, ((0, 8),))
    key_weight = centred(seeds[4], (D, D), D ** -0.5, 0.21875, ((0, 8),))
    value_weight = centred(seeds[5], (D, D), D ** -0.5, 0.21875, ((0, 8),))
    out_weight = centred(seeds[6], (D, D), 1 ** -0.5, 6.0, ((0, 8),))
    query_bias = centred(seeds[7], (D,), 0.2, 1.0, ((0, 8),))
    value_bias = centred(seeds[8], (D,), 0.2, 1.0, ((0, 8),))
    out_bias = centred(seeds[9], (D,), 0.2, 1.0, ((0, 8),))
    first_gain = jnp.clip(1.0 + 0.1 * jax.random.normal(seeds[10], (D,), jnp.float32), 0.5, 1.5).astype(jnp.bfloat16)
    first_shift = centred(seeds[11], (D,), 0.2, 1.0, ((0, 8),))
    up_weight = centred(seeds[12], (D, FF), D ** -0.5, 0.21875, ((0, 8),))
    up_bias = centred(seeds[13], (FF,), 0.2, 1.0, ((0, 8),))
    down_weight = centred(seeds[14], (FF, D), FF ** -0.5, 0.109375, ((0, 8),))
    down_bias = centred(seeds[15], (D,), 0.2, 1.0, ((0, 8),))
    second_gain = jnp.clip(1.0 + 0.1 * jax.random.normal(seeds[16], (D,), jnp.float32), 0.5, 1.5).astype(jnp.bfloat16)
    second_shift = centred(seeds[17], (D,), 0.2, 1.0, ((0, 8),))
    cotangent = heavy_noise(seeds[18], (SEQS, SEQLEN, D), 1.0, 6.0, ((0, 8), (1, 4)), (0, 2, 8, 2.0))
    return {"tokens": tokens, "segments": segments, "live_mask": live_mask, "query_weight": query_weight, "key_weight": key_weight, "value_weight": value_weight, "out_weight": out_weight, "query_bias": query_bias, "value_bias": value_bias, "out_bias": out_bias, "first_gain": first_gain, "first_shift": first_shift, "up_weight": up_weight, "up_bias": up_bias, "down_weight": down_weight, "down_bias": down_bias, "second_gain": second_gain, "second_shift": second_shift, "cotangent": cotangent}


EPSILON = 1e-06
MASKED = -1e+30

@jax.custom_vjp
def low(v):
    return lax.optimization_barrier(v.astype(jnp.bfloat16)).astype(jnp.float32)

@jax.custom_vjp
def low_back(v):
    return v

def low_keep(v):
    return (low(v), None)

def low_pass(kept, grad):
    return (grad,)

def back_keep(v):
    return (v, None)

def back_low(kept, grad):
    return (low(grad),)
low.defvjp(low_keep, low_pass)
low_back.defvjp(back_keep, back_low)

def product(left, right):
    return jnp.dot(left, right, precision=lax.Precision.HIGHEST)

def normalize(hidden, gain, shift):
    center = hidden - lax.optimization_barrier(jnp.mean(hidden, axis=-1, keepdims=True))
    spread = lax.optimization_barrier(jnp.mean(center * center, axis=-1, keepdims=True))
    return center * lax.rsqrt(spread + EPSILON) * gain + shift

def attend(queries, keyset, valueset, doc_ids, live_all):
    places = jnp.arange(SEQLEN, dtype=jnp.int32)
    key_heads = keyset.reshape(SEQLEN, HEADS, HEAD_DIM)
    value_heads = valueset.reshape(SEQLEN, HEADS, HEAD_DIM)

    def block(item):
        query_block, query_doc, query_place = item
        raw = low_back(jnp.einsum('qhd,khd->hqk', query_block, key_heads, precision=lax.Precision.HIGHEST))
        mask = (query_doc[:, None] == doc_ids[None, :]) & ((live_all[None, :] > 0) | (query_place[:, None] == places[None, :]))
        masked = jnp.where(mask[None], raw, MASKED)
        top = lax.optimization_barrier(jnp.max(masked, axis=-1, keepdims=True))
        log_mass = top + jnp.log(lax.optimization_barrier(jnp.sum(jnp.exp(masked - top), axis=-1, keepdims=True)))
        shares = low(jnp.exp(masked - log_mass))
        result = jnp.einsum('hqk,khd->qhd', shares, value_heads, precision=lax.Precision.HIGHEST)
        return result.reshape(TOK_DEV, D)
    items = (queries.reshape(N_BLK, TOK_DEV, HEADS, HEAD_DIM), doc_ids.reshape(N_BLK, TOK_DEV), places.reshape(N_BLK, TOK_DEV))
    return lax.map(jax.checkpoint(block), items).reshape(SEQLEN, D)

def layer_one(inputs, doc_ids, live_all, weights):
    query_weight, key_weight, value_weight, out_weight, query_bias, value_bias, out_bias, first_gain, first_shift, up_weight, up_bias, down_weight, down_bias, second_gain, second_shift = weights
    scale = HEAD_DIM ** (-0.5)
    queries = low((low_back(product(inputs, query_weight)) + query_bias) * scale)
    keyset = low(low_back(product(inputs, key_weight)))
    valueset = low(low_back(product(inputs, value_weight)) + value_bias)
    attended = low(low_back(attend(queries, keyset, valueset, doc_ids, live_all)))
    first_sum = inputs + low_back(product(attended, out_weight)) + out_bias
    first_norm = normalize(first_sum, first_gain, first_shift)
    hidden = low_back(product(low(first_norm), up_weight)) + up_bias
    gated = low(jax.nn.gelu(hidden, approximate=False))
    second_sum = first_norm + low_back(product(gated, down_weight)) + down_bias
    return normalize(second_sum, second_gain, second_shift)

def reference(tokens, segments, live_mask, query_weight, key_weight, value_weight, out_weight, query_bias, value_bias, out_bias, first_gain, first_shift, up_weight, up_bias, down_weight, down_bias, second_gain, second_shift, cotangent):
    params = tuple((a.astype(jnp.float32) for a in (query_weight, key_weight, value_weight, out_weight, query_bias, value_bias, out_bias, first_gain, first_shift, up_weight, up_bias, down_weight, down_bias, second_gain, second_shift)))

    def whole(inputs, weights):
        return lax.map(lambda item: layer_one(item[0], item[1], item[2], weights), (inputs, segments, live_mask))
    result, pull = jax.vjp(whole, tokens.astype(jnp.float32), params)
    token_grad, grads = pull(cotangent.astype(jnp.float32))
    return (result.astype(jnp.bfloat16), token_grad.astype(jnp.bfloat16), grads[0], grads[1], grads[2], grads[3], grads[4], grads[5], grads[6], grads[7], grads[8], grads[9], grads[10], grads[11], grads[12], grads[13], grads[14])
```

```python
import functools
import jax
import jax.numpy as jnp
from jax import lax
from jax.experimental import pallas as pl
from jax.experimental.pallas import tpu as pltpu
from jax.sharding import PartitionSpec as P

MESH = pl.DeviceIdType.MESH
ANY = pl.BlockSpec(memory_space=pl.ANY)
VMEM_LIMIT = 56 << 20
VM = pl.BlockSpec(memory_space=pltpu.VMEM)


class Place:
    def __init__(self):
        b = lax.axis_index("blk")
        s = lax.axis_index("seq")
        h = lax.axis_index("shard")
        x = h // 2
        c = h % 2
        self.b, self.s, self.h, self.x, self.c = b, s, h, x, c
        self.X = (b, s, (1 - x) * 2 + c)
        self.Y = (b, 1 - s, h)
        self.C = (b, s, x * 2 + 1 - c)
        self.L = (b - 1, s, h)
        self.R = (b + 1, s, h)
        self.me = s * 4 + h
        self.xi = s * 4 + (1 - x) * 2 + c
        self.yi = (1 - s) * 4 + h
        self.di = (1 - s) * 4 + (1 - x) * 2 + c

    def z(self, j):
        return (j, self.s, self.h)


def enter(p, nb, plane, line):
    bar = pltpu.get_barrier_semaphore()
    count = 0
    if plane:
        for peer in (p.X, p.Y, p.C):
            pl.semaphore_signal(bar, inc=1, device_id=peer, device_id_type=MESH)
        count = count + 3
    if line == "near":
        @pl.when(p.b > 0)
        def _():
            pl.semaphore_signal(bar, inc=1, device_id=p.L, device_id_type=MESH)

        @pl.when(p.b < nb - 1)
        def _():
            pl.semaphore_signal(bar, inc=1, device_id=p.R, device_id_type=MESH)
        count = count + jnp.where(p.b > 0, 1, 0) + jnp.where(p.b < nb - 1, 1, 0)
    if line == "all":
        for j in range(nb):
            @pl.when(p.b != j)
            def _():
                pl.semaphore_signal(bar, inc=1, device_id=p.z(j), device_id_type=MESH)
        count = count + nb - 1
    pl.semaphore_wait(bar, count)


def rcopy(src, dst, ss, rs, dev):
    return pltpu.make_async_remote_copy(
        src_ref=src, dst_ref=dst, send_sem=ss, recv_sem=rs, device_id=dev, device_id_type=MESH
    )


class LineGather:
    def __init__(self, p, nb, own, out, ssem, rsem):
        self.p, self.nb, self.own, self.out, self.ssem, self.rsem = p, nb, own, out, ssem, rsem

    def _copies(self, t):
        p, nb = self.p, self.nb
        rb = p.b - t
        lb = p.b + t
        src_r = self.own if t == 0 else self.out.at[jnp.maximum(rb, 0)]
        src_l = self.own if t == 0 else self.out.at[jnp.minimum(lb, nb - 1)]
        right = rcopy(src_r, self.out.at[jnp.maximum(rb, 0)], self.ssem.at[0, t], self.rsem.at[0, t], p.R)
        left = rcopy(src_l, self.out.at[jnp.minimum(lb, nb - 1)], self.ssem.at[1, t], self.rsem.at[1, t], p.L)
        return right, left, (rb >= 0) & (p.b < nb - 1), (lb <= nb - 1) & (p.b > 0)

    def start(self, t):
        right, left, cr, cl = self._copies(t)
        pl.when(cr)(right.start)
        pl.when(cl)(left.start)

    def wait_recv(self, t):
        p, nb = self.p, self.nb
        right, left, _, _ = self._copies(t)
        pl.when(p.b - 1 - t >= 0)(right.wait_recv)
        pl.when(p.b + 1 + t <= nb - 1)(left.wait_recv)

    def wait_send(self, t):
        right, left, cr, cl = self._copies(t)
        pl.when(cr)(right.wait_send)
        pl.when(cl)(left.wait_send)


class PlaneGather:
    def __init__(self, p, own, out, ssem, rsem, lsem):
        self.p = p
        rows = own.shape[0]
        half = rows // 2
        lo, hi = pl.ds(0, half), pl.ds(half, half)
        o = out
        self.x = rcopy(own, o.at[p.me], ssem.at[0], rsem.at[0], p.X)
        self.y = rcopy(own, o.at[p.me], ssem.at[1], rsem.at[1], p.Y)
        self.c = rcopy(own, o.at[p.me], ssem.at[2], rsem.at[2], p.C)
        self.local = pltpu.make_async_copy(own, o.at[p.me], lsem)
        self.fx = rcopy(o.at[p.yi, hi], o.at[p.yi, hi], ssem.at[3], rsem.at[3], p.X)
        self.fy = rcopy(o.at[p.xi, lo], o.at[p.xi, lo], ssem.at[4], rsem.at[4], p.Y)
        self.cx = rcopy(o.at[p.xi], o.at[p.xi], ssem.at[5], rsem.at[5], p.C)
        self.cy = rcopy(o.at[p.yi], o.at[p.yi], ssem.at[6], rsem.at[6], p.C)
        self.cd0 = rcopy(o.at[p.di, lo], o.at[p.di, lo], ssem.at[7], rsem.at[7], p.C)
        self.cd1 = rcopy(o.at[p.di, hi], o.at[p.di, hi], ssem.at[8], rsem.at[8], p.C)

    def start(self):
        self.x.start(); self.y.start(); self.c.start(); self.local.start()

    def forward(self):
        self.x.wait_recv()
        self.fy.start()
        self.cx.start()
        self.y.wait_recv()
        self.fx.start()
        self.cy.start()

    def diag(self):
        self.fy.wait_recv()
        self.cd0.start()
        self.fx.wait_recv()
        self.cd1.start()

    def finish(self):
        self.local.wait()
        self.c.wait_recv(); self.cx.wait_recv(); self.cy.wait_recv()
        self.cd0.wait_recv(); self.cd1.wait_recv()

    def drain(self):
        for k in (self.x, self.y, self.c, self.fx, self.fy, self.cx, self.cy, self.cd0, self.cd1):
            k.wait_send()


def gather_kernel(nb, nw, *refs):
    x_ref, ws = refs[0], refs[1:1 + nw]
    xall, outs = refs[1 + nw], refs[2 + nw:2 + 2 * nw]
    zs, zr, ws_s, ws_r, ls = refs[2 + 2 * nw:]
    p = Place()
    enter(p, nb, True, "near")
    line = LineGather(p, nb, x_ref, xall, zs, zr)
    own = pltpu.make_async_copy(x_ref, xall.at[p.b], ls.at[nw])
    g = [PlaneGather(p, ws[i], outs[i], ws_s.at[i], ws_r.at[i], ls.at[i]) for i in range(nw)]
    n0 = nw - 2
    line.start(0)
    own.start()
    for k in g[:n0 + 1]:
        k.start()
    for k in g[:n0]:
        k.forward()
    g[n0 + 1].start()
    line.wait_recv(0)
    if nb > 2:
        line.start(1)
    g[n0].forward()
    for t in range(1, nb - 2):
        line.wait_recv(t)
        line.start(t + 1)
    g[n0 + 1].forward()
    for k in g:
        k.diag()
    line.wait_recv(nb - 2)
    for k in g:
        k.finish()
    own.wait()
    for t in range(nb - 1):
        line.wait_send(t)
    for k in g:
        k.drain()


def gather_all(x, weights, nb):
    nw = len(weights)
    outs = (jax.ShapeDtypeStruct((nb,) + x.shape, x.dtype),) + tuple(
        jax.ShapeDtypeStruct((8,) + w.shape, w.dtype) for w in weights
    )
    return pl.pallas_call(
        functools.partial(gather_kernel, nb, nw),
        out_shape=outs,
        in_specs=[VM] * (1 + nw),
        out_specs=(ANY,) * (1 + nw),
        scratch_shapes=[
            pltpu.SemaphoreType.DMA((2, nb - 1)),
            pltpu.SemaphoreType.DMA((2, nb - 1)),
            pltpu.SemaphoreType.DMA((nw, 9)),
            pltpu.SemaphoreType.DMA((nw, 9)),
            pltpu.SemaphoreType.DMA((nw + 1,)),
        ],
        compiler_params=pltpu.CompilerParams(
            collective_id=1, has_side_effects=True, vmem_limit_bytes=VMEM_LIMIT
        ),
        name="gather_all",
    )(x, *weights)


def line_kernel(nb, na, *refs):
    ins, outs = refs[:na], refs[na:2 * na]
    zs, zr, ls = refs[2 * na:]
    p = Place()
    enter(p, nb, False, "near")
    lines = [LineGather(p, nb, ins[i], outs[i], zs.at[i], zr.at[i]) for i in range(na)]
    own = [pltpu.make_async_copy(ins[i], outs[i].at[p.b], ls.at[i]) for i in range(na)]
    for k in lines:
        k.start(0)
    for k in own:
        k.start()
    for t in range(nb - 1):
        for k in lines:
            k.wait_recv(t)
            if t + 1 < nb - 1:
                k.start(t + 1)
    for k in own:
        k.wait()
    for t in range(nb - 1):
        for k in lines:
            k.wait_send(t)


def line_gather(arrays, nb):
    na = len(arrays)
    return pl.pallas_call(
        functools.partial(line_kernel, nb, na),
        out_shape=tuple(jax.ShapeDtypeStruct((nb,) + a.shape, a.dtype) for a in arrays),
        in_specs=[VM] * na,
        out_specs=(ANY,) * na,
        scratch_shapes=[
            pltpu.SemaphoreType.DMA((na, 2, nb - 1)),
            pltpu.SemaphoreType.DMA((na, 2, nb - 1)),
            pltpu.SemaphoreType.DMA((na,)),
        ],
        compiler_params=pltpu.CompilerParams(
            collective_id=2, has_side_effects=True, vmem_limit_bytes=VMEM_LIMIT
        ),
        name="line_gather",
    )(*arrays)


def row_loop(rows, chunk, body):
    if rows == chunk:
        body(0)
    else:
        def step(i, _):
            body(pl.multiple_of(i * chunk, chunk))
            return 0
        lax.fori_loop(0, rows // chunk, step, 0)


class PlaneReduce:
    def __init__(self, p, nb, g, out, buf, ss, rs):
        self.p, self.nb, self.g, self.out = p, nb, g, out
        self.A, self.P, self.BX, self.BY, self.CX, self.CY, self.F, self.Z, self.O = buf
        self.R, self.C = g.shape[-2:]
        self.dt = g.dtype
        self.ss, self.rs = ss, rs
        R, C = self.R, self.C
        h = R // 2
        self.h = h
        lo, hi = pl.ds(0, h), pl.ds(h, h)
        self.chunk = 16 if C > 1024 else (48 if h % 48 == 0 else h)
        self.cA = rcopy(g.at[:, :, 1 - p.c], self.A, ss.at[0], rs.at[0], p.C)
        self.cBX = rcopy(self.P.at[:, 1 - p.x, lo], self.BX, ss.at[1], rs.at[1], p.X)
        self.cBY = rcopy(self.P.at[1 - p.s, :, hi], self.BY, ss.at[2], rs.at[2], p.Y)
        self.cCX = rcopy(self.P.at[p.s, 1 - p.x, hi], self.CX, ss.at[3], rs.at[3], p.X)
        self.cCY = rcopy(self.P.at[1 - p.s, p.x, lo], self.CY, ss.at[4], rs.at[4], p.Y)

    def quarter(self, ref, j):
        R, C = self.R, self.C
        if isinstance(j, int):
            return ref.at[pl.ds((j // 2) * (R // 2), R // 2), pl.ds((j % 2) * (C // 2), C // 2)]
        r = pl.multiple_of((j // 2) * (R // 2), R // 2)
        c = pl.multiple_of((j % 2) * (C // 2), C // 2)
        return ref.at[pl.ds(r, R // 2), pl.ds(c, C // 2)]

    def a_start(self):
        self.cA.start()

    def b_start(self):
        self.cA.wait_recv()
        p, g, A, P, dt = self.p, self.g, self.A, self.P, self.dt

        def block(i, _):
            s, x = i // 2, i % 2

            def body(r):
                rows = pl.ds(r, self.chunk)
                P[s, x, rows] = (
                    g[s, x, p.c, rows].astype(jnp.float32) + A[s, x, rows].astype(jnp.float32)
                ).astype(dt)
            row_loop(self.R, self.chunk, body)
            return 0
        lax.fori_loop(0, 4, block, 0)
        self.cBX.start()
        self.cBY.start()

    def _add(self, dst, src):
        def body(r):
            rows = pl.ds(r, self.chunk)
            dst[rows] = (dst[rows].astype(jnp.float32) + src[rows].astype(jnp.float32)).astype(self.dt)
        row_loop(self.h, self.chunk, body)

    def c_start(self):
        p, h = self.p, self.h
        lo, hi = pl.ds(0, h), pl.ds(h, h)
        self.cBX.wait_recv()
        self._add(self.P.at[1 - p.s, p.x, lo], self.BX.at[1 - p.s])
        self.cCY.start()
        self.cBY.wait_recv()
        self._add(self.P.at[p.s, 1 - p.x, hi], self.BY.at[1 - p.x])
        self.cCX.start()
        self._add(self.P.at[p.s, p.x, lo], self.BX.at[p.s])
        self._add(self.P.at[p.s, p.x, hi], self.BY.at[p.x])

    def _z1(self, j, slot):
        return rcopy(self.quarter(self.F, j), self.Z.at[slot], self.ss.at[5 + j], self.rs.at[5 + slot], self.p.z(j))

    def _z2(self, j, slot):
        q = self.quarter(self.O, slot)
        return rcopy(q, q, self.ss.at[5 + self.nb + j], self.rs.at[5 + self.nb + slot], self.p.z(j))

    def d_start(self):
        p, h, nb = self.p, self.h, self.nb
        self.cCY.wait_recv()
        self.cCX.wait_recv()

        def lo_body(r):
            rows = pl.ds(r, self.chunk)
            self.F[rows] = (
                self.P[p.s, p.x, rows].astype(jnp.float32) + self.CY[rows].astype(jnp.float32)
            ).astype(self.dt)
        row_loop(h, self.chunk, lo_body)

        def hi_body(r):
            rows = pl.ds(r + h, self.chunk)
            self.F[rows] = (
                self.P[p.s, p.x, rows].astype(jnp.float32)
                + self.CX[pl.ds(r, self.chunk)].astype(jnp.float32)
            ).astype(self.dt)
        row_loop(h, self.chunk, hi_body)
        for j in range(nb):
            @pl.when(p.b != j)
            def _():
                self._z1(j, p.b).start()

    def e_start(self):
        p, nb = self.p, self.nb
        mine = self.quarter(self.F, p.b)
        total = self.quarter(self.O, p.b)
        for i in range(nb):
            @pl.when(p.b != i)
            def _():
                self._z1(i, i).wait_recv()

        def body(r):
            rows = pl.ds(r, self.chunk)
            acc = mine[rows].astype(jnp.float32)
            for d in range(1, nb):
                acc = acc + self.Z[(p.b + d) % nb, rows].astype(jnp.float32)
            total[rows] = acc.astype(self.dt)
        row_loop(self.h, self.chunk, body)
        for j in range(nb):
            @pl.when(p.b != j)
            def _():
                self._z2(j, p.b).start()

    def finish(self):
        p, nb = self.p, self.nb
        for i in range(nb):
            @pl.when(p.b != i)
            def _():
                self._z2(i, i).wait_recv()

        def body(r):
            rows = pl.ds(r, self.chunk)
            self.out[rows] = self.O[rows].astype(jnp.float32)
        row_loop(self.R, self.chunk, body)

    def drain(self):
        for k in (self.cA, self.cBX, self.cBY, self.cCX, self.cCY):
            k.wait_send()
        for j in range(self.nb):
            @pl.when(self.p.b != j)
            def _():
                self._z1(j, self.p.b).wait_send()
                self._z2(j, self.p.b).wait_send()


def reduce_scratch(shape, dt, nb):
    R, C = shape
    h = R // 2
    return [
        pltpu.VMEM((2, 2, R, C), dt),
        pltpu.VMEM((2, 2, R, C), dt),
        pltpu.VMEM((2, h, C), dt),
        pltpu.VMEM((2, h, C), dt),
        pltpu.VMEM((h, C), dt),
        pltpu.VMEM((h, C), dt),
        pltpu.VMEM((R, C), dt),
        pltpu.VMEM((nb, h, C // 2), dt),
        pltpu.VMEM((R, C), dt),
    ]


def wave(items, stages):
    n, m = len(items), len(stages)
    for step in range(n + m - 1):
        for k in range(m):
            i = step - k
            if 0 <= i < n:
                getattr(items[i], stages[k])()


def reduce_kernel(nb, nw, *refs):
    gs, outs = refs[:nw], refs[nw:2 * nw]
    bufs = refs[2 * nw:2 * nw + 9 * nw]
    ss, rs = refs[11 * nw:]
    p = Place()
    enter(p, nb, True, "all")
    items = [
        PlaneReduce(p, nb, gs[i], outs[i], bufs[9 * i:9 * i + 9], ss.at[i], rs.at[i]) for i in range(nw)
    ]
    for k in items:
        k.a_start()
    wave(items, ("b_start", "c_start", "d_start", "e_start"))
    for k in items:
        k.finish()
    for k in items:
        k.drain()


def reduce_all(grads, nb):
    nw = len(grads)
    scratch = []
    for g in grads:
        scratch += reduce_scratch(g.shape[-2:], g.dtype, nb)
    ns = 5 + 2 * nb
    return pl.pallas_call(
        functools.partial(reduce_kernel, nb, nw),
        out_shape=tuple(jax.ShapeDtypeStruct(g.shape[-2:], jnp.float32) for g in grads),
        in_specs=[VM] * nw,
        out_specs=(VM,) * nw,
        scratch_shapes=scratch + [pltpu.SemaphoreType.DMA((nw, ns)), pltpu.SemaphoreType.DMA((nw, ns))],
        compiler_params=pltpu.CompilerParams(
            collective_id=3, has_side_effects=True, vmem_limit_bytes=VMEM_LIMIT
        ),
        name="reduce_all",
    )(*grads)


HEAD_DIM = 64
PAIR = 128
MASKED = -1e30
TILE = 256


def dot(a, b, ca, cb):
    return lax.dot_general(a, b, (((ca,), (cb,)), ((), ())), preferred_element_type=jnp.float32)


def left_lanes(shape):
    return lax.broadcasted_iota(jnp.int32, shape, 1) < HEAD_DIM


def one_head(pair, left, first):
    keep = left if first else jnp.logical_not(left)
    return jnp.where(keep, pair, jnp.zeros_like(pair))


def attn_fwd_kernel(span, col_ref, row_ref, q_ref, k_ref, v_ref, o_ref, ob_ref, lse_ref, m_ref, l_ref, acc_ref):
    rows = q_ref.shape[0]
    left = left_lanes((rows, PAIR))
    m_ref[...] = jnp.full_like(m_ref, MASKED)
    l_ref[...] = jnp.zeros_like(l_ref)
    acc_ref[...] = jnp.zeros_like(acc_ref)
    q = q_ref[...]
    heads = [one_head(q, left, True), one_head(q, left, False)]
    codes = col_ref[...]

    def step(t, _):
        at = pl.multiple_of(t * TILE, TILE)
        k = k_ref[pl.ds(at, TILE), :]
        v = v_ref[pl.ds(at, TILE), :]
        mask = codes == row_ref[:, pl.ds(at, TILE)]
        alphas, parts = [], []
        for i in range(2):
            s = jnp.where(mask, dot(heads[i], k, 1, 1), MASKED)
            old = m_ref[i]
            new = jnp.maximum(old, jnp.max(s, axis=1, keepdims=True))
            p = jnp.exp(s - new)
            alpha = jnp.exp(old - new)
            m_ref[i] = new
            l_ref[i] = l_ref[i] * alpha + jnp.sum(p, axis=1, keepdims=True)
            alphas.append(alpha)
            parts.append(dot(p.astype(jnp.bfloat16), v, 1, 0))
        acc_ref[...] = acc_ref[...] * jnp.where(left, alphas[0], alphas[1]) + jnp.where(left, parts[0], parts[1])
        return 0

    lax.fori_loop(span[0], span[1], step, 0)
    total = jnp.where(left, l_ref[0], l_ref[1])
    o = acc_ref[...] / total
    o_ref[...] = o
    ob_ref[...] = o.astype(jnp.bfloat16)
    lse_ref[...] = jnp.where(left, m_ref[0], m_ref[1]) + jnp.log(total)


def attention(q, k_all, v_all, codes, own_codes, span):
    rows, width = q.shape
    total = k_all.shape[0]
    pairs = width // PAIR
    own = pl.BlockSpec((rows, PAIR), lambda h, s: (0, h))
    every = pl.BlockSpec((total, PAIR), lambda h, s: (0, h))
    return pl.pallas_call(
        attn_fwd_kernel,
        grid_spec=pltpu.PrefetchScalarGridSpec(
            num_scalar_prefetch=1,
            grid=(pairs,),
            in_specs=[
                pl.BlockSpec((rows, 1), lambda h, s: (0, 0)),
                pl.BlockSpec((1, total), lambda h, s: (0, 0)),
                own, every, every,
            ],
            out_specs=[own, own, own],
            scratch_shapes=[
                pltpu.VMEM((2, rows, 1), jnp.float32),
                pltpu.VMEM((2, rows, 1), jnp.float32),
                pltpu.VMEM((rows, PAIR), jnp.float32),
            ],
        ),
        out_shape=[
            jax.ShapeDtypeStruct((rows, width), jnp.float32),
            jax.ShapeDtypeStruct((rows, width), jnp.bfloat16),
            jax.ShapeDtypeStruct((rows, width), jnp.float32),
        ],
        compiler_params=pltpu.CompilerParams(vmem_limit_bytes=48 << 20),
        name="attention",
    )(span, own_codes.reshape(rows, 1), codes.reshape(1, total), q, k_all, v_all)


def stats_kernel(g_ref, o_ref, lse_ref, out_ref, delta_ref):
    rows = g_ref.shape[0]
    left = left_lanes((rows, PAIR))
    t = g_ref[...].astype(jnp.float32) * o_ref[...]
    d0 = jnp.sum(jnp.where(left, t, 0.0), axis=1, keepdims=True)
    d1 = jnp.sum(jnp.where(left, 0.0, t), axis=1, keepdims=True)
    delta_ref[...] = jnp.where(left, d0, d1)
    lane = lax.broadcasted_iota(jnp.int32, (rows, PAIR), 1)
    lse = lse_ref[...]
    packed = jnp.where(lane == 0, lse[:, :1], jnp.where(lane == 1, lse[:, HEAD_DIM:HEAD_DIM + 1], jnp.where(lane == 2, d0, d1)))
    out_ref[0] = packed.T[:8]


def row_stats(grad, o, lse):
    rows, width = grad.shape
    pairs = width // PAIR
    own = pl.BlockSpec((rows, PAIR), lambda h: (0, h))
    return pl.pallas_call(
        stats_kernel,
        grid=(pairs,),
        in_specs=[own, own, own],
        out_specs=[pl.BlockSpec((1, 8, rows), lambda h: (h, 0, 0)), own],
        out_shape=[
            jax.ShapeDtypeStruct((pairs, 8, rows), jnp.float32),
            jax.ShapeDtypeStruct((rows, width), jnp.float32),
        ],
        name="row_stats",
    )(grad, o, lse)


def attn_bwd_kernel(span, col_ref, row_ref, q_ref, k_ref, v_ref, g_ref, lse_ref, delta_ref,
                    qa_ref, ka_ref, va_ref, ga_ref, st_ref, r_ref, rk_ref, rv_ref, dq_ref, dk_ref, dv_ref):
    rows = q_ref.shape[0]
    left = left_lanes((rows, PAIR))
    dq_ref[...] = jnp.zeros_like(dq_ref)
    dk_ref[...] = jnp.zeros_like(dk_ref)
    dv_ref[...] = jnp.zeros_like(dv_ref)
    codes = col_ref[...]
    qs = [one_head(q_ref[...], left, i == 0) for i in range(2)]
    ks = [one_head(k_ref[...], left, i == 0) for i in range(2)]
    vs = [one_head(v_ref[...], left, i == 0) for i in range(2)]
    gs = [one_head(g_ref[...], left, i == 0) for i in range(2)]
    lses = [lse_ref[:, i * HEAD_DIM:i * HEAD_DIM + 1] for i in range(2)]
    deltas = [delta_ref[:, i * HEAD_DIM:i * HEAD_DIM + 1] for i in range(2)]

    def step(t, _):
        at = pl.multiple_of(t * TILE, TILE)
        tile = pl.ds(at, TILE)
        mask = codes == row_ref[:, tile]
        k, v, q, g = ka_ref[tile, :], va_ref[tile, :], qa_ref[tile, :], ga_ref[tile, :]
        dqs, dks, dvs = [], [], []
        for i in range(2):
            s = jnp.where(mask, dot(qs[i], k, 1, 1), MASKED)
            p = jnp.exp(s - lses[i])
            dp = dot(gs[i], v, 1, 1)
            ds = (p * (dp - deltas[i])).astype(jnp.bfloat16)
            dqs.append(dot(ds, k, 1, 0))
            st = jnp.where(mask, dot(ks[i], q, 1, 1), MASKED)
            pt = jnp.exp(st - st_ref[0, i:i + 1, tile])
            dvs.append(dot(pt.astype(jnp.bfloat16), g, 1, 0))
            dpt = dot(vs[i], g, 1, 1)
            dst = (pt * (dpt - st_ref[0, 2 + i:3 + i, tile])).astype(jnp.bfloat16)
            dks.append(dot(dst, q, 1, 0))
        dq_ref[...] += jnp.where(left, dqs[0], dqs[1])
        dk_ref[...] += jnp.where(left, dks[0], dks[1])
        dv_ref[...] += jnp.where(left, dvs[0], dvs[1])
        return 0

    lax.fori_loop(span[0], span[1], step, 0)
    r_ref[...] = dq_ref[...] * (HEAD_DIM ** (-0.5))
    rk_ref[...] = dk_ref[...].astype(jnp.bfloat16)
    rv_ref[...] = dv_ref[...]


def attention_grad(q, k, v, g, lse, delta, q_all, k_all, v_all, g_all, stats, codes, own_codes, span):
    rows, width = q.shape
    total = k_all.shape[0]
    pairs = width // PAIR
    own = pl.BlockSpec((rows, PAIR), lambda h, s: (0, h))
    every = pl.BlockSpec((total, PAIR), lambda h, s: (0, h))
    return pl.pallas_call(
        attn_bwd_kernel,
        grid_spec=pltpu.PrefetchScalarGridSpec(
            num_scalar_prefetch=1,
            grid=(pairs,),
            in_specs=[
                pl.BlockSpec((rows, 1), lambda h, s: (0, 0)),
                pl.BlockSpec((1, total), lambda h, s: (0, 0)),
                own, own, own, own, own, own, every, every, every, every,
                pl.BlockSpec((1, 8, total), lambda h, s: (h, 0, 0)),
            ],
            out_specs=[own, own, own],
            scratch_shapes=[pltpu.VMEM((rows, PAIR), jnp.float32)] * 3,
        ),
        out_shape=[
            jax.ShapeDtypeStruct((rows, width), jnp.float32),
            jax.ShapeDtypeStruct((rows, width), jnp.bfloat16),
            jax.ShapeDtypeStruct((rows, width), jnp.float32),
        ],
        compiler_params=pltpu.CompilerParams(vmem_limit_bytes=48 << 20),
        name="attention_grad",
    )(span, own_codes.reshape(rows, 1), codes.reshape(1, total), q, k, v, g, lse, delta, q_all, k_all, v_all, g_all, stats)


EPSILON = 1e-06
PLANE = ("seq", "shard")


def normalize(hidden, gain, shift):
    center = hidden - jnp.mean(hidden, axis=-1, keepdims=True)
    spread = jnp.mean(center * center, axis=-1, keepdims=True)
    return center * lax.rsqrt(spread + EPSILON) * gain + shift


def smooth_gate(hidden):
    return jax.nn.gelu(hidden, approximate=False)


def mm(left, right):
    return jnp.dot(left, right, preferred_element_type=jnp.float32)


def contract_rows(left, right):
    return dot(left, right, 0, 0)


def times_transpose(left, right):
    return dot(left, right, 1, 1)


def tuned_plane():
    return lax.axis_size("seq") == 2 and lax.axis_size("shard") == 4 and lax.axis_size("blk") == 4


def gather_inputs(x, mats, vecs):
    nb = lax.axis_size("blk")
    if not tuned_plane():
        x_all = lax.all_gather(x, "blk", axis=0)
        mats = [lax.all_gather(w, PLANE, axis=0, tiled=True) for w in mats]
        vecs = [lax.all_gather(v, PLANE, axis=0, tiled=True) for v in vecs]
        return x_all, mats, vecs
    sizes = [v.shape[0] for v in vecs]
    packed = jnp.concatenate(vecs)
    packed = jnp.pad(packed, (0, 32 * 128 - packed.shape[0])).reshape(32, 128)
    out = gather_all(x, [packed] + list(mats), nb)
    flat = out[1].reshape(8, 32 * 128)
    whole, at = [], 0
    for size in sizes:
        whole.append(flat[:, at:at + size].reshape(8 * size))
        at += size
    return out[0], [w.reshape(-1, w.shape[-1]) for w in out[2:]], whole


def gather_line(arrays):
    nb = lax.axis_size("blk")
    if not tuned_plane():
        return [lax.all_gather(a, "blk", axis=0) for a in arrays]
    return line_gather(arrays, nb)


def reduce_grads(mats, vecs):
    nb = lax.axis_size("blk")
    if not tuned_plane():
        def total(g):
            part = lax.psum_scatter(g.astype(jnp.bfloat16), PLANE, scatter_dimension=0, tiled=True)
            return lax.psum(part, "blk").astype(jnp.float32)
        return [total(g) for g in mats], [total(g) for g in vecs]
    rows = [v.shape[0] // 8 for v in vecs]
    packed = jnp.concatenate([v.reshape(8, -1) for v in vecs], axis=1)
    packed = jnp.pad(packed, ((0, 0), (0, 16 * 256 - packed.shape[1])))
    args = [g.astype(jnp.bfloat16).reshape(2, 2, 2, g.shape[0] // 8, g.shape[1]) for g in mats]
    out = reduce_all(args + [packed.reshape(2, 2, 2, 16, 256)], nb)
    flat = out[-1].reshape(-1)
    parts, at = [], 0
    for n in rows:
        parts.append(flat[at:at + n])
        at += n
    return list(out[:-1]), parts


def per_device(
    tokens, segments, live_mask, query_weight, key_weight, value_weight, out_weight,
    query_bias, value_bias, out_bias, first_gain, first_shift, up_weight, up_bias,
    down_weight, down_bias, second_gain, second_shift, cotangent,
):
    inputs = tokens[0]
    rows, width = inputs.shape
    nb = lax.axis_size("blk")
    place = lax.axis_index("blk")
    seg, live = segments[0], live_mask[0]
    total = seg.shape[0]
    x_all, mats, vecs = gather_inputs(
        inputs,
        [query_weight, key_weight, value_weight, out_weight, up_weight, down_weight],
        [query_bias, value_bias, out_bias, first_gain, first_shift, up_bias, down_bias, second_gain, second_shift],
    )
    wq, wk, wv, wo, wup, wdn = mats
    bq, bv, bo, g1, s1, bup, bdn, g2, s2 = [v.astype(jnp.float32) for v in vecs]
    start = place * rows
    codes = jnp.where(live > 0, seg, -1 - jnp.arange(total, dtype=jnp.int32))
    own_codes = lax.dynamic_slice_in_dim(codes, start, rows)
    own_seg = lax.dynamic_slice_in_dim(seg, start, rows)
    low = jnp.sum((seg < own_seg[0]).astype(jnp.int32))
    high = jnp.sum((seg <= own_seg[rows - 1]).astype(jnp.int32))
    span = jnp.stack([low // TILE, (high + TILE - 1) // TILE])

    xs = x_all.reshape(total, width)
    scale = HEAD_DIM ** (-0.5)
    q_all = ((mm(xs, wq) + bq) * scale).astype(jnp.bfloat16)
    k_all = mm(xs, wk).astype(jnp.bfloat16)
    v_all = (mm(xs, wv) + bv).astype(jnp.bfloat16)
    q, k, v = [lax.dynamic_slice_in_dim(a, start, rows) for a in (q_all, k_all, v_all)]
    summed, attended, lse = attention(q, k_all, v_all, codes, own_codes, span)

    first_sum = inputs.astype(jnp.float32) + (mm(attended, wo) + bo)
    first_norm, first_pull = jax.vjp(normalize, first_sum, g1, s1)
    first_low = first_norm.astype(jnp.bfloat16)
    hidden = mm(first_low, wup) + bup
    gated, gate_pull = jax.vjp(smooth_gate, hidden)
    gated_low = gated.astype(jnp.bfloat16)
    second_sum = first_norm + (mm(gated_low, wdn) + bdn)
    result, second_pull = jax.vjp(normalize, second_sum, g2, s2)
    second_grad, g2_grad, s2_grad = second_pull(cotangent[0].astype(jnp.float32))
    bdn_grad = jnp.sum(second_grad, axis=0)
    second_low = second_grad.astype(jnp.bfloat16)
    wdn_grad = contract_rows(gated_low, second_low)
    (hidden_grad,) = gate_pull(times_transpose(second_low, wdn))
    bup_grad = jnp.sum(hidden_grad, axis=0)
    hidden_low = hidden_grad.astype(jnp.bfloat16)
    wup_grad = contract_rows(first_low, hidden_low)
    norm_grad = second_grad + times_transpose(hidden_low, wup)
    first_grad, g1_grad, s1_grad = first_pull(norm_grad)
    bo_grad = jnp.sum(first_grad, axis=0)
    first_grad_low = first_grad.astype(jnp.bfloat16)
    wo_grad = contract_rows(attended, first_grad_low)
    do = times_transpose(first_grad_low, wo).astype(jnp.bfloat16)

    stats, delta = row_stats(do, summed, lse)
    do_all, stats_all = gather_line([do, stats])
    stats_all = jnp.transpose(stats_all, (1, 2, 0, 3)).reshape(stats.shape[0], 8, total)
    r, rk, dv = attention_grad(
        q, k, v, do, lse, delta, q_all, k_all, v_all, do_all.reshape(total, width), stats_all,
        codes, own_codes, span,
    )
    bq_grad = jnp.sum(r, axis=0)
    bv_grad = jnp.sum(dv, axis=0)
    rq = r.astype(jnp.bfloat16)
    rv = dv.astype(jnp.bfloat16)
    wq_grad = contract_rows(inputs, rq)
    wk_grad = contract_rows(inputs, rk)
    wv_grad = contract_rows(inputs, rv)
    token_grad = first_grad + times_transpose(rq, wq) + times_transpose(rk, wk) + times_transpose(rv, wv)

    big, small = reduce_grads(
        [wdn_grad, wup_grad, wo_grad, wq_grad, wk_grad, wv_grad],
        [bq_grad, bv_grad, bo_grad, g1_grad, s1_grad, bup_grad, bdn_grad, g2_grad, s2_grad],
    )
    rdn, rup, ro, rwq, rwk, rwv = big
    return (
        result.astype(jnp.bfloat16)[None], token_grad.astype(jnp.bfloat16)[None],
        rwq, rwk, rwv, ro, small[0], small[1], small[2], small[3], small[4],
        rup, small[5], rdn, small[6], small[7], small[8],
    )


def solution(mesh):
    flat = P(PLANE, "blk", None)
    mat = P(PLANE, None)
    vec = P(PLANE)
    return jax.shard_map(
        per_device,
        mesh=mesh,
        in_specs=(
            flat, mat, mat, mat, mat, mat, mat, vec, vec, vec, vec, vec, mat, vec, mat, vec, vec, vec, flat,
        ),
        out_specs=(flat, flat, mat, mat, mat, mat, vec, vec, vec, vec, vec, mat, vec, mat, vec, vec, vec),
        check_vma=False,
    )
```

```python
import functools
import jax
import jax.numpy as jnp
from jax import lax
from jax.experimental import pallas as pl
from jax.experimental.pallas import tpu as pltpu
from jax.sharding import PartitionSpec as P

MESH = pl.DeviceIdType.MESH
ANY = pl.BlockSpec(memory_space=pl.ANY)
VMEM_LIMIT = 56 << 20
VM = pl.BlockSpec(memory_space=pltpu.VMEM)


class Place:
    def __init__(self):
        b = lax.axis_index("blk")
        s = lax.axis_index("seq")
        h = lax.axis_index("shard")
        x = h // 2
        c = h % 2
        self.b, self.s, self.h, self.x, self.c = b, s, h, x, c
        self.X = (b, s, (1 - x) * 2 + c)
        self.Y = (b, 1 - s, h)
        self.C = (b, s, x * 2 + 1 - c)
        self.L = (b - 1, s, h)
        self.R = (b + 1, s, h)
        self.me = s * 4 + h
        self.xi = s * 4 + (1 - x) * 2 + c
        self.yi = (1 - s) * 4 + h
        self.di = (1 - s) * 4 + (1 - x) * 2 + c

    def z(self, j):
        return (j, self.s, self.h)


def enter(p, nb, plane, line):
    bar = pltpu.get_barrier_semaphore()
    count = 0
    if plane:
        for peer in (p.X, p.Y, p.C):
            pl.semaphore_signal(bar, inc=1, device_id=peer, device_id_type=MESH)
        count = count + 3
    if line == "near":
        @pl.when(p.b > 0)
        def _():
            pl.semaphore_signal(bar, inc=1, device_id=p.L, device_id_type=MESH)

        @pl.when(p.b < nb - 1)
        def _():
            pl.semaphore_signal(bar, inc=1, device_id=p.R, device_id_type=MESH)
        count = count + jnp.where(p.b > 0, 1, 0) + jnp.where(p.b < nb - 1, 1, 0)
    if line == "all":
        for j in range(nb):
            @pl.when(p.b != j)
            def _():
                pl.semaphore_signal(bar, inc=1, device_id=p.z(j), device_id_type=MESH)
        count = count + nb - 1
    pl.semaphore_wait(bar, count)


def rcopy(src, dst, ss, rs, dev):
    return pltpu.make_async_remote_copy(
        src_ref=src, dst_ref=dst, send_sem=ss, recv_sem=rs, device_id=dev, device_id_type=MESH
    )


class LineGather:
    def __init__(self, p, nb, own, out, ssem, rsem):
        self.p, self.nb, self.own, self.out, self.ssem, self.rsem = p, nb, own, out, ssem, rsem

    def _copies(self, t):
        p, nb = self.p, self.nb
        rb = p.b - t
        lb = p.b + t
        src_r = self.own if t == 0 else self.out.at[jnp.maximum(rb, 0)]
        src_l = self.own if t == 0 else self.out.at[jnp.minimum(lb, nb - 1)]
        right = rcopy(src_r, self.out.at[jnp.maximum(rb, 0)], self.ssem.at[0, t], self.rsem.at[0, t], p.R)
        left = rcopy(src_l, self.out.at[jnp.minimum(lb, nb - 1)], self.ssem.at[1, t], self.rsem.at[1, t], p.L)
        return right, left, (rb >= 0) & (p.b < nb - 1), (lb <= nb - 1) & (p.b > 0)

    def start(self, t):
        right, left, cr, cl = self._copies(t)
        pl.when(cr)(right.start)
        pl.when(cl)(left.start)

    def wait_recv(self, t):
        p, nb = self.p, self.nb
        right, left, _, _ = self._copies(t)
        pl.when(p.b - 1 - t >= 0)(right.wait_recv)
        pl.when(p.b + 1 + t <= nb - 1)(left.wait_recv)

    def wait_send(self, t):
        right, left, cr, cl = self._copies(t)
        pl.when(cr)(right.wait_send)
        pl.when(cl)(left.wait_send)


class PlaneGather:
    def __init__(self, p, own, out, ssem, rsem, lsem):
        self.p = p
        rows = own.shape[0]
        half = rows // 2
        lo, hi = pl.ds(0, half), pl.ds(half, half)
        o = out
        self.x = rcopy(own, o.at[p.me], ssem.at[0], rsem.at[0], p.X)
        self.y = rcopy(own, o.at[p.me], ssem.at[1], rsem.at[1], p.Y)
        self.c = rcopy(own, o.at[p.me], ssem.at[2], rsem.at[2], p.C)
        self.local = pltpu.make_async_copy(own, o.at[p.me], lsem)
        self.fx = rcopy(o.at[p.yi, hi], o.at[p.yi, hi], ssem.at[3], rsem.at[3], p.X)
        self.fy = rcopy(o.at[p.xi, lo], o.at[p.xi, lo], ssem.at[4], rsem.at[4], p.Y)
        self.cx = rcopy(o.at[p.xi], o.at[p.xi], ssem.at[5], rsem.at[5], p.C)
        self.cy = rcopy(o.at[p.yi], o.at[p.yi], ssem.at[6], rsem.at[6], p.C)
        self.cd0 = rcopy(o.at[p.di, lo], o.at[p.di, lo], ssem.at[7], rsem.at[7], p.C)
        self.cd1 = rcopy(o.at[p.di, hi], o.at[p.di, hi], ssem.at[8], rsem.at[8], p.C)

    def start(self):
        self.x.start(); self.y.start(); self.c.start(); self.local.start()

    def forward(self):
        self.x.wait_recv()
        self.fy.start()
        self.cx.start()
        self.y.wait_recv()
        self.fx.start()
        self.cy.start()

    def diag(self):
        self.fy.wait_recv()
        self.cd0.start()
        self.fx.wait_recv()
        self.cd1.start()

    def finish(self):
        self.local.wait()
        self.c.wait_recv(); self.cx.wait_recv(); self.cy.wait_recv()
        self.cd0.wait_recv(); self.cd1.wait_recv()

    def drain(self):
        for k in (self.x, self.y, self.c, self.fx, self.fy, self.cx, self.cy, self.cd0, self.cd1):
            k.wait_send()


def gather_kernel(nb, nw, *refs):
    x_ref, ws = refs[0], refs[1:1 + nw]
    xall, outs = refs[1 + nw], refs[2 + nw:2 + 2 * nw]
    zs, zr, ws_s, ws_r, ls = refs[2 + 2 * nw:]
    p = Place()
    enter(p, nb, True, "near")
    line = LineGather(p, nb, x_ref, xall, zs, zr)
    own = pltpu.make_async_copy(x_ref, xall.at[p.b], ls.at[nw])
    g = [PlaneGather(p, ws[i], outs[i], ws_s.at[i], ws_r.at[i], ls.at[i]) for i in range(nw)]
    n0 = nw - 2
    line.start(0)
    own.start()
    for k in g[:n0 + 1]:
        k.start()
    for k in g[:n0]:
        k.forward()
    g[n0 + 1].start()
    line.wait_recv(0)
    if nb > 2:
        line.start(1)
    g[n0].forward()
    for t in range(1, nb - 2):
        line.wait_recv(t)
        line.start(t + 1)
    g[n0 + 1].forward()
    for k in g:
        k.diag()
    line.wait_recv(nb - 2)
    for k in g:
        k.finish()
    own.wait()
    for t in range(nb - 1):
        line.wait_send(t)
    for k in g:
        k.drain()


def gather_all(x, weights, nb):
    nw = len(weights)
    outs = (jax.ShapeDtypeStruct((nb,) + x.shape, x.dtype),) + tuple(
        jax.ShapeDtypeStruct((8,) + w.shape, w.dtype) for w in weights
    )
    return pl.pallas_call(
        functools.partial(gather_kernel, nb, nw),
        out_shape=outs,
        in_specs=[VM] * (1 + nw),
        out_specs=(ANY,) * (1 + nw),
        scratch_shapes=[
            pltpu.SemaphoreType.DMA((2, nb - 1)),
            pltpu.SemaphoreType.DMA((2, nb - 1)),
            pltpu.SemaphoreType.DMA((nw, 9)),
            pltpu.SemaphoreType.DMA((nw, 9)),
            pltpu.SemaphoreType.DMA((nw + 1,)),
        ],
        compiler_params=pltpu.CompilerParams(
            collective_id=1, has_side_effects=True, vmem_limit_bytes=VMEM_LIMIT
        ),
        name="gather_all",
    )(x, *weights)


def row_loop(rows, chunk, body):
    if rows == chunk:
        body(0)
    else:
        def step(i, _):
            body(pl.multiple_of(i * chunk, chunk))
            return 0
        lax.fori_loop(0, rows // chunk, step, 0)


class PlaneReduce:
    def __init__(self, p, nb, g, out, buf, ss, rs, ls):
        self.p, self.nb, self.out = p, nb, out
        self.G, self.P, self.BX, self.BY, self.CX, self.CY, self.Z, self.O = buf
        self.R, self.C = g.shape[-2:]
        self.dt = g.dtype
        self.ss, self.rs = ss, rs
        R, C = self.R, self.C
        h = R // 2
        self.h = h
        lo, hi = pl.ds(0, h), pl.ds(h, h)
        self.chunk = 16 if C > 1024 else (48 if h % 48 == 0 else h)
        self.own = pltpu.make_async_copy(g.at[:, :, p.c], self.G, ls)
        self.cA = rcopy(g.at[:, :, 1 - p.c], self.P, ss.at[0], rs.at[0], p.C)
        self.cBX = rcopy(self.P.at[:, 1 - p.x, lo], self.BX, ss.at[1], rs.at[1], p.X)
        self.cBY = rcopy(self.P.at[1 - p.s, :, hi], self.BY, ss.at[2], rs.at[2], p.Y)
        self.cCX = rcopy(self.P.at[p.s, 1 - p.x, hi], self.CX, ss.at[3], rs.at[3], p.X)
        self.cCY = rcopy(self.P.at[1 - p.s, p.x, lo], self.CY, ss.at[4], rs.at[4], p.Y)
        self.F = self.P.at[p.s, p.x]

    def quarter(self, ref, j):
        R, C = self.R, self.C
        if isinstance(j, int):
            return ref.at[pl.ds((j // 2) * (R // 2), R // 2), pl.ds((j % 2) * (C // 2), C // 2)]
        r = pl.multiple_of((j // 2) * (R // 2), R // 2)
        c = pl.multiple_of((j % 2) * (C // 2), C // 2)
        return ref.at[pl.ds(r, R // 2), pl.ds(c, C // 2)]

    def a_start(self):
        self.cA.start()
        self.own.start()

    def b_start(self):
        self.own.wait()
        self.cA.wait_recv()

        def block(i, _):
            s, x = i // 2, i % 2

            def body(r):
                rows = pl.ds(r, self.chunk)
                self.P[s, x, rows] = (
                    self.G[s, x, rows].astype(jnp.float32) + self.P[s, x, rows].astype(jnp.float32)
                ).astype(self.dt)
            row_loop(self.R, self.chunk, body)
            return 0
        lax.fori_loop(0, 4, block, 0)
        self.cBX.start()
        self.cBY.start()

    def _add(self, dst, src):
        def body(r):
            rows = pl.ds(r, self.chunk)
            dst[rows] = (dst[rows].astype(jnp.float32) + src[rows].astype(jnp.float32)).astype(self.dt)
        row_loop(self.h, self.chunk, body)

    def c_start(self):
        p, h = self.p, self.h
        lo, hi = pl.ds(0, h), pl.ds(h, h)
        self.cBX.wait_recv()
        self._add(self.P.at[1 - p.s, p.x, lo], self.BX.at[1 - p.s])
        self.cCY.start()
        self.cBY.wait_recv()
        self._add(self.P.at[p.s, 1 - p.x, hi], self.BY.at[1 - p.x])
        self.cCX.start()
        self._add(self.P.at[p.s, p.x, lo], self.BX.at[p.s])
        self._add(self.P.at[p.s, p.x, hi], self.BY.at[p.x])

    def _z1(self, j, slot):
        return rcopy(self.quarter(self.F, j), self.Z.at[slot], self.ss.at[5 + j], self.rs.at[5 + slot], self.p.z(j))

    def _z2(self, j, slot):
        q = self.quarter(self.O, slot)
        return rcopy(q, q, self.ss.at[5 + self.nb + j], self.rs.at[5 + self.nb + slot], self.p.z(j))

    def d_start(self):
        p, h, nb = self.p, self.h, self.nb
        lo, hi = pl.ds(0, h), pl.ds(h, h)
        self.cCY.wait_recv()
        self._add(self.F.at[lo], self.CY)
        self.cCX.wait_recv()
        self._add(self.F.at[hi], self.CX)
        for j in range(nb):
            @pl.when(p.b != j)
            def _():
                self._z1(j, p.b).start()

    def e_start(self):
        p, nb = self.p, self.nb
        mine = self.quarter(self.F, p.b)
        total = self.quarter(self.O, p.b)
        for i in range(nb):
            @pl.when(p.b != i)
            def _():
                self._z1(i, i).wait_recv()

        def body(r):
            rows = pl.ds(r, self.chunk)
            acc = mine[rows].astype(jnp.float32)
            for d in range(1, nb):
                acc = acc + self.Z[(p.b + d) % nb, rows].astype(jnp.float32)
            total[rows] = acc.astype(self.dt)
        row_loop(self.h, self.chunk, body)
        for j in range(nb):
            @pl.when(p.b != j)
            def _():
                self._z2(j, p.b).start()

    def finish(self):
        p, nb = self.p, self.nb
        for i in range(nb):
            @pl.when(p.b != i)
            def _():
                self._z2(i, i).wait_recv()

        def body(r):
            rows = pl.ds(r, self.chunk)
            self.out[rows] = self.O[rows].astype(jnp.float32)
        row_loop(self.R, self.chunk, body)

    def drain(self):
        for k in (self.cA, self.cBX, self.cBY, self.cCX, self.cCY):
            k.wait_send()
        for j in range(self.nb):
            @pl.when(self.p.b != j)
            def _():
                self._z1(j, self.p.b).wait_send()
                self._z2(j, self.p.b).wait_send()


def reduce_scratch(shape, dt, nb):
    R, C = shape
    h = R // 2
    return [
        pltpu.VMEM((2, 2, R, C), dt),
        pltpu.VMEM((2, 2, R, C), dt),
        pltpu.VMEM((2, h, C), dt),
        pltpu.VMEM((2, h, C), dt),
        pltpu.VMEM((h, C), dt),
        pltpu.VMEM((h, C), dt),
        pltpu.VMEM((nb, h, C // 2), dt),
        pltpu.VMEM((R, C), dt),
    ]


def wave(items, stages):
    n, m = len(items), len(stages)
    for step in range(n + m - 1):
        for k in range(m):
            i = step - k
            if 0 <= i < n:
                getattr(items[i], stages[k])()


NBUF = 8


def reducers(p, nb, nw, gs, outs, bufs, ss, rs, ls):
    return [
        PlaneReduce(
            p, nb, gs[i], outs[i], bufs[NBUF * i:NBUF * (i + 1)], ss.at[i], rs.at[i], ls.at[i]
        )
        for i in range(nw)
    ]


def reduce_kernel(nb, nw, *refs):
    gs, outs = refs[:nw], refs[nw:2 * nw]
    bufs = refs[2 * nw:(2 + NBUF) * nw]
    ss, rs, ls = refs[(2 + NBUF) * nw:]
    p = Place()
    enter(p, nb, True, "all")
    items = reducers(p, nb, nw, gs, outs, bufs, ss, rs, ls)
    for k in items:
        k.a_start()
    wave(items, ("b_start", "c_start", "d_start", "e_start"))
    for k in items:
        k.finish()
    for k in items:
        k.drain()


def reduce_all(grads, nb):
    nw = len(grads)
    scratch = []
    for g in grads:
        scratch += reduce_scratch(g.shape[-2:], g.dtype, nb)
    ns = 5 + 2 * nb
    return pl.pallas_call(
        functools.partial(reduce_kernel, nb, nw),
        out_shape=tuple(jax.ShapeDtypeStruct(g.shape[-2:], jnp.float32) for g in grads),
        in_specs=[ANY] * nw,
        out_specs=(VM,) * nw,
        scratch_shapes=scratch + [
            pltpu.SemaphoreType.DMA((nw, ns)), pltpu.SemaphoreType.DMA((nw, ns)), pltpu.SemaphoreType.DMA((nw,)),
        ],
        compiler_params=pltpu.CompilerParams(
            collective_id=3, has_side_effects=True, vmem_limit_bytes=VMEM_LIMIT
        ),
        name="reduce_all",
    )(*grads)


HEAD_DIM = 64
PAIR = 128
MASKED = -1e30
TILE = 512


def dot(a, b, ca, cb):
    return lax.dot_general(a, b, (((ca,), (cb,)), ((), ())), preferred_element_type=jnp.float32)


def left_lanes(shape):
    return lax.broadcasted_iota(jnp.int32, shape, 1) < HEAD_DIM


def one_head(pair, left, first):
    keep = left if first else jnp.logical_not(left)
    return jnp.where(keep, pair, jnp.zeros_like(pair))


def lane_groups(op, a):
    out = a[:, :PAIR]
    for g in range(1, a.shape[1] // PAIR):
        out = op(out, a[:, g * PAIR:(g + 1) * PAIR])
    return out


def attn_fwd_kernel(span, col_ref, row_ref, q_ref, k_ref, v_ref, o_ref, ob_ref, lse_ref, s_ref, m_ref, l_ref, acc_ref):
    rows = q_ref.shape[0]
    left = left_lanes((rows, PAIR))
    m_ref[...] = jnp.full_like(m_ref, MASKED)
    l_ref[...] = jnp.zeros_like(l_ref)
    acc_ref[...] = jnp.zeros_like(acc_ref)
    q = q_ref[...]
    heads = [one_head(q, left, i == 0) for i in range(2)]
    codes = col_ref[...]

    def score(t, _):
        at = pl.multiple_of(t * TILE, TILE)
        k = k_ref[pl.ds(at, TILE), :]
        mask = codes == row_ref[:, pl.ds(at, TILE)]
        for i in range(2):
            s = jnp.where(mask, dot(heads[i], k, 1, 1), MASKED)
            s_ref[i, t] = s
            m_ref[i] = jnp.maximum(m_ref[i], lane_groups(jnp.maximum, s))
        return 0

    lax.fori_loop(span[0], span[1], score, 0)
    tops = [jnp.max(m_ref[i], axis=1, keepdims=True) for i in range(2)]

    def mix(t, _):
        v = v_ref[pl.ds(pl.multiple_of(t * TILE, TILE), TILE), :]
        parts = []
        for i in range(2):
            p = jnp.exp(s_ref[i, t] - tops[i])
            l_ref[i] += lane_groups(jnp.add, p)
            parts.append(dot(p.astype(jnp.bfloat16), v, 1, 0))
        acc_ref[...] += jnp.where(left, parts[0], parts[1])
        return 0

    lax.fori_loop(span[0], span[1], mix, 0)
    sums = [jnp.sum(l_ref[i], axis=1, keepdims=True) for i in range(2)]
    total = jnp.where(left, sums[0], sums[1])
    o = acc_ref[...] / total
    o_ref[...] = o
    ob_ref[...] = o.astype(jnp.bfloat16)
    lse_ref[...] = jnp.where(left, tops[0], tops[1]) + jnp.log(total)


def attention(q, k_all, v_all, codes, own_codes, span):
    rows, width = q.shape
    total = k_all.shape[0]
    pairs = width // PAIR
    own = pl.BlockSpec((rows, PAIR), lambda h, s: (0, h))
    every = pl.BlockSpec((total, PAIR), lambda h, s: (0, h))
    return pl.pallas_call(
        attn_fwd_kernel,
        grid_spec=pltpu.PrefetchScalarGridSpec(
            num_scalar_prefetch=1,
            grid=(pairs,),
            in_specs=[
                pl.BlockSpec((rows, 1), lambda h, s: (0, 0)),
                pl.BlockSpec((1, total), lambda h, s: (0, 0)),
                own, every, every,
            ],
            out_specs=[own, own, own],
            scratch_shapes=[
                pltpu.VMEM((2, total // TILE, rows, TILE), jnp.float32),
                pltpu.VMEM((2, rows, PAIR), jnp.float32),
                pltpu.VMEM((2, rows, PAIR), jnp.float32),
                pltpu.VMEM((rows, PAIR), jnp.float32),
            ],
        ),
        out_shape=[
            jax.ShapeDtypeStruct((rows, width), jnp.float32),
            jax.ShapeDtypeStruct((rows, width), jnp.bfloat16),
            jax.ShapeDtypeStruct((rows, width), jnp.float32),
        ],
        compiler_params=pltpu.CompilerParams(vmem_limit_bytes=48 << 20),
        name="attention",
    )(span, own_codes.reshape(rows, 1), codes.reshape(1, total), q, k_all, v_all)


def stats_kernel(g_ref, o_ref, lse_ref, out_ref, delta_ref):
    rows = g_ref.shape[0]
    left = left_lanes((rows, PAIR))
    t = g_ref[...].astype(jnp.float32) * o_ref[...]
    d0 = jnp.sum(jnp.where(left, t, 0.0), axis=1, keepdims=True)
    d1 = jnp.sum(jnp.where(left, 0.0, t), axis=1, keepdims=True)
    delta_ref[...] = jnp.where(left, d0, d1)
    lane = lax.broadcasted_iota(jnp.int32, (rows, PAIR), 1)
    lse = lse_ref[...]
    packed = jnp.where(lane == 0, lse[:, :1], jnp.where(lane == 1, lse[:, HEAD_DIM:HEAD_DIM + 1], jnp.where(lane == 2, d0, d1)))
    out_ref[0] = packed.T[:8]


def row_stats(grad, o, lse):
    rows, width = grad.shape
    pairs = width // PAIR
    own = pl.BlockSpec((rows, PAIR), lambda h: (0, h))
    return pl.pallas_call(
        stats_kernel,
        grid=(pairs,),
        in_specs=[own, own, own],
        out_specs=[pl.BlockSpec((1, 8, rows), lambda h: (h, 0, 0)), own],
        out_shape=[
            jax.ShapeDtypeStruct((pairs, 8, rows), jnp.float32),
            jax.ShapeDtypeStruct((rows, width), jnp.float32),
        ],
        name="row_stats",
    )(grad, o, lse)


def attn_bwd_kernel(span, col_ref, row_ref, q_ref, k_ref, v_ref, g_ref, lse_ref, delta_ref,
                    qa_ref, ka_ref, va_ref, ga_ref, st_ref, dq_ref, dk_ref, dv_ref):
    rows = q_ref.shape[0]
    left = left_lanes((rows, PAIR))
    dq_ref[...] = jnp.zeros_like(dq_ref)
    dk_ref[...] = jnp.zeros_like(dk_ref)
    dv_ref[...] = jnp.zeros_like(dv_ref)
    codes = col_ref[...]
    qs = [one_head(q_ref[...], left, i == 0) for i in range(2)]
    ks = [one_head(k_ref[...], left, i == 0) for i in range(2)]
    vs = [one_head(v_ref[...], left, i == 0) for i in range(2)]
    gs = [one_head(g_ref[...], left, i == 0) for i in range(2)]
    lses = [lse_ref[:, i * HEAD_DIM:i * HEAD_DIM + 1] for i in range(2)]
    deltas = [delta_ref[:, i * HEAD_DIM:i * HEAD_DIM + 1] for i in range(2)]

    def step(t, _):
        at = pl.multiple_of(t * TILE, TILE)
        tile = pl.ds(at, TILE)
        mask = codes == row_ref[:, tile]
        k, v, q, g = ka_ref[tile, :], va_ref[tile, :], qa_ref[tile, :], ga_ref[tile, :]
        dqs, dks, dvs = [], [], []
        for i in range(2):
            s = jnp.where(mask, dot(qs[i], k, 1, 1), MASKED)
            p = jnp.exp(s - lses[i])
            dp = dot(gs[i], v, 1, 1)
            ds = (p * (dp - deltas[i])).astype(jnp.bfloat16)
            dqs.append(dot(ds, k, 1, 0))
            st = jnp.where(mask, dot(ks[i], q, 1, 1), MASKED)
            pt = jnp.exp(st - st_ref[0, i:i + 1, tile])
            dvs.append(dot(pt.astype(jnp.bfloat16), g, 1, 0))
            dpt = dot(vs[i], g, 1, 1)
            dst = (pt * (dpt - st_ref[0, 2 + i:3 + i, tile])).astype(jnp.bfloat16)
            dks.append(dot(dst, q, 1, 0))
        dq_ref[...] += jnp.where(left, dqs[0], dqs[1])
        dk_ref[...] += jnp.where(left, dks[0], dks[1])
        dv_ref[...] += jnp.where(left, dvs[0], dvs[1])
        return 0

    lax.fori_loop(span[0], span[1], step, 0)


def attention_grad(q, k, v, g, lse, delta, q_all, k_all, v_all, g_all, stats, codes, own_codes, span):
    rows, width = q.shape
    total = k_all.shape[0]
    pairs = width // PAIR
    own = pl.BlockSpec((rows, PAIR), lambda h, s: (0, h))
    every = pl.BlockSpec((total, PAIR), lambda h, s: (0, h))
    return pl.pallas_call(
        attn_bwd_kernel,
        grid_spec=pltpu.PrefetchScalarGridSpec(
            num_scalar_prefetch=1,
            grid=(pairs,),
            in_specs=[
                pl.BlockSpec((rows, 1), lambda h, s: (0, 0)),
                pl.BlockSpec((1, total), lambda h, s: (0, 0)),
                own, own, own, own, own, own, every, every, every, every,
                pl.BlockSpec((1, 8, total), lambda h, s: (h, 0, 0)),
            ],
            out_specs=[own, own, own],
        ),
        out_shape=[
            jax.ShapeDtypeStruct((rows, width), jnp.float32),
            jax.ShapeDtypeStruct((rows, width), jnp.float32),
            jax.ShapeDtypeStruct((rows, width), jnp.float32),
        ],
        compiler_params=pltpu.CompilerParams(vmem_limit_bytes=48 << 20),
        name="attention_grad",
    )(span, own_codes.reshape(rows, 1), codes.reshape(1, total), q, k, v, g, lse, delta, q_all, k_all, v_all, g_all, stats)


class AttentionGrad:
    def __init__(self, codes, rows, q, k, v, g, lse, delta, stats, own, dq, dk, dv):
        self.codes, self.rows = codes, rows
        self.q, self.k, self.v, self.g = q, k, v, g
        self.lse, self.delta, self.stats = lse, delta, stats
        self.own = own
        self.dq, self.dk, self.dv = dq, dk, dv
        self.n = dq.shape[0]
        self.pairs = dq.shape[1] // PAIR

    def queries(self, j, first):
        own = self.own

        def pair(h, _):
            left = left_lanes((self.n, PAIR))
            lanes = pl.ds(pl.multiple_of(h * PAIR, PAIR), PAIR)
            mask = self.codes[...] == self.rows[j]
            q, g = self.q[own, :, lanes], self.g[own, :, lanes]
            k, v = self.k[j, :, lanes], self.v[j, :, lanes]
            lse, delta = self.lse[:, lanes], self.delta[:, lanes]
            parts = []
            for i in range(2):
                at = slice(i * HEAD_DIM, i * HEAD_DIM + 1)
                s = jnp.where(mask, dot(one_head(q, left, i == 0), k, 1, 1), MASKED)
                p = jnp.exp(s - lse[:, at])
                dp = dot(one_head(g, left, i == 0), v, 1, 1)
                ds = (p * (dp - delta[:, at])).astype(jnp.bfloat16)
                parts.append(dot(ds, k, 1, 0))
            new = jnp.where(left, parts[0], parts[1])
            if first:
                self.dq[:, lanes] = new
            else:
                self.dq[:, lanes] += new
            return 0

        lax.fori_loop(0, self.pairs, pair, 0)

    def keys(self, j, first):
        own = self.own

        def pair(h, _):
            left = left_lanes((self.n, PAIR))
            lanes = pl.ds(pl.multiple_of(h * PAIR, PAIR), PAIR)
            mask = self.codes[...] == self.rows[j]
            k, v = self.k[own, :, lanes], self.v[own, :, lanes]
            q, g = self.q[j, :, lanes], self.g[j, :, lanes]
            dks, dvs = [], []
            for i in range(2):
                st = jnp.where(mask, dot(one_head(k, left, i == 0), q, 1, 1), MASKED)
                pt = jnp.exp(st - self.stats[j, h, i:i + 1])
                dvs.append(dot(pt.astype(jnp.bfloat16), g, 1, 0))
                dpt = dot(one_head(v, left, i == 0), g, 1, 1)
                dst = (pt * (dpt - self.stats[j, h, 2 + i:3 + i])).astype(jnp.bfloat16)
                dks.append(dot(dst, q, 1, 0))
            dk, dv = jnp.where(left, dks[0], dks[1]), jnp.where(left, dvs[0], dvs[1])
            if first:
                self.dk[:, lanes] = dk
                self.dv[:, lanes] = dv
            else:
                self.dk[:, lanes] += dk
                self.dv[:, lanes] += dv
            return 0

        lax.fori_loop(0, self.pairs, pair, 0)


def backward_kernel(nb, nw, *refs):
    codes, rows, g_own, st_own, lse, delta, q_hbm, k_hbm, v_hbm = refs[:9]
    gs = refs[9:9 + nw]
    dq, dk, dv = refs[9 + nw:12 + nw]
    outs = refs[12 + nw:12 + 2 * nw]
    rest = refs[12 + 2 * nw:]
    q, k, v, g, stats, zs, zr, ls = rest[:8]
    bufs = rest[8:8 + NBUF * nw]
    ss, rs, rls = rest[8 + NBUF * nw:]
    p = Place()
    loads = [
        pltpu.make_async_copy(a, b, ls.at[i])
        for i, (a, b) in enumerate(((k_hbm, k), (v_hbm, v), (q_hbm, q), (g_own, g.at[p.b]), (st_own, stats.at[p.b])))
    ]
    for c in loads:
        c.start()
    enter(p, nb, True, "all")
    lines = [
        LineGather(p, nb, g_own, g, zs.at[0], zr.at[0]),
        LineGather(p, nb, st_own, stats, zs.at[1], zr.at[1]),
    ]
    items = reducers(p, nb, nw, gs, outs, bufs, ss, rs, rls)
    for c in lines:
        c.start(0)
    for c in items:
        c.a_start()
    work = AttentionGrad(codes, rows, q, k, v, g, lse, delta, stats, p.b, dq, dk, dv)
    for c in loads:
        c.wait()

    def arrived(t):
        @pl.when(p.b - 1 - t >= 0)
        def _():
            work.keys(jnp.maximum(p.b - 1 - t, 0), False)

        @pl.when(p.b + 1 + t <= nb - 1)
        def _():
            work.keys(jnp.minimum(p.b + 1 + t, nb - 1), False)

    work.queries(p.b, True)
    items[0].b_start()
    work.queries((p.b + 1) % nb, False)
    for c in items[1:]:
        c.b_start()
    work.queries((p.b + 2) % nb, False)
    for c in lines:
        c.wait_recv(0)
        c.start(1)
    items[0].c_start()
    work.queries((p.b + 3) % nb, False)
    items[1].c_start()
    work.keys(p.b, True)
    for c in lines:
        c.wait_recv(1)
        c.start(2)
    items[0].d_start()
    arrived(0)
    items[2].c_start()
    items[1].d_start()
    arrived(1)
    items[2].d_start()
    items[0].e_start()
    for c in lines:
        c.wait_recv(2)
    items[1].e_start()
    arrived(2)
    items[2].e_start()
    for c in items:
        c.finish()
    for t in range(nb - 1):
        for c in lines:
            c.wait_send(t)
    for c in items:
        c.drain()


def backward(codes, own_codes, do, stats, lse, delta, q_all, k_all, v_all, grads, nb):
    rows, width = do.shape
    nw = len(grads)
    scratch = []
    for g in grads:
        scratch += reduce_scratch(g.shape[-2:], g.dtype, nb)
    ns = 5 + 2 * nb
    block = jax.ShapeDtypeStruct((rows, width), jnp.float32)
    every = pltpu.VMEM((nb, rows, width), jnp.bfloat16)
    return pl.pallas_call(
        functools.partial(backward_kernel, nb, nw),
        out_shape=(block,) * 3 + tuple(jax.ShapeDtypeStruct(g.shape[-2:], jnp.float32) for g in grads),
        in_specs=[VM, VM, VM, VM, VM, VM, ANY, ANY, ANY] + [ANY] * nw,
        out_specs=(VM,) * (3 + nw),
        scratch_shapes=[
            every, every, every, every,
            pltpu.VMEM((nb,) + stats.shape, jnp.float32),
            pltpu.SemaphoreType.DMA((2, 2, nb - 1)),
            pltpu.SemaphoreType.DMA((2, 2, nb - 1)),
            pltpu.SemaphoreType.DMA((5,)),
        ] + scratch + [
            pltpu.SemaphoreType.DMA((nw, ns)), pltpu.SemaphoreType.DMA((nw, ns)), pltpu.SemaphoreType.DMA((nw,)),
        ],
        compiler_params=pltpu.CompilerParams(
            collective_id=4, has_side_effects=True, vmem_limit_bytes=60 << 20
        ),
        name="backward",
    )(own_codes.reshape(rows, 1), codes.reshape(nb, 1, rows), do, stats, lse, delta, q_all, k_all, v_all, *grads)


EPSILON = 1e-06
PLANE = ("seq", "shard")


def normalize(hidden, gain, shift):
    center = hidden - jnp.mean(hidden, axis=-1, keepdims=True)
    spread = jnp.mean(center * center, axis=-1, keepdims=True)
    return center * lax.rsqrt(spread + EPSILON) * gain + shift


def smooth_gate(hidden):
    return jax.nn.gelu(hidden, approximate=False)


def mm(left, right):
    return jnp.dot(left, right, preferred_element_type=jnp.float32)


def contract_rows(left, right):
    return dot(left, right, 0, 0)


def times_transpose(left, right):
    return dot(left, right, 1, 1)


def tuned_plane():
    return lax.axis_size("seq") == 2 and lax.axis_size("shard") == 4 and lax.axis_size("blk") == 4


def gather_inputs(x, mats, vecs):
    nb = lax.axis_size("blk")
    if not tuned_plane():
        x_all = lax.all_gather(x, "blk", axis=0)
        mats = [lax.all_gather(w, PLANE, axis=0, tiled=True) for w in mats]
        vecs = [lax.all_gather(v, PLANE, axis=0, tiled=True) for v in vecs]
        return x_all, mats, vecs
    sizes = [v.shape[0] for v in vecs]
    packed = jnp.concatenate(vecs)
    packed = jnp.pad(packed, (0, 32 * 128 - packed.shape[0])).reshape(32, 128)
    out = gather_all(x, [packed] + list(mats), nb)
    flat = out[1].reshape(8, 32 * 128)
    whole, at = [], 0
    for size in sizes:
        whole.append(flat[:, at:at + size].reshape(8 * size))
        at += size
    return out[0], [w.reshape(-1, w.shape[-1]) for w in out[2:]], whole


def gather_line(arrays):
    return [lax.all_gather(a, "blk", axis=0) for a in arrays]


def shards(g):
    return g.astype(jnp.bfloat16).reshape(2, 2, 2, g.shape[0] // 8, g.shape[1])


def reduce_grads(mats, vecs):
    nb = lax.axis_size("blk")
    if not tuned_plane():
        def total(g):
            part = lax.psum_scatter(g.astype(jnp.bfloat16), PLANE, scatter_dimension=0, tiled=True)
            return lax.psum(part, "blk").astype(jnp.float32)
        return [total(g) for g in mats], [total(g) for g in vecs]
    rows = [v.shape[0] // 8 for v in vecs]
    packed = jnp.concatenate([v.reshape(8, -1) for v in vecs], axis=1)
    packed = jnp.pad(packed, ((0, 0), (0, 16 * 256 - packed.shape[1])))
    args = [shards(g) for g in mats]
    out = reduce_all(args + [packed.reshape(2, 2, 2, 16, 256)], nb)
    flat = out[-1].reshape(-1)
    parts, at = [], 0
    for n in rows:
        parts.append(flat[at:at + n])
        at += n
    return list(out[:-1]), parts


def per_device(
    tokens, segments, live_mask, query_weight, key_weight, value_weight, out_weight,
    query_bias, value_bias, out_bias, first_gain, first_shift, up_weight, up_bias,
    down_weight, down_bias, second_gain, second_shift, cotangent,
):
    inputs = tokens[0]
    rows, width = inputs.shape
    nb = lax.axis_size("blk")
    place = lax.axis_index("blk")
    seg, live = segments[0], live_mask[0]
    total = seg.shape[0]
    x_all, mats, vecs = gather_inputs(
        inputs,
        [query_weight, key_weight, value_weight, out_weight, up_weight, down_weight],
        [query_bias, value_bias, out_bias, first_gain, first_shift, up_bias, down_bias, second_gain, second_shift],
    )
    wq, wk, wv, wo, wup, wdn = mats
    bq, bv, bo, g1, s1, bup, bdn, g2, s2 = [v.astype(jnp.float32) for v in vecs]
    start = place * rows
    codes = jnp.where(live > 0, seg, -1 - jnp.arange(total, dtype=jnp.int32))
    own_codes = lax.dynamic_slice_in_dim(codes, start, rows)
    own_seg = lax.dynamic_slice_in_dim(seg, start, rows)
    low = jnp.sum((seg < own_seg[0]).astype(jnp.int32))
    high = jnp.sum((seg <= own_seg[rows - 1]).astype(jnp.int32))
    span = jnp.stack([low // TILE, (high + TILE - 1) // TILE])

    xs = x_all.reshape(total, width)
    scale = HEAD_DIM ** (-0.5)
    q_all = ((mm(xs, wq) + bq) * scale).astype(jnp.bfloat16)
    k_all = mm(xs, wk).astype(jnp.bfloat16)
    v_all = (mm(xs, wv) + bv).astype(jnp.bfloat16)
    q, k, v = [lax.dynamic_slice_in_dim(a, start, rows) for a in (q_all, k_all, v_all)]
    summed, attended, lse = attention(q, k_all, v_all, codes, own_codes, span)

    first_sum = inputs.astype(jnp.float32) + (mm(attended, wo) + bo)
    first_norm, first_pull = jax.vjp(normalize, first_sum, g1, s1)
    first_low = first_norm.astype(jnp.bfloat16)
    hidden = mm(first_low, wup) + bup
    gated, gate_pull = jax.vjp(smooth_gate, hidden)
    gated_low = gated.astype(jnp.bfloat16)
    second_sum = first_norm + (mm(gated_low, wdn) + bdn)
    result, second_pull = jax.vjp(normalize, second_sum, g2, s2)
    second_grad, g2_grad, s2_grad = second_pull(cotangent[0].astype(jnp.float32))
    bdn_grad = jnp.sum(second_grad, axis=0)
    second_low = second_grad.astype(jnp.bfloat16)
    wdn_grad = contract_rows(gated_low, second_low)
    (hidden_grad,) = gate_pull(times_transpose(second_low, wdn))
    bup_grad = jnp.sum(hidden_grad, axis=0)
    hidden_low = hidden_grad.astype(jnp.bfloat16)
    wup_grad = contract_rows(first_low, hidden_low)
    norm_grad = second_grad + times_transpose(hidden_low, wup)
    first_grad, g1_grad, s1_grad = first_pull(norm_grad)
    bo_grad = jnp.sum(first_grad, axis=0)
    first_grad_low = first_grad.astype(jnp.bfloat16)
    wo_grad = contract_rows(attended, first_grad_low)
    do = times_transpose(first_grad_low, wo).astype(jnp.bfloat16)

    stats, delta = row_stats(do, summed, lse)
    if tuned_plane():
        early = [shards(g) for g in (wdn_grad, wup_grad, wo_grad)]
        dq, dk, dv, rdn, rup, ro = backward(
            codes, own_codes, do, stats, lse, delta, *[a.reshape(nb, rows, width) for a in (q_all, k_all, v_all)],
            early, nb,
        )
    else:
        do_all, stats_all = gather_line([do, stats])
        stats_all = jnp.transpose(stats_all, (1, 2, 0, 3)).reshape(stats.shape[0], 8, total)
        dq, dk, dv = attention_grad(
            q, k, v, do, lse, delta, q_all, k_all, v_all, do_all.reshape(total, width), stats_all,
            codes, own_codes, span,
        )
        (rdn, rup, ro), _ = reduce_grads([wdn_grad, wup_grad, wo_grad], [])
    r = dq * scale
    rk = dk.astype(jnp.bfloat16)
    bq_grad = jnp.sum(r, axis=0)
    bv_grad = jnp.sum(dv, axis=0)
    rq = r.astype(jnp.bfloat16)
    rv = dv.astype(jnp.bfloat16)
    wq_grad = contract_rows(inputs, rq)
    wk_grad = contract_rows(inputs, rk)
    wv_grad = contract_rows(inputs, rv)
    token_grad = first_grad + times_transpose(rq, wq) + times_transpose(rk, wk) + times_transpose(rv, wv)

    big, small = reduce_grads(
        [wq_grad, wk_grad, wv_grad],
        [bq_grad, bv_grad, bo_grad, g1_grad, s1_grad, bup_grad, bdn_grad, g2_grad, s2_grad],
    )
    rwq, rwk, rwv = big
    return (
        result.astype(jnp.bfloat16)[None], token_grad.astype(jnp.bfloat16)[None],
        rwq, rwk, rwv, ro, small[0], small[1], small[2], small[3], small[4],
        rup, small[5], rdn, small[6], small[7], small[8],
    )


def solution(mesh):
    flat = P(PLANE, "blk", None)
    mat = P(PLANE, None)
    vec = P(PLANE)
    return jax.shard_map(
        per_device,
        mesh=mesh,
        in_specs=(
            flat, mat, mat, mat, mat, mat, mat, vec, vec, vec, vec, vec, mat, vec, mat, vec, vec, vec, flat,
        ),
        out_specs=(flat, flat, mat, mat, mat, mat, vec, vec, vec, vec, vec, mat, vec, mat, vec, vec, vec),
        check_vma=False,
    )
```

```python
import functools
import jax
import jax.numpy as jnp
from jax import lax
from jax.experimental import pallas as pl
from jax.experimental.pallas import tpu as pltpu
from jax.sharding import PartitionSpec as P

MESH = pl.DeviceIdType.MESH
ANY = pl.BlockSpec(memory_space=pl.ANY)
VMEM_LIMIT = 56 << 20
VM = pl.BlockSpec(memory_space=pltpu.VMEM)


class Place:
    def __init__(self):
        b = lax.axis_index("blk")
        s = lax.axis_index("seq")
        h = lax.axis_index("shard")
        x = h // 2
        c = h % 2
        self.b, self.s, self.h, self.x, self.c = b, s, h, x, c
        self.X = (b, s, (1 - x) * 2 + c)
        self.Y = (b, 1 - s, h)
        self.C = (b, s, x * 2 + 1 - c)
        self.L = (b - 1, s, h)
        self.R = (b + 1, s, h)
        self.me = s * 4 + h
        self.xi = s * 4 + (1 - x) * 2 + c
        self.yi = (1 - s) * 4 + h
        self.di = (1 - s) * 4 + (1 - x) * 2 + c

    def z(self, j):
        return (j, self.s, self.h)


def enter(p, nb, plane, line):
    bar = pltpu.get_barrier_semaphore()
    count = 0
    if plane:
        for peer in (p.X, p.Y, p.C):
            pl.semaphore_signal(bar, inc=1, device_id=peer, device_id_type=MESH)
        count = count + 3
    if line == "near":
        @pl.when(p.b > 0)
        def _():
            pl.semaphore_signal(bar, inc=1, device_id=p.L, device_id_type=MESH)

        @pl.when(p.b < nb - 1)
        def _():
            pl.semaphore_signal(bar, inc=1, device_id=p.R, device_id_type=MESH)
        count = count + jnp.where(p.b > 0, 1, 0) + jnp.where(p.b < nb - 1, 1, 0)
    if line == "all":
        for j in range(nb):
            @pl.when(p.b != j)
            def _():
                pl.semaphore_signal(bar, inc=1, device_id=p.z(j), device_id_type=MESH)
        count = count + nb - 1
    pl.semaphore_wait(bar, count)


def rcopy(src, dst, ss, rs, dev):
    return pltpu.make_async_remote_copy(
        src_ref=src, dst_ref=dst, send_sem=ss, recv_sem=rs, device_id=dev, device_id_type=MESH
    )


class LineGather:
    def __init__(self, p, nb, own, out, ssem, rsem):
        self.p, self.nb, self.own, self.out, self.ssem, self.rsem = p, nb, own, out, ssem, rsem

    def _copies(self, t):
        p, nb = self.p, self.nb
        rb = p.b - t
        lb = p.b + t
        src_r = self.own if t == 0 else self.out.at[jnp.maximum(rb, 0)]
        src_l = self.own if t == 0 else self.out.at[jnp.minimum(lb, nb - 1)]
        right = rcopy(src_r, self.out.at[jnp.maximum(rb, 0)], self.ssem.at[0, t], self.rsem.at[0, t], p.R)
        left = rcopy(src_l, self.out.at[jnp.minimum(lb, nb - 1)], self.ssem.at[1, t], self.rsem.at[1, t], p.L)
        return right, left, (rb >= 0) & (p.b < nb - 1), (lb <= nb - 1) & (p.b > 0)

    def start(self, t):
        right, left, cr, cl = self._copies(t)
        pl.when(cr)(right.start)
        pl.when(cl)(left.start)

    def wait_recv(self, t):
        p, nb = self.p, self.nb
        right, left, _, _ = self._copies(t)
        pl.when(p.b - 1 - t >= 0)(right.wait_recv)
        pl.when(p.b + 1 + t <= nb - 1)(left.wait_recv)

    def wait_send(self, t):
        right, left, cr, cl = self._copies(t)
        pl.when(cr)(right.wait_send)
        pl.when(cl)(left.wait_send)


class PlaneGather:
    def __init__(self, p, own, out, ssem, rsem, lsem):
        rows = own.shape[0]
        half = rows // 2

        def whole(i):
            return out.at[pl.ds(pl.multiple_of(i * rows, rows), rows)]

        def low(i):
            return out.at[pl.ds(pl.multiple_of(i * rows, rows), half)]

        def high(i):
            return out.at[pl.ds(pl.multiple_of(i * rows + half, half), half)]

        def send(k, src, dst, dev):
            return rcopy(src, dst, ssem.at[k], rsem.at[k], dev)

        self.x = send(0, own, whole(p.me), p.X)
        self.y = send(1, own, whole(p.me), p.Y)
        self.c = send(2, own, whole(p.me), p.C)
        self.local = pltpu.make_async_copy(own, whole(p.me), lsem)
        self.fx = send(3, high(p.yi), high(p.yi), p.X)
        self.fy = send(4, low(p.xi), low(p.xi), p.Y)
        self.cx = send(5, whole(p.xi), whole(p.xi), p.C)
        self.cy = send(6, whole(p.yi), whole(p.yi), p.C)
        self.cd0 = send(7, low(p.di), low(p.di), p.C)
        self.cd1 = send(8, high(p.di), high(p.di), p.C)

    def start(self):
        for k in (self.x, self.y, self.c, self.local):
            k.start()

    def forward(self):
        self.x.wait_recv()
        self.fy.start()
        self.cx.start()
        self.y.wait_recv()
        self.fx.start()
        self.cy.start()

    def diag(self):
        self.fy.wait_recv()
        self.cd0.start()
        self.fx.wait_recv()
        self.cd1.start()

    def finish(self):
        self.local.wait()
        for k in (self.c, self.cx, self.cy, self.cd0, self.cd1):
            k.wait_recv()

    def drain(self):
        for k in (self.x, self.y, self.c, self.fx, self.fy, self.cx, self.cy, self.cd0, self.cd1):
            k.wait_send()


def row_loop(rows, chunk, body):
    if rows == chunk:
        body(0)
    else:
        def step(i, _):
            body(pl.multiple_of(i * chunk, chunk))
            return 0
        lax.fori_loop(0, rows // chunk, step, 0)


class PlaneReduce:
    def __init__(self, p, nb, g, out, buf, ss, rs, ls):
        self.p, self.nb, self.out = p, nb, out
        self.G, self.P, self.BX, self.BY, self.CX, self.CY, self.Z, self.O = buf
        self.R, self.C = g.shape[-2:]
        self.dt = g.dtype
        self.ss, self.rs = ss, rs
        R, C = self.R, self.C
        h = R // 2
        self.h = h
        lo, hi = pl.ds(0, h), pl.ds(h, h)
        self.chunk = 16 if C > 1024 else (48 if h % 48 == 0 else h)
        self.own = pltpu.make_async_copy(g.at[:, :, p.c], self.G, ls)
        self.cA = rcopy(g.at[:, :, 1 - p.c], self.P, ss.at[0], rs.at[0], p.C)
        self.cBX = rcopy(self.P.at[:, 1 - p.x, lo], self.BX, ss.at[1], rs.at[1], p.X)
        self.cBY = rcopy(self.P.at[1 - p.s, :, hi], self.BY, ss.at[2], rs.at[2], p.Y)
        self.cCX = rcopy(self.P.at[p.s, 1 - p.x, hi], self.CX, ss.at[3], rs.at[3], p.X)
        self.cCY = rcopy(self.P.at[1 - p.s, p.x, lo], self.CY, ss.at[4], rs.at[4], p.Y)
        self.F = self.P.at[p.s, p.x]

    def quarter(self, ref, j):
        R, C = self.R, self.C
        if isinstance(j, int):
            return ref.at[pl.ds((j // 2) * (R // 2), R // 2), pl.ds((j % 2) * (C // 2), C // 2)]
        r = pl.multiple_of((j // 2) * (R // 2), R // 2)
        c = pl.multiple_of((j % 2) * (C // 2), C // 2)
        return ref.at[pl.ds(r, R // 2), pl.ds(c, C // 2)]

    def a_start(self):
        self.cA.start()
        self.own.start()

    def b_start(self):
        self.own.wait()
        self.cA.wait_recv()

        def block(i, _):
            s, x = i // 2, i % 2

            def body(r):
                rows = pl.ds(r, self.chunk)
                self.P[s, x, rows] = (
                    self.G[s, x, rows].astype(jnp.float32) + self.P[s, x, rows].astype(jnp.float32)
                ).astype(self.dt)
            row_loop(self.R, self.chunk, body)
            return 0
        lax.fori_loop(0, 4, block, 0)
        self.cBX.start()
        self.cBY.start()

    def _add(self, dst, src):
        def body(r):
            rows = pl.ds(r, self.chunk)
            dst[rows] = (dst[rows].astype(jnp.float32) + src[rows].astype(jnp.float32)).astype(self.dt)
        row_loop(self.h, self.chunk, body)

    def c_start(self):
        p, h = self.p, self.h
        lo, hi = pl.ds(0, h), pl.ds(h, h)
        self.cBX.wait_recv()
        self._add(self.P.at[1 - p.s, p.x, lo], self.BX.at[1 - p.s])
        self.cCY.start()
        self.cBY.wait_recv()
        self._add(self.P.at[p.s, 1 - p.x, hi], self.BY.at[1 - p.x])
        self.cCX.start()
        self._add(self.P.at[p.s, p.x, lo], self.BX.at[p.s])
        self._add(self.P.at[p.s, p.x, hi], self.BY.at[p.x])

    def _z1(self, j, slot):
        return rcopy(self.quarter(self.F, j), self.Z.at[slot], self.ss.at[5 + j], self.rs.at[5 + slot], self.p.z(j))

    def _z2(self, j, slot):
        q = self.quarter(self.O, slot)
        return rcopy(q, q, self.ss.at[5 + self.nb + j], self.rs.at[5 + self.nb + slot], self.p.z(j))

    def d_start(self):
        p, h, nb = self.p, self.h, self.nb
        lo, hi = pl.ds(0, h), pl.ds(h, h)
        self.cCY.wait_recv()
        self._add(self.F.at[lo], self.CY)
        self.cCX.wait_recv()
        self._add(self.F.at[hi], self.CX)
        for j in range(nb):
            @pl.when(p.b != j)
            def _():
                self._z1(j, p.b).start()

    def e_start(self):
        p, nb = self.p, self.nb
        mine = self.quarter(self.F, p.b)
        total = self.quarter(self.O, p.b)
        for i in range(nb):
            @pl.when(p.b != i)
            def _():
                self._z1(i, i).wait_recv()

        def body(r):
            rows = pl.ds(r, self.chunk)
            acc = mine[rows].astype(jnp.float32)
            for d in range(1, nb):
                acc = acc + self.Z[(p.b + d) % nb, rows].astype(jnp.float32)
            total[rows] = acc.astype(self.dt)
        row_loop(self.h, self.chunk, body)
        for j in range(nb):
            @pl.when(p.b != j)
            def _():
                self._z2(j, p.b).start()

    def finish(self):
        p, nb = self.p, self.nb
        for i in range(nb):
            @pl.when(p.b != i)
            def _():
                self._z2(i, i).wait_recv()

        def body(r):
            rows = pl.ds(r, self.chunk)
            self.out[rows] = self.O[rows].astype(jnp.float32)
        row_loop(self.R, self.chunk, body)

    def drain(self):
        for k in (self.cA, self.cBX, self.cBY, self.cCX, self.cCY):
            k.wait_send()
        for j in range(self.nb):
            @pl.when(self.p.b != j)
            def _():
                self._z1(j, self.p.b).wait_send()
                self._z2(j, self.p.b).wait_send()


def reduce_scratch(shape, dt, nb):
    R, C = shape
    h = R // 2
    return [
        pltpu.VMEM((2, 2, R, C), dt),
        pltpu.VMEM((2, 2, R, C), dt),
        pltpu.VMEM((2, h, C), dt),
        pltpu.VMEM((2, h, C), dt),
        pltpu.VMEM((h, C), dt),
        pltpu.VMEM((h, C), dt),
        pltpu.VMEM((nb, h, C // 2), dt),
        pltpu.VMEM((R, C), dt),
    ]


def wave(items, stages):
    n, m = len(items), len(stages)
    for step in range(n + m - 1):
        for k in range(m):
            i = step - k
            if 0 <= i < n:
                getattr(items[i], stages[k])()


NBUF = 8


def reducers(p, nb, nw, gs, outs, bufs, ss, rs, ls):
    return [
        PlaneReduce(
            p, nb, gs[i], outs[i], bufs[NBUF * i:NBUF * (i + 1)], ss.at[i], rs.at[i], ls.at[i]
        )
        for i in range(nw)
    ]


def reduce_kernel(nb, nw, *refs):
    gs, outs = refs[:nw], refs[nw:2 * nw]
    bufs = refs[2 * nw:(2 + NBUF) * nw]
    ss, rs, ls = refs[(2 + NBUF) * nw:]
    p = Place()
    enter(p, nb, True, "all")
    items = reducers(p, nb, nw, gs, outs, bufs, ss, rs, ls)
    for k in items:
        k.a_start()
    wave(items, ("b_start", "c_start", "d_start", "e_start"))
    for k in items:
        k.finish()
    for k in items:
        k.drain()


def reduce_all(grads, nb):
    nw = len(grads)
    scratch = []
    for g in grads:
        scratch += reduce_scratch(g.shape[-2:], g.dtype, nb)
    ns = 5 + 2 * nb
    return pl.pallas_call(
        functools.partial(reduce_kernel, nb, nw),
        out_shape=tuple(jax.ShapeDtypeStruct(g.shape[-2:], jnp.float32) for g in grads),
        in_specs=[ANY] * nw,
        out_specs=(VM,) * nw,
        scratch_shapes=scratch + [
            pltpu.SemaphoreType.DMA((nw, ns)), pltpu.SemaphoreType.DMA((nw, ns)), pltpu.SemaphoreType.DMA((nw,)),
        ],
        compiler_params=pltpu.CompilerParams(
            collective_id=3, has_side_effects=True, vmem_limit_bytes=VMEM_LIMIT
        ),
        name="reduce_all",
    )(*grads)


HEAD_DIM = 64
PAIR = 128
MASKED = -1e30
TILE = 512


def dot(a, b, ca, cb):
    return lax.dot_general(a, b, (((ca,), (cb,)), ((), ())), preferred_element_type=jnp.float32)


def left_lanes(shape):
    return lax.broadcasted_iota(jnp.int32, shape, 1) < HEAD_DIM


def one_head(pair, left, first):
    keep = left if first else jnp.logical_not(left)
    return jnp.where(keep, pair, jnp.zeros_like(pair))


def lane_groups(op, a):
    out = a[:, :PAIR]
    for g in range(1, a.shape[1] // PAIR):
        out = op(out, a[:, g * PAIR:(g + 1) * PAIR])
    return out


def attn_fwd_kernel(span, col_ref, row_ref, q_ref, k_ref, v_ref, o_ref, ob_ref, lse_ref, s_ref, m_ref, l_ref, acc_ref):
    rows = q_ref.shape[0]
    left = left_lanes((rows, PAIR))
    m_ref[...] = jnp.full_like(m_ref, MASKED)
    l_ref[...] = jnp.zeros_like(l_ref)
    acc_ref[...] = jnp.zeros_like(acc_ref)
    q = q_ref[...]
    heads = [one_head(q, left, i == 0) for i in range(2)]
    codes = col_ref[...]

    def score(t, _):
        at = pl.multiple_of(t * TILE, TILE)
        k = k_ref[pl.ds(at, TILE), :]
        mask = codes == row_ref[:, pl.ds(at, TILE)]
        for i in range(2):
            s = jnp.where(mask, dot(heads[i], k, 1, 1), MASKED)
            s_ref[i, t] = s
            m_ref[i] = jnp.maximum(m_ref[i], lane_groups(jnp.maximum, s))
        return 0

    lax.fori_loop(span[0], span[1], score, 0)
    tops = [jnp.max(m_ref[i], axis=1, keepdims=True) for i in range(2)]

    def mix(t, _):
        v = v_ref[pl.ds(pl.multiple_of(t * TILE, TILE), TILE), :]
        parts = []
        for i in range(2):
            p = jnp.exp(s_ref[i, t] - tops[i])
            l_ref[i] += lane_groups(jnp.add, p)
            parts.append(dot(p.astype(jnp.bfloat16), v, 1, 0))
        acc_ref[...] += jnp.where(left, parts[0], parts[1])
        return 0

    lax.fori_loop(span[0], span[1], mix, 0)
    sums = [jnp.sum(l_ref[i], axis=1, keepdims=True) for i in range(2)]
    total = jnp.where(left, sums[0], sums[1])
    o = acc_ref[...] / total
    o_ref[...] = o
    ob_ref[...] = o.astype(jnp.bfloat16)
    lse_ref[...] = jnp.where(left, tops[0], tops[1]) + jnp.log(total)


def attention(q, k_all, v_all, codes, own_codes, span):
    rows, width = q.shape
    total = k_all.shape[0]
    pairs = width // PAIR
    own = pl.BlockSpec((rows, PAIR), lambda h, s: (0, h))
    every = pl.BlockSpec((total, PAIR), lambda h, s: (0, h))
    return pl.pallas_call(
        attn_fwd_kernel,
        grid_spec=pltpu.PrefetchScalarGridSpec(
            num_scalar_prefetch=1,
            grid=(pairs,),
            in_specs=[
                pl.BlockSpec((rows, 1), lambda h, s: (0, 0)),
                pl.BlockSpec((1, total), lambda h, s: (0, 0)),
                own, every, every,
            ],
            out_specs=[own, own, own],
            scratch_shapes=[
                pltpu.VMEM((2, total // TILE, rows, TILE), jnp.float32),
                pltpu.VMEM((2, rows, PAIR), jnp.float32),
                pltpu.VMEM((2, rows, PAIR), jnp.float32),
                pltpu.VMEM((rows, PAIR), jnp.float32),
            ],
        ),
        out_shape=[
            jax.ShapeDtypeStruct((rows, width), jnp.float32),
            jax.ShapeDtypeStruct((rows, width), jnp.bfloat16),
            jax.ShapeDtypeStruct((rows, width), jnp.float32),
        ],
        compiler_params=pltpu.CompilerParams(vmem_limit_bytes=48 << 20),
        name="attention",
    )(span, own_codes.reshape(rows, 1), codes.reshape(1, total), q, k_all, v_all)


def stats_kernel(g_ref, o_ref, lse_ref, out_ref, delta_ref):
    rows = g_ref.shape[0]
    left = left_lanes((rows, PAIR))
    t = g_ref[...].astype(jnp.float32) * o_ref[...]
    d0 = jnp.sum(jnp.where(left, t, 0.0), axis=1, keepdims=True)
    d1 = jnp.sum(jnp.where(left, 0.0, t), axis=1, keepdims=True)
    delta_ref[...] = jnp.where(left, d0, d1)
    lane = lax.broadcasted_iota(jnp.int32, (rows, PAIR), 1)
    lse = lse_ref[...]
    packed = jnp.where(lane == 0, lse[:, :1], jnp.where(lane == 1, lse[:, HEAD_DIM:HEAD_DIM + 1], jnp.where(lane == 2, d0, d1)))
    out_ref[0] = packed.T[:8]


def row_stats(grad, o, lse):
    rows, width = grad.shape
    pairs = width // PAIR
    own = pl.BlockSpec((rows, PAIR), lambda h: (0, h))
    return pl.pallas_call(
        stats_kernel,
        grid=(pairs,),
        in_specs=[own, own, own],
        out_specs=[pl.BlockSpec((1, 8, rows), lambda h: (h, 0, 0)), own],
        out_shape=[
            jax.ShapeDtypeStruct((pairs, 8, rows), jnp.float32),
            jax.ShapeDtypeStruct((rows, width), jnp.float32),
        ],
        name="row_stats",
    )(grad, o, lse)


def attn_bwd_kernel(span, col_ref, row_ref, q_ref, k_ref, v_ref, g_ref, lse_ref, delta_ref,
                    qa_ref, ka_ref, va_ref, ga_ref, st_ref, dq_ref, dk_ref, dv_ref):
    rows = q_ref.shape[0]
    left = left_lanes((rows, PAIR))
    dq_ref[...] = jnp.zeros_like(dq_ref)
    dk_ref[...] = jnp.zeros_like(dk_ref)
    dv_ref[...] = jnp.zeros_like(dv_ref)
    codes = col_ref[...]
    qs = [one_head(q_ref[...], left, i == 0) for i in range(2)]
    ks = [one_head(k_ref[...], left, i == 0) for i in range(2)]
    vs = [one_head(v_ref[...], left, i == 0) for i in range(2)]
    gs = [one_head(g_ref[...], left, i == 0) for i in range(2)]
    lses = [lse_ref[:, i * HEAD_DIM:i * HEAD_DIM + 1] for i in range(2)]
    deltas = [delta_ref[:, i * HEAD_DIM:i * HEAD_DIM + 1] for i in range(2)]

    def step(t, _):
        at = pl.multiple_of(t * TILE, TILE)
        tile = pl.ds(at, TILE)
        mask = codes == row_ref[:, tile]
        k, v, q, g = ka_ref[tile, :], va_ref[tile, :], qa_ref[tile, :], ga_ref[tile, :]
        dqs, dks, dvs = [], [], []
        for i in range(2):
            s = jnp.where(mask, dot(qs[i], k, 1, 1), MASKED)
            p = jnp.exp(s - lses[i])
            dp = dot(gs[i], v, 1, 1)
            ds = (p * (dp - deltas[i])).astype(jnp.bfloat16)
            dqs.append(dot(ds, k, 1, 0))
            st = jnp.where(mask, dot(ks[i], q, 1, 1), MASKED)
            pt = jnp.exp(st - st_ref[0, i:i + 1, tile])
            dvs.append(dot(pt.astype(jnp.bfloat16), g, 1, 0))
            dpt = dot(vs[i], g, 1, 1)
            dst = (pt * (dpt - st_ref[0, 2 + i:3 + i, tile])).astype(jnp.bfloat16)
            dks.append(dot(dst, q, 1, 0))
        dq_ref[...] += jnp.where(left, dqs[0], dqs[1])
        dk_ref[...] += jnp.where(left, dks[0], dks[1])
        dv_ref[...] += jnp.where(left, dvs[0], dvs[1])
        return 0

    lax.fori_loop(span[0], span[1], step, 0)


def attention_grad(q, k, v, g, lse, delta, q_all, k_all, v_all, g_all, stats, codes, own_codes, span):
    rows, width = q.shape
    total = k_all.shape[0]
    pairs = width // PAIR
    own = pl.BlockSpec((rows, PAIR), lambda h, s: (0, h))
    every = pl.BlockSpec((total, PAIR), lambda h, s: (0, h))
    return pl.pallas_call(
        attn_bwd_kernel,
        grid_spec=pltpu.PrefetchScalarGridSpec(
            num_scalar_prefetch=1,
            grid=(pairs,),
            in_specs=[
                pl.BlockSpec((rows, 1), lambda h, s: (0, 0)),
                pl.BlockSpec((1, total), lambda h, s: (0, 0)),
                own, own, own, own, own, own, every, every, every, every,
                pl.BlockSpec((1, 8, total), lambda h, s: (h, 0, 0)),
            ],
            out_specs=[own, own, own],
        ),
        out_shape=[
            jax.ShapeDtypeStruct((rows, width), jnp.float32),
            jax.ShapeDtypeStruct((rows, width), jnp.float32),
            jax.ShapeDtypeStruct((rows, width), jnp.float32),
        ],
        compiler_params=pltpu.CompilerParams(vmem_limit_bytes=48 << 20),
        name="attention_grad",
    )(span, own_codes.reshape(rows, 1), codes.reshape(1, total), q, k, v, g, lse, delta, q_all, k_all, v_all, g_all, stats)


VEC_ROWS = 8


def forward_kernel(nb, *refs):
    x_ref, codes, rows = refs[:3]
    shards_in = refs[3:9]
    vecs_in = refs[9:18]
    wq_o, wk_o, wv_o, wo_o, wup_o, wdn_o = refs[18:24]
    q_o, k_o, v_o = refs[24:27]
    o_ref, ob_ref, lse_ref, vec_ref, bup_ref = refs[27:32]
    rest = refs[32:]
    x_all, wq, wk, wv, pack, packs, q, k, v, m_ref, l_ref = rest[:11]
    zs, zr, gs, gr, gl, ws, es = rest[11:]
    n, width = x_ref.shape
    pairs = width // PAIR
    p = Place()
    own = pltpu.make_async_copy(x_ref, x_all.at[p.b], ws.at[3])
    own.start()
    pack[...] = jnp.zeros_like(pack)
    for i in range(VEC_ROWS):
        pack[i:i + 1, :vecs_in[i].shape[1]] = vecs_in[i][...].astype(jnp.float32)
    for i in range(vecs_in[8].shape[1] // PAIR):
        pack[VEC_ROWS + i:VEC_ROWS + i + 1, :] = vecs_in[8][:, i * PAIR:(i + 1) * PAIR].astype(jnp.float32)
    enter(p, nb, True, "near")
    line = LineGather(p, nb, x_ref, x_all, zs, zr)
    targets = (packs, wq, wk, wv, wo_o, wup_o, wdn_o)
    sources = (pack,) + tuple(shards_in)
    g = [PlaneGather(p, sources[i], targets[i], gs.at[i], gr.at[i], gl.at[i]) for i in range(7)]
    line.start(0)
    for c in g[:5]:
        c.start()
    for c in g[:4]:
        c.forward()
    g[5].start()
    g[6].start()
    for c in g[:4]:
        c.diag()
    for c in g[:4]:
        c.finish()
    own.wait()
    keep = [
        pltpu.make_async_copy(a, b, ws.at[i]) for i, (a, b) in enumerate(((wq, wq_o), (wk, wk_o), (wv, wv_o)))
    ]
    for c in keep:
        c.start()

    piece = width // 8
    r = lax.broadcasted_iota(jnp.int32, (PAIR, width), 0)
    c = lax.broadcasted_iota(jnp.int32, (PAIR, width), 1)
    total = jnp.zeros((2 * VEC_ROWS, width), jnp.float32)
    for i in range(8):
        pick = ((c == r + i * piece) & (r < piece)).astype(jnp.bfloat16)
        total += dot(packs[2 * VEC_ROWS * i:2 * VEC_ROWS * (i + 1), :].astype(jnp.bfloat16), pick, 1, 0)
    vec_ref[...] = total[:VEC_ROWS]
    up_piece = bup_ref.shape[1] // 8
    for i in range(8):
        for t in range(up_piece // PAIR):
            at = i * up_piece + t * PAIR
            row = 2 * VEC_ROWS * i + VEC_ROWS + t
            bup_ref[:, at:at + PAIR] = packs[row:row + 1, :]

    scale = HEAD_DIM ** (-0.5)
    step = 256

    def outs(j, e):
        return [
            pltpu.make_async_copy(a.at[j], b.at[j], es.at[i, e])
            for i, (a, b) in enumerate(((q, q_o), (k, k_o), (v, v_o)))
        ]

    def project(j):
        def columns(t, _):
            at = pl.ds(pl.multiple_of(t * step, step), step)
            xs = x_all[j]
            q[j, :, at] = ((dot(xs, wq[:, at], 1, 0) + vec_ref[0:1, at]) * scale).astype(jnp.bfloat16)
            k[j, :, at] = dot(xs, wk[:, at], 1, 0).astype(jnp.bfloat16)
            v[j, :, at] = (dot(xs, wv[:, at], 1, 0) + vec_ref[1:2, at]).astype(jnp.bfloat16)
            return 0
        lax.fori_loop(0, width // step, columns, 0)

    def attend(j, first):
        def pair(h, _):
            left = left_lanes((n, PAIR))
            lanes = pl.ds(pl.multiple_of(h * PAIR, PAIR), PAIR)
            mask = codes[...] == rows[j]
            qs, ks, vs = q[p.b, :, lanes], k[j, :, lanes], v[j, :, lanes]
            parts, alphas = [], []
            for i in range(2):
                s = jnp.where(mask, dot(one_head(qs, left, i == 0), ks, 1, 1), MASKED)
                top = jnp.max(lane_groups(jnp.maximum, s), axis=1, keepdims=True)
                if first:
                    new = jnp.broadcast_to(top, (n, PAIR))
                else:
                    old = m_ref[2 * h + i]
                    new = jnp.maximum(old, top)
                    alpha = jnp.exp(old - new)
                    alphas.append(alpha)
                e = jnp.exp(s - jnp.concatenate([new] * (n // PAIR), axis=1))
                mass = lane_groups(jnp.add, e)
                m_ref[2 * h + i] = new
                l_ref[2 * h + i] = mass if first else l_ref[2 * h + i] * alpha + mass
                parts.append(dot(e.astype(jnp.bfloat16), vs, 1, 0))
            got = jnp.where(left, parts[0], parts[1])
            if first:
                o_ref[:, lanes] = got
            else:
                o_ref[:, lanes] = o_ref[:, lanes] * jnp.where(left, alphas[0], alphas[1]) + got
            return 0
        lax.fori_loop(0, pairs, pair, 0)

    def block(j, e):
        project(j)
        for c in outs(j, e):
            c.start()
        attend(j, e == 0)

    def left_of(t):
        return p.b - 1 - t >= 0, jnp.maximum(p.b - 1 - t, 0)

    def right_of(t):
        return p.b + 1 + t <= nb - 1, jnp.minimum(p.b + 1 + t, nb - 1)

    def arrived(t):
        for side, (ok, j) in enumerate((left_of(t), right_of(t))):
            @pl.when(ok)
            def _():
                block(j, 1 + 2 * t + side)

    project(p.b)
    for c in outs(p.b, 0):
        c.start()
    line.wait_recv(0)
    line.start(1)
    g[4].forward()
    attend(p.b, True)
    arrived(0)
    g[5].forward()
    line.wait_recv(1)
    line.start(2)
    arrived(1)
    g[6].forward()
    g[4].diag()
    g[5].diag()
    line.wait_recv(2)
    arrived(2)

    def close(h, _):
        left = left_lanes((n, PAIR))
        lanes = pl.ds(pl.multiple_of(h * PAIR, PAIR), PAIR)
        sums = [jnp.sum(l_ref[2 * h + i], axis=1, keepdims=True) for i in range(2)]
        mass = jnp.where(left, sums[0], sums[1])
        out = o_ref[:, lanes] / mass
        o_ref[:, lanes] = out
        ob_ref[:, lanes] = out.astype(jnp.bfloat16)
        lse_ref[:, lanes] = jnp.where(left, m_ref[2 * h], m_ref[2 * h + 1]) + jnp.log(mass)
        return 0
    lax.fori_loop(0, pairs, close, 0)
    g[6].diag()
    for c in g[4:]:
        c.finish()
    for c in keep:
        c.wait()
    for c in outs(p.b, 0):
        c.wait()
    for t in range(nb - 1):
        for side, (ok, j) in enumerate((left_of(t), right_of(t))):
            @pl.when(ok)
            def _():
                for c in outs(j, 1 + 2 * t + side):
                    c.wait()
    for t in range(nb - 1):
        line.wait_send(t)
    for c in g:
        c.drain()


def forward(x, codes, own_codes, weights, vecs, nb):
    n, width = x.shape
    hidden = weights[4].shape[1]
    bf, f32 = jnp.bfloat16, jnp.float32
    every = jax.ShapeDtypeStruct((nb, n, width), bf)
    block = jax.ShapeDtypeStruct((n, width), f32)
    mats = [jax.ShapeDtypeStruct((8 * w.shape[0], w.shape[1]), w.dtype) for w in weights]
    dma = pltpu.SemaphoreType.DMA
    return pl.pallas_call(
        functools.partial(forward_kernel, nb),
        out_shape=(
            *mats, every, every, every, block, jax.ShapeDtypeStruct((n, width), bf), block,
            jax.ShapeDtypeStruct((VEC_ROWS, width), f32), jax.ShapeDtypeStruct((1, hidden), f32),
        ),
        in_specs=[VM] * 18,
        out_specs=(ANY,) * 9 + (VM,) * 5,
        scratch_shapes=[
            pltpu.VMEM((nb, n, width), bf),
            pltpu.VMEM((width, width), bf), pltpu.VMEM((width, width), bf), pltpu.VMEM((width, width), bf),
            pltpu.VMEM((2 * VEC_ROWS, PAIR), f32), pltpu.VMEM((16 * VEC_ROWS, PAIR), f32),
            pltpu.VMEM((nb, n, width), bf), pltpu.VMEM((nb, n, width), bf), pltpu.VMEM((nb, n, width), bf),
            pltpu.VMEM((width // HEAD_DIM, n, PAIR), f32), pltpu.VMEM((width // HEAD_DIM, n, PAIR), f32),
            dma((2, nb - 1)), dma((2, nb - 1)), dma((7, 9)), dma((7, 9)), dma((7,)), dma((4,)), dma((3, 2 * nb)),
        ],
        compiler_params=pltpu.CompilerParams(
            collective_id=1, has_side_effects=True, vmem_limit_bytes=60 << 20
        ),
        name="forward",
    )(
        x, own_codes.reshape(n, 1), codes.reshape(nb, 1, n), *weights, *[v.reshape(1, -1) for v in vecs]
    )


class AttentionGrad:
    def __init__(self, codes, rows, q, k, v, g, lse, delta, stats, own, dq, dk, dv):
        self.codes, self.rows = codes, rows
        self.q, self.k, self.v, self.g = q, k, v, g
        self.lse, self.delta, self.stats = lse, delta, stats
        self.own = own
        self.dq, self.dk, self.dv = dq, dk, dv
        self.n = dq.shape[0]
        self.pairs = dq.shape[1] // PAIR

    def queries(self, j, first):
        own = self.own

        def pair(h, _):
            left = left_lanes((self.n, PAIR))
            lanes = pl.ds(pl.multiple_of(h * PAIR, PAIR), PAIR)
            mask = self.codes[...] == self.rows[j]
            q, g = self.q[own, :, lanes], self.g[own, :, lanes]
            k, v = self.k[j, :, lanes], self.v[j, :, lanes]
            lse, delta = self.lse[:, lanes], self.delta[:, lanes]
            parts = []
            for i in range(2):
                at = slice(i * HEAD_DIM, i * HEAD_DIM + 1)
                s = jnp.where(mask, dot(one_head(q, left, i == 0), k, 1, 1), MASKED)
                p = jnp.exp(s - lse[:, at])
                dp = dot(one_head(g, left, i == 0), v, 1, 1)
                ds = (p * (dp - delta[:, at])).astype(jnp.bfloat16)
                parts.append(dot(ds, k, 1, 0))
            new = jnp.where(left, parts[0], parts[1])
            if first:
                self.dq[:, lanes] = new
            else:
                self.dq[:, lanes] += new
            return 0

        lax.fori_loop(0, self.pairs, pair, 0)

    def keys(self, j, first):
        own = self.own

        def pair(h, _):
            left = left_lanes((self.n, PAIR))
            lanes = pl.ds(pl.multiple_of(h * PAIR, PAIR), PAIR)
            mask = self.codes[...] == self.rows[j]
            k, v = self.k[own, :, lanes], self.v[own, :, lanes]
            q, g = self.q[j, :, lanes], self.g[j, :, lanes]
            dks, dvs = [], []
            for i in range(2):
                st = jnp.where(mask, dot(one_head(k, left, i == 0), q, 1, 1), MASKED)
                pt = jnp.exp(st - self.stats[j, h, i:i + 1])
                dvs.append(dot(pt.astype(jnp.bfloat16), g, 1, 0))
                dpt = dot(one_head(v, left, i == 0), g, 1, 1)
                dst = (pt * (dpt - self.stats[j, h, 2 + i:3 + i])).astype(jnp.bfloat16)
                dks.append(dot(dst, q, 1, 0))
            dk, dv = jnp.where(left, dks[0], dks[1]), jnp.where(left, dvs[0], dvs[1])
            if first:
                self.dk[:, lanes] = dk
                self.dv[:, lanes] = dv
            else:
                self.dk[:, lanes] += dk
                self.dv[:, lanes] += dv
            return 0

        lax.fori_loop(0, self.pairs, pair, 0)


def backward_kernel(nb, nw, *refs):
    codes, rows, g_own, st_own, lse, delta, q_hbm, k_hbm, v_hbm = refs[:9]
    gs = refs[9:9 + nw]
    dq, dk, dv = refs[9 + nw:12 + nw]
    outs = refs[12 + nw:12 + 2 * nw]
    rest = refs[12 + 2 * nw:]
    q, k, v, g, stats, zs, zr, ls = rest[:8]
    bufs = rest[8:8 + NBUF * nw]
    ss, rs, rls = rest[8 + NBUF * nw:]
    p = Place()
    loads = [
        pltpu.make_async_copy(a, b, ls.at[i])
        for i, (a, b) in enumerate(((k_hbm, k), (v_hbm, v), (q_hbm, q), (g_own, g.at[p.b]), (st_own, stats.at[p.b])))
    ]
    for c in loads:
        c.start()
    enter(p, nb, True, "all")
    lines = [
        LineGather(p, nb, g_own, g, zs.at[0], zr.at[0]),
        LineGather(p, nb, st_own, stats, zs.at[1], zr.at[1]),
    ]
    items = reducers(p, nb, nw, gs, outs, bufs, ss, rs, rls)
    for c in lines:
        c.start(0)
    for c in items:
        c.a_start()
    work = AttentionGrad(codes, rows, q, k, v, g, lse, delta, stats, p.b, dq, dk, dv)
    for c in loads:
        c.wait()

    def arrived(t):
        @pl.when(p.b - 1 - t >= 0)
        def _():
            work.keys(jnp.maximum(p.b - 1 - t, 0), False)

        @pl.when(p.b + 1 + t <= nb - 1)
        def _():
            work.keys(jnp.minimum(p.b + 1 + t, nb - 1), False)

    work.queries(p.b, True)
    items[0].b_start()
    work.queries((p.b + 1) % nb, False)
    for c in items[1:]:
        c.b_start()
    work.queries((p.b + 2) % nb, False)
    for c in lines:
        c.wait_recv(0)
        c.start(1)
    items[0].c_start()
    work.queries((p.b + 3) % nb, False)
    items[1].c_start()
    work.keys(p.b, True)
    for c in lines:
        c.wait_recv(1)
        c.start(2)
    items[0].d_start()
    arrived(0)
    items[2].c_start()
    items[1].d_start()
    arrived(1)
    items[2].d_start()
    items[0].e_start()
    for c in lines:
        c.wait_recv(2)
    items[1].e_start()
    arrived(2)
    items[2].e_start()
    for c in items:
        c.finish()
    for t in range(nb - 1):
        for c in lines:
            c.wait_send(t)
    for c in items:
        c.drain()


def backward(codes, own_codes, do, stats, lse, delta, q_all, k_all, v_all, grads, nb):
    rows, width = do.shape
    nw = len(grads)
    scratch = []
    for g in grads:
        scratch += reduce_scratch(g.shape[-2:], g.dtype, nb)
    ns = 5 + 2 * nb
    block = jax.ShapeDtypeStruct((rows, width), jnp.float32)
    every = pltpu.VMEM((nb, rows, width), jnp.bfloat16)
    return pl.pallas_call(
        functools.partial(backward_kernel, nb, nw),
        out_shape=(block,) * 3 + tuple(jax.ShapeDtypeStruct(g.shape[-2:], jnp.float32) for g in grads),
        in_specs=[VM, VM, VM, VM, VM, VM, ANY, ANY, ANY] + [ANY] * nw,
        out_specs=(VM,) * (3 + nw),
        scratch_shapes=[
            every, every, every, every,
            pltpu.VMEM((nb,) + stats.shape, jnp.float32),
            pltpu.SemaphoreType.DMA((2, 2, nb - 1)),
            pltpu.SemaphoreType.DMA((2, 2, nb - 1)),
            pltpu.SemaphoreType.DMA((5,)),
        ] + scratch + [
            pltpu.SemaphoreType.DMA((nw, ns)), pltpu.SemaphoreType.DMA((nw, ns)), pltpu.SemaphoreType.DMA((nw,)),
        ],
        compiler_params=pltpu.CompilerParams(
            collective_id=4, has_side_effects=True, vmem_limit_bytes=60 << 20
        ),
        name="backward",
    )(own_codes.reshape(rows, 1), codes.reshape(nb, 1, rows), do, stats, lse, delta, q_all, k_all, v_all, *grads)


EPSILON = 1e-06
PLANE = ("seq", "shard")


def normalize(hidden, gain, shift):
    center = hidden - jnp.mean(hidden, axis=-1, keepdims=True)
    spread = jnp.mean(center * center, axis=-1, keepdims=True)
    return center * lax.rsqrt(spread + EPSILON) * gain + shift


def smooth_gate(hidden):
    return jax.nn.gelu(hidden, approximate=False)


def mm(left, right):
    return jnp.dot(left, right, preferred_element_type=jnp.float32)


def contract_rows(left, right):
    return dot(left, right, 0, 0)


def times_transpose(left, right):
    return dot(left, right, 1, 1)


def tuned_plane():
    return lax.axis_size("seq") == 2 and lax.axis_size("shard") == 4 and lax.axis_size("blk") == 4


def gather_line(arrays):
    return [lax.all_gather(a, "blk", axis=0) for a in arrays]


def shards(g):
    return g.astype(jnp.bfloat16).reshape(2, 2, 2, g.shape[0] // 8, g.shape[1])


def reduce_grads(mats, vecs):
    nb = lax.axis_size("blk")
    if not tuned_plane():
        def total(g):
            part = lax.psum_scatter(g.astype(jnp.bfloat16), PLANE, scatter_dimension=0, tiled=True)
            return lax.psum(part, "blk").astype(jnp.float32)
        return [total(g) for g in mats], [total(g) for g in vecs]
    rows = [v.shape[0] // 8 for v in vecs]
    packed = jnp.concatenate([v.reshape(8, -1) for v in vecs], axis=1)
    packed = jnp.pad(packed, ((0, 0), (0, 16 * 256 - packed.shape[1])))
    args = [shards(g) for g in mats]
    out = reduce_all(args + [packed.reshape(2, 2, 2, 16, 256)], nb)
    flat = out[-1].reshape(-1)
    parts, at = [], 0
    for n in rows:
        parts.append(flat[at:at + n])
        at += n
    return list(out[:-1]), parts


def per_device(
    tokens, segments, live_mask, query_weight, key_weight, value_weight, out_weight,
    query_bias, value_bias, out_bias, first_gain, first_shift, up_weight, up_bias,
    down_weight, down_bias, second_gain, second_shift, cotangent,
):
    inputs = tokens[0]
    rows, width = inputs.shape
    nb = lax.axis_size("blk")
    place = lax.axis_index("blk")
    seg, live = segments[0], live_mask[0]
    total = seg.shape[0]
    start = place * rows
    codes = jnp.where(live > 0, seg, -1 - jnp.arange(total, dtype=jnp.int32))
    own_codes = lax.dynamic_slice_in_dim(codes, start, rows)
    scale = HEAD_DIM ** (-0.5)
    mats = [query_weight, key_weight, value_weight, out_weight, up_weight, down_weight]
    vecs = [query_bias, value_bias, out_bias, first_gain, first_shift, down_bias, second_gain, second_shift, up_bias]
    if tuned_plane():
        out = forward(inputs, codes, own_codes, mats, vecs, nb)
        wq, wk, wv, wo, wup, wdn, q_all, k_all, v_all, summed, attended, lse, table, bup = out
        bq, bv, bo, g1, s1, bdn, g2, s2 = [table[i] for i in range(8)]
        bup = bup[0]
    else:
        xs = lax.all_gather(inputs, "blk", axis=0, tiled=True)
        wq, wk, wv, wo, wup, wdn = [lax.all_gather(w, PLANE, axis=0, tiled=True) for w in mats]
        whole = [lax.all_gather(v, PLANE, axis=0, tiled=True).astype(jnp.float32) for v in vecs]
        bq, bv, bo, g1, s1, bdn, g2, s2, bup = whole
        own_seg = lax.dynamic_slice_in_dim(seg, start, rows)
        low = jnp.sum((seg < own_seg[0]).astype(jnp.int32))
        high = jnp.sum((seg <= own_seg[rows - 1]).astype(jnp.int32))
        span = jnp.stack([low // TILE, (high + TILE - 1) // TILE])
        q_all = ((mm(xs, wq) + bq) * scale).astype(jnp.bfloat16)
        k_all = mm(xs, wk).astype(jnp.bfloat16)
        v_all = (mm(xs, wv) + bv).astype(jnp.bfloat16)
        q, k, v = [lax.dynamic_slice_in_dim(a, start, rows) for a in (q_all, k_all, v_all)]
        summed, attended, lse = attention(q, k_all, v_all, codes, own_codes, span)

    first_sum = inputs.astype(jnp.float32) + (mm(attended, wo) + bo)
    first_norm, first_pull = jax.vjp(normalize, first_sum, g1, s1)
    first_low = first_norm.astype(jnp.bfloat16)
    hidden = mm(first_low, wup) + bup
    gated, gate_pull = jax.vjp(smooth_gate, hidden)
    gated_low = gated.astype(jnp.bfloat16)
    second_sum = first_norm + (mm(gated_low, wdn) + bdn)
    result, second_pull = jax.vjp(normalize, second_sum, g2, s2)
    second_grad, g2_grad, s2_grad = second_pull(cotangent[0].astype(jnp.float32))
    bdn_grad = jnp.sum(second_grad, axis=0)
    second_low = second_grad.astype(jnp.bfloat16)
    wdn_grad = contract_rows(gated_low, second_low)
    (hidden_grad,) = gate_pull(times_transpose(second_low, wdn))
    bup_grad = jnp.sum(hidden_grad, axis=0)
    hidden_low = hidden_grad.astype(jnp.bfloat16)
    wup_grad = contract_rows(first_low, hidden_low)
    norm_grad = second_grad + times_transpose(hidden_low, wup)
    first_grad, g1_grad, s1_grad = first_pull(norm_grad)
    bo_grad = jnp.sum(first_grad, axis=0)
    first_grad_low = first_grad.astype(jnp.bfloat16)
    wo_grad = contract_rows(attended, first_grad_low)
    do = times_transpose(first_grad_low, wo).astype(jnp.bfloat16)

    stats, delta = row_stats(do, summed, lse)
    if tuned_plane():
        early = [shards(g) for g in (wdn_grad, wup_grad, wo_grad)]
        dq, dk, dv, rdn, rup, ro = backward(
            codes, own_codes, do, stats, lse, delta, q_all, k_all, v_all, early, nb,
        )
    else:
        do_all, stats_all = gather_line([do, stats])
        stats_all = jnp.transpose(stats_all, (1, 2, 0, 3)).reshape(stats.shape[0], 8, total)
        dq, dk, dv = attention_grad(
            q, k, v, do, lse, delta, q_all, k_all, v_all, do_all.reshape(total, width), stats_all,
            codes, own_codes, span,
        )
        (rdn, rup, ro), _ = reduce_grads([wdn_grad, wup_grad, wo_grad], [])
    r = dq * scale
    rk = dk.astype(jnp.bfloat16)
    bq_grad = jnp.sum(r, axis=0)
    bv_grad = jnp.sum(dv, axis=0)
    rq = r.astype(jnp.bfloat16)
    rv = dv.astype(jnp.bfloat16)
    wq_grad = contract_rows(inputs, rq)
    wk_grad = contract_rows(inputs, rk)
    wv_grad = contract_rows(inputs, rv)
    token_grad = first_grad + times_transpose(rq, wq) + times_transpose(rk, wk) + times_transpose(rv, wv)

    big, small = reduce_grads(
        [wq_grad, wk_grad, wv_grad],
        [bq_grad, bv_grad, bo_grad, g1_grad, s1_grad, bup_grad, bdn_grad, g2_grad, s2_grad],
    )
    rwq, rwk, rwv = big
    return (
        result.astype(jnp.bfloat16)[None], token_grad.astype(jnp.bfloat16)[None],
        rwq, rwk, rwv, ro, small[0], small[1], small[2], small[3], small[4],
        rup, small[5], rdn, small[6], small[7], small[8],
    )


def solution(mesh):
    flat = P(PLANE, "blk", None)
    mat = P(PLANE, None)
    vec = P(PLANE)
    return jax.shard_map(
        per_device,
        mesh=mesh,
        in_specs=(
            flat, mat, mat, mat, mat, mat, mat, vec, vec, vec, vec, vec, mat, vec, mat, vec, vec, vec, flat,
        ),
        out_specs=(flat, flat, mat, mat, mat, mat, vec, vec, vec, vec, vec, mat, vec, mat, vec, vec, vec),
        check_vma=False,
    )
```

```python
import functools
import jax
import jax.numpy as jnp
from jax import lax
from jax.experimental import pallas as pl
from jax.experimental.pallas import tpu as pltpu
from jax.sharding import PartitionSpec as P

MESH = pl.DeviceIdType.MESH
ANY = pl.BlockSpec(memory_space=pl.ANY)
VMEM_LIMIT = 56 << 20
VM = pl.BlockSpec(memory_space=pltpu.VMEM)


class Place:
    def __init__(self):
        b = lax.axis_index("blk")
        s = lax.axis_index("seq")
        h = lax.axis_index("shard")
        x = h // 2
        c = h % 2
        self.b, self.s, self.h, self.x, self.c = b, s, h, x, c
        self.X = (b, s, (1 - x) * 2 + c)
        self.Y = (b, 1 - s, h)
        self.C = (b, s, x * 2 + 1 - c)
        self.L = (b - 1, s, h)
        self.R = (b + 1, s, h)
        self.me = s * 4 + h
        self.xi = s * 4 + (1 - x) * 2 + c
        self.yi = (1 - s) * 4 + h
        self.di = (1 - s) * 4 + (1 - x) * 2 + c

    def z(self, j):
        return (j, self.s, self.h)


def enter(p, nb, plane, line):
    bar = pltpu.get_barrier_semaphore()
    count = 0
    if plane:
        for peer in (p.X, p.Y, p.C):
            pl.semaphore_signal(bar, inc=1, device_id=peer, device_id_type=MESH)
        count = count + 3
    if line == "near":
        @pl.when(p.b > 0)
        def _():
            pl.semaphore_signal(bar, inc=1, device_id=p.L, device_id_type=MESH)

        @pl.when(p.b < nb - 1)
        def _():
            pl.semaphore_signal(bar, inc=1, device_id=p.R, device_id_type=MESH)
        count = count + jnp.where(p.b > 0, 1, 0) + jnp.where(p.b < nb - 1, 1, 0)
    if line == "all":
        for j in range(nb):
            @pl.when(p.b != j)
            def _():
                pl.semaphore_signal(bar, inc=1, device_id=p.z(j), device_id_type=MESH)
        count = count + nb - 1
    pl.semaphore_wait(bar, count)


def rcopy(src, dst, ss, rs, dev):
    return pltpu.make_async_remote_copy(
        src_ref=src, dst_ref=dst, send_sem=ss, recv_sem=rs, device_id=dev, device_id_type=MESH
    )


class LineGather:
    def __init__(self, p, nb, own, out, ssem, rsem):
        self.p, self.nb, self.own, self.out, self.ssem, self.rsem = p, nb, own, out, ssem, rsem

    def _copies(self, t):
        p, nb = self.p, self.nb
        rb = p.b - t
        lb = p.b + t
        src_r = self.own if t == 0 else self.out.at[jnp.maximum(rb, 0)]
        src_l = self.own if t == 0 else self.out.at[jnp.minimum(lb, nb - 1)]
        right = rcopy(src_r, self.out.at[jnp.maximum(rb, 0)], self.ssem.at[0, t], self.rsem.at[0, t], p.R)
        left = rcopy(src_l, self.out.at[jnp.minimum(lb, nb - 1)], self.ssem.at[1, t], self.rsem.at[1, t], p.L)
        return right, left, (rb >= 0) & (p.b < nb - 1), (lb <= nb - 1) & (p.b > 0)

    def start(self, t):
        right, left, cr, cl = self._copies(t)
        pl.when(cr)(right.start)
        pl.when(cl)(left.start)

    def wait_recv(self, t):
        p, nb = self.p, self.nb
        right, left, _, _ = self._copies(t)
        pl.when(p.b - 1 - t >= 0)(right.wait_recv)
        pl.when(p.b + 1 + t <= nb - 1)(left.wait_recv)

    def wait_send(self, t):
        right, left, cr, cl = self._copies(t)
        pl.when(cr)(right.wait_send)
        pl.when(cl)(left.wait_send)


class PlaneGather:
    def __init__(self, p, own, out, ssem, rsem, lsem):
        rows = own.shape[0]
        half = rows // 2

        def whole(i):
            return out.at[pl.ds(pl.multiple_of(i * rows, rows), rows)]

        def low(i):
            return out.at[pl.ds(pl.multiple_of(i * rows, rows), half)]

        def high(i):
            return out.at[pl.ds(pl.multiple_of(i * rows + half, half), half)]

        def send(k, src, dst, dev):
            return rcopy(src, dst, ssem.at[k], rsem.at[k], dev)

        self.x = send(0, own, whole(p.me), p.X)
        self.y = send(1, own, whole(p.me), p.Y)
        self.c = send(2, own, whole(p.me), p.C)
        self.local = pltpu.make_async_copy(own, whole(p.me), lsem)
        self.fx = send(3, high(p.yi), high(p.yi), p.X)
        self.fy = send(4, low(p.xi), low(p.xi), p.Y)
        self.cx = send(5, whole(p.xi), whole(p.xi), p.C)
        self.cy = send(6, whole(p.yi), whole(p.yi), p.C)
        self.cd0 = send(7, low(p.di), low(p.di), p.C)
        self.cd1 = send(8, high(p.di), high(p.di), p.C)

    def start(self):
        for k in (self.x, self.y, self.c, self.local):
            k.start()

    def forward(self):
        self.x.wait_recv()
        self.fy.start()
        self.cx.start()
        self.y.wait_recv()
        self.fx.start()
        self.cy.start()

    def diag(self):
        self.fy.wait_recv()
        self.cd0.start()
        self.fx.wait_recv()
        self.cd1.start()

    def finish(self):
        self.local.wait()
        for k in (self.c, self.cx, self.cy, self.cd0, self.cd1):
            k.wait_recv()

    def drain(self):
        for k in (self.x, self.y, self.c, self.fx, self.fy, self.cx, self.cy, self.cd0, self.cd1):
            k.wait_send()


def row_loop(rows, chunk, body):
    if rows == chunk:
        body(0)
    else:
        def step(i, _):
            body(pl.multiple_of(i * chunk, chunk))
            return 0
        lax.fori_loop(0, rows // chunk, step, 0)


class PlaneReduce:
    def __init__(self, p, nb, g, out, buf, stage, ss, rs, ls):
        self.p, self.nb = p, nb
        self.P, self.BX, self.BY, self.CX, self.CY, self.Z = buf
        self.O = out
        self.R, self.C = g.shape[-2:]
        self.dt = g.dtype
        self.ss, self.rs = ss, rs
        h = self.R // 2
        self.h = h
        lo, hi = pl.ds(0, h), pl.ds(h, h)
        self.chunk = 16 if self.C > 1024 else 48
        self.g = g
        self.stage = stage
        self.own = None if stage is None else pltpu.make_async_copy(g.at[:, :, p.c], stage, ls)
        self.cA = rcopy(g.at[:, :, 1 - p.c], self.P, ss.at[0], rs.at[0], p.C)
        self.cBX = rcopy(self.P.at[:, 1 - p.x, lo], self.BX, ss.at[1], rs.at[1], p.X)
        self.cBY = rcopy(self.P.at[1 - p.s, :, hi], self.BY, ss.at[2], rs.at[2], p.Y)
        self.cCX = rcopy(self.P.at[p.s, 1 - p.x, hi], self.CX, ss.at[3], rs.at[3], p.X)
        self.cCY = rcopy(self.P.at[1 - p.s, p.x, lo], self.CY, ss.at[4], rs.at[4], p.Y)
        self.F = self.P.at[p.s, p.x]

    def quarter(self, ref, j):
        R, C = self.R, self.C
        r, c = (j // 2) * (R // 2), (j % 2) * (C // 2)
        if not isinstance(j, int):
            r, c = pl.multiple_of(r, R // 2), pl.multiple_of(c, C // 2)
        return ref.at[pl.ds(r, R // 2), pl.ds(c, C // 2)]

    def a_start(self):
        self.cA.start()

    def own_start(self):
        self.own.start()

    def b_start(self):
        if self.own is not None:
            self.own.wait()
        self.cA.wait_recv()

        def block(i, _):
            s, x = i // 2, i % 2

            def body(r):
                rows = pl.ds(r, self.chunk)
                mine = self.g[s, x, self.p.c, rows] if self.stage is None else self.stage[s, x, rows]
                self.P[s, x, rows] = (
                    mine.astype(jnp.float32) + self.P[s, x, rows].astype(jnp.float32)
                ).astype(self.dt)
            row_loop(self.R, self.chunk, body)
            return 0
        lax.fori_loop(0, 4, block, 0)
        self.cBX.start()
        self.cBY.start()

    def _add(self, dst, src):
        chunk = min(self.chunk * 2, self.h)

        def body(r):
            rows = pl.ds(r, chunk)
            dst[rows] = (dst[rows].astype(jnp.float32) + src[rows].astype(jnp.float32)).astype(self.dt)
        row_loop(self.h, chunk if self.h % chunk == 0 else self.h, body)

    def c_start(self):
        p, h = self.p, self.h
        lo, hi = pl.ds(0, h), pl.ds(h, h)
        self.cBX.wait_recv()
        self._add(self.P.at[1 - p.s, p.x, lo], self.BX.at[1 - p.s])
        self.cCY.start()
        self.cBY.wait_recv()
        self._add(self.P.at[p.s, 1 - p.x, hi], self.BY.at[1 - p.x])
        self.cCX.start()
        self._add(self.P.at[p.s, p.x, lo], self.BX.at[p.s])
        self._add(self.P.at[p.s, p.x, hi], self.BY.at[p.x])


    def _right(self, j):
        return rcopy(self.quarter(self.F, j), self.Z.at[j], self.ss.at[5 + j], self.rs.at[5 + j], self.p.R)

    def _left(self, j, last):
        slot = self.nb if last else j
        k = 5 + self.nb + j
        return rcopy(self.quarter(self.F, j), self.Z.at[slot], self.ss.at[k], self.rs.at[k], self.p.L)

    def plane_end(self):
        h = self.h
        self.cCY.wait_recv()
        self._add(self.F.at[pl.ds(0, h)], self.CY)
        self.cCX.wait_recv()
        self._add(self.F.at[pl.ds(h, h)], self.CX)

    def hop(self, t):
        nb, p = self.nb, self.p
        if t == 0:
            self.plane_end()

        @pl.when(p.b == t)
        def _():
            for j in range(nb - 1, t, -1):
                if t > 0:
                    self._right(j).wait_recv()
                    self._add(self.quarter(self.F, j), self.Z.at[j])
                self._right(j).start()

        @pl.when(p.b == nb - 1 - t)
        def _():
            for j in range(nb - 1 - t):
                if t > 0:
                    self._left(j, False).wait_recv()
                    self._add(self.quarter(self.F, j), self.Z.at[j])
                self._left(j, j == nb - 2 - t).start()

    def _spread(self, t):
        p, nb = self.p, self.nb
        k = 5 + 2 * nb + 2 * t
        r, l = p.b - t, p.b + t
        qr = self.quarter(self.O, jnp.maximum(r, 0))
        ql = self.quarter(self.O, jnp.minimum(l, nb - 1))
        right = rcopy(qr, qr, self.ss.at[k], self.rs.at[k], p.R)
        left = rcopy(ql, ql, self.ss.at[k + 1], self.rs.at[k + 1], p.L)
        return right, left, (r >= 0) & (p.b < nb - 1), (l <= nb - 1) & (p.b > 0)

    def _spread_recv(self, t):
        right, left, _, _ = self._spread(t)
        p, nb = self.p, self.nb
        pl.when(p.b - 1 - t >= 0)(right.wait_recv)
        pl.when(p.b + 1 + t <= nb - 1)(left.wait_recv)

    def spread(self, t):
        p, nb = self.p, self.nb
        if t == 0:
            mine = self.quarter(self.F, p.b)
            for j in range(nb):
                @pl.when(p.b == j)
                def _():
                    if j > 0:
                        self._right(j).wait_recv()
                        self._add(mine, self.Z.at[j])
                    if j < nb - 1:
                        self._left(j, True).wait_recv()
                        self._add(mine, self.Z.at[nb])
            total = self.quarter(self.O, p.b)

            def body(r):
                rows = pl.ds(r, self.chunk)
                total[rows] = mine[rows]
            row_loop(self.h, self.chunk, body)
        else:
            self._spread_recv(t - 1)
        right, left, cr, cl = self._spread(t)
        pl.when(cr)(right.start)
        pl.when(cl)(left.start)

    def finish(self):
        self._spread_recv(self.nb - 2)

    def drain(self):
        nb, p = self.nb, self.p
        for k in (self.cA, self.cBX, self.cBY, self.cCX, self.cCY):
            k.wait_send()
        for t in range(nb - 1):
            @pl.when(p.b == t)
            def _():
                for j in range(nb - 1, t, -1):
                    self._right(j).wait_send()

            @pl.when(p.b == nb - 1 - t)
            def _():
                for j in range(nb - 1 - t):
                    self._left(j, j == nb - 2 - t).wait_send()
            right, left, cr, cl = self._spread(t)
            pl.when(cr)(right.wait_send)
            pl.when(cl)(left.wait_send)


def reduce_scratch(shape, dt, nb):
    R, C = shape
    h = R // 2
    return [
        pltpu.VMEM((2, 2, R, C), dt),
        pltpu.VMEM((2, h, C), dt),
        pltpu.VMEM((2, h, C), dt),
        pltpu.VMEM((h, C), dt),
        pltpu.VMEM((h, C), dt),
        pltpu.VMEM((nb + 1, h, C // 2), dt),
    ]


NBUF = 6


def reduce_sems(nb):
    return 5 + 2 * nb + 2 * (nb - 1)


class TableSum:
    def __init__(self, p, nb, t, bufs, line, ss, rs):
        self.p, self.nb, self.t, self.bufs, self.line = p, nb, t, bufs, line
        self.steps = [
            rcopy(t if i == 0 else bufs.at[i - 1], bufs.at[3 + i], ss.at[i], rs.at[i], dev)
            for i, dev in enumerate((p.C, p.X, p.Y))
        ]
        self.ss, self.rs = ss, rs

    def start(self):
        self.steps[0].start()

    def step(self, i):
        self.steps[i].wait_recv()
        self.bufs[i] = (self.t[...] if i == 0 else self.bufs[i - 1]) + self.bufs[3 + i]
        if i < 2:
            self.steps[i + 1].start()
        else:
            self.line[self.p.b] = self.bufs[2]
            for j in range(self.nb):
                pl.when(self.p.b != j)(self._z(j, self.p.b).start)

    def _z(self, j, slot):
        return rcopy(
            self.bufs.at[2], self.line.at[slot], self.ss.at[3 + j], self.rs.at[3 + slot], self.p.z(j)
        )

    def finish(self, out):
        for j in range(self.nb):
            pl.when(self.p.b != j)(self._z(j, j).wait_recv)
        total = self.line[0]
        for j in range(1, self.nb):
            total = total + self.line[j]
        out[...] = total

    def drain(self):
        for k in self.steps:
            k.wait_send()
        for j in range(self.nb):
            pl.when(self.p.b != j)(self._z(j, self.p.b).wait_send)


HEAD_DIM = 64
PAIR = 128
MASKED = -1e30
TILE = 512


def dot(a, b, ca, cb):
    return lax.dot_general(a, b, (((ca,), (cb,)), ((), ())), preferred_element_type=jnp.float32)


def left_lanes(shape):
    return lax.broadcasted_iota(jnp.int32, shape, 1) < HEAD_DIM


def one_head(pair, left, first):
    keep = left if first else jnp.logical_not(left)
    return jnp.where(keep, pair, jnp.zeros_like(pair))


def lane_groups(op, a):
    out = a[:, :PAIR]
    for g in range(1, a.shape[1] // PAIR):
        out = op(out, a[:, g * PAIR:(g + 1) * PAIR])
    return out


def attn_fwd_kernel(span, col_ref, row_ref, q_ref, k_ref, v_ref, o_ref, ob_ref, lse_ref, s_ref, m_ref, l_ref, acc_ref):
    rows = q_ref.shape[0]
    left = left_lanes((rows, PAIR))
    m_ref[...] = jnp.full_like(m_ref, MASKED)
    l_ref[...] = jnp.zeros_like(l_ref)
    acc_ref[...] = jnp.zeros_like(acc_ref)
    q = q_ref[...]
    heads = [one_head(q, left, i == 0) for i in range(2)]
    codes = col_ref[...]

    def score(t, _):
        at = pl.multiple_of(t * TILE, TILE)
        k = k_ref[pl.ds(at, TILE), :]
        mask = codes == row_ref[:, pl.ds(at, TILE)]
        for i in range(2):
            s = jnp.where(mask, dot(heads[i], k, 1, 1), MASKED)
            s_ref[i, t] = s
            m_ref[i] = jnp.maximum(m_ref[i], lane_groups(jnp.maximum, s))
        return 0

    lax.fori_loop(span[0], span[1], score, 0)
    tops = [jnp.max(m_ref[i], axis=1, keepdims=True) for i in range(2)]

    def mix(t, _):
        v = v_ref[pl.ds(pl.multiple_of(t * TILE, TILE), TILE), :]
        parts = []
        for i in range(2):
            p = jnp.exp(s_ref[i, t] - tops[i])
            l_ref[i] += lane_groups(jnp.add, p)
            parts.append(dot(p.astype(jnp.bfloat16), v, 1, 0))
        acc_ref[...] += jnp.where(left, parts[0], parts[1])
        return 0

    lax.fori_loop(span[0], span[1], mix, 0)
    sums = [jnp.sum(l_ref[i], axis=1, keepdims=True) for i in range(2)]
    total = jnp.where(left, sums[0], sums[1])
    o = acc_ref[...] / total
    o_ref[...] = o
    ob_ref[...] = o.astype(jnp.bfloat16)
    lse_ref[...] = jnp.where(left, tops[0], tops[1]) + jnp.log(total)


def attention(q, k_all, v_all, codes, own_codes, span):
    rows, width = q.shape
    total = k_all.shape[0]
    pairs = width // PAIR
    own = pl.BlockSpec((rows, PAIR), lambda h, s: (0, h))
    every = pl.BlockSpec((total, PAIR), lambda h, s: (0, h))
    return pl.pallas_call(
        attn_fwd_kernel,
        grid_spec=pltpu.PrefetchScalarGridSpec(
            num_scalar_prefetch=1,
            grid=(pairs,),
            in_specs=[
                pl.BlockSpec((rows, 1), lambda h, s: (0, 0)),
                pl.BlockSpec((1, total), lambda h, s: (0, 0)),
                own, every, every,
            ],
            out_specs=[own, own, own],
            scratch_shapes=[
                pltpu.VMEM((2, total // TILE, rows, TILE), jnp.float32),
                pltpu.VMEM((2, rows, PAIR), jnp.float32),
                pltpu.VMEM((2, rows, PAIR), jnp.float32),
                pltpu.VMEM((rows, PAIR), jnp.float32),
            ],
        ),
        out_shape=[
            jax.ShapeDtypeStruct((rows, width), jnp.float32),
            jax.ShapeDtypeStruct((rows, width), jnp.bfloat16),
            jax.ShapeDtypeStruct((rows, width), jnp.float32),
        ],
        compiler_params=pltpu.CompilerParams(vmem_limit_bytes=48 << 20),
        name="attention",
    )(span, own_codes.reshape(rows, 1), codes.reshape(1, total), q, k_all, v_all)


def stats_kernel(g_ref, o_ref, lse_ref, out_ref, delta_ref):
    rows = g_ref.shape[0]
    left = left_lanes((rows, PAIR))
    t = g_ref[...].astype(jnp.float32) * o_ref[...]
    d0 = jnp.sum(jnp.where(left, t, 0.0), axis=1, keepdims=True)
    d1 = jnp.sum(jnp.where(left, 0.0, t), axis=1, keepdims=True)
    delta_ref[...] = jnp.where(left, d0, d1)
    lane = lax.broadcasted_iota(jnp.int32, (rows, PAIR), 1)
    lse = lse_ref[...]
    packed = jnp.where(lane == 0, lse[:, :1], jnp.where(lane == 1, lse[:, HEAD_DIM:HEAD_DIM + 1], jnp.where(lane == 2, d0, d1)))
    out_ref[0] = packed.T[:8]


def row_stats(grad, o, lse):
    rows, width = grad.shape
    pairs = width // PAIR
    own = pl.BlockSpec((rows, PAIR), lambda h: (0, h))
    return pl.pallas_call(
        stats_kernel,
        grid=(pairs,),
        in_specs=[own, own, own],
        out_specs=[pl.BlockSpec((1, 8, rows), lambda h: (h, 0, 0)), own],
        out_shape=[
            jax.ShapeDtypeStruct((pairs, 8, rows), jnp.float32),
            jax.ShapeDtypeStruct((rows, width), jnp.float32),
        ],
        name="row_stats",
    )(grad, o, lse)


def attn_bwd_kernel(span, col_ref, row_ref, q_ref, k_ref, v_ref, g_ref, lse_ref, delta_ref,
                    qa_ref, ka_ref, va_ref, ga_ref, st_ref, dq_ref, dk_ref, dv_ref):
    rows = q_ref.shape[0]
    left = left_lanes((rows, PAIR))
    dq_ref[...] = jnp.zeros_like(dq_ref)
    dk_ref[...] = jnp.zeros_like(dk_ref)
    dv_ref[...] = jnp.zeros_like(dv_ref)
    codes = col_ref[...]
    qs = [one_head(q_ref[...], left, i == 0) for i in range(2)]
    ks = [one_head(k_ref[...], left, i == 0) for i in range(2)]
    vs = [one_head(v_ref[...], left, i == 0) for i in range(2)]
    gs = [one_head(g_ref[...], left, i == 0) for i in range(2)]
    lses = [lse_ref[:, i * HEAD_DIM:i * HEAD_DIM + 1] for i in range(2)]
    deltas = [delta_ref[:, i * HEAD_DIM:i * HEAD_DIM + 1] for i in range(2)]

    def step(t, _):
        at = pl.multiple_of(t * TILE, TILE)
        tile = pl.ds(at, TILE)
        mask = codes == row_ref[:, tile]
        k, v, q, g = ka_ref[tile, :], va_ref[tile, :], qa_ref[tile, :], ga_ref[tile, :]
        dqs, dks, dvs = [], [], []
        for i in range(2):
            s = jnp.where(mask, dot(qs[i], k, 1, 1), MASKED)
            p = jnp.exp(s - lses[i])
            dp = dot(gs[i], v, 1, 1)
            ds = (p * (dp - deltas[i])).astype(jnp.bfloat16)
            dqs.append(dot(ds, k, 1, 0))
            st = jnp.where(mask, dot(ks[i], q, 1, 1), MASKED)
            pt = jnp.exp(st - st_ref[0, i:i + 1, tile])
            dvs.append(dot(pt.astype(jnp.bfloat16), g, 1, 0))
            dpt = dot(vs[i], g, 1, 1)
            dst = (pt * (dpt - st_ref[0, 2 + i:3 + i, tile])).astype(jnp.bfloat16)
            dks.append(dot(dst, q, 1, 0))
        dq_ref[...] += jnp.where(left, dqs[0], dqs[1])
        dk_ref[...] += jnp.where(left, dks[0], dks[1])
        dv_ref[...] += jnp.where(left, dvs[0], dvs[1])
        return 0

    lax.fori_loop(span[0], span[1], step, 0)


def attention_grad(q, k, v, g, lse, delta, q_all, k_all, v_all, g_all, stats, codes, own_codes, span):
    rows, width = q.shape
    total = k_all.shape[0]
    pairs = width // PAIR
    own = pl.BlockSpec((rows, PAIR), lambda h, s: (0, h))
    every = pl.BlockSpec((total, PAIR), lambda h, s: (0, h))
    return pl.pallas_call(
        attn_bwd_kernel,
        grid_spec=pltpu.PrefetchScalarGridSpec(
            num_scalar_prefetch=1,
            grid=(pairs,),
            in_specs=[
                pl.BlockSpec((rows, 1), lambda h, s: (0, 0)),
                pl.BlockSpec((1, total), lambda h, s: (0, 0)),
                own, own, own, own, own, own, every, every, every, every,
                pl.BlockSpec((1, 8, total), lambda h, s: (h, 0, 0)),
            ],
            out_specs=[own, own, own],
        ),
        out_shape=[
            jax.ShapeDtypeStruct((rows, width), jnp.float32),
            jax.ShapeDtypeStruct((rows, width), jnp.float32),
            jax.ShapeDtypeStruct((rows, width), jnp.float32),
        ],
        compiler_params=pltpu.CompilerParams(vmem_limit_bytes=48 << 20),
        name="attention_grad",
    )(span, own_codes.reshape(rows, 1), codes.reshape(1, total), q, k, v, g, lse, delta, q_all, k_all, v_all, g_all, stats)


VEC_ROWS = 8


def forward_kernel(nb, *refs):
    x_ref, codes, rows = refs[:3]
    shards_in = refs[3:9]
    vecs_in = refs[9:18]
    wq_o, wk_o, wv_o, wo_o, wup_o, wdn_o = refs[18:24]
    q_o, k_o, v_o = refs[24:27]
    o_ref, ob_ref, lse_ref, vec_ref, bup_ref = refs[27:32]
    rest = refs[32:]
    x_all, wq, wk, wv, pack, packs, q, k, v, m_ref, l_ref = rest[:11]
    zs, zr, gs, gr, gl, ws, es = rest[11:]
    n, width = x_ref.shape
    pairs = width // PAIR
    p = Place()
    own = pltpu.make_async_copy(x_ref, x_all.at[p.b], ws.at[3])
    own.start()
    pack[...] = jnp.zeros_like(pack)
    for i in range(VEC_ROWS):
        pack[i:i + 1, :vecs_in[i].shape[1]] = vecs_in[i][...].astype(jnp.float32)
    for i in range(vecs_in[8].shape[1] // PAIR):
        pack[VEC_ROWS + i:VEC_ROWS + i + 1, :] = vecs_in[8][:, i * PAIR:(i + 1) * PAIR].astype(jnp.float32)
    enter(p, nb, True, "near")
    line = LineGather(p, nb, x_ref, x_all, zs, zr)
    targets = (packs, wq, wk, wv, wo_o, wup_o, wdn_o)
    sources = (pack,) + tuple(shards_in)
    g = [PlaneGather(p, sources[i], targets[i], gs.at[i], gr.at[i], gl.at[i]) for i in range(7)]
    line.start(0)
    for c in g[:5]:
        c.start()
    for c in g[:4]:
        c.forward()
    g[5].start()
    g[6].start()
    line.wait_recv(0)
    line.start(1)
    for c in g[:4]:
        c.diag()
    for c in g[:4]:
        c.finish()
    own.wait()
    keep = [
        pltpu.make_async_copy(a, b, ws.at[i]) for i, (a, b) in enumerate(((wq, wq_o), (wk, wk_o), (wv, wv_o)))
    ]
    for c in keep:
        c.start()

    piece = width // 8
    r = lax.broadcasted_iota(jnp.int32, (PAIR, width), 0)
    c = lax.broadcasted_iota(jnp.int32, (PAIR, width), 1)
    total = jnp.zeros((2 * VEC_ROWS, width), jnp.float32)
    for i in range(8):
        pick = ((c == r + i * piece) & (r < piece)).astype(jnp.bfloat16)
        total += dot(packs[2 * VEC_ROWS * i:2 * VEC_ROWS * (i + 1), :].astype(jnp.bfloat16), pick, 1, 0)
    vec_ref[...] = total[:VEC_ROWS]
    up_piece = bup_ref.shape[1] // 8
    for i in range(8):
        for t in range(up_piece // PAIR):
            at = i * up_piece + t * PAIR
            row = 2 * VEC_ROWS * i + VEC_ROWS + t
            bup_ref[:, at:at + PAIR] = packs[row:row + 1, :]

    scale = HEAD_DIM ** (-0.5)
    step = 256

    def outs(j, e):
        return [
            pltpu.make_async_copy(a.at[j], b.at[j], es.at[i, e])
            for i, (a, b) in enumerate(((q, q_o), (k, k_o), (v, v_o)))
        ]

    def project(j):
        def columns(t, _):
            at = pl.ds(pl.multiple_of(t * step, step), step)
            xs = x_all[j]
            q[j, :, at] = ((dot(xs, wq[:, at], 1, 0) + vec_ref[0:1, at]) * scale).astype(jnp.bfloat16)
            k[j, :, at] = dot(xs, wk[:, at], 1, 0).astype(jnp.bfloat16)
            v[j, :, at] = (dot(xs, wv[:, at], 1, 0) + vec_ref[1:2, at]).astype(jnp.bfloat16)
            return 0
        lax.fori_loop(0, width // step, columns, 0)

    def attend(j, first):
        def pair(h, _):
            left = left_lanes((n, PAIR))
            lanes = pl.ds(pl.multiple_of(h * PAIR, PAIR), PAIR)
            mask = codes[...] == rows[j]
            qs, ks, vs = q[p.b, :, lanes], k[j, :, lanes], v[j, :, lanes]
            parts, alphas = [], []
            for i in range(2):
                s = jnp.where(mask, dot(one_head(qs, left, i == 0), ks, 1, 1), MASKED)
                top = jnp.max(lane_groups(jnp.maximum, s), axis=1, keepdims=True)
                if first:
                    new = jnp.broadcast_to(top, (n, PAIR))
                else:
                    old = m_ref[2 * h + i]
                    new = jnp.maximum(old, top)
                    alpha = jnp.exp(old - new)
                    alphas.append(alpha)
                e = jnp.exp(s - jnp.concatenate([new] * (n // PAIR), axis=1))
                mass = lane_groups(jnp.add, e)
                m_ref[2 * h + i] = new
                l_ref[2 * h + i] = mass if first else l_ref[2 * h + i] * alpha + mass
                parts.append(dot(e.astype(jnp.bfloat16), vs, 1, 0))
            got = jnp.where(left, parts[0], parts[1])
            if first:
                o_ref[:, lanes] = got
            else:
                o_ref[:, lanes] = o_ref[:, lanes] * jnp.where(left, alphas[0], alphas[1]) + got
            return 0
        lax.fori_loop(0, pairs, pair, 0)

    def block(j, e):
        project(j)
        for c in outs(j, e):
            c.start()
        attend(j, e == 0)

    def left_of(t):
        return p.b - 1 - t >= 0, jnp.maximum(p.b - 1 - t, 0)

    def right_of(t):
        return p.b + 1 + t <= nb - 1, jnp.minimum(p.b + 1 + t, nb - 1)

    def arrived(t, side):
        ok, j = (left_of(t), right_of(t))[side]

        @pl.when(ok)
        def _():
            block(j, 1 + 2 * t + side)

    project(p.b)
    for c in outs(p.b, 0):
        c.start()
    g[4].forward()
    attend(p.b, True)
    g[5].forward()
    arrived(0, 0)
    line.wait_recv(1)
    line.start(2)
    arrived(0, 1)
    g[6].forward()
    g[4].diag()
    arrived(1, 0)
    arrived(1, 1)
    g[5].diag()
    line.wait_recv(2)
    g[6].diag()
    arrived(2, 0)
    arrived(2, 1)

    def close(h, _):
        left = left_lanes((n, PAIR))
        lanes = pl.ds(pl.multiple_of(h * PAIR, PAIR), PAIR)
        sums = [jnp.sum(l_ref[2 * h + i], axis=1, keepdims=True) for i in range(2)]
        mass = jnp.where(left, sums[0], sums[1])
        out = o_ref[:, lanes] / mass
        o_ref[:, lanes] = out
        ob_ref[:, lanes] = out.astype(jnp.bfloat16)
        lse_ref[:, lanes] = jnp.where(left, m_ref[2 * h], m_ref[2 * h + 1]) + jnp.log(mass)
        return 0
    lax.fori_loop(0, pairs, close, 0)
    for c in g[4:]:
        c.finish()
    for c in keep:
        c.wait()
    for c in outs(p.b, 0):
        c.wait()
    for t in range(nb - 1):
        for side, (ok, j) in enumerate((left_of(t), right_of(t))):
            @pl.when(ok)
            def _():
                for c in outs(j, 1 + 2 * t + side):
                    c.wait()
    for t in range(nb - 1):
        line.wait_send(t)
    for c in g:
        c.drain()


def forward(x, codes, own_codes, weights, vecs, nb):
    n, width = x.shape
    hidden = weights[4].shape[1]
    bf, f32 = jnp.bfloat16, jnp.float32
    every = jax.ShapeDtypeStruct((nb, n, width), bf)
    block = jax.ShapeDtypeStruct((n, width), f32)
    mats = [jax.ShapeDtypeStruct((8 * w.shape[0], w.shape[1]), w.dtype) for w in weights]
    dma = pltpu.SemaphoreType.DMA
    return pl.pallas_call(
        functools.partial(forward_kernel, nb),
        out_shape=(
            *mats, every, every, every, block, jax.ShapeDtypeStruct((n, width), bf), block,
            jax.ShapeDtypeStruct((VEC_ROWS, width), f32), jax.ShapeDtypeStruct((1, hidden), f32),
        ),
        in_specs=[VM] * 18,
        out_specs=(ANY,) * 9 + (VM,) * 5,
        scratch_shapes=[
            pltpu.VMEM((nb, n, width), bf),
            pltpu.VMEM((width, width), bf), pltpu.VMEM((width, width), bf), pltpu.VMEM((width, width), bf),
            pltpu.VMEM((2 * VEC_ROWS, PAIR), f32), pltpu.VMEM((16 * VEC_ROWS, PAIR), f32),
            pltpu.VMEM((nb, n, width), bf), pltpu.VMEM((nb, n, width), bf), pltpu.VMEM((nb, n, width), bf),
            pltpu.VMEM((width // HEAD_DIM, n, PAIR), f32), pltpu.VMEM((width // HEAD_DIM, n, PAIR), f32),
            dma((2, nb - 1)), dma((2, nb - 1)), dma((7, 9)), dma((7, 9)), dma((7,)), dma((4,)), dma((3, 2 * nb)),
        ],
        compiler_params=pltpu.CompilerParams(
            collective_id=1, has_side_effects=True, vmem_limit_bytes=60 << 20
        ),
        name="forward",
    )(
        x, own_codes.reshape(n, 1), codes.reshape(nb, 1, n), *weights, *[v.reshape(1, -1) for v in vecs]
    )


class AttentionGrad:
    def __init__(self, codes, rows, q, k, v, g, lse, delta, stats, own, dq, dk, dv):
        self.codes, self.rows = codes, rows
        self.q, self.k, self.v, self.g = q, k, v, g
        self.lse, self.delta, self.stats = lse, delta, stats
        self.own = own
        self.dq, self.dk, self.dv = dq, dk, dv
        self.n = dq.shape[0]
        self.pairs = dq.shape[1] // PAIR

    def queries(self, j, first):
        own = self.own

        def pair(h, _):
            left = left_lanes((self.n, PAIR))
            lanes = pl.ds(pl.multiple_of(h * PAIR, PAIR), PAIR)
            mask = self.codes[...] == self.rows[j]
            q, g = self.q[own, :, lanes], self.g[own, :, lanes]
            k, v = self.k[j, :, lanes], self.v[j, :, lanes]
            lse, delta = self.lse[:, lanes], self.delta[:, lanes]
            parts = []
            for i in range(2):
                at = slice(i * HEAD_DIM, i * HEAD_DIM + 1)
                s = jnp.where(mask, dot(one_head(q, left, i == 0), k, 1, 1), MASKED)
                p = jnp.exp(s - lse[:, at])
                dp = dot(one_head(g, left, i == 0), v, 1, 1)
                ds = (p * (dp - delta[:, at])).astype(jnp.bfloat16)
                parts.append(dot(ds, k, 1, 0))
            new = jnp.where(left, parts[0], parts[1])
            if first:
                self.dq[:, lanes] = new
            else:
                self.dq[:, lanes] += new
            return 0

        lax.fori_loop(0, self.pairs, pair, 0)

    def keys(self, j, first):
        own = self.own

        def pair(h, _):
            left = left_lanes((self.n, PAIR))
            lanes = pl.ds(pl.multiple_of(h * PAIR, PAIR), PAIR)
            mask = self.codes[...] == self.rows[j]
            k, v = self.k[own, :, lanes], self.v[own, :, lanes]
            q, g = self.q[j, :, lanes], self.g[j, :, lanes]
            dks, dvs = [], []
            for i in range(2):
                st = jnp.where(mask, dot(one_head(k, left, i == 0), q, 1, 1), MASKED)
                pt = jnp.exp(st - self.stats[j, h, i:i + 1])
                dvs.append(dot(pt.astype(jnp.bfloat16), g, 1, 0))
                dpt = dot(one_head(v, left, i == 0), g, 1, 1)
                dst = (pt * (dpt - self.stats[j, h, 2 + i:3 + i])).astype(jnp.bfloat16)
                dks.append(dot(dst, q, 1, 0))
            dk, dv = jnp.where(left, dks[0], dks[1]), jnp.where(left, dvs[0], dvs[1])
            if first:
                self.dk[:, lanes] = dk
                self.dv[:, lanes] = dv
            else:
                self.dk[:, lanes] += dk
                self.dv[:, lanes] += dv
            return 0

        lax.fori_loop(0, self.pairs, pair, 0)


TABLE = 16


def backward_kernel(nb, *refs):
    codes, rows, g_own, st_own, lse, delta, x_ref, rest_ref, table = refs[:9]
    q_hbm, k_hbm, v_hbm, wq_hbm, wk_hbm, wv_hbm = refs[9:15]
    early = refs[15:18]
    token_ref, table_out = refs[18:20]
    outs = refs[20:26]
    rest = refs[26:]
    q, k, v, g, stats, dq, dk, dv, wq, wk, wv, gw, stage_a, stage_b, tab, tsum, tline = rest[:17]
    bufs = rest[17:17 + 6 * NBUF]
    zs, zr, ls, ss, rs, rls, ts, tr = rest[17 + 6 * NBUF:]
    n, width = g_own.shape
    p = Place()
    loads = [
        pltpu.make_async_copy(a, b, ls.at[i])
        for i, (a, b) in enumerate((
            (k_hbm, k), (v_hbm, v), (q_hbm, q), (g_own, g.at[p.b]), (st_own, stats.at[p.b]),
            (wq_hbm, wq), (wk_hbm, wk), (wv_hbm, wv),
        ))
    ]
    for c in loads:
        c.start()
    enter(p, nb, True, "all")
    lines = [
        LineGather(p, nb, g_own, g, zs.at[0], zr.at[0]),
        LineGather(p, nb, st_own, stats, zs.at[1], zr.at[1]),
    ]
    sources = tuple(early) + tuple(gw.at[i] for i in range(3))
    stages = (stage_a, stage_a, stage_b, None, None, None)
    dn, up, wo, gq, gk, gv = [
        PlaneReduce(
            p, nb, sources[i], outs[i], bufs[NBUF * i:NBUF * (i + 1)],
            None if stages[i] is None else stages[i].reshape(sources[i].shape[:2] + sources[i].shape[3:]),
            ss.at[i], rs.at[i], rls.at[i],
        )
        for i in range(6)
    ]
    vec = TableSum(p, nb, tab, tsum, tline, ts, tr)
    for c in lines:
        c.start(0)
    for c in (dn, up, wo):
        c.a_start()
    dn.own_start()
    wo.own_start()
    work = AttentionGrad(codes, rows, q, k, v, g, lse, delta, stats, p.b, dq, dk, dv)
    for c in loads:
        c.wait()

    def take(t, side):
        ok, j = ((p.b - 1 - t >= 0, p.b - 1 - t), (p.b + 1 + t <= nb - 1, p.b + 1 + t))[side]

        @pl.when(ok)
        def _():
            work.keys(jnp.clip(j, 0, nb - 1), False)

    low = k
    def slot(i):
        return (p.b + 1 + i) % nb

    def settle(i, src, scale, row):
        value = src[...] if scale is None else src[...] * scale
        if row is not None:
            tab[row:row + 1, :] = jnp.sum(value, axis=0, keepdims=True)
        low[slot(i)] = value.astype(jnp.bfloat16)

    def weight_grad(i):
        half = width // 2
        for m in range(2):
            part = dot(x_ref[:, m * half:(m + 1) * half], low[slot(i)], 0, 0).astype(jnp.bfloat16)
            r = gw.shape[-2]
            for a in range(2):
                for b in range(2):
                    at = (2 * a + b) * r
                    gw[i, m, a, b] = part[at:at + r]

    work.queries(p.b, True)
    dn.b_start()
    up.own_start()
    work.queries((p.b + 1) % nb, False)
    up.b_start()
    wo.b_start()
    for c in lines:
        c.wait_recv(0)
        c.start(1)
    work.queries((p.b + 2) % nb, False)
    dn.c_start()
    work.queries((p.b + 3) % nb, False)
    tab[...] = table[...]
    settle(0, dq, HEAD_DIM ** (-0.5), 0)
    weight_grad(0)
    gq.a_start()
    for c in lines:
        c.wait_recv(1)
        c.start(2)
    up.c_start()
    work.keys(p.b, True)
    gq.b_start()
    wo.c_start()
    take(0, 0)
    dn.hop(0)
    take(0, 1)
    up.hop(0)
    wo.hop(0)
    gq.c_start()
    dn.hop(1)
    take(1, 0)
    take(1, 1)
    up.hop(1)
    wo.hop(1)
    dn.hop(2)
    for c in lines:
        c.wait_recv(2)
    take(2, 0)
    take(2, 1)
    settle(1, dk, None, None)
    settle(2, dv, None, 1)
    vec.start()
    weight_grad(1)
    gk.a_start()
    weight_grad(2)
    gv.a_start()
    up.hop(2)
    wo.hop(2)
    dn.spread(0)
    vec.step(0)
    gk.b_start()
    gv.b_start()
    gq.hop(0)
    vec.step(1)

    part = 256

    def columns(t, _):
        at = pl.ds(pl.multiple_of(t * part, part), part)
        total = rest_ref[:, at]
        for i, w in enumerate((wq, wk, wv)):
            total = total + dot(low[slot(i)], w[at, :], 1, 1)
        token_ref[:, at] = total.astype(jnp.bfloat16)
        return 0
    lax.fori_loop(0, width // part, columns, 0)

    up.spread(0)
    wo.spread(0)
    dn.spread(1)
    vec.step(2)
    gk.c_start()
    gv.c_start()
    gq.hop(1)
    up.spread(1)
    wo.spread(1)
    dn.spread(2)
    gq.hop(2)
    gk.hop(0)
    gv.hop(0)
    gq.spread(0)
    gk.hop(1)
    gv.hop(1)
    up.spread(2)
    wo.spread(2)
    gk.hop(2)
    gv.hop(2)
    gq.spread(1)
    gk.spread(0)
    gv.spread(0)
    gq.spread(2)
    gk.spread(1)
    gv.spread(1)
    gk.spread(2)
    gv.spread(2)
    vec.finish(table_out)
    every = (dn, up, wo, gq, gk, gv)
    for c in every:
        c.finish()
    for t in range(nb - 1):
        for c in lines:
            c.wait_send(t)
    for c in every:
        c.drain()
    vec.drain()


def backward(codes, own_codes, do, stats, lse, delta, x, rest, table, q_all, k_all, v_all, weights, early, nb):
    n, width = do.shape
    bf, f32 = jnp.bfloat16, jnp.float32
    late = jax.ShapeDtypeStruct((2, 2, 2, width // 8, width), bf)
    kinds = list(early) + [late] * 3
    scratch = []
    for g in kinds:
        scratch += reduce_scratch(g.shape[-2:], bf, nb)
    ns = reduce_sems(nb)
    every = pltpu.VMEM((nb, n, width), bf)
    total = pltpu.VMEM((n, width), f32)
    square = pltpu.VMEM((width, width), bf)
    dma = pltpu.SemaphoreType.DMA
    big, small = early[0].shape, early[2].shape
    return pl.pallas_call(
        functools.partial(backward_kernel, nb),
        out_shape=(
            jax.ShapeDtypeStruct((n, width), bf), jax.ShapeDtypeStruct((TABLE, width), f32),
            *[jax.ShapeDtypeStruct(g.shape[-2:], bf) for g in kinds],
        ),
        in_specs=[VM] * 9 + [ANY] * 9,
        out_specs=(VM,) * 8,
        scratch_shapes=[
            every, every, every, every, pltpu.VMEM((nb,) + stats.shape, f32), total, total, total,
            square, square, square, pltpu.VMEM((3,) + late.shape, bf),
            pltpu.VMEM(big[:2] + big[3:], bf), pltpu.VMEM(small[:2] + small[3:], bf),
            pltpu.VMEM((TABLE, width), f32), pltpu.VMEM((6, TABLE, width), f32), pltpu.VMEM((nb, TABLE, width), f32),
        ] + scratch + [
            dma((2, 2, nb - 1)), dma((2, 2, nb - 1)), dma((8,)), dma((6, ns)), dma((6, ns)), dma((3,)),
            dma((3 + nb,)), dma((3 + nb,)),
        ],
        compiler_params=pltpu.CompilerParams(
            collective_id=4, has_side_effects=True, vmem_limit_bytes=63 << 20
        ),
        name="backward",
    )(
        own_codes.reshape(n, 1), codes.reshape(nb, 1, n), do, stats, lse, delta, x, rest, table,
        q_all, k_all, v_all, *weights, *early,
    )


EPSILON = 1e-06
PLANE = ("seq", "shard")


def normalize(hidden, gain, shift):
    center = hidden - jnp.mean(hidden, axis=-1, keepdims=True)
    spread = jnp.mean(center * center, axis=-1, keepdims=True)
    return center * lax.rsqrt(spread + EPSILON) * gain + shift


def smooth_gate(hidden):
    return jax.nn.gelu(hidden, approximate=False)


def mm(left, right):
    return jnp.dot(left, right, preferred_element_type=jnp.float32)


def contract_rows(left, right):
    return dot(left, right, 0, 0)


def times_transpose(left, right):
    return dot(left, right, 1, 1)


def tuned_plane():
    return lax.axis_size("seq") == 2 and lax.axis_size("shard") == 4 and lax.axis_size("blk") == 4


def total(g):
    part = lax.psum_scatter(g.astype(jnp.bfloat16), PLANE, scatter_dimension=0, tiled=True)
    return lax.psum(part, "blk").astype(jnp.float32)


def shards(g):
    return g.astype(jnp.bfloat16).reshape(2, 2, 2, g.shape[0] // 8, g.shape[1])


def folded(g, width):
    g = g.reshape(8, g.shape[0] // 8, -1, width)
    return jnp.swapaxes(g, 1, 2).reshape(-1, width)


def per_device(
    tokens, segments, live_mask, query_weight, key_weight, value_weight, out_weight,
    query_bias, value_bias, out_bias, first_gain, first_shift, up_weight, up_bias,
    down_weight, down_bias, second_gain, second_shift, cotangent,
):
    inputs = tokens[0]
    rows, width = inputs.shape
    nb = lax.axis_size("blk")
    place = lax.axis_index("blk")
    seg, live = segments[0], live_mask[0]
    length = seg.shape[0]
    start = place * rows
    codes = jnp.where(live > 0, seg, -1 - jnp.arange(length, dtype=jnp.int32))
    own_codes = lax.dynamic_slice_in_dim(codes, start, rows)
    scale = HEAD_DIM ** (-0.5)
    mats = [query_weight, key_weight, value_weight, out_weight, up_weight, down_weight]
    vecs = [query_bias, value_bias, out_bias, first_gain, first_shift, down_bias, second_gain, second_shift, up_bias]
    if tuned_plane():
        out = forward(inputs, codes, own_codes, mats, vecs, nb)
        wq, wk, wv, wo, wup, wdn, q_all, k_all, v_all, summed, attended, lse, table, bup = out
        bq, bv, bo, g1, s1, bdn, g2, s2 = [table[i] for i in range(8)]
        bup = bup[0]
    else:
        xs = lax.all_gather(inputs, "blk", axis=0, tiled=True)
        wq, wk, wv, wo, wup, wdn = [lax.all_gather(w, PLANE, axis=0, tiled=True) for w in mats]
        whole = [lax.all_gather(v, PLANE, axis=0, tiled=True).astype(jnp.float32) for v in vecs]
        bq, bv, bo, g1, s1, bdn, g2, s2, bup = whole
        own_seg = lax.dynamic_slice_in_dim(seg, start, rows)
        low = jnp.sum((seg < own_seg[0]).astype(jnp.int32))
        high = jnp.sum((seg <= own_seg[rows - 1]).astype(jnp.int32))
        span = jnp.stack([low // TILE, (high + TILE - 1) // TILE])
        q_all = ((mm(xs, wq) + bq) * scale).astype(jnp.bfloat16)
        k_all = mm(xs, wk).astype(jnp.bfloat16)
        v_all = (mm(xs, wv) + bv).astype(jnp.bfloat16)
        q, k, v = [lax.dynamic_slice_in_dim(a, start, rows) for a in (q_all, k_all, v_all)]
        summed, attended, lse = attention(q, k_all, v_all, codes, own_codes, span)

    first_sum = inputs.astype(jnp.float32) + (mm(attended, wo) + bo)
    first_norm, first_pull = jax.vjp(normalize, first_sum, g1, s1)
    first_low = first_norm.astype(jnp.bfloat16)
    hidden = mm(first_low, wup) + bup
    gated, gate_pull = jax.vjp(smooth_gate, hidden)
    gated_low = gated.astype(jnp.bfloat16)
    second_sum = first_norm + (mm(gated_low, wdn) + bdn)
    result, second_pull = jax.vjp(normalize, second_sum, g2, s2)
    second_grad, g2_grad, s2_grad = second_pull(cotangent[0].astype(jnp.float32))
    bdn_grad = jnp.sum(second_grad, axis=0)
    second_low = second_grad.astype(jnp.bfloat16)
    wdn_grad = contract_rows(gated_low, second_low)
    (hidden_grad,) = gate_pull(times_transpose(second_low, wdn))
    bup_grad = jnp.sum(hidden_grad, axis=0)
    hidden_low = hidden_grad.astype(jnp.bfloat16)
    wup_grad = contract_rows(first_low, hidden_low)
    norm_grad = second_grad + times_transpose(hidden_low, wup)
    first_grad, g1_grad, s1_grad = first_pull(norm_grad)
    bo_grad = jnp.sum(first_grad, axis=0)
    first_grad_low = first_grad.astype(jnp.bfloat16)
    wo_grad = contract_rows(attended, first_grad_low)
    do = times_transpose(first_grad_low, wo).astype(jnp.bfloat16)

    stats, delta = row_stats(do, summed, lse)
    later = [bo_grad, g1_grad, s1_grad, bdn_grad, g2_grad, s2_grad]
    if tuned_plane():
        zero = jnp.zeros_like(bo_grad)
        table = jnp.stack([zero, zero] + later + list(bup_grad.reshape(-1, width)))
        table = jnp.pad(table, ((0, TABLE - table.shape[0]), (0, 0)))
        out = backward(
            codes, own_codes, do, stats, lse, delta, inputs, first_grad, table, q_all, k_all, v_all,
            [wq, wk, wv], [shards(wdn_grad), shards(folded(wup_grad, width)), shards(wo_grad)], nb,
        )
        token_grad, table, rdn, rup, ro, rwq, rwk, rwv = out
        rup = jnp.swapaxes(rup.reshape(-1, up_weight.shape[0], width), 0, 1).reshape(up_weight.shape)
        rdn, rup, ro, rwq, rwk, rwv = [a.astype(jnp.float32) for a in (rdn, rup, ro, rwq, rwk, rwv)]
        shard = lax.axis_index(PLANE)
        piece = width // 8
        small = lax.dynamic_slice_in_dim(table[:8], shard * piece, piece, axis=1)
        wide = up_bias.shape[0]
        rbup = lax.dynamic_slice_in_dim(table[8:8 + 8 * wide // width].reshape(-1), shard * wide, wide)
        rbq, rbv, rbo, rg1, rs1, rbdn, rg2, rs2 = [small[i] for i in range(8)]
    else:
        do_all, stats_all = [lax.all_gather(a, "blk", axis=0) for a in (do, stats)]
        stats_all = jnp.transpose(stats_all, (1, 2, 0, 3)).reshape(stats.shape[0], 8, length)
        dq, dk, dv = attention_grad(
            q, k, v, do, lse, delta, q_all, k_all, v_all, do_all.reshape(length, width), stats_all,
            codes, own_codes, span,
        )
        r = dq * scale
        rq, rk, rv = [a.astype(jnp.bfloat16) for a in (r, dk, dv)]
        token_grad = first_grad + times_transpose(rq, wq) + times_transpose(rk, wk) + times_transpose(rv, wv)
        token_grad = token_grad.astype(jnp.bfloat16)
        grads = [wdn_grad, wup_grad, wo_grad] + [contract_rows(inputs, a) for a in (rq, rk, rv)]
        rdn, rup, ro, rwq, rwk, rwv = [total(g) for g in grads]
        vectors = [jnp.sum(r, axis=0), jnp.sum(dv, axis=0)] + later + [bup_grad]
        rbq, rbv, rbo, rg1, rs1, rbdn, rg2, rs2, rbup = [total(g) for g in vectors]
    return (
        result.astype(jnp.bfloat16)[None], token_grad[None],
        rwq, rwk, rwv, ro, rbq, rbv, rbo, rg1, rs1, rup, rbup, rdn, rbdn, rg2, rs2,
    )


def solution(mesh):
    flat = P(PLANE, "blk", None)
    mat = P(PLANE, None)
    vec = P(PLANE)
    return jax.shard_map(
        per_device,
        mesh=mesh,
        in_specs=(
            flat, mat, mat, mat, mat, mat, mat, vec, vec, vec, vec, vec, mat, vec, mat, vec, vec, vec, flat,
        ),
        out_specs=(flat, flat, mat, mat, mat, mat, vec, vec, vec, vec, vec, mat, vec, mat, vec, vec, vec),
        check_vma=False,
    )
```

```python
import functools
import jax
import jax.numpy as jnp
from jax import lax
from jax.experimental import pallas as pl
from jax.experimental.pallas import tpu as pltpu
from jax.sharding import PartitionSpec as P

MESH = pl.DeviceIdType.MESH
ANY = pl.BlockSpec(memory_space=pl.ANY)
VMEM_LIMIT = 56 << 20
VM = pl.BlockSpec(memory_space=pltpu.VMEM)


class Place:
    def __init__(self):
        b = lax.axis_index("blk")
        s = lax.axis_index("seq")
        h = lax.axis_index("shard")
        x = h // 2
        c = h % 2
        self.b, self.s, self.h, self.x, self.c = b, s, h, x, c
        self.X = (b, s, (1 - x) * 2 + c)
        self.Y = (b, 1 - s, h)
        self.C = (b, s, x * 2 + 1 - c)
        self.L = (b - 1, s, h)
        self.R = (b + 1, s, h)
        self.me = s * 4 + h
        self.xi = s * 4 + (1 - x) * 2 + c
        self.yi = (1 - s) * 4 + h
        self.di = (1 - s) * 4 + (1 - x) * 2 + c

    def z(self, j):
        return (j, self.s, self.h)


def enter(p, nb, plane, line):
    bar = pltpu.get_barrier_semaphore()
    count = 0
    if plane:
        for peer in (p.X, p.Y, p.C):
            pl.semaphore_signal(bar, inc=1, device_id=peer, device_id_type=MESH)
        count = count + 3
    if line == "near":
        @pl.when(p.b > 0)
        def _():
            pl.semaphore_signal(bar, inc=1, device_id=p.L, device_id_type=MESH)

        @pl.when(p.b < nb - 1)
        def _():
            pl.semaphore_signal(bar, inc=1, device_id=p.R, device_id_type=MESH)
        count = count + jnp.where(p.b > 0, 1, 0) + jnp.where(p.b < nb - 1, 1, 0)
    if line == "all":
        for j in range(nb):
            @pl.when(p.b != j)
            def _():
                pl.semaphore_signal(bar, inc=1, device_id=p.z(j), device_id_type=MESH)
        count = count + nb - 1
    pl.semaphore_wait(bar, count)


def rcopy(src, dst, ss, rs, dev):
    return pltpu.make_async_remote_copy(
        src_ref=src, dst_ref=dst, send_sem=ss, recv_sem=rs, device_id=dev, device_id_type=MESH
    )


class LineGather:
    def __init__(self, p, nb, own, out, ssem, rsem):
        self.p, self.nb, self.own, self.out, self.ssem, self.rsem = p, nb, own, out, ssem, rsem

    def _copies(self, t):
        p, nb = self.p, self.nb
        rb = p.b - t
        lb = p.b + t
        src_r = self.own if t == 0 else self.out.at[jnp.maximum(rb, 0)]
        src_l = self.own if t == 0 else self.out.at[jnp.minimum(lb, nb - 1)]
        right = rcopy(src_r, self.out.at[jnp.maximum(rb, 0)], self.ssem.at[0, t], self.rsem.at[0, t], p.R)
        left = rcopy(src_l, self.out.at[jnp.minimum(lb, nb - 1)], self.ssem.at[1, t], self.rsem.at[1, t], p.L)
        return right, left, (rb >= 0) & (p.b < nb - 1), (lb <= nb - 1) & (p.b > 0)

    def start(self, t):
        right, left, cr, cl = self._copies(t)
        pl.when(cr)(right.start)
        pl.when(cl)(left.start)

    def wait_recv(self, t):
        p, nb = self.p, self.nb
        right, left, _, _ = self._copies(t)
        pl.when(p.b - 1 - t >= 0)(right.wait_recv)
        pl.when(p.b + 1 + t <= nb - 1)(left.wait_recv)

    def wait_send(self, t):
        right, left, cr, cl = self._copies(t)
        pl.when(cr)(right.wait_send)
        pl.when(cl)(left.wait_send)


class PlaneGather:
    def __init__(self, p, own, out, ssem, rsem, lsem):
        rows = own.shape[0]
        half = rows // 2

        def whole(i):
            return out.at[pl.ds(pl.multiple_of(i * rows, rows), rows)]

        def low(i):
            return out.at[pl.ds(pl.multiple_of(i * rows, rows), half)]

        def high(i):
            return out.at[pl.ds(pl.multiple_of(i * rows + half, half), half)]

        def send(k, src, dst, dev):
            return rcopy(src, dst, ssem.at[k], rsem.at[k], dev)

        self.x = send(0, own, whole(p.me), p.X)
        self.y = send(1, own, whole(p.me), p.Y)
        self.c = send(2, own, whole(p.me), p.C)
        self.local = pltpu.make_async_copy(own, whole(p.me), lsem)
        self.fx = send(3, high(p.yi), high(p.yi), p.X)
        self.fy = send(4, low(p.xi), low(p.xi), p.Y)
        self.cx = send(5, whole(p.xi), whole(p.xi), p.C)
        self.cy = send(6, whole(p.yi), whole(p.yi), p.C)
        self.cd0 = send(7, low(p.di), low(p.di), p.C)
        self.cd1 = send(8, high(p.di), high(p.di), p.C)

    def start(self):
        for k in (self.x, self.y, self.c, self.local):
            k.start()

    def forward(self):
        self.x.wait_recv()
        self.fy.start()
        self.cx.start()
        self.y.wait_recv()
        self.fx.start()
        self.cy.start()

    def diag(self):
        self.fy.wait_recv()
        self.cd0.start()
        self.fx.wait_recv()
        self.cd1.start()

    def finish(self):
        self.local.wait()
        for k in (self.c, self.cx, self.cy, self.cd0, self.cd1):
            k.wait_recv()

    def drain(self):
        for k in (self.x, self.y, self.c, self.fx, self.fy, self.cx, self.cy, self.cd0, self.cd1):
            k.wait_send()


def row_loop(rows, chunk, body):
    if rows == chunk:
        body(0)
    else:
        def step(i, _):
            body(pl.multiple_of(i * chunk, chunk))
            return 0
        lax.fori_loop(0, rows // chunk, step, 0)


class PlaneReduce:
    def __init__(self, p, nb, g, out, buf, stage, ss, rs, ls):
        self.p, self.nb = p, nb
        self.P, self.BX, self.BY, self.CX, self.CY, self.Z = buf
        self.O = out
        self.R, self.C = g.shape[-2:]
        self.dt = g.dtype
        self.ss, self.rs = ss, rs
        h = self.R // 2
        self.h = h
        lo, hi = pl.ds(0, h), pl.ds(h, h)
        self.chunk = 16 if self.C > 1024 else 48
        self.g = g
        self.stage = stage
        self.own = None if stage is None else pltpu.make_async_copy(g.at[:, :, p.c], stage, ls)
        self.cA = rcopy(g.at[:, :, 1 - p.c], self.P, ss.at[0], rs.at[0], p.C)
        self.cBX = rcopy(self.P.at[:, 1 - p.x, lo], self.BX, ss.at[1], rs.at[1], p.X)
        self.cBY = rcopy(self.P.at[1 - p.s, :, hi], self.BY, ss.at[2], rs.at[2], p.Y)
        self.cCX = rcopy(self.P.at[p.s, 1 - p.x, hi], self.CX, ss.at[3], rs.at[3], p.X)
        self.cCY = rcopy(self.P.at[1 - p.s, p.x, lo], self.CY, ss.at[4], rs.at[4], p.Y)
        self.F = self.P.at[p.s, p.x]

    def quarter(self, ref, j):
        R, C = self.R, self.C
        r, c = (j // 2) * (R // 2), (j % 2) * (C // 2)
        if not isinstance(j, int):
            r, c = pl.multiple_of(r, R // 2), pl.multiple_of(c, C // 2)
        return ref.at[pl.ds(r, R // 2), pl.ds(c, C // 2)]

    def a_start(self):
        self.cA.start()

    def own_start(self):
        self.own.start()

    def b_start(self):
        if self.own is not None:
            self.own.wait()
        self.cA.wait_recv()

        def block(i, _):
            s, x = i // 2, i % 2

            def body(r):
                rows = pl.ds(r, self.chunk)
                mine = self.g[s, x, self.p.c, rows] if self.stage is None else self.stage[s, x, rows]
                self.P[s, x, rows] = (
                    mine.astype(jnp.float32) + self.P[s, x, rows].astype(jnp.float32)
                ).astype(self.dt)
            row_loop(self.R, self.chunk, body)
            return 0
        lax.fori_loop(0, 4, block, 0)
        self.cBX.start()
        self.cBY.start()

    def _add(self, dst, src):
        chunk = min(self.chunk * 2, self.h)

        def body(r):
            rows = pl.ds(r, chunk)
            dst[rows] = (dst[rows].astype(jnp.float32) + src[rows].astype(jnp.float32)).astype(self.dt)
        row_loop(self.h, chunk if self.h % chunk == 0 else self.h, body)

    def c_start(self):
        p, h = self.p, self.h
        lo, hi = pl.ds(0, h), pl.ds(h, h)
        self.cBX.wait_recv()
        self._add(self.P.at[1 - p.s, p.x, lo], self.BX.at[1 - p.s])
        self.cCY.start()
        self.cBY.wait_recv()
        self._add(self.P.at[p.s, 1 - p.x, hi], self.BY.at[1 - p.x])
        self.cCX.start()
        self._add(self.P.at[p.s, p.x, lo], self.BX.at[p.s])
        self._add(self.P.at[p.s, p.x, hi], self.BY.at[p.x])


    def _right(self, j):
        return rcopy(self.quarter(self.F, j), self.Z.at[j], self.ss.at[5 + j], self.rs.at[5 + j], self.p.R)

    def _left(self, j, last):
        slot = self.nb if last else j
        k = 5 + self.nb + j
        return rcopy(self.quarter(self.F, j), self.Z.at[slot], self.ss.at[k], self.rs.at[k], self.p.L)

    def plane_end(self):
        h = self.h
        self.cCY.wait_recv()
        self._add(self.F.at[pl.ds(0, h)], self.CY)
        self.cCX.wait_recv()
        self._add(self.F.at[pl.ds(h, h)], self.CX)

    def hop(self, t):
        nb, p = self.nb, self.p
        if t == 0:
            self.plane_end()

        @pl.when(p.b == t)
        def _():
            for j in range(nb - 1, t, -1):
                if t > 0:
                    self._right(j).wait_recv()
                    self._add(self.quarter(self.F, j), self.Z.at[j])
                self._right(j).start()

        @pl.when(p.b == nb - 1 - t)
        def _():
            for j in range(nb - 1 - t):
                if t > 0:
                    self._left(j, False).wait_recv()
                    self._add(self.quarter(self.F, j), self.Z.at[j])
                self._left(j, j == nb - 2 - t).start()

    def _spread(self, t):
        p, nb = self.p, self.nb
        k = 5 + 2 * nb + 2 * t
        r, l = p.b - t, p.b + t
        qr = self.quarter(self.O, jnp.maximum(r, 0))
        ql = self.quarter(self.O, jnp.minimum(l, nb - 1))
        right = rcopy(qr, qr, self.ss.at[k], self.rs.at[k], p.R)
        left = rcopy(ql, ql, self.ss.at[k + 1], self.rs.at[k + 1], p.L)
        return right, left, (r >= 0) & (p.b < nb - 1), (l <= nb - 1) & (p.b > 0)

    def _spread_recv(self, t):
        right, left, _, _ = self._spread(t)
        p, nb = self.p, self.nb
        pl.when(p.b - 1 - t >= 0)(right.wait_recv)
        pl.when(p.b + 1 + t <= nb - 1)(left.wait_recv)

    def spread(self, t):
        p, nb = self.p, self.nb
        if t == 0:
            mine = self.quarter(self.F, p.b)
            for j in range(nb):
                @pl.when(p.b == j)
                def _():
                    if j > 0:
                        self._right(j).wait_recv()
                        self._add(mine, self.Z.at[j])
                    if j < nb - 1:
                        self._left(j, True).wait_recv()
                        self._add(mine, self.Z.at[nb])
            total = self.quarter(self.O, p.b)

            def body(r):
                rows = pl.ds(r, self.chunk)
                total[rows] = mine[rows]
            row_loop(self.h, self.chunk, body)
        else:
            self._spread_recv(t - 1)
        right, left, cr, cl = self._spread(t)
        pl.when(cr)(right.start)
        pl.when(cl)(left.start)

    def finish(self):
        self._spread_recv(self.nb - 2)

    def drain(self):
        nb, p = self.nb, self.p
        for k in (self.cA, self.cBX, self.cBY, self.cCX, self.cCY):
            k.wait_send()
        for t in range(nb - 1):
            @pl.when(p.b == t)
            def _():
                for j in range(nb - 1, t, -1):
                    self._right(j).wait_send()

            @pl.when(p.b == nb - 1 - t)
            def _():
                for j in range(nb - 1 - t):
                    self._left(j, j == nb - 2 - t).wait_send()
            right, left, cr, cl = self._spread(t)
            pl.when(cr)(right.wait_send)
            pl.when(cl)(left.wait_send)


def reduce_scratch(shape, dt, nb):
    R, C = shape
    h = R // 2
    return [
        pltpu.VMEM((2, 2, R, C), dt),
        pltpu.VMEM((2, h, C), dt),
        pltpu.VMEM((2, h, C), dt),
        pltpu.VMEM((h, C), dt),
        pltpu.VMEM((h, C), dt),
        pltpu.VMEM((nb + 1, h, C // 2), dt),
    ]


NBUF = 6


def reduce_sems(nb):
    return 5 + 2 * nb + 2 * (nb - 1)


class TableSum:
    def __init__(self, p, nb, t, bufs, line, ss, rs):
        self.p, self.nb, self.t, self.bufs, self.line = p, nb, t, bufs, line
        self.steps = [
            rcopy(t if i == 0 else bufs.at[i - 1], bufs.at[3 + i], ss.at[i], rs.at[i], dev)
            for i, dev in enumerate((p.C, p.X, p.Y))
        ]
        self.ss, self.rs = ss, rs

    def start(self):
        self.steps[0].start()

    def step(self, i):
        self.steps[i].wait_recv()
        self.bufs[i] = (self.t[...] if i == 0 else self.bufs[i - 1]) + self.bufs[3 + i]
        if i < 2:
            self.steps[i + 1].start()
        else:
            self.line[self.p.b] = self.bufs[2]
            for j in range(self.nb):
                pl.when(self.p.b != j)(self._z(j, self.p.b).start)

    def _z(self, j, slot):
        return rcopy(
            self.bufs.at[2], self.line.at[slot], self.ss.at[3 + j], self.rs.at[3 + slot], self.p.z(j)
        )

    def finish(self, out):
        for j in range(self.nb):
            pl.when(self.p.b != j)(self._z(j, j).wait_recv)
        total = self.line[0]
        for j in range(1, self.nb):
            total = total + self.line[j]
        out[...] = total

    def drain(self):
        for k in self.steps:
            k.wait_send()
        for j in range(self.nb):
            pl.when(self.p.b != j)(self._z(j, self.p.b).wait_send)


HEAD_DIM = 64
PAIR = 128
MASKED = -1e30
TILE = 512


def dot(a, b, ca, cb):
    return lax.dot_general(a, b, (((ca,), (cb,)), ((), ())), preferred_element_type=jnp.float32)


def left_lanes(shape):
    return lax.broadcasted_iota(jnp.int32, shape, 1) < HEAD_DIM


def one_head(pair, left, first):
    keep = left if first else jnp.logical_not(left)
    return jnp.where(keep, pair, jnp.zeros_like(pair))


def lane_groups(op, a):
    out = a[:, :PAIR]
    for g in range(1, a.shape[1] // PAIR):
        out = op(out, a[:, g * PAIR:(g + 1) * PAIR])
    return out


def attn_fwd_kernel(span, col_ref, row_ref, q_ref, k_ref, v_ref, o_ref, ob_ref, lse_ref, s_ref, m_ref, l_ref, acc_ref):
    rows = q_ref.shape[0]
    left = left_lanes((rows, PAIR))
    m_ref[...] = jnp.full_like(m_ref, MASKED)
    l_ref[...] = jnp.zeros_like(l_ref)
    acc_ref[...] = jnp.zeros_like(acc_ref)
    q = q_ref[...]
    heads = [one_head(q, left, i == 0) for i in range(2)]
    codes = col_ref[...]

    def score(t, _):
        at = pl.multiple_of(t * TILE, TILE)
        k = k_ref[pl.ds(at, TILE), :]
        mask = codes == row_ref[:, pl.ds(at, TILE)]
        for i in range(2):
            s = jnp.where(mask, dot(heads[i], k, 1, 1), MASKED)
            s_ref[i, t] = s
            m_ref[i] = jnp.maximum(m_ref[i], lane_groups(jnp.maximum, s))
        return 0

    lax.fori_loop(span[0], span[1], score, 0)
    tops = [jnp.max(m_ref[i], axis=1, keepdims=True) for i in range(2)]

    def mix(t, _):
        v = v_ref[pl.ds(pl.multiple_of(t * TILE, TILE), TILE), :]
        parts = []
        for i in range(2):
            p = jnp.exp(s_ref[i, t] - tops[i])
            l_ref[i] += lane_groups(jnp.add, p)
            parts.append(dot(p.astype(jnp.bfloat16), v, 1, 0))
        acc_ref[...] += jnp.where(left, parts[0], parts[1])
        return 0

    lax.fori_loop(span[0], span[1], mix, 0)
    sums = [jnp.sum(l_ref[i], axis=1, keepdims=True) for i in range(2)]
    total = jnp.where(left, sums[0], sums[1])
    o = acc_ref[...] / total
    o_ref[...] = o
    ob_ref[...] = o.astype(jnp.bfloat16)
    lse_ref[...] = jnp.where(left, tops[0], tops[1]) + jnp.log(total)


def attention(q, k_all, v_all, codes, own_codes, span):
    rows, width = q.shape
    total = k_all.shape[0]
    pairs = width // PAIR
    own = pl.BlockSpec((rows, PAIR), lambda h, s: (0, h))
    every = pl.BlockSpec((total, PAIR), lambda h, s: (0, h))
    return pl.pallas_call(
        attn_fwd_kernel,
        grid_spec=pltpu.PrefetchScalarGridSpec(
            num_scalar_prefetch=1,
            grid=(pairs,),
            in_specs=[
                pl.BlockSpec((rows, 1), lambda h, s: (0, 0)),
                pl.BlockSpec((1, total), lambda h, s: (0, 0)),
                own, every, every,
            ],
            out_specs=[own, own, own],
            scratch_shapes=[
                pltpu.VMEM((2, total // TILE, rows, TILE), jnp.float32),
                pltpu.VMEM((2, rows, PAIR), jnp.float32),
                pltpu.VMEM((2, rows, PAIR), jnp.float32),
                pltpu.VMEM((rows, PAIR), jnp.float32),
            ],
        ),
        out_shape=[
            jax.ShapeDtypeStruct((rows, width), jnp.float32),
            jax.ShapeDtypeStruct((rows, width), jnp.bfloat16),
            jax.ShapeDtypeStruct((rows, width), jnp.float32),
        ],
        compiler_params=pltpu.CompilerParams(vmem_limit_bytes=48 << 20),
        name="attention",
    )(span, own_codes.reshape(rows, 1), codes.reshape(1, total), q, k_all, v_all)


def stats_kernel(g_ref, o_ref, lse_ref, out_ref, delta_ref):
    rows = g_ref.shape[0]
    left = left_lanes((rows, PAIR))
    t = g_ref[...].astype(jnp.float32) * o_ref[...]
    d0 = jnp.sum(jnp.where(left, t, 0.0), axis=1, keepdims=True)
    d1 = jnp.sum(jnp.where(left, 0.0, t), axis=1, keepdims=True)
    delta_ref[...] = jnp.where(left, d0, d1)
    lane = lax.broadcasted_iota(jnp.int32, (rows, PAIR), 1)
    lse = lse_ref[...]
    packed = jnp.where(lane == 0, lse[:, :1], jnp.where(lane == 1, lse[:, HEAD_DIM:HEAD_DIM + 1], jnp.where(lane == 2, d0, d1)))
    out_ref[0] = packed.T[:8]


def row_stats(grad, o, lse):
    rows, width = grad.shape
    pairs = width // PAIR
    own = pl.BlockSpec((rows, PAIR), lambda h: (0, h))
    return pl.pallas_call(
        stats_kernel,
        grid=(pairs,),
        in_specs=[own, own, own],
        out_specs=[pl.BlockSpec((1, 8, rows), lambda h: (h, 0, 0)), own],
        out_shape=[
            jax.ShapeDtypeStruct((pairs, 8, rows), jnp.float32),
            jax.ShapeDtypeStruct((rows, width), jnp.float32),
        ],
        name="row_stats",
    )(grad, o, lse)


def attn_bwd_kernel(span, col_ref, row_ref, q_ref, k_ref, v_ref, g_ref, lse_ref, delta_ref,
                    qa_ref, ka_ref, va_ref, ga_ref, st_ref, dq_ref, dk_ref, dv_ref):
    rows = q_ref.shape[0]
    left = left_lanes((rows, PAIR))
    dq_ref[...] = jnp.zeros_like(dq_ref)
    dk_ref[...] = jnp.zeros_like(dk_ref)
    dv_ref[...] = jnp.zeros_like(dv_ref)
    codes = col_ref[...]
    qs = [one_head(q_ref[...], left, i == 0) for i in range(2)]
    ks = [one_head(k_ref[...], left, i == 0) for i in range(2)]
    vs = [one_head(v_ref[...], left, i == 0) for i in range(2)]
    gs = [one_head(g_ref[...], left, i == 0) for i in range(2)]
    lses = [lse_ref[:, i * HEAD_DIM:i * HEAD_DIM + 1] for i in range(2)]
    deltas = [delta_ref[:, i * HEAD_DIM:i * HEAD_DIM + 1] for i in range(2)]

    def step(t, _):
        at = pl.multiple_of(t * TILE, TILE)
        tile = pl.ds(at, TILE)
        mask = codes == row_ref[:, tile]
        k, v, q, g = ka_ref[tile, :], va_ref[tile, :], qa_ref[tile, :], ga_ref[tile, :]
        dqs, dks, dvs = [], [], []
        for i in range(2):
            s = jnp.where(mask, dot(qs[i], k, 1, 1), MASKED)
            p = jnp.exp(s - lses[i])
            dp = dot(gs[i], v, 1, 1)
            ds = (p * (dp - deltas[i])).astype(jnp.bfloat16)
            dqs.append(dot(ds, k, 1, 0))
            st = jnp.where(mask, dot(ks[i], q, 1, 1), MASKED)
            pt = jnp.exp(st - st_ref[0, i:i + 1, tile])
            dvs.append(dot(pt.astype(jnp.bfloat16), g, 1, 0))
            dpt = dot(vs[i], g, 1, 1)
            dst = (pt * (dpt - st_ref[0, 2 + i:3 + i, tile])).astype(jnp.bfloat16)
            dks.append(dot(dst, q, 1, 0))
        dq_ref[...] += jnp.where(left, dqs[0], dqs[1])
        dk_ref[...] += jnp.where(left, dks[0], dks[1])
        dv_ref[...] += jnp.where(left, dvs[0], dvs[1])
        return 0

    lax.fori_loop(span[0], span[1], step, 0)


def attention_grad(q, k, v, g, lse, delta, q_all, k_all, v_all, g_all, stats, codes, own_codes, span):
    rows, width = q.shape
    total = k_all.shape[0]
    pairs = width // PAIR
    own = pl.BlockSpec((rows, PAIR), lambda h, s: (0, h))
    every = pl.BlockSpec((total, PAIR), lambda h, s: (0, h))
    return pl.pallas_call(
        attn_bwd_kernel,
        grid_spec=pltpu.PrefetchScalarGridSpec(
            num_scalar_prefetch=1,
            grid=(pairs,),
            in_specs=[
                pl.BlockSpec((rows, 1), lambda h, s: (0, 0)),
                pl.BlockSpec((1, total), lambda h, s: (0, 0)),
                own, own, own, own, own, own, every, every, every, every,
                pl.BlockSpec((1, 8, total), lambda h, s: (h, 0, 0)),
            ],
            out_specs=[own, own, own],
        ),
        out_shape=[
            jax.ShapeDtypeStruct((rows, width), jnp.float32),
            jax.ShapeDtypeStruct((rows, width), jnp.float32),
            jax.ShapeDtypeStruct((rows, width), jnp.float32),
        ],
        compiler_params=pltpu.CompilerParams(vmem_limit_bytes=48 << 20),
        name="attention_grad",
    )(span, own_codes.reshape(rows, 1), codes.reshape(1, total), q, k, v, g, lse, delta, q_all, k_all, v_all, g_all, stats)


VEC_ROWS = 8


def forward_kernel(nb, *refs):
    x_ref, codes, rows = refs[:3]
    shards_in = refs[3:9]
    vecs_in = refs[9:18]
    wq_o, wk_o, wv_o, wo_o, wup_o, wdn_o = refs[18:24]
    q_o, k_o, v_o = refs[24:27]
    o_ref, ob_ref, lse_ref, vec_ref, bup_ref = refs[27:32]
    rest = refs[32:]
    x_all, wq, wk, wv, pack, packs, q, k, v, m_ref, l_ref = rest[:11]
    zs, zr, gs, gr, gl, ws, es = rest[11:]
    n, width = x_ref.shape
    pairs = width // PAIR
    p = Place()
    own = pltpu.make_async_copy(x_ref, x_all.at[p.b], ws.at[3])
    own.start()
    pack[...] = jnp.zeros_like(pack)
    for i in range(VEC_ROWS):
        pack[i:i + 1, :vecs_in[i].shape[1]] = vecs_in[i][...].astype(jnp.float32)
    for i in range(vecs_in[8].shape[1] // PAIR):
        pack[VEC_ROWS + i:VEC_ROWS + i + 1, :] = vecs_in[8][:, i * PAIR:(i + 1) * PAIR].astype(jnp.float32)
    enter(p, nb, True, "near")
    line = LineGather(p, nb, x_ref, x_all, zs, zr)
    targets = (packs, wq, wk, wv, wo_o, wup_o, wdn_o)
    sources = (pack,) + tuple(shards_in)
    g = [PlaneGather(p, sources[i], targets[i], gs.at[i], gr.at[i], gl.at[i]) for i in range(7)]
    line.start(0)
    for c in g[:5]:
        c.start()
    for c in g[:4]:
        c.forward()
    g[5].start()
    g[6].start()
    line.wait_recv(0)
    line.start(1)
    for c in g[:4]:
        c.diag()
    for c in g[:4]:
        c.finish()
    own.wait()
    keep = [
        pltpu.make_async_copy(a, b, ws.at[i]) for i, (a, b) in enumerate(((wq, wq_o), (wk, wk_o), (wv, wv_o)))
    ]
    for c in keep:
        c.start()

    piece = width // 8
    r = lax.broadcasted_iota(jnp.int32, (PAIR, width), 0)
    c = lax.broadcasted_iota(jnp.int32, (PAIR, width), 1)
    total = jnp.zeros((2 * VEC_ROWS, width), jnp.float32)
    for i in range(8):
        pick = ((c == r + i * piece) & (r < piece)).astype(jnp.bfloat16)
        total += dot(packs[2 * VEC_ROWS * i:2 * VEC_ROWS * (i + 1), :].astype(jnp.bfloat16), pick, 1, 0)
    vec_ref[...] = total[:VEC_ROWS]
    up_piece = bup_ref.shape[1] // 8
    for i in range(8):
        for t in range(up_piece // PAIR):
            at = i * up_piece + t * PAIR
            row = 2 * VEC_ROWS * i + VEC_ROWS + t
            bup_ref[:, at:at + PAIR] = packs[row:row + 1, :]

    scale = HEAD_DIM ** (-0.5)
    step = 256

    def outs(j, e):
        return [
            pltpu.make_async_copy(a.at[j], b.at[j], es.at[i, e])
            for i, (a, b) in enumerate(((q, q_o), (k, k_o), (v, v_o)))
        ]

    def project(j):
        def columns(t, _):
            at = pl.ds(pl.multiple_of(t * step, step), step)
            xs = x_all[j]
            q[j, :, at] = ((dot(xs, wq[:, at], 1, 0) + vec_ref[0:1, at]) * scale).astype(jnp.bfloat16)
            k[j, :, at] = dot(xs, wk[:, at], 1, 0).astype(jnp.bfloat16)
            v[j, :, at] = (dot(xs, wv[:, at], 1, 0) + vec_ref[1:2, at]).astype(jnp.bfloat16)
            return 0
        lax.fori_loop(0, width // step, columns, 0)

    def attend(j, first):
        def pair(h, _):
            left = left_lanes((n, PAIR))
            lanes = pl.ds(pl.multiple_of(h * PAIR, PAIR), PAIR)
            mask = codes[...] == rows[j]
            qs, ks, vs = q[p.b, :, lanes], k[j, :, lanes], v[j, :, lanes]
            parts, alphas = [], []
            for i in range(2):
                s = jnp.where(mask, dot(one_head(qs, left, i == 0), ks, 1, 1), MASKED)
                top = jnp.max(lane_groups(jnp.maximum, s), axis=1, keepdims=True)
                if first:
                    new = jnp.broadcast_to(top, (n, PAIR))
                else:
                    old = m_ref[2 * h + i]
                    new = jnp.maximum(old, top)
                    alpha = jnp.exp(old - new)
                    alphas.append(alpha)
                e = jnp.exp(s - jnp.concatenate([new] * (n // PAIR), axis=1))
                mass = lane_groups(jnp.add, e)
                m_ref[2 * h + i] = new
                l_ref[2 * h + i] = mass if first else l_ref[2 * h + i] * alpha + mass
                parts.append(dot(e.astype(jnp.bfloat16), vs, 1, 0))
            got = jnp.where(left, parts[0], parts[1])
            if first:
                o_ref[:, lanes] = got
            else:
                o_ref[:, lanes] = o_ref[:, lanes] * jnp.where(left, alphas[0], alphas[1]) + got
            return 0
        lax.fori_loop(0, pairs, pair, 0)

    def block(j, e):
        project(j)
        for c in outs(j, e):
            c.start()
        attend(j, e == 0)

    def left_of(t):
        return p.b - 1 - t >= 0, jnp.maximum(p.b - 1 - t, 0)

    def right_of(t):
        return p.b + 1 + t <= nb - 1, jnp.minimum(p.b + 1 + t, nb - 1)

    def arrived(t, side):
        ok, j = (left_of(t), right_of(t))[side]

        @pl.when(ok)
        def _():
            block(j, 1 + 2 * t + side)

    project(p.b)
    for c in outs(p.b, 0):
        c.start()
    g[4].forward()
    attend(p.b, True)
    g[5].forward()
    arrived(0, 0)
    line.wait_recv(1)
    line.start(2)
    arrived(0, 1)
    g[6].forward()
    g[4].diag()
    arrived(1, 0)
    arrived(1, 1)
    g[5].diag()
    line.wait_recv(2)
    g[6].diag()
    arrived(2, 0)
    arrived(2, 1)

    def close(h, _):
        left = left_lanes((n, PAIR))
        lanes = pl.ds(pl.multiple_of(h * PAIR, PAIR), PAIR)
        sums = [jnp.sum(l_ref[2 * h + i], axis=1, keepdims=True) for i in range(2)]
        mass = jnp.where(left, sums[0], sums[1])
        out = o_ref[:, lanes] / mass
        o_ref[:, lanes] = out
        ob_ref[:, lanes] = out.astype(jnp.bfloat16)
        lse_ref[:, lanes] = jnp.where(left, m_ref[2 * h], m_ref[2 * h + 1]) + jnp.log(mass)
        return 0
    lax.fori_loop(0, pairs, close, 0)
    for c in g[4:]:
        c.finish()
    for c in keep:
        c.wait()
    for c in outs(p.b, 0):
        c.wait()
    for t in range(nb - 1):
        for side, (ok, j) in enumerate((left_of(t), right_of(t))):
            @pl.when(ok)
            def _():
                for c in outs(j, 1 + 2 * t + side):
                    c.wait()
    for t in range(nb - 1):
        line.wait_send(t)
    for c in g:
        c.drain()


def forward(x, codes, own_codes, weights, vecs, nb):
    n, width = x.shape
    hidden = weights[4].shape[1]
    bf, f32 = jnp.bfloat16, jnp.float32
    every = jax.ShapeDtypeStruct((nb, n, width), bf)
    block = jax.ShapeDtypeStruct((n, width), f32)
    mats = [jax.ShapeDtypeStruct((8 * w.shape[0], w.shape[1]), w.dtype) for w in weights]
    dma = pltpu.SemaphoreType.DMA
    return pl.pallas_call(
        functools.partial(forward_kernel, nb),
        out_shape=(
            *mats, every, every, every, block, jax.ShapeDtypeStruct((n, width), bf), block,
            jax.ShapeDtypeStruct((VEC_ROWS, width), f32), jax.ShapeDtypeStruct((1, hidden), f32),
        ),
        in_specs=[VM] * 18,
        out_specs=(ANY,) * 9 + (VM,) * 5,
        scratch_shapes=[
            pltpu.VMEM((nb, n, width), bf),
            pltpu.VMEM((width, width), bf), pltpu.VMEM((width, width), bf), pltpu.VMEM((width, width), bf),
            pltpu.VMEM((2 * VEC_ROWS, PAIR), f32), pltpu.VMEM((16 * VEC_ROWS, PAIR), f32),
            pltpu.VMEM((nb, n, width), bf), pltpu.VMEM((nb, n, width), bf), pltpu.VMEM((nb, n, width), bf),
            pltpu.VMEM((width // HEAD_DIM, n, PAIR), f32), pltpu.VMEM((width // HEAD_DIM, n, PAIR), f32),
            dma((2, nb - 1)), dma((2, nb - 1)), dma((7, 9)), dma((7, 9)), dma((7,)), dma((4,)), dma((3, 2 * nb)),
        ],
        compiler_params=pltpu.CompilerParams(
            collective_id=1, has_side_effects=True, vmem_limit_bytes=60 << 20
        ),
        name="forward",
    )(
        x, own_codes.reshape(n, 1), codes.reshape(nb, 1, n), *weights, *[v.reshape(1, -1) for v in vecs]
    )


ROOT_HALF = 0.7071067811865476
ROOT_TWO_PI = 0.3989422804014327
CHUNK = 768
PART = 256


def erf_parts(x):
    x = jnp.clip(x, -3.832506856900711, 3.832506856900711)
    y = x * x
    top = jnp.full_like(y, 0.00022905065861350646)
    for a in (0.0034082910107109506, 0.050955695062380861, 0.18520832239976145, 1.128379143519084):
        top = top * y + a
    low = jnp.full_like(y, -1.1791602954361697e-7)
    for a in (
        0.000023547966471313185, 0.0010179625278914885, 0.014070470171167667,
        0.11098505178285362, 0.49746925110067538, 1.0,
    ):
        low = low * y + a
    return x * top / low


def middle_kernel(
    att_ref, x_ref, cot_ref, o_ref, lse_ref, vec_ref, bup_ref, wo_hbm, wup_hbm, wdn_hbm,
    out_ref, rest_ref, do_ref, stats_ref, delta_ref, table_ref, gdn_hbm, gup_hbm, gwo_ref,
    wo, wup, wdn, u_ref, slope_ref, y_ref, dh_ref, low_ref, gdn, gup, sems, osems,
):
    n, width = x_ref.shape
    hidden = wup.shape[1]
    chunks = hidden // CHUNK
    f32, bf = jnp.float32, jnp.bfloat16
    loads = [
        pltpu.make_async_copy(a, b, sems.at[i])
        for i, (a, b) in enumerate(((wo_hbm, wo), (wup_hbm, wup), (wdn_hbm, wdn)))
    ]
    for c in loads:
        c.start()
    table_ref[...] = jnp.zeros_like(table_ref)

    def vec(i):
        return vec_ref[i:i + 1, :]

    def mean(a):
        return jnp.sum(a, axis=1, keepdims=True) * (1.0 / width)

    def centred(h):
        c = h - mean(h)
        inv = lax.rsqrt(mean(c * c) + EPSILON)
        return c * inv, inv

    def pull(grad, hat, inv, gain):
        d = grad * gain
        return inv * (d - mean(d) - hat * mean(d * hat))

    def column_sum(a):
        return jnp.sum(a, axis=0, keepdims=True)

    blocks = 4
    m = n // blocks

    def rows_of(i):
        return pl.ds(pl.multiple_of(i * m, m), m)

    loads[0].wait()

    def first(i, _):
        r = rows_of(i)
        h = x_ref[r, :].astype(f32) + dot(att_ref[r, :], wo[...], 1, 0) + vec(2)
        hat, _ = centred(h)
        y = hat * vec(3) + vec(4)
        rest_ref[r, :] = h
        dh_ref[r, :] = y + vec(5)
        low_ref[r, :] = y.astype(bf)
        return 0
    lax.fori_loop(0, blocks, first, 0)
    for c in loads[1:]:
        c.wait()

    def up(t, _):
        total = dh_ref[...]
        for s in range(CHUNK // PART):
            at = pl.ds(pl.multiple_of(t * CHUNK + s * PART, PART), PART)
            z = dot(low_ref[...], wup[:, at], 1, 0) + bup_ref[:, at]
            cdf = 0.5 + 0.5 * erf_parts(z * ROOT_HALF)
            low = (z * cdf).astype(bf)
            u_ref[:, at] = low
            slope_ref[:, at] = cdf + z * (jnp.exp(-0.5 * z * z) * ROOT_TWO_PI)
            total = total + dot(low, wdn[at, :], 1, 0)
        dh_ref[...] = total
        return 0
    lax.fori_loop(0, chunks, up, 0)

    def second(i, _):
        r = rows_of(i)
        hat, inv = centred(dh_ref[r, :])
        out_ref[r, :] = (hat * vec(6) + vec(7)).astype(bf)
        g = cot_ref[r, :].astype(f32)
        table_ref[6:7, :] += column_sum(g * hat)
        table_ref[7:8, :] += column_sum(g)
        dh = pull(g, hat, inv, vec(6))
        table_ref[5:6, :] += column_sum(dh)
        dh_ref[r, :] = dh
        y_ref[r, :] = dh.astype(bf)
        return 0
    lax.fori_loop(0, blocks, second, 0)

    def down(t, _):
        at = pl.ds(pl.multiple_of(t * CHUNK, CHUNK), CHUNK)
        parts = []
        total = dh_ref[...]
        for s in range(CHUNK // PART):
            cols = pl.ds(pl.multiple_of(t * CHUNK + s * PART, PART), PART)
            dz = dot(y_ref[...], wdn[cols, :], 1, 1) * slope_ref[:, cols]
            table_ref[pl.ds(8 + t, 1), s * PART:(s + 1) * PART] = column_sum(dz)
            c = dz.astype(bf)
            parts.append(c)
            total = total + dot(c, wup[:, cols], 1, 1)
            gdn[cols, :] = dot(u_ref[:, cols], y_ref[...], 0, 0).astype(bf)
        dh_ref[...] = total
        c = jnp.concatenate(parts, axis=1)
        r = width // 8
        for i in range(2):
            half = width // 2
            g = dot(low_ref[:, i * half:(i + 1) * half], c, 0, 0).astype(bf)
            for k in range(4):
                gup[4 * i + k, t] = g[k * r:(k + 1) * r]
        pltpu.make_async_copy(gdn.at[at], gdn_hbm.at[at], osems.at[0, t]).start()
        pltpu.make_async_copy(gup.at[:, t], gup_hbm.at[:, t], osems.at[1, t]).start()
        return 0
    lax.fori_loop(0, chunks, down, 0)

    def third(i, _):
        r = rows_of(i)
        hat, inv = centred(rest_ref[r, :])
        g = dh_ref[r, :]
        table_ref[3:4, :] += column_sum(g * hat)
        table_ref[4:5, :] += column_sum(g)
        dh = pull(g, hat, inv, vec(3))
        table_ref[2:3, :] += column_sum(dh)
        rest_ref[r, :] = dh
        low = dh.astype(bf)
        low_ref[r, :] = low
        do_ref[r, :] = dot(low, wo[...], 1, 1).astype(bf)
        return 0
    lax.fori_loop(0, blocks, third, 0)

    def heads(h, _):
        lanes = pl.ds(pl.multiple_of(h * PAIR, PAIR), PAIR)
        left = left_lanes((n, PAIR))
        t = do_ref[:, lanes].astype(f32) * o_ref[:, lanes]
        d0 = jnp.sum(jnp.where(left, t, 0.0), axis=1, keepdims=True)
        d1 = jnp.sum(jnp.where(left, 0.0, t), axis=1, keepdims=True)
        delta_ref[:, lanes] = jnp.where(left, d0, d1)
        lane = lax.broadcasted_iota(jnp.int32, (n, PAIR), 1)
        lse = lse_ref[:, lanes]
        packed = jnp.where(lane == 0, lse[:, :1], jnp.where(
            lane == 1, lse[:, HEAD_DIM:HEAD_DIM + 1], jnp.where(lane == 2, d0, d1)))
        stats_ref[h] = packed.T[:8]
        gwo_ref[lanes, :] = dot(att_ref[:, lanes], low_ref[...], 0, 0).astype(bf)
        return 0
    lax.fori_loop(0, width // PAIR, heads, 0)
    for t in range(chunks):
        at = pl.ds(t * CHUNK, CHUNK)
        pltpu.make_async_copy(gdn.at[at], gdn_hbm.at[at], osems.at[0, t]).wait()
        pltpu.make_async_copy(gup.at[:, t], gup_hbm.at[:, t], osems.at[1, t]).wait()


def middle(att, x, cot, o, lse, vecs, bup, wo, wup, wdn):
    n, width = x.shape
    hidden = wup.shape[1]
    chunks = hidden // CHUNK
    bf, f32 = jnp.bfloat16, jnp.float32
    S = jax.ShapeDtypeStruct
    dma = pltpu.SemaphoreType.DMA
    return pl.pallas_call(
        middle_kernel,
        out_shape=(
            S((n, width), bf), S((n, width), f32), S((n, width), bf), S((width // PAIR, 8, n), f32),
            S((n, width), f32), S((16, width), f32), S((hidden, width), bf),
            S((8, chunks, width // 8, CHUNK), bf), S((width, width), bf),
        ),
        in_specs=[VM] * 7 + [ANY] * 3,
        out_specs=(VM,) * 6 + (ANY, ANY, VM),
        scratch_shapes=[
            pltpu.VMEM((width, width), bf), pltpu.VMEM((width, hidden), bf), pltpu.VMEM((hidden, width), bf),
            pltpu.VMEM((n, hidden), bf), pltpu.VMEM((n, hidden), f32), pltpu.VMEM((n, width), bf),
            pltpu.VMEM((n, width), f32), pltpu.VMEM((n, width), bf),
            pltpu.VMEM((hidden, width), bf), pltpu.VMEM((8, chunks, width // 8, CHUNK), bf),
            dma((3,)), dma((2, chunks)),
        ],
        compiler_params=pltpu.CompilerParams(vmem_limit_bytes=60 << 20),
        name="middle",
    )(att, x, cot, o, lse, vecs, bup, wo, wup, wdn)


class AttentionGrad:
    def __init__(self, codes, rows, q, k, v, g, lse, delta, stats, own, dq, dk, dv):
        self.codes, self.rows = codes, rows
        self.q, self.k, self.v, self.g = q, k, v, g
        self.lse, self.delta, self.stats = lse, delta, stats
        self.own = own
        self.dq, self.dk, self.dv = dq, dk, dv
        self.n = dq.shape[0]
        self.pairs = dq.shape[1] // PAIR

    def queries(self, j, first):
        own = self.own

        def pair(h, _):
            left = left_lanes((self.n, PAIR))
            lanes = pl.ds(pl.multiple_of(h * PAIR, PAIR), PAIR)
            mask = self.codes[...] == self.rows[j]
            q, g = self.q[own, :, lanes], self.g[own, :, lanes]
            k, v = self.k[j, :, lanes], self.v[j, :, lanes]
            lse, delta = self.lse[:, lanes], self.delta[:, lanes]
            parts = []
            for i in range(2):
                at = slice(i * HEAD_DIM, i * HEAD_DIM + 1)
                s = jnp.where(mask, dot(one_head(q, left, i == 0), k, 1, 1), MASKED)
                p = jnp.exp(s - lse[:, at])
                dp = dot(one_head(g, left, i == 0), v, 1, 1)
                ds = (p * (dp - delta[:, at])).astype(jnp.bfloat16)
                parts.append(dot(ds, k, 1, 0))
            new = jnp.where(left, parts[0], parts[1])
            if first:
                self.dq[:, lanes] = new
            else:
                self.dq[:, lanes] += new
            return 0

        lax.fori_loop(0, self.pairs, pair, 0)

    def keys(self, j, first):
        own = self.own

        def pair(h, _):
            left = left_lanes((self.n, PAIR))
            lanes = pl.ds(pl.multiple_of(h * PAIR, PAIR), PAIR)
            mask = self.codes[...] == self.rows[j]
            k, v = self.k[own, :, lanes], self.v[own, :, lanes]
            q, g = self.q[j, :, lanes], self.g[j, :, lanes]
            dks, dvs = [], []
            for i in range(2):
                st = jnp.where(mask, dot(one_head(k, left, i == 0), q, 1, 1), MASKED)
                pt = jnp.exp(st - self.stats[j, h, i:i + 1])
                dvs.append(dot(pt.astype(jnp.bfloat16), g, 1, 0))
                dpt = dot(one_head(v, left, i == 0), g, 1, 1)
                dst = (pt * (dpt - self.stats[j, h, 2 + i:3 + i])).astype(jnp.bfloat16)
                dks.append(dot(dst, q, 1, 0))
            dk, dv = jnp.where(left, dks[0], dks[1]), jnp.where(left, dvs[0], dvs[1])
            if first:
                self.dk[:, lanes] = dk
                self.dv[:, lanes] = dv
            else:
                self.dk[:, lanes] += dk
                self.dv[:, lanes] += dv
            return 0

        lax.fori_loop(0, self.pairs, pair, 0)


TABLE = 16


def backward_kernel(nb, *refs):
    codes, rows, g_own, st_own, lse, delta, x_ref, rest_ref, table = refs[:9]
    q_hbm, k_hbm, v_hbm, wq_hbm, wk_hbm, wv_hbm = refs[9:15]
    early = refs[15:18]
    token_ref, table_out = refs[18:20]
    outs = refs[20:26]
    rest = refs[26:]
    q, k, v, g, stats, dq, dk, dv, wq, wk, wv, gw, stage_a, stage_b, tab, tsum, tline = rest[:17]
    bufs = rest[17:17 + 6 * NBUF]
    zs, zr, ls, ss, rs, rls, ts, tr = rest[17 + 6 * NBUF:]
    n, width = g_own.shape
    p = Place()
    loads = [
        pltpu.make_async_copy(a, b, ls.at[i])
        for i, (a, b) in enumerate((
            (k_hbm, k), (v_hbm, v), (q_hbm, q), (g_own, g.at[p.b]), (st_own, stats.at[p.b]),
            (wq_hbm, wq), (wk_hbm, wk), (wv_hbm, wv),
        ))
    ]
    for c in loads:
        c.start()
    enter(p, nb, True, "all")
    lines = [
        LineGather(p, nb, g_own, g, zs.at[0], zr.at[0]),
        LineGather(p, nb, st_own, stats, zs.at[1], zr.at[1]),
    ]
    sources = tuple(early) + tuple(gw.at[i] for i in range(3))
    stages = (stage_a, stage_a, stage_b, None, None, None)
    dn, up, wo, gq, gk, gv = [
        PlaneReduce(
            p, nb, sources[i], outs[i], bufs[NBUF * i:NBUF * (i + 1)],
            None if stages[i] is None else stages[i].reshape(sources[i].shape[:2] + sources[i].shape[3:]),
            ss.at[i], rs.at[i], rls.at[i],
        )
        for i in range(6)
    ]
    vec = TableSum(p, nb, tab, tsum, tline, ts, tr)
    for c in lines:
        c.start(0)
    for c in (dn, up, wo):
        c.a_start()
    dn.own_start()
    wo.own_start()
    work = AttentionGrad(codes, rows, q, k, v, g, lse, delta, stats, p.b, dq, dk, dv)
    for c in loads:
        c.wait()

    def take(t, side):
        ok, j = ((p.b - 1 - t >= 0, p.b - 1 - t), (p.b + 1 + t <= nb - 1, p.b + 1 + t))[side]

        @pl.when(ok)
        def _():
            work.keys(jnp.clip(j, 0, nb - 1), False)

    low = k
    def slot(i):
        return (p.b + 1 + i) % nb

    def settle(i, src, scale, row):
        value = src[...] if scale is None else src[...] * scale
        if row is not None:
            tab[row:row + 1, :] = jnp.sum(value, axis=0, keepdims=True)
        low[slot(i)] = value.astype(jnp.bfloat16)

    def weight_grad(i):
        half = width // 2
        for m in range(2):
            part = dot(x_ref[:, m * half:(m + 1) * half], low[slot(i)], 0, 0).astype(jnp.bfloat16)
            r = gw.shape[-2]
            for a in range(2):
                for b in range(2):
                    at = (2 * a + b) * r
                    gw[i, m, a, b] = part[at:at + r]

    work.queries(p.b, True)
    dn.b_start()
    up.own_start()
    work.queries((p.b + 1) % nb, False)
    up.b_start()
    wo.b_start()
    for c in lines:
        c.wait_recv(0)
        c.start(1)
    work.queries((p.b + 2) % nb, False)
    dn.c_start()
    work.queries((p.b + 3) % nb, False)
    tab[...] = table[...]
    settle(0, dq, HEAD_DIM ** (-0.5), 0)
    weight_grad(0)
    gq.a_start()
    for c in lines:
        c.wait_recv(1)
        c.start(2)
    up.c_start()
    work.keys(p.b, True)
    gq.b_start()
    wo.c_start()
    take(0, 0)
    dn.hop(0)
    take(0, 1)
    up.hop(0)
    wo.hop(0)
    gq.c_start()
    dn.hop(1)
    take(1, 0)
    take(1, 1)
    up.hop(1)
    wo.hop(1)
    dn.hop(2)
    for c in lines:
        c.wait_recv(2)
    take(2, 0)
    take(2, 1)
    settle(1, dk, None, None)
    settle(2, dv, None, 1)
    vec.start()
    weight_grad(1)
    gk.a_start()
    weight_grad(2)
    gv.a_start()
    up.hop(2)
    wo.hop(2)
    dn.spread(0)
    vec.step(0)
    gk.b_start()
    gv.b_start()
    gq.hop(0)
    vec.step(1)

    part = 256

    def columns(t, _):
        at = pl.ds(pl.multiple_of(t * part, part), part)
        total = rest_ref[:, at]
        for i, w in enumerate((wq, wk, wv)):
            total = total + dot(low[slot(i)], w[at, :], 1, 1)
        token_ref[:, at] = total.astype(jnp.bfloat16)
        return 0
    lax.fori_loop(0, width // part, columns, 0)

    up.spread(0)
    wo.spread(0)
    dn.spread(1)
    vec.step(2)
    gk.c_start()
    gv.c_start()
    gq.hop(1)
    up.spread(1)
    wo.spread(1)
    dn.spread(2)
    gq.hop(2)
    gk.hop(0)
    gv.hop(0)
    gq.spread(0)
    gk.hop(1)
    gv.hop(1)
    up.spread(2)
    wo.spread(2)
    gk.hop(2)
    gv.hop(2)
    gq.spread(1)
    gk.spread(0)
    gv.spread(0)
    gq.spread(2)
    gk.spread(1)
    gv.spread(1)
    gk.spread(2)
    gv.spread(2)
    vec.finish(table_out)
    every = (dn, up, wo, gq, gk, gv)
    for c in every:
        c.finish()
    for t in range(nb - 1):
        for c in lines:
            c.wait_send(t)
    for c in every:
        c.drain()
    vec.drain()


def backward(codes, own_codes, do, stats, lse, delta, x, rest, table, q_all, k_all, v_all, weights, early, nb):
    n, width = do.shape
    bf, f32 = jnp.bfloat16, jnp.float32
    late = jax.ShapeDtypeStruct((2, 2, 2, width // 8, width), bf)
    kinds = list(early) + [late] * 3
    scratch = []
    for g in kinds:
        scratch += reduce_scratch(g.shape[-2:], bf, nb)
    ns = reduce_sems(nb)
    every = pltpu.VMEM((nb, n, width), bf)
    total = pltpu.VMEM((n, width), f32)
    square = pltpu.VMEM((width, width), bf)
    dma = pltpu.SemaphoreType.DMA
    big, small = early[0].shape, early[2].shape
    return pl.pallas_call(
        functools.partial(backward_kernel, nb),
        out_shape=(
            jax.ShapeDtypeStruct((n, width), bf), jax.ShapeDtypeStruct((TABLE, width), f32),
            *[jax.ShapeDtypeStruct(g.shape[-2:], bf) for g in kinds],
        ),
        in_specs=[VM] * 9 + [ANY] * 9,
        out_specs=(VM,) * 8,
        scratch_shapes=[
            every, every, every, every, pltpu.VMEM((nb,) + stats.shape, f32), total, total, total,
            square, square, square, pltpu.VMEM((3,) + late.shape, bf),
            pltpu.VMEM(big[:2] + big[3:], bf), pltpu.VMEM(small[:2] + small[3:], bf),
            pltpu.VMEM((TABLE, width), f32), pltpu.VMEM((6, TABLE, width), f32), pltpu.VMEM((nb, TABLE, width), f32),
        ] + scratch + [
            dma((2, 2, nb - 1)), dma((2, 2, nb - 1)), dma((8,)), dma((6, ns)), dma((6, ns)), dma((3,)),
            dma((3 + nb,)), dma((3 + nb,)),
        ],
        compiler_params=pltpu.CompilerParams(
            collective_id=4, has_side_effects=True, vmem_limit_bytes=63 << 20
        ),
        name="backward",
    )(
        own_codes.reshape(n, 1), codes.reshape(nb, 1, n), do, stats, lse, delta, x, rest, table,
        q_all, k_all, v_all, *weights, *early,
    )


def finish_kernel(dn, up, wo, wq, wk, wv, table, *outs):
    f32 = jnp.float32
    for a, b in zip((wq, wk, wv, wo, dn), outs[:5]):
        b[...] = a[...].astype(f32)
    rows = outs[5].shape[0]
    width = up.shape[1]
    for t in range(outs[5].shape[1] // width):
        outs[5][:, t * width:(t + 1) * width] = up[t * rows:(t + 1) * rows, :].astype(f32)
    shard = lax.axis_index("seq") * 4 + lax.axis_index("shard")
    piece = outs[6].shape[1]
    r = lax.broadcasted_iota(jnp.int32, (width, PAIR), 0)
    c = lax.broadcasted_iota(jnp.int32, (width, PAIR), 1)
    pick = ((r == c + shard * piece) & (c < piece)).astype(f32)
    small = lax.dot_general(
        table[:8, :], pick, (((1,), (0,)), ((), ())), precision=lax.Precision.HIGHEST,
        preferred_element_type=f32,
    )
    for i in range(8):
        outs[6 + i][...] = small[i:i + 1, :piece]
    wide = outs[14].shape[1]
    per = width // wide
    at = pl.multiple_of((shard % per) * wide, wide)
    outs[14][...] = table[pl.ds(8 + shard // per, 1), pl.ds(at, wide)]


def finish(dn, up, wo, wq, wk, wv, table, wide):
    width = table.shape[1]
    f32 = jnp.float32
    S = jax.ShapeDtypeStruct
    piece = width // 8
    chunks = up.shape[0] // piece
    out = pl.pallas_call(
        finish_kernel,
        out_shape=(
            *[S(a.shape, f32) for a in (wq, wk, wv, wo, dn)], S((piece, chunks * width), f32),
            *[S((1, piece), f32)] * 8, S((1, wide), f32),
        ),
        in_specs=[VM] * 7,
        out_specs=(VM,) * 15,
        compiler_params=pltpu.CompilerParams(vmem_limit_bytes=32 << 20),
        name="finish",
    )(dn, up, wo, wq, wk, wv, table)
    return list(out[:6]) + [a.reshape(-1) for a in out[6:]]


EPSILON = 1e-06
PLANE = ("seq", "shard")


def normalize(hidden, gain, shift):
    center = hidden - jnp.mean(hidden, axis=-1, keepdims=True)
    spread = jnp.mean(center * center, axis=-1, keepdims=True)
    return center * lax.rsqrt(spread + EPSILON) * gain + shift


def smooth_gate(hidden):
    return jax.nn.gelu(hidden, approximate=False)


def mm(left, right):
    return jnp.dot(left, right, preferred_element_type=jnp.float32)


def contract_rows(left, right):
    return dot(left, right, 0, 0)


def times_transpose(left, right):
    return dot(left, right, 1, 1)


def tuned_plane():
    return lax.axis_size("seq") == 2 and lax.axis_size("shard") == 4 and lax.axis_size("blk") == 4


def total(g):
    part = lax.psum_scatter(g.astype(jnp.bfloat16), PLANE, scatter_dimension=0, tiled=True)
    return lax.psum(part, "blk").astype(jnp.float32)


def whole_line(
    inputs, seg, live, mats, vecs, cotangent, codes, own_codes, start,
):
    rows, width = inputs.shape
    length = seg.shape[0]
    scale = HEAD_DIM ** (-0.5)
    xs = lax.all_gather(inputs, "blk", axis=0, tiled=True)
    wq, wk, wv, wo, wup, wdn = [lax.all_gather(w, PLANE, axis=0, tiled=True) for w in mats]
    whole = [lax.all_gather(v, PLANE, axis=0, tiled=True).astype(jnp.float32) for v in vecs]
    bq, bv, bo, g1, s1, bdn, g2, s2, bup = whole
    own_seg = lax.dynamic_slice_in_dim(seg, start, rows)
    low = jnp.sum((seg < own_seg[0]).astype(jnp.int32))
    high = jnp.sum((seg <= own_seg[rows - 1]).astype(jnp.int32))
    span = jnp.stack([low // TILE, (high + TILE - 1) // TILE])
    q_all = ((mm(xs, wq) + bq) * scale).astype(jnp.bfloat16)
    k_all = mm(xs, wk).astype(jnp.bfloat16)
    v_all = (mm(xs, wv) + bv).astype(jnp.bfloat16)
    q, k, v = [lax.dynamic_slice_in_dim(a, start, rows) for a in (q_all, k_all, v_all)]
    summed, attended, lse = attention(q, k_all, v_all, codes, own_codes, span)

    first_sum = inputs.astype(jnp.float32) + (mm(attended, wo) + bo)
    first_norm, first_pull = jax.vjp(normalize, first_sum, g1, s1)
    first_low = first_norm.astype(jnp.bfloat16)
    hidden = mm(first_low, wup) + bup
    gated, gate_pull = jax.vjp(smooth_gate, hidden)
    gated_low = gated.astype(jnp.bfloat16)
    second_sum = first_norm + (mm(gated_low, wdn) + bdn)
    result, second_pull = jax.vjp(normalize, second_sum, g2, s2)
    second_grad, g2_grad, s2_grad = second_pull(cotangent.astype(jnp.float32))
    bdn_grad = jnp.sum(second_grad, axis=0)
    second_low = second_grad.astype(jnp.bfloat16)
    wdn_grad = contract_rows(gated_low, second_low)
    (hidden_grad,) = gate_pull(times_transpose(second_low, wdn))
    bup_grad = jnp.sum(hidden_grad, axis=0)
    hidden_low = hidden_grad.astype(jnp.bfloat16)
    wup_grad = contract_rows(first_low, hidden_low)
    norm_grad = second_grad + times_transpose(hidden_low, wup)
    first_grad, g1_grad, s1_grad = first_pull(norm_grad)
    bo_grad = jnp.sum(first_grad, axis=0)
    first_grad_low = first_grad.astype(jnp.bfloat16)
    wo_grad = contract_rows(attended, first_grad_low)
    do = times_transpose(first_grad_low, wo).astype(jnp.bfloat16)

    stats, delta = row_stats(do, summed, lse)
    do_all, stats_all = [lax.all_gather(a, "blk", axis=0) for a in (do, stats)]
    stats_all = jnp.transpose(stats_all, (1, 2, 0, 3)).reshape(stats.shape[0], 8, length)
    dq, dk, dv = attention_grad(
        q, k, v, do, lse, delta, q_all, k_all, v_all, do_all.reshape(length, width), stats_all,
        codes, own_codes, span,
    )
    r = dq * scale
    rq, rk, rv = [a.astype(jnp.bfloat16) for a in (r, dk, dv)]
    token_grad = first_grad + times_transpose(rq, wq) + times_transpose(rk, wk) + times_transpose(rv, wv)
    grads = [contract_rows(inputs, a) for a in (rq, rk, rv)] + [wo_grad, wdn_grad, wup_grad]
    vectors = [
        jnp.sum(r, axis=0), jnp.sum(dv, axis=0), bo_grad, g1_grad, s1_grad, bdn_grad, g2_grad, s2_grad, bup_grad,
    ]
    return result.astype(jnp.bfloat16), token_grad.astype(jnp.bfloat16), [total(g) for g in grads + vectors]


def tuned_line(inputs, mats, vecs, cotangent, codes, own_codes, nb):
    out = forward(inputs, codes, own_codes, mats, vecs, nb)
    wq, wk, wv, wo, wup, wdn, q_all, k_all, v_all, summed, attended, lse, table, bup = out
    out = middle(attended, inputs, cotangent, summed, lse, table, bup, wo, wup, wdn)
    result, rest, do, stats, delta, table, gdn, gup, gwo = out
    width = inputs.shape[1]
    early = [g.reshape(2, 2, 2, -1, width) for g in (gdn, gup, gwo)]
    token_grad, table, rdn, rup, ro, rwq, rwk, rwv = backward(
        codes, own_codes, do, stats, lse, delta, inputs, rest, table, q_all, k_all, v_all, [wq, wk, wv], early, nb,
    )
    return result, token_grad, finish(rdn, rup, ro, rwq, rwk, rwv, table, vecs[8].shape[0])


def per_device(
    tokens, segments, live_mask, query_weight, key_weight, value_weight, out_weight,
    query_bias, value_bias, out_bias, first_gain, first_shift, up_weight, up_bias,
    down_weight, down_bias, second_gain, second_shift, cotangent,
):
    inputs = tokens[0]
    rows = inputs.shape[0]
    nb = lax.axis_size("blk")
    seg, live = segments[0], live_mask[0]
    start = lax.axis_index("blk") * rows
    codes = jnp.where(live > 0, seg, -1 - jnp.arange(seg.shape[0], dtype=jnp.int32))
    own_codes = lax.dynamic_slice_in_dim(codes, start, rows)
    mats = [query_weight, key_weight, value_weight, out_weight, up_weight, down_weight]
    vecs = [query_bias, value_bias, out_bias, first_gain, first_shift, down_bias, second_gain, second_shift, up_bias]
    if tuned_plane():
        result, token_grad, sums = tuned_line(inputs, mats, vecs, cotangent[0], codes, own_codes, nb)
    else:
        result, token_grad, sums = whole_line(
            inputs, seg, live, mats, vecs, cotangent[0], codes, own_codes, start
        )
    rwq, rwk, rwv, ro, rdn, rup, rbq, rbv, rbo, rg1, rs1, rbdn, rg2, rs2, rbup = sums
    return (
        result[None], token_grad[None],
        rwq, rwk, rwv, ro, rbq, rbv, rbo, rg1, rs1, rup, rbup, rdn, rbdn, rg2, rs2,
    )


def solution(mesh):
    flat = P(PLANE, "blk", None)
    mat = P(PLANE, None)
    vec = P(PLANE)
    return jax.shard_map(
        per_device,
        mesh=mesh,
        in_specs=(
            flat, mat, mat, mat, mat, mat, mat, vec, vec, vec, vec, vec, mat, vec, mat, vec, vec, vec, flat,
        ),
        out_specs=(flat, flat, mat, mat, mat, mat, vec, vec, vec, vec, vec, mat, vec, mat, vec, vec, vec),
        check_vma=False,
    )
```

```python
import functools
import jax
import jax.numpy as jnp
from jax import lax
from jax.experimental import pallas as pl
from jax.experimental.pallas import tpu as pltpu
from jax.sharding import PartitionSpec as P

MESH = pl.DeviceIdType.MESH
ANY = pl.BlockSpec(memory_space=pl.ANY)
VMEM_LIMIT = 56 << 20
VM = pl.BlockSpec(memory_space=pltpu.VMEM)


class Place:
    def __init__(self):
        b = lax.axis_index("blk")
        s = lax.axis_index("seq")
        h = lax.axis_index("shard")
        x = h // 2
        c = h % 2
        self.b, self.s, self.h, self.x, self.c = b, s, h, x, c
        self.X = (b, s, (1 - x) * 2 + c)
        self.Y = (b, 1 - s, h)
        self.C = (b, s, x * 2 + 1 - c)
        self.L = (b - 1, s, h)
        self.R = (b + 1, s, h)
        self.me = s * 4 + h
        self.xi = s * 4 + (1 - x) * 2 + c
        self.yi = (1 - s) * 4 + h
        self.di = (1 - s) * 4 + (1 - x) * 2 + c

    def z(self, j):
        return (j, self.s, self.h)


def enter(p, nb, plane, line):
    bar = pltpu.get_barrier_semaphore()
    count = 0
    if plane:
        for peer in (p.X, p.Y, p.C):
            pl.semaphore_signal(bar, inc=1, device_id=peer, device_id_type=MESH)
        count = count + 3
    if line == "near":
        @pl.when(p.b > 0)
        def _():
            pl.semaphore_signal(bar, inc=1, device_id=p.L, device_id_type=MESH)

        @pl.when(p.b < nb - 1)
        def _():
            pl.semaphore_signal(bar, inc=1, device_id=p.R, device_id_type=MESH)
        count = count + jnp.where(p.b > 0, 1, 0) + jnp.where(p.b < nb - 1, 1, 0)
    if line == "all":
        for j in range(nb):
            @pl.when(p.b != j)
            def _():
                pl.semaphore_signal(bar, inc=1, device_id=p.z(j), device_id_type=MESH)
        count = count + nb - 1
    pl.semaphore_wait(bar, count)


def rcopy(src, dst, ss, rs, dev):
    return pltpu.make_async_remote_copy(
        src_ref=src, dst_ref=dst, send_sem=ss, recv_sem=rs, device_id=dev, device_id_type=MESH
    )


class LineGather:
    def __init__(self, p, nb, own, out, ssem, rsem):
        self.p, self.nb, self.own, self.out, self.ssem, self.rsem = p, nb, own, out, ssem, rsem

    def _copies(self, t):
        p, nb = self.p, self.nb
        rb = p.b - t
        lb = p.b + t
        src_r = self.own if t == 0 else self.out.at[jnp.maximum(rb, 0)]
        src_l = self.own if t == 0 else self.out.at[jnp.minimum(lb, nb - 1)]
        right = rcopy(src_r, self.out.at[jnp.maximum(rb, 0)], self.ssem.at[0, t], self.rsem.at[0, t], p.R)
        left = rcopy(src_l, self.out.at[jnp.minimum(lb, nb - 1)], self.ssem.at[1, t], self.rsem.at[1, t], p.L)
        return right, left, (rb >= 0) & (p.b < nb - 1), (lb <= nb - 1) & (p.b > 0)

    def start(self, t):
        right, left, cr, cl = self._copies(t)
        pl.when(cr)(right.start)
        pl.when(cl)(left.start)

    def wait_recv(self, t):
        p, nb = self.p, self.nb
        right, left, _, _ = self._copies(t)
        pl.when(p.b - 1 - t >= 0)(right.wait_recv)
        pl.when(p.b + 1 + t <= nb - 1)(left.wait_recv)

    def wait_send(self, t):
        right, left, cr, cl = self._copies(t)
        pl.when(cr)(right.wait_send)
        pl.when(cl)(left.wait_send)


class PlaneGather:
    def __init__(self, p, own, out, ssem, rsem, lsem):
        rows = own.shape[0]
        half = rows // 2

        def whole(i):
            return out.at[pl.ds(pl.multiple_of(i * rows, rows), rows)]

        def low(i):
            return out.at[pl.ds(pl.multiple_of(i * rows, rows), half)]

        def high(i):
            return out.at[pl.ds(pl.multiple_of(i * rows + half, half), half)]

        def send(k, src, dst, dev):
            return rcopy(src, dst, ssem.at[k], rsem.at[k], dev)

        self.x = send(0, own, whole(p.me), p.X)
        self.y = send(1, own, whole(p.me), p.Y)
        self.c = send(2, own, whole(p.me), p.C)
        self.local = pltpu.make_async_copy(own, whole(p.me), lsem)
        self.fx = send(3, high(p.yi), high(p.yi), p.X)
        self.fy = send(4, low(p.xi), low(p.xi), p.Y)
        self.cx = send(5, whole(p.xi), whole(p.xi), p.C)
        self.cy = send(6, whole(p.yi), whole(p.yi), p.C)
        self.cd0 = send(7, low(p.di), low(p.di), p.C)
        self.cd1 = send(8, high(p.di), high(p.di), p.C)

    def start(self):
        for k in (self.x, self.y, self.c, self.local):
            k.start()

    def forward(self):
        self.x.wait_recv()
        self.fy.start()
        self.cx.start()
        self.y.wait_recv()
        self.fx.start()
        self.cy.start()

    def diag(self):
        self.fy.wait_recv()
        self.cd0.start()
        self.fx.wait_recv()
        self.cd1.start()

    def finish(self):
        self.local.wait()
        for k in (self.c, self.cx, self.cy, self.cd0, self.cd1):
            k.wait_recv()

    def drain(self):
        for k in (self.x, self.y, self.c, self.fx, self.fy, self.cx, self.cy, self.cd0, self.cd1):
            k.wait_send()


def staged(count, steps, body):
    def once(i, _):
        for at, todo in steps.items():
            @pl.when(i == at)
            def _():
                for f in todo:
                    f()
        body(i)
        return 0
    lax.fori_loop(0, count, once, 0)


def turn(b, nb, i):
    far = (i + 1) // 2
    j = jnp.where(i % 2 == 1, b - far, b + far)
    return (j >= 0) & (j <= nb - 1), jnp.clip(j, 0, nb - 1)


def row_loop(rows, chunk, body):
    if rows == chunk:
        body(0)
    else:
        def step(i, _):
            body(pl.multiple_of(i * chunk, chunk))
            return 0
        lax.fori_loop(0, rows // chunk, step, 0)


class PlaneReduce:
    def __init__(self, p, nb, g, out, buf, stage, ss, rs, ls):
        self.p, self.nb = p, nb
        self.P, self.BX, self.BY, self.CX, self.CY, self.Z = buf
        self.O = out
        self.R, self.C = g.shape[-2:]
        self.dt = g.dtype
        self.ss, self.rs = ss, rs
        h = self.R // 2
        self.h = h
        lo, hi = pl.ds(0, h), pl.ds(h, h)
        self.chunk = 16 if self.C > 1024 else 48
        self.g = g
        self.stage = stage
        self.own = None if stage is None else pltpu.make_async_copy(g.at[:, :, p.c], stage, ls)
        self.cA = rcopy(g.at[:, :, 1 - p.c], self.P, ss.at[0], rs.at[0], p.C)
        self.cBX = rcopy(self.P.at[:, 1 - p.x, lo], self.BX, ss.at[1], rs.at[1], p.X)
        self.cBY = rcopy(self.P.at[1 - p.s, :, hi], self.BY, ss.at[2], rs.at[2], p.Y)
        self.cCX = rcopy(self.P.at[p.s, 1 - p.x, hi], self.CX, ss.at[3], rs.at[3], p.X)
        self.cCY = rcopy(self.P.at[1 - p.s, p.x, lo], self.CY, ss.at[4], rs.at[4], p.Y)
        self.F = self.P.at[p.s, p.x]

    def quarter(self, ref, j):
        R, C = self.R, self.C
        r, c = (j // 2) * (R // 2), (j % 2) * (C // 2)
        if not isinstance(j, int):
            r, c = pl.multiple_of(r, R // 2), pl.multiple_of(c, C // 2)
        return ref.at[pl.ds(r, R // 2), pl.ds(c, C // 2)]

    def a_start(self):
        self.cA.start()

    def own_start(self):
        self.own.start()

    def b_start(self):
        if self.own is not None:
            self.own.wait()
        self.cA.wait_recv()

        def block(i, _):
            s, x = i // 2, i % 2

            def body(r):
                rows = pl.ds(r, self.chunk)
                mine = self.g[s, x, self.p.c, rows] if self.stage is None else self.stage[s, x, rows]
                self.P[s, x, rows] = (
                    mine.astype(jnp.float32) + self.P[s, x, rows].astype(jnp.float32)
                ).astype(self.dt)
            row_loop(self.R, self.chunk, body)
            return 0
        lax.fori_loop(0, 4, block, 0)
        self.cBX.start()
        self.cBY.start()

    def _add(self, dst, src):
        chunk = min(self.chunk * 2, self.h)

        def body(r):
            rows = pl.ds(r, chunk)
            dst[rows] = (dst[rows].astype(jnp.float32) + src[rows].astype(jnp.float32)).astype(self.dt)
        row_loop(self.h, chunk if self.h % chunk == 0 else self.h, body)

    def c_start(self):
        p, h = self.p, self.h
        lo, hi = pl.ds(0, h), pl.ds(h, h)
        self.cBX.wait_recv()
        self._add(self.P.at[1 - p.s, p.x, lo], self.BX.at[1 - p.s])
        self.cCY.start()
        self.cBY.wait_recv()
        self._add(self.P.at[p.s, 1 - p.x, hi], self.BY.at[1 - p.x])
        self.cCX.start()
        self._add(self.P.at[p.s, p.x, lo], self.BX.at[p.s])
        self._add(self.P.at[p.s, p.x, hi], self.BY.at[p.x])


    def _right(self, j):
        return rcopy(self.quarter(self.F, j), self.Z.at[j], self.ss.at[5 + j], self.rs.at[5 + j], self.p.R)

    def _left(self, j, last):
        slot = self.nb if last else j
        k = 5 + self.nb + j
        return rcopy(self.quarter(self.F, j), self.Z.at[slot], self.ss.at[k], self.rs.at[k], self.p.L)

    def plane_end(self):
        h = self.h
        self.cCY.wait_recv()
        self._add(self.F.at[pl.ds(0, h)], self.CY)
        self.cCX.wait_recv()
        self._add(self.F.at[pl.ds(h, h)], self.CX)

    def hop(self, t):
        nb, p = self.nb, self.p
        if t == 0:
            self.plane_end()

        @pl.when(p.b == t)
        def _():
            for j in range(nb - 1, t, -1):
                if t > 0:
                    self._right(j).wait_recv()
                    self._add(self.quarter(self.F, j), self.Z.at[j])
                self._right(j).start()

        @pl.when(p.b == nb - 1 - t)
        def _():
            for j in range(nb - 1 - t):
                if t > 0:
                    self._left(j, False).wait_recv()
                    self._add(self.quarter(self.F, j), self.Z.at[j])
                self._left(j, j == nb - 2 - t).start()

    def _spread(self, t):
        p, nb = self.p, self.nb
        k = 5 + 2 * nb + 2 * t
        r, l = p.b - t, p.b + t
        qr = self.quarter(self.O, jnp.maximum(r, 0))
        ql = self.quarter(self.O, jnp.minimum(l, nb - 1))
        right = rcopy(qr, qr, self.ss.at[k], self.rs.at[k], p.R)
        left = rcopy(ql, ql, self.ss.at[k + 1], self.rs.at[k + 1], p.L)
        return right, left, (r >= 0) & (p.b < nb - 1), (l <= nb - 1) & (p.b > 0)

    def _spread_recv(self, t):
        right, left, _, _ = self._spread(t)
        p, nb = self.p, self.nb
        pl.when(p.b - 1 - t >= 0)(right.wait_recv)
        pl.when(p.b + 1 + t <= nb - 1)(left.wait_recv)

    def spread(self, t):
        p, nb = self.p, self.nb
        if t == 0:
            mine = self.quarter(self.F, p.b)
            for j in range(nb):
                @pl.when(p.b == j)
                def _():
                    if j > 0:
                        self._right(j).wait_recv()
                        self._add(mine, self.Z.at[j])
                    if j < nb - 1:
                        self._left(j, True).wait_recv()
                        self._add(mine, self.Z.at[nb])
            total = self.quarter(self.O, p.b)

            def body(r):
                rows = pl.ds(r, self.chunk)
                total[rows] = mine[rows]
            row_loop(self.h, self.chunk, body)
        else:
            self._spread_recv(t - 1)
        right, left, cr, cl = self._spread(t)
        pl.when(cr)(right.start)
        pl.when(cl)(left.start)

    def finish(self):
        self._spread_recv(self.nb - 2)

    def drain(self):
        nb, p = self.nb, self.p
        for k in (self.cA, self.cBX, self.cBY, self.cCX, self.cCY):
            k.wait_send()
        for t in range(nb - 1):
            @pl.when(p.b == t)
            def _():
                for j in range(nb - 1, t, -1):
                    self._right(j).wait_send()

            @pl.when(p.b == nb - 1 - t)
            def _():
                for j in range(nb - 1 - t):
                    self._left(j, j == nb - 2 - t).wait_send()
            right, left, cr, cl = self._spread(t)
            pl.when(cr)(right.wait_send)
            pl.when(cl)(left.wait_send)


def reduce_scratch(shape, dt, nb):
    R, C = shape
    h = R // 2
    return [
        pltpu.VMEM((2, 2, R, C), dt),
        pltpu.VMEM((2, h, C), dt),
        pltpu.VMEM((2, h, C), dt),
        pltpu.VMEM((h, C), dt),
        pltpu.VMEM((h, C), dt),
        pltpu.VMEM((nb + 1, h, C // 2), dt),
    ]


NBUF = 6


def reduce_sems(nb):
    return 5 + 2 * nb + 2 * (nb - 1)


class TableSum:
    def __init__(self, p, nb, t, bufs, line, ss, rs):
        self.p, self.nb, self.t, self.bufs, self.line = p, nb, t, bufs, line
        self.steps = [
            rcopy(t if i == 0 else bufs.at[i - 1], bufs.at[3 + i], ss.at[i], rs.at[i], dev)
            for i, dev in enumerate((p.C, p.X, p.Y))
        ]
        self.ss, self.rs = ss, rs

    def start(self):
        self.steps[0].start()

    def step(self, i):
        self.steps[i].wait_recv()
        self.bufs[i] = (self.t[...] if i == 0 else self.bufs[i - 1]) + self.bufs[3 + i]
        if i < 2:
            self.steps[i + 1].start()
        else:
            self.line[self.p.b] = self.bufs[2]
            for j in range(self.nb):
                pl.when(self.p.b != j)(self._z(j, self.p.b).start)

    def _z(self, j, slot):
        return rcopy(
            self.bufs.at[2], self.line.at[slot], self.ss.at[3 + j], self.rs.at[3 + slot], self.p.z(j)
        )

    def finish(self, out):
        for j in range(self.nb):
            pl.when(self.p.b != j)(self._z(j, j).wait_recv)
        total = self.line[0]
        for j in range(1, self.nb):
            total = total + self.line[j]
        out[...] = total

    def drain(self):
        for k in self.steps:
            k.wait_send()
        for j in range(self.nb):
            pl.when(self.p.b != j)(self._z(j, self.p.b).wait_send)


HEAD_DIM = 64
PAIR = 128
MASKED = -1e30
TILE = 512


def dot(a, b, ca, cb):
    return lax.dot_general(a, b, (((ca,), (cb,)), ((), ())), preferred_element_type=jnp.float32)


def left_lanes(shape):
    return lax.broadcasted_iota(jnp.int32, shape, 1) < HEAD_DIM


def one_head(pair, left, first):
    keep = left if first else jnp.logical_not(left)
    return jnp.where(keep, pair, jnp.zeros_like(pair))


def lane_groups(op, a):
    out = a[:, :PAIR]
    for g in range(1, a.shape[1] // PAIR):
        out = op(out, a[:, g * PAIR:(g + 1) * PAIR])
    return out


def attn_fwd_kernel(span, col_ref, row_ref, q_ref, k_ref, v_ref, o_ref, ob_ref, lse_ref, s_ref, m_ref, l_ref, acc_ref):
    rows = q_ref.shape[0]
    left = left_lanes((rows, PAIR))
    m_ref[...] = jnp.full_like(m_ref, MASKED)
    l_ref[...] = jnp.zeros_like(l_ref)
    acc_ref[...] = jnp.zeros_like(acc_ref)
    q = q_ref[...]
    heads = [one_head(q, left, i == 0) for i in range(2)]
    codes = col_ref[...]

    def score(t, _):
        at = pl.multiple_of(t * TILE, TILE)
        k = k_ref[pl.ds(at, TILE), :]
        mask = codes == row_ref[:, pl.ds(at, TILE)]
        for i in range(2):
            s = jnp.where(mask, dot(heads[i], k, 1, 1), MASKED)
            s_ref[i, t] = s
            m_ref[i] = jnp.maximum(m_ref[i], lane_groups(jnp.maximum, s))
        return 0

    lax.fori_loop(span[0], span[1], score, 0)
    tops = [jnp.max(m_ref[i], axis=1, keepdims=True) for i in range(2)]

    def mix(t, _):
        v = v_ref[pl.ds(pl.multiple_of(t * TILE, TILE), TILE), :]
        parts = []
        for i in range(2):
            p = jnp.exp(s_ref[i, t] - tops[i])
            l_ref[i] += lane_groups(jnp.add, p)
            parts.append(dot(p.astype(jnp.bfloat16), v, 1, 0))
        acc_ref[...] += jnp.where(left, parts[0], parts[1])
        return 0

    lax.fori_loop(span[0], span[1], mix, 0)
    sums = [jnp.sum(l_ref[i], axis=1, keepdims=True) for i in range(2)]
    total = jnp.where(left, sums[0], sums[1])
    o = acc_ref[...] / total
    o_ref[...] = o
    ob_ref[...] = o.astype(jnp.bfloat16)
    lse_ref[...] = jnp.where(left, tops[0], tops[1]) + jnp.log(total)


def attention(q, k_all, v_all, codes, own_codes, span):
    rows, width = q.shape
    total = k_all.shape[0]
    pairs = width // PAIR
    own = pl.BlockSpec((rows, PAIR), lambda h, s: (0, h))
    every = pl.BlockSpec((total, PAIR), lambda h, s: (0, h))
    return pl.pallas_call(
        attn_fwd_kernel,
        grid_spec=pltpu.PrefetchScalarGridSpec(
            num_scalar_prefetch=1,
            grid=(pairs,),
            in_specs=[
                pl.BlockSpec((rows, 1), lambda h, s: (0, 0)),
                pl.BlockSpec((1, total), lambda h, s: (0, 0)),
                own, every, every,
            ],
            out_specs=[own, own, own],
            scratch_shapes=[
                pltpu.VMEM((2, total // TILE, rows, TILE), jnp.float32),
                pltpu.VMEM((2, rows, PAIR), jnp.float32),
                pltpu.VMEM((2, rows, PAIR), jnp.float32),
                pltpu.VMEM((rows, PAIR), jnp.float32),
            ],
        ),
        out_shape=[
            jax.ShapeDtypeStruct((rows, width), jnp.float32),
            jax.ShapeDtypeStruct((rows, width), jnp.bfloat16),
            jax.ShapeDtypeStruct((rows, width), jnp.float32),
        ],
        compiler_params=pltpu.CompilerParams(vmem_limit_bytes=48 << 20),
        name="attention",
    )(span, own_codes.reshape(rows, 1), codes.reshape(1, total), q, k_all, v_all)


def stats_kernel(g_ref, o_ref, lse_ref, out_ref, delta_ref):
    rows = g_ref.shape[0]
    left = left_lanes((rows, PAIR))
    t = g_ref[...].astype(jnp.float32) * o_ref[...]
    d0 = jnp.sum(jnp.where(left, t, 0.0), axis=1, keepdims=True)
    d1 = jnp.sum(jnp.where(left, 0.0, t), axis=1, keepdims=True)
    delta_ref[...] = jnp.where(left, d0, d1)
    lane = lax.broadcasted_iota(jnp.int32, (rows, PAIR), 1)
    lse = lse_ref[...]
    packed = jnp.where(lane == 0, lse[:, :1], jnp.where(lane == 1, lse[:, HEAD_DIM:HEAD_DIM + 1], jnp.where(lane == 2, d0, d1)))
    out_ref[0] = packed.T[:8]


def row_stats(grad, o, lse):
    rows, width = grad.shape
    pairs = width // PAIR
    own = pl.BlockSpec((rows, PAIR), lambda h: (0, h))
    return pl.pallas_call(
        stats_kernel,
        grid=(pairs,),
        in_specs=[own, own, own],
        out_specs=[pl.BlockSpec((1, 8, rows), lambda h: (h, 0, 0)), own],
        out_shape=[
            jax.ShapeDtypeStruct((pairs, 8, rows), jnp.float32),
            jax.ShapeDtypeStruct((rows, width), jnp.float32),
        ],
        name="row_stats",
    )(grad, o, lse)


def attn_bwd_kernel(span, col_ref, row_ref, q_ref, k_ref, v_ref, g_ref, lse_ref, delta_ref,
                    qa_ref, ka_ref, va_ref, ga_ref, st_ref, dq_ref, dk_ref, dv_ref):
    rows = q_ref.shape[0]
    left = left_lanes((rows, PAIR))
    dq_ref[...] = jnp.zeros_like(dq_ref)
    dk_ref[...] = jnp.zeros_like(dk_ref)
    dv_ref[...] = jnp.zeros_like(dv_ref)
    codes = col_ref[...]
    qs = [one_head(q_ref[...], left, i == 0) for i in range(2)]
    ks = [one_head(k_ref[...], left, i == 0) for i in range(2)]
    vs = [one_head(v_ref[...], left, i == 0) for i in range(2)]
    gs = [one_head(g_ref[...], left, i == 0) for i in range(2)]
    lses = [lse_ref[:, i * HEAD_DIM:i * HEAD_DIM + 1] for i in range(2)]
    deltas = [delta_ref[:, i * HEAD_DIM:i * HEAD_DIM + 1] for i in range(2)]

    def step(t, _):
        at = pl.multiple_of(t * TILE, TILE)
        tile = pl.ds(at, TILE)
        mask = codes == row_ref[:, tile]
        k, v, q, g = ka_ref[tile, :], va_ref[tile, :], qa_ref[tile, :], ga_ref[tile, :]
        dqs, dks, dvs = [], [], []
        for i in range(2):
            s = jnp.where(mask, dot(qs[i], k, 1, 1), MASKED)
            p = jnp.exp(s - lses[i])
            dp = dot(gs[i], v, 1, 1)
            ds = (p * (dp - deltas[i])).astype(jnp.bfloat16)
            dqs.append(dot(ds, k, 1, 0))
            st = jnp.where(mask, dot(ks[i], q, 1, 1), MASKED)
            pt = jnp.exp(st - st_ref[0, i:i + 1, tile])
            dvs.append(dot(pt.astype(jnp.bfloat16), g, 1, 0))
            dpt = dot(vs[i], g, 1, 1)
            dst = (pt * (dpt - st_ref[0, 2 + i:3 + i, tile])).astype(jnp.bfloat16)
            dks.append(dot(dst, q, 1, 0))
        dq_ref[...] += jnp.where(left, dqs[0], dqs[1])
        dk_ref[...] += jnp.where(left, dks[0], dks[1])
        dv_ref[...] += jnp.where(left, dvs[0], dvs[1])
        return 0

    lax.fori_loop(span[0], span[1], step, 0)


def attention_grad(q, k, v, g, lse, delta, q_all, k_all, v_all, g_all, stats, codes, own_codes, span):
    rows, width = q.shape
    total = k_all.shape[0]
    pairs = width // PAIR
    own = pl.BlockSpec((rows, PAIR), lambda h, s: (0, h))
    every = pl.BlockSpec((total, PAIR), lambda h, s: (0, h))
    return pl.pallas_call(
        attn_bwd_kernel,
        grid_spec=pltpu.PrefetchScalarGridSpec(
            num_scalar_prefetch=1,
            grid=(pairs,),
            in_specs=[
                pl.BlockSpec((rows, 1), lambda h, s: (0, 0)),
                pl.BlockSpec((1, total), lambda h, s: (0, 0)),
                own, own, own, own, own, own, every, every, every, every,
                pl.BlockSpec((1, 8, total), lambda h, s: (h, 0, 0)),
            ],
            out_specs=[own, own, own],
        ),
        out_shape=[
            jax.ShapeDtypeStruct((rows, width), jnp.float32),
            jax.ShapeDtypeStruct((rows, width), jnp.float32),
            jax.ShapeDtypeStruct((rows, width), jnp.float32),
        ],
        compiler_params=pltpu.CompilerParams(vmem_limit_bytes=48 << 20),
        name="attention_grad",
    )(span, own_codes.reshape(rows, 1), codes.reshape(1, total), q, k, v, g, lse, delta, q_all, k_all, v_all, g_all, stats)


VEC_ROWS = 8


def forward_kernel(nb, *refs):
    x_ref, codes, rows = refs[:3]
    shards_in = refs[3:9]
    vecs_in = refs[9:18]
    wq_o, wk_o, wv_o, wo_o, wup_o, wdn_o = refs[18:24]
    q_o, k_o, v_o = refs[24:27]
    o_ref, ob_ref, lse_ref, vec_ref, bup_ref = refs[27:32]
    rest = refs[32:]
    x_all, wq, wk, wv, pack, packs, q, k, v, m_ref, l_ref = rest[:11]
    zs, zr, gs, gr, gl, ws, es = rest[11:]
    n, width = x_ref.shape
    pairs = width // PAIR
    p = Place()
    own = pltpu.make_async_copy(x_ref, x_all.at[p.b], ws.at[3])
    own.start()
    pack[...] = jnp.zeros_like(pack)
    for i in range(VEC_ROWS):
        pack[i:i + 1, :vecs_in[i].shape[1]] = vecs_in[i][...].astype(jnp.float32)
    for i in range(vecs_in[8].shape[1] // PAIR):
        pack[VEC_ROWS + i:VEC_ROWS + i + 1, :] = vecs_in[8][:, i * PAIR:(i + 1) * PAIR].astype(jnp.float32)
    enter(p, nb, True, "near")
    line = LineGather(p, nb, x_ref, x_all, zs, zr)
    targets = (packs, wq, wk, wv, wo_o, wup_o, wdn_o)
    sources = (pack,) + tuple(shards_in)
    g = [PlaneGather(p, sources[i], targets[i], gs.at[i], gr.at[i], gl.at[i]) for i in range(7)]
    line.start(0)
    for c in g[:5]:
        c.start()
    for c in g[:4]:
        c.forward()
    g[5].start()
    g[6].start()
    line.wait_recv(0)
    line.start(1)
    for c in g[:4]:
        c.diag()
    for c in g[:4]:
        c.finish()
    own.wait()
    keep = [
        pltpu.make_async_copy(a, b, ws.at[i]) for i, (a, b) in enumerate(((wq, wq_o), (wk, wk_o), (wv, wv_o)))
    ]
    for c in keep:
        c.start()

    piece = width // 8
    r = lax.broadcasted_iota(jnp.int32, (PAIR, width), 0)
    c = lax.broadcasted_iota(jnp.int32, (PAIR, width), 1)
    total = jnp.zeros((2 * VEC_ROWS, width), jnp.float32)
    for i in range(8):
        pick = ((c == r + i * piece) & (r < piece)).astype(jnp.bfloat16)
        total += dot(packs[2 * VEC_ROWS * i:2 * VEC_ROWS * (i + 1), :].astype(jnp.bfloat16), pick, 1, 0)
    vec_ref[...] = total[:VEC_ROWS]
    up_piece = bup_ref.shape[1] // 8
    for i in range(8):
        for t in range(up_piece // PAIR):
            at = i * up_piece + t * PAIR
            row = 2 * VEC_ROWS * i + VEC_ROWS + t
            bup_ref[:, at:at + PAIR] = packs[row:row + 1, :]

    scale = HEAD_DIM ** (-0.5)
    step = 256

    def outs(j, e):
        return [
            pltpu.make_async_copy(a.at[j], b.at[j], es.at[i, e])
            for i, (a, b) in enumerate(((q, q_o), (k, k_o), (v, v_o)))
        ]

    def project(j):
        def columns(t, _):
            at = pl.ds(pl.multiple_of(t * step, step), step)
            xs = x_all[j]
            q[j, :, at] = ((dot(xs, wq[:, at], 1, 0) + vec_ref[0:1, at]) * scale).astype(jnp.bfloat16)
            k[j, :, at] = dot(xs, wk[:, at], 1, 0).astype(jnp.bfloat16)
            v[j, :, at] = (dot(xs, wv[:, at], 1, 0) + vec_ref[1:2, at]).astype(jnp.bfloat16)
            return 0
        lax.fori_loop(0, width // step, columns, 0, unroll=True)

    def attend(j):
        def pair(h, _):
            left = left_lanes((n, PAIR))
            lanes = pl.ds(pl.multiple_of(h * PAIR, PAIR), PAIR)
            mask = codes[...] == rows[j]
            qs, ks, vs = q[p.b, :, lanes], k[j, :, lanes], v[j, :, lanes]
            parts, alphas = [], []
            for i in range(2):
                s = jnp.where(mask, dot(one_head(qs, left, i == 0), ks, 1, 1), MASKED)
                top = jnp.max(lane_groups(jnp.maximum, s), axis=1, keepdims=True)
                old = m_ref[2 * h + i]
                new = jnp.maximum(old, top)
                alpha = jnp.exp(old - new)
                e = jnp.exp(s - jnp.concatenate([new] * (n // PAIR), axis=1))
                m_ref[2 * h + i] = new
                l_ref[2 * h + i] = l_ref[2 * h + i] * alpha + lane_groups(jnp.add, e)
                alphas.append(alpha)
                parts.append(dot(e.astype(jnp.bfloat16), vs, 1, 0))
            got = jnp.where(left, parts[0], parts[1])
            o_ref[:, lanes] = o_ref[:, lanes] * jnp.where(left, alphas[0], alphas[1]) + got
            return 0
        lax.fori_loop(0, pairs, pair, 0, unroll=2)

    def block(i):
        ok, j = turn(p.b, nb, i)

        @pl.when(ok)
        def _():
            project(j)
            for c in outs(j, i):
                c.start()
            attend(j)

    def hop(t, last=False):
        line.wait_recv(t)
        if not last:
            line.start(t + 1)

    m_ref[...] = jnp.full_like(m_ref, MASKED)
    l_ref[...] = jnp.zeros_like(l_ref)
    o_ref[...] = jnp.zeros_like(o_ref)
    staged(
        2 * nb - 1,
        {
            1: [g[4].forward, g[5].forward],
            2: [lambda: hop(1)],
            3: [g[6].forward, g[4].diag],
            5: [g[5].diag, g[6].diag, lambda: hop(2, True)],
        },
        block,
    )

    def close(h, _):
        left = left_lanes((n, PAIR))
        lanes = pl.ds(pl.multiple_of(h * PAIR, PAIR), PAIR)
        sums = [jnp.sum(l_ref[2 * h + i], axis=1, keepdims=True) for i in range(2)]
        mass = jnp.where(left, sums[0], sums[1])
        out = o_ref[:, lanes] / mass
        o_ref[:, lanes] = out
        ob_ref[:, lanes] = out.astype(jnp.bfloat16)
        lse_ref[:, lanes] = jnp.where(left, m_ref[2 * h], m_ref[2 * h + 1]) + jnp.log(mass)
        return 0
    lax.fori_loop(0, pairs, close, 0)
    for c in g[4:]:
        c.finish()
    for c in keep:
        c.wait()
    for i in range(2 * nb - 1):
        ok, j = turn(p.b, nb, i)

        @pl.when(ok)
        def _():
            for c in outs(j, i):
                c.wait()
    for t in range(nb - 1):
        line.wait_send(t)
    for c in g:
        c.drain()


def forward(x, codes, own_codes, weights, vecs, nb):
    n, width = x.shape
    hidden = weights[4].shape[1]
    bf, f32 = jnp.bfloat16, jnp.float32
    every = jax.ShapeDtypeStruct((nb, n, width), bf)
    block = jax.ShapeDtypeStruct((n, width), f32)
    mats = [jax.ShapeDtypeStruct((8 * w.shape[0], w.shape[1]), w.dtype) for w in weights]
    dma = pltpu.SemaphoreType.DMA
    return pl.pallas_call(
        functools.partial(forward_kernel, nb),
        out_shape=(
            *mats, every, every, every, block, jax.ShapeDtypeStruct((n, width), bf), block,
            jax.ShapeDtypeStruct((VEC_ROWS, width), f32), jax.ShapeDtypeStruct((1, hidden), f32),
        ),
        in_specs=[VM] * 18,
        out_specs=(ANY,) * 9 + (VM,) * 5,
        scratch_shapes=[
            pltpu.VMEM((nb, n, width), bf),
            pltpu.VMEM((width, width), bf), pltpu.VMEM((width, width), bf), pltpu.VMEM((width, width), bf),
            pltpu.VMEM((2 * VEC_ROWS, PAIR), f32), pltpu.VMEM((16 * VEC_ROWS, PAIR), f32),
            pltpu.VMEM((nb, n, width), bf), pltpu.VMEM((nb, n, width), bf), pltpu.VMEM((nb, n, width), bf),
            pltpu.VMEM((width // HEAD_DIM, n, PAIR), f32), pltpu.VMEM((width // HEAD_DIM, n, PAIR), f32),
            dma((2, nb - 1)), dma((2, nb - 1)), dma((7, 9)), dma((7, 9)), dma((7,)), dma((4,)), dma((3, 2 * nb)),
        ],
        compiler_params=pltpu.CompilerParams(
            collective_id=1, has_side_effects=True, vmem_limit_bytes=60 << 20
        ),
        name="forward",
    )(
        x, own_codes.reshape(n, 1), codes.reshape(nb, 1, n), *weights, *[v.reshape(1, -1) for v in vecs]
    )


ROOT_HALF = 0.7071067811865476
ROOT_TWO_PI = 0.3989422804014327
CHUNK = 768
PART = 256


def erf_parts(x):
    x = jnp.clip(x, -3.832506856900711, 3.832506856900711)
    y = x * x
    top = jnp.full_like(y, 0.00022905065861350646)
    for a in (0.0034082910107109506, 0.050955695062380861, 0.18520832239976145, 1.128379143519084):
        top = top * y + a
    low = jnp.full_like(y, -1.1791602954361697e-7)
    for a in (
        0.000023547966471313185, 0.0010179625278914885, 0.014070470171167667,
        0.11098505178285362, 0.49746925110067538, 1.0,
    ):
        low = low * y + a
    return x * top / low


def middle_kernel(
    att_ref, x_ref, cot_ref, o_ref, lse_ref, vec_ref, bup_ref, wo_hbm, wup_hbm, wdn_hbm,
    out_ref, rest_ref, do_ref, stats_ref, delta_ref, table_ref, gdn_hbm, gup_hbm, gwo_ref,
    wo, wup, wdn, u_ref, slope_ref, y_ref, dh_ref, low_ref, gdn, gup, sems, osems,
):
    n, width = x_ref.shape
    hidden = wup.shape[1]
    chunks = hidden // CHUNK
    f32, bf = jnp.float32, jnp.bfloat16
    loads = [
        pltpu.make_async_copy(a, b, sems.at[i])
        for i, (a, b) in enumerate(((wo_hbm, wo), (wup_hbm, wup), (wdn_hbm, wdn)))
    ]
    for c in loads:
        c.start()
    table_ref[...] = jnp.zeros_like(table_ref)

    def vec(i):
        return vec_ref[i:i + 1, :]

    def mean(a):
        return jnp.sum(a, axis=1, keepdims=True) * (1.0 / width)

    def centred(h):
        c = h - mean(h)
        inv = lax.rsqrt(mean(c * c) + EPSILON)
        return c * inv, inv

    def pull(grad, hat, inv, gain):
        d = grad * gain
        return inv * (d - mean(d) - hat * mean(d * hat))

    def column_sum(a):
        return jnp.sum(a, axis=0, keepdims=True)

    blocks = 4
    m = n // blocks

    def rows_of(i):
        return pl.ds(pl.multiple_of(i * m, m), m)

    loads[0].wait()

    def first(i, _):
        r = rows_of(i)
        h = x_ref[r, :].astype(f32) + dot(att_ref[r, :], wo[...], 1, 0) + vec(2)
        hat, _ = centred(h)
        y = hat * vec(3) + vec(4)
        rest_ref[r, :] = h
        dh_ref[r, :] = y + vec(5)
        low_ref[r, :] = y.astype(bf)
        return 0
    lax.fori_loop(0, blocks, first, 0)
    for c in loads[1:]:
        c.wait()

    def up(t, _):
        total = dh_ref[...]
        for s in range(CHUNK // PART):
            at = pl.ds(pl.multiple_of(t * CHUNK + s * PART, PART), PART)
            z = dot(low_ref[...], wup[:, at], 1, 0) + bup_ref[:, at]
            cdf = 0.5 + 0.5 * erf_parts(z * ROOT_HALF)
            low = (z * cdf).astype(bf)
            u_ref[:, at] = low
            slope_ref[:, at] = cdf + z * (jnp.exp(-0.5 * z * z) * ROOT_TWO_PI)
            total = total + dot(low, wdn[at, :], 1, 0)
        dh_ref[...] = total
        return 0
    lax.fori_loop(0, chunks, up, 0)

    def second(i, _):
        r = rows_of(i)
        hat, inv = centred(dh_ref[r, :])
        out_ref[r, :] = (hat * vec(6) + vec(7)).astype(bf)
        g = cot_ref[r, :].astype(f32)
        table_ref[6:7, :] += column_sum(g * hat)
        table_ref[7:8, :] += column_sum(g)
        dh = pull(g, hat, inv, vec(6))
        table_ref[5:6, :] += column_sum(dh)
        dh_ref[r, :] = dh
        y_ref[r, :] = dh.astype(bf)
        return 0
    lax.fori_loop(0, blocks, second, 0)

    def down(t, _):
        at = pl.ds(pl.multiple_of(t * CHUNK, CHUNK), CHUNK)
        parts = []
        total = dh_ref[...]
        for s in range(CHUNK // PART):
            cols = pl.ds(pl.multiple_of(t * CHUNK + s * PART, PART), PART)
            dz = dot(y_ref[...], wdn[cols, :], 1, 1) * slope_ref[:, cols]
            table_ref[pl.ds(8 + t, 1), s * PART:(s + 1) * PART] = column_sum(dz)
            c = dz.astype(bf)
            parts.append(c)
            total = total + dot(c, wup[:, cols], 1, 1)
            gdn[cols, :] = dot(u_ref[:, cols], y_ref[...], 0, 0).astype(bf)
        dh_ref[...] = total
        c = jnp.concatenate(parts, axis=1)
        r = width // 8
        for i in range(2):
            half = width // 2
            g = dot(low_ref[:, i * half:(i + 1) * half], c, 0, 0).astype(bf)
            for k in range(4):
                gup[4 * i + k, t] = g[k * r:(k + 1) * r]
        pltpu.make_async_copy(gdn.at[at], gdn_hbm.at[at], osems.at[0, t]).start()
        pltpu.make_async_copy(gup.at[:, t], gup_hbm.at[:, t], osems.at[1, t]).start()
        return 0
    lax.fori_loop(0, chunks, down, 0)

    def third(i, _):
        r = rows_of(i)
        hat, inv = centred(rest_ref[r, :])
        g = dh_ref[r, :]
        table_ref[3:4, :] += column_sum(g * hat)
        table_ref[4:5, :] += column_sum(g)
        dh = pull(g, hat, inv, vec(3))
        table_ref[2:3, :] += column_sum(dh)
        rest_ref[r, :] = dh
        low = dh.astype(bf)
        low_ref[r, :] = low
        do_ref[r, :] = dot(low, wo[...], 1, 1).astype(bf)
        return 0
    lax.fori_loop(0, blocks, third, 0)

    def heads(h, _):
        lanes = pl.ds(pl.multiple_of(h * PAIR, PAIR), PAIR)
        left = left_lanes((n, PAIR))
        t = do_ref[:, lanes].astype(f32) * o_ref[:, lanes]
        d0 = jnp.sum(jnp.where(left, t, 0.0), axis=1, keepdims=True)
        d1 = jnp.sum(jnp.where(left, 0.0, t), axis=1, keepdims=True)
        delta_ref[:, lanes] = jnp.where(left, d0, d1)
        lane = lax.broadcasted_iota(jnp.int32, (n, PAIR), 1)
        lse = lse_ref[:, lanes]
        packed = jnp.where(lane == 0, lse[:, :1], jnp.where(
            lane == 1, lse[:, HEAD_DIM:HEAD_DIM + 1], jnp.where(lane == 2, d0, d1)))
        stats_ref[h] = packed.T[:8]
        gwo_ref[lanes, :] = dot(att_ref[:, lanes], low_ref[...], 0, 0).astype(bf)
        return 0
    lax.fori_loop(0, width // PAIR, heads, 0)
    for t in range(chunks):
        at = pl.ds(t * CHUNK, CHUNK)
        pltpu.make_async_copy(gdn.at[at], gdn_hbm.at[at], osems.at[0, t]).wait()
        pltpu.make_async_copy(gup.at[:, t], gup_hbm.at[:, t], osems.at[1, t]).wait()


def middle(att, x, cot, o, lse, vecs, bup, wo, wup, wdn):
    n, width = x.shape
    hidden = wup.shape[1]
    chunks = hidden // CHUNK
    bf, f32 = jnp.bfloat16, jnp.float32
    S = jax.ShapeDtypeStruct
    dma = pltpu.SemaphoreType.DMA
    return pl.pallas_call(
        middle_kernel,
        out_shape=(
            S((n, width), bf), S((n, width), f32), S((n, width), bf), S((width // PAIR, 8, n), f32),
            S((n, width), f32), S((16, width), f32), S((hidden, width), bf),
            S((8, chunks, width // 8, CHUNK), bf), S((width, width), bf),
        ),
        in_specs=[VM] * 7 + [ANY] * 3,
        out_specs=(VM,) * 6 + (ANY, ANY, VM),
        scratch_shapes=[
            pltpu.VMEM((width, width), bf), pltpu.VMEM((width, hidden), bf), pltpu.VMEM((hidden, width), bf),
            pltpu.VMEM((n, hidden), bf), pltpu.VMEM((n, hidden), f32), pltpu.VMEM((n, width), bf),
            pltpu.VMEM((n, width), f32), pltpu.VMEM((n, width), bf),
            pltpu.VMEM((hidden, width), bf), pltpu.VMEM((8, chunks, width // 8, CHUNK), bf),
            dma((3,)), dma((2, chunks)),
        ],
        compiler_params=pltpu.CompilerParams(vmem_limit_bytes=60 << 20),
        name="middle",
    )(att, x, cot, o, lse, vecs, bup, wo, wup, wdn)


class AttentionGrad:
    def __init__(self, codes, rows, q, k, v, g, lse, delta, stats, own, dq, dk, dv):
        self.codes, self.rows = codes, rows
        self.q, self.k, self.v, self.g = q, k, v, g
        self.lse, self.delta, self.stats = lse, delta, stats
        self.own = own
        self.dq, self.dk, self.dv = dq, dk, dv
        self.n = dq.shape[0]
        self.pairs = dq.shape[1] // PAIR

    def queries(self, j):
        own = self.own

        def pair(h, _):
            left = left_lanes((self.n, PAIR))
            lanes = pl.ds(pl.multiple_of(h * PAIR, PAIR), PAIR)
            mask = self.codes[...] == self.rows[j]
            q, g = self.q[own, :, lanes], self.g[own, :, lanes]
            k, v = self.k[j, :, lanes], self.v[j, :, lanes]
            lse, delta = self.lse[:, lanes], self.delta[:, lanes]
            parts = []
            for i in range(2):
                at = slice(i * HEAD_DIM, i * HEAD_DIM + 1)
                s = jnp.where(mask, dot(one_head(q, left, i == 0), k, 1, 1), MASKED)
                p = jnp.exp(s - lse[:, at])
                dp = dot(one_head(g, left, i == 0), v, 1, 1)
                ds = (p * (dp - delta[:, at])).astype(jnp.bfloat16)
                parts.append(dot(ds, k, 1, 0))
            self.dq[:, lanes] += jnp.where(left, parts[0], parts[1])
            return 0

        lax.fori_loop(0, self.pairs, pair, 0, unroll=2)

    def keys(self, j):
        own = self.own

        def pair(h, _):
            left = left_lanes((self.n, PAIR))
            lanes = pl.ds(pl.multiple_of(h * PAIR, PAIR), PAIR)
            mask = self.codes[...] == self.rows[j]
            k, v = self.k[own, :, lanes], self.v[own, :, lanes]
            q, g = self.q[j, :, lanes], self.g[j, :, lanes]
            dks, dvs = [], []
            for i in range(2):
                st = jnp.where(mask, dot(one_head(k, left, i == 0), q, 1, 1), MASKED)
                pt = jnp.exp(st - self.stats[j, h, i:i + 1])
                dvs.append(dot(pt.astype(jnp.bfloat16), g, 1, 0))
                dpt = dot(one_head(v, left, i == 0), g, 1, 1)
                dst = (pt * (dpt - self.stats[j, h, 2 + i:3 + i])).astype(jnp.bfloat16)
                dks.append(dot(dst, q, 1, 0))
            self.dk[:, lanes] += jnp.where(left, dks[0], dks[1])
            self.dv[:, lanes] += jnp.where(left, dvs[0], dvs[1])
            return 0

        lax.fori_loop(0, self.pairs, pair, 0, unroll=2)


TABLE = 16


def backward_kernel(nb, *refs):
    codes, rows, g_own, st_own, lse, delta, x_ref, rest_ref, table = refs[:9]
    q_hbm, k_hbm, v_hbm, wq_hbm, wk_hbm, wv_hbm = refs[9:15]
    early = refs[15:18]
    token_ref, table_out = refs[18:20]
    outs = refs[20:26]
    rest = refs[26:]
    q, k, v, g, stats, dq, dk, dv, wq, wk, wv, gw, stage_a, stage_b, tab, tsum, tline = rest[:17]
    bufs = rest[17:17 + 6 * NBUF]
    zs, zr, ls, ss, rs, rls, ts, tr = rest[17 + 6 * NBUF:]
    n, width = g_own.shape
    p = Place()
    loads = [
        pltpu.make_async_copy(a, b, ls.at[i])
        for i, (a, b) in enumerate((
            (k_hbm, k), (v_hbm, v), (q_hbm, q), (g_own, g.at[p.b]), (st_own, stats.at[p.b]),
            (wq_hbm, wq), (wk_hbm, wk), (wv_hbm, wv),
        ))
    ]
    for c in loads:
        c.start()
    enter(p, nb, True, "all")
    lines = [
        LineGather(p, nb, g_own, g, zs.at[0], zr.at[0]),
        LineGather(p, nb, st_own, stats, zs.at[1], zr.at[1]),
    ]
    sources = tuple(early) + tuple(gw.at[i] for i in range(3))
    stages = (stage_a, stage_a, stage_b, None, None, None)
    dn, up, wo, gq, gk, gv = [
        PlaneReduce(
            p, nb, sources[i], outs[i], bufs[NBUF * i:NBUF * (i + 1)],
            None if stages[i] is None else stages[i].reshape(sources[i].shape[:2] + sources[i].shape[3:]),
            ss.at[i], rs.at[i], rls.at[i],
        )
        for i in range(6)
    ]
    vec = TableSum(p, nb, tab, tsum, tline, ts, tr)
    for c in lines:
        c.start(0)
    for c in (dn, up, wo):
        c.a_start()
    dn.own_start()
    wo.own_start()
    work = AttentionGrad(codes, rows, q, k, v, g, lse, delta, stats, p.b, dq, dk, dv)
    for c in (dq, dk, dv):
        c[...] = jnp.zeros_like(c)
    for i in (0, 1, 2, 3):
        loads[i].wait()

    low = k
    def slot(i):
        return (p.b + 1 + i) % nb

    def settle(i, src, scale, row):
        value = src[...] if scale is None else src[...] * scale
        if row is not None:
            tab[row:row + 1, :] = jnp.sum(value, axis=0, keepdims=True)
        low[slot(i)] = value.astype(jnp.bfloat16)

    def weight_grad(i):
        half = width // 2
        for m in range(2):
            part = dot(x_ref[:, m * half:(m + 1) * half], low[slot(i)], 0, 0).astype(jnp.bfloat16)
            r = gw.shape[-2]
            for a in range(2):
                for b in range(2):
                    at = (2 * a + b) * r
                    gw[i, m, a, b] = part[at:at + r]

    def hop(t, last=False):
        for c in lines:
            c.wait_recv(t)
            if not last:
                c.start(t + 1)

    staged(
        nb,
        {
            1: [dn.b_start, up.own_start],
            2: [up.b_start, wo.b_start, lambda: hop(0)],
            3: [dn.c_start],
        },
        lambda i: work.queries((p.b + i) % nb),
    )
    for i in (4, 5, 6, 7):
        loads[i].wait()
    tab[...] = table[...]
    settle(0, dq, HEAD_DIM ** (-0.5), 0)
    weight_grad(0)
    gq.a_start()
    hop(1)
    up.c_start()

    def keys(i):
        ok, j = turn(p.b, nb, i)
        pl.when(ok)(lambda: work.keys(j))

    staged(
        2 * nb - 1,
        {
            1: [gq.b_start, wo.c_start],
            2: [lambda: dn.hop(0)],
            3: [lambda: up.hop(0), lambda: wo.hop(0), gq.c_start, lambda: dn.hop(1)],
            5: [lambda: up.hop(1), lambda: wo.hop(1), lambda: dn.hop(2), lambda: hop(2, True)],
        },
        keys,
    )
    settle(1, dk, None, None)
    settle(2, dv, None, 1)
    vec.start()
    weight_grad(1)
    gk.a_start()
    weight_grad(2)
    gv.a_start()
    up.hop(2)
    wo.hop(2)
    dn.spread(0)
    vec.step(0)
    gk.b_start()
    gv.b_start()
    gq.hop(0)
    vec.step(1)

    part = 256

    def columns(t, _):
        at = pl.ds(pl.multiple_of(t * part, part), part)
        total = rest_ref[:, at]
        for i, w in enumerate((wq, wk, wv)):
            total = total + dot(low[slot(i)], w[at, :], 1, 1)
        token_ref[:, at] = total.astype(jnp.bfloat16)
        return 0
    lax.fori_loop(0, width // part, columns, 0)

    up.spread(0)
    wo.spread(0)
    dn.spread(1)
    vec.step(2)
    gk.c_start()
    gv.c_start()
    gq.hop(1)
    up.spread(1)
    wo.spread(1)
    dn.spread(2)
    gq.hop(2)
    gk.hop(0)
    gv.hop(0)
    gq.spread(0)
    gk.hop(1)
    gv.hop(1)
    up.spread(2)
    wo.spread(2)
    gk.hop(2)
    gv.hop(2)
    gq.spread(1)
    gk.spread(0)
    gv.spread(0)
    gq.spread(2)
    gk.spread(1)
    gv.spread(1)
    gk.spread(2)
    gv.spread(2)
    vec.finish(table_out)
    every = (dn, up, wo, gq, gk, gv)
    for c in every:
        c.finish()
    for t in range(nb - 1):
        for c in lines:
            c.wait_send(t)
    for c in every:
        c.drain()
    vec.drain()


def backward(codes, own_codes, do, stats, lse, delta, x, rest, table, q_all, k_all, v_all, weights, early, nb):
    n, width = do.shape
    bf, f32 = jnp.bfloat16, jnp.float32
    late = jax.ShapeDtypeStruct((2, 2, 2, width // 8, width), bf)
    kinds = list(early) + [late] * 3
    scratch = []
    for g in kinds:
        scratch += reduce_scratch(g.shape[-2:], bf, nb)
    ns = reduce_sems(nb)
    every = pltpu.VMEM((nb, n, width), bf)
    total = pltpu.VMEM((n, width), f32)
    square = pltpu.VMEM((width, width), bf)
    dma = pltpu.SemaphoreType.DMA
    big, small = early[0].shape, early[2].shape
    return pl.pallas_call(
        functools.partial(backward_kernel, nb),
        out_shape=(
            jax.ShapeDtypeStruct((n, width), bf), jax.ShapeDtypeStruct((TABLE, width), f32),
            *[jax.ShapeDtypeStruct(g.shape[-2:], bf) for g in kinds],
        ),
        in_specs=[VM] * 9 + [ANY] * 9,
        out_specs=(VM,) * 8,
        scratch_shapes=[
            every, every, every, every, pltpu.VMEM((nb,) + stats.shape, f32), total, total, total,
            square, square, square, pltpu.VMEM((3,) + late.shape, bf),
            pltpu.VMEM(big[:2] + big[3:], bf), pltpu.VMEM(small[:2] + small[3:], bf),
            pltpu.VMEM((TABLE, width), f32), pltpu.VMEM((6, TABLE, width), f32), pltpu.VMEM((nb, TABLE, width), f32),
        ] + scratch + [
            dma((2, 2, nb - 1)), dma((2, 2, nb - 1)), dma((8,)), dma((6, ns)), dma((6, ns)), dma((3,)),
            dma((3 + nb,)), dma((3 + nb,)),
        ],
        compiler_params=pltpu.CompilerParams(
            collective_id=4, has_side_effects=True, vmem_limit_bytes=63 << 20
        ),
        name="backward",
    )(
        own_codes.reshape(n, 1), codes.reshape(nb, 1, n), do, stats, lse, delta, x, rest, table,
        q_all, k_all, v_all, *weights, *early,
    )


def finish_kernel(dn, up, wo, wq, wk, wv, table, token, *outs):
    f32 = jnp.float32
    outs[15][...] = token[...]
    for a, b in zip((wq, wk, wv, wo, dn), outs[:5]):
        b[...] = a[...].astype(f32)
    rows = outs[5].shape[0]
    width = up.shape[1]
    for t in range(outs[5].shape[1] // width):
        outs[5][:, t * width:(t + 1) * width] = up[t * rows:(t + 1) * rows, :].astype(f32)
    shard = lax.axis_index("seq") * 4 + lax.axis_index("shard")
    piece = outs[6].shape[1]
    r = lax.broadcasted_iota(jnp.int32, (width, PAIR), 0)
    c = lax.broadcasted_iota(jnp.int32, (width, PAIR), 1)
    pick = ((r == c + shard * piece) & (c < piece)).astype(f32)
    small = lax.dot_general(
        table[:8, :], pick, (((1,), (0,)), ((), ())), precision=lax.Precision.HIGHEST,
        preferred_element_type=f32,
    )
    for i in range(8):
        outs[6 + i][...] = small[i:i + 1, :piece]
    wide = outs[14].shape[1]
    per = width // wide
    at = pl.multiple_of((shard % per) * wide, wide)
    outs[14][...] = table[pl.ds(8 + shard // per, 1), pl.ds(at, wide)]


def finish(dn, up, wo, wq, wk, wv, table, token, wide):
    width = table.shape[1]
    f32 = jnp.float32
    S = jax.ShapeDtypeStruct
    piece = width // 8
    chunks = up.shape[0] // piece
    out = pl.pallas_call(
        finish_kernel,
        out_shape=(
            *[S(a.shape, f32) for a in (wq, wk, wv, wo, dn)], S((piece, chunks * width), f32),
            *[S((1, piece), f32)] * 8, S((1, wide), f32), S(token.shape, token.dtype),
        ),
        in_specs=[VM] * 8,
        out_specs=(VM,) * 16,
        compiler_params=pltpu.CompilerParams(vmem_limit_bytes=60 << 20),
        name="finish",
    )(dn, up, wo, wq, wk, wv, table, token)
    return out[15], list(out[:6]) + [a.reshape(-1) for a in out[6:15]]


EPSILON = 1e-06
PLANE = ("seq", "shard")


def normalize(hidden, gain, shift):
    center = hidden - jnp.mean(hidden, axis=-1, keepdims=True)
    spread = jnp.mean(center * center, axis=-1, keepdims=True)
    return center * lax.rsqrt(spread + EPSILON) * gain + shift


def smooth_gate(hidden):
    return jax.nn.gelu(hidden, approximate=False)


def mm(left, right):
    return jnp.dot(left, right, preferred_element_type=jnp.float32)


def contract_rows(left, right):
    return dot(left, right, 0, 0)


def times_transpose(left, right):
    return dot(left, right, 1, 1)


def tuned_plane():
    return lax.axis_size("seq") == 2 and lax.axis_size("shard") == 4 and lax.axis_size("blk") == 4


def total(g):
    part = lax.psum_scatter(g.astype(jnp.bfloat16), PLANE, scatter_dimension=0, tiled=True)
    return lax.psum(part, "blk").astype(jnp.float32)


def whole_line(
    inputs, seg, live, mats, vecs, cotangent, codes, own_codes, start,
):
    rows, width = inputs.shape
    length = seg.shape[0]
    scale = HEAD_DIM ** (-0.5)
    xs = lax.all_gather(inputs, "blk", axis=0, tiled=True)
    wq, wk, wv, wo, wup, wdn = [lax.all_gather(w, PLANE, axis=0, tiled=True) for w in mats]
    whole = [lax.all_gather(v, PLANE, axis=0, tiled=True).astype(jnp.float32) for v in vecs]
    bq, bv, bo, g1, s1, bdn, g2, s2, bup = whole
    own_seg = lax.dynamic_slice_in_dim(seg, start, rows)
    low = jnp.sum((seg < own_seg[0]).astype(jnp.int32))
    high = jnp.sum((seg <= own_seg[rows - 1]).astype(jnp.int32))
    span = jnp.stack([low // TILE, (high + TILE - 1) // TILE])
    q_all = ((mm(xs, wq) + bq) * scale).astype(jnp.bfloat16)
    k_all = mm(xs, wk).astype(jnp.bfloat16)
    v_all = (mm(xs, wv) + bv).astype(jnp.bfloat16)
    q, k, v = [lax.dynamic_slice_in_dim(a, start, rows) for a in (q_all, k_all, v_all)]
    summed, attended, lse = attention(q, k_all, v_all, codes, own_codes, span)

    first_sum = inputs.astype(jnp.float32) + (mm(attended, wo) + bo)
    first_norm, first_pull = jax.vjp(normalize, first_sum, g1, s1)
    first_low = first_norm.astype(jnp.bfloat16)
    hidden = mm(first_low, wup) + bup
    gated, gate_pull = jax.vjp(smooth_gate, hidden)
    gated_low = gated.astype(jnp.bfloat16)
    second_sum = first_norm + (mm(gated_low, wdn) + bdn)
    result, second_pull = jax.vjp(normalize, second_sum, g2, s2)
    second_grad, g2_grad, s2_grad = second_pull(cotangent.astype(jnp.float32))
    bdn_grad = jnp.sum(second_grad, axis=0)
    second_low = second_grad.astype(jnp.bfloat16)
    wdn_grad = contract_rows(gated_low, second_low)
    (hidden_grad,) = gate_pull(times_transpose(second_low, wdn))
    bup_grad = jnp.sum(hidden_grad, axis=0)
    hidden_low = hidden_grad.astype(jnp.bfloat16)
    wup_grad = contract_rows(first_low, hidden_low)
    norm_grad = second_grad + times_transpose(hidden_low, wup)
    first_grad, g1_grad, s1_grad = first_pull(norm_grad)
    bo_grad = jnp.sum(first_grad, axis=0)
    first_grad_low = first_grad.astype(jnp.bfloat16)
    wo_grad = contract_rows(attended, first_grad_low)
    do = times_transpose(first_grad_low, wo).astype(jnp.bfloat16)

    stats, delta = row_stats(do, summed, lse)
    do_all, stats_all = [lax.all_gather(a, "blk", axis=0) for a in (do, stats)]
    stats_all = jnp.transpose(stats_all, (1, 2, 0, 3)).reshape(stats.shape[0], 8, length)
    dq, dk, dv = attention_grad(
        q, k, v, do, lse, delta, q_all, k_all, v_all, do_all.reshape(length, width), stats_all,
        codes, own_codes, span,
    )
    r = dq * scale
    rq, rk, rv = [a.astype(jnp.bfloat16) for a in (r, dk, dv)]
    token_grad = first_grad + times_transpose(rq, wq) + times_transpose(rk, wk) + times_transpose(rv, wv)
    grads = [contract_rows(inputs, a) for a in (rq, rk, rv)] + [wo_grad, wdn_grad, wup_grad]
    vectors = [
        jnp.sum(r, axis=0), jnp.sum(dv, axis=0), bo_grad, g1_grad, s1_grad, bdn_grad, g2_grad, s2_grad, bup_grad,
    ]
    return result.astype(jnp.bfloat16), token_grad.astype(jnp.bfloat16), [total(g) for g in grads + vectors]


def tuned_line(inputs, mats, vecs, cotangent, codes, own_codes, nb):
    out = forward(inputs, codes, own_codes, mats, vecs, nb)
    wq, wk, wv, wo, wup, wdn, q_all, k_all, v_all, summed, attended, lse, table, bup = out
    out = middle(attended, inputs, cotangent, summed, lse, table, bup, wo, wup, wdn)
    result, rest, do, stats, delta, table, gdn, gup, gwo = out
    width = inputs.shape[1]
    early = [g.reshape(2, 2, 2, -1, width) for g in (gdn, gup, gwo)]
    token_grad, table, rdn, rup, ro, rwq, rwk, rwv = backward(
        codes, own_codes, do, stats, lse, delta, inputs, rest, table, q_all, k_all, v_all, [wq, wk, wv], early, nb,
    )
    token_grad, sums = finish(rdn, rup, ro, rwq, rwk, rwv, table, token_grad, vecs[8].shape[0])
    return result, token_grad, sums


def per_device(
    tokens, segments, live_mask, query_weight, key_weight, value_weight, out_weight,
    query_bias, value_bias, out_bias, first_gain, first_shift, up_weight, up_bias,
    down_weight, down_bias, second_gain, second_shift, cotangent,
):
    inputs = tokens[0]
    rows = inputs.shape[0]
    nb = lax.axis_size("blk")
    seg, live = segments[0], live_mask[0]
    start = lax.axis_index("blk") * rows
    codes = jnp.where(live > 0, seg, -1 - jnp.arange(seg.shape[0], dtype=jnp.int32))
    own_codes = lax.dynamic_slice_in_dim(codes, start, rows)
    mats = [query_weight, key_weight, value_weight, out_weight, up_weight, down_weight]
    vecs = [query_bias, value_bias, out_bias, first_gain, first_shift, down_bias, second_gain, second_shift, up_bias]
    if tuned_plane():
        result, token_grad, sums = tuned_line(inputs, mats, vecs, cotangent[0], codes, own_codes, nb)
    else:
        result, token_grad, sums = whole_line(
            inputs, seg, live, mats, vecs, cotangent[0], codes, own_codes, start
        )
    rwq, rwk, rwv, ro, rdn, rup, rbq, rbv, rbo, rg1, rs1, rbdn, rg2, rs2, rbup = sums
    return (
        result[None], token_grad[None],
        rwq, rwk, rwv, ro, rbq, rbv, rbo, rg1, rs1, rup, rbup, rdn, rbdn, rg2, rs2,
    )


def solution(mesh):
    flat = P(PLANE, "blk", None)
    mat = P(PLANE, None)
    vec = P(PLANE)
    return jax.shard_map(
        per_device,
        mesh=mesh,
        in_specs=(
            flat, mat, mat, mat, mat, mat, mat, vec, vec, vec, vec, vec, mat, vec, mat, vec, vec, vec, flat,
        ),
        out_specs=(flat, flat, mat, mat, mat, mat, vec, vec, vec, vec, vec, mat, vec, mat, vec, vec, vec),
        check_vma=False,
    )
```

```python
import functools
import jax
import jax.numpy as jnp
from jax import lax
from jax.experimental import pallas as pl
from jax.experimental.pallas import tpu as pltpu
from jax.sharding import PartitionSpec as P

MESH = pl.DeviceIdType.MESH
ANY = pl.BlockSpec(memory_space=pl.ANY)
VMEM_LIMIT = 56 << 20
VM = pl.BlockSpec(memory_space=pltpu.VMEM)


class Place:
    def __init__(self):
        b = lax.axis_index("blk")
        s = lax.axis_index("seq")
        h = lax.axis_index("shard")
        x = h // 2
        c = h % 2
        self.b, self.s, self.h, self.x, self.c = b, s, h, x, c
        self.X = (b, s, (1 - x) * 2 + c)
        self.Y = (b, 1 - s, h)
        self.C = (b, s, x * 2 + 1 - c)
        self.L = (b - 1, s, h)
        self.R = (b + 1, s, h)
        self.me = s * 4 + h
        self.xi = s * 4 + (1 - x) * 2 + c
        self.yi = (1 - s) * 4 + h
        self.di = (1 - s) * 4 + (1 - x) * 2 + c

    def z(self, j):
        return (j, self.s, self.h)


def greet(p, nb, plane, line):
    bar = pltpu.get_barrier_semaphore()
    count = 0
    if plane:
        for peer in (p.X, p.Y, p.C):
            pl.semaphore_signal(bar, inc=1, device_id=peer, device_id_type=MESH)
        count = count + 3
    if line == "near":
        @pl.when(p.b > 0)
        def _():
            pl.semaphore_signal(bar, inc=1, device_id=p.L, device_id_type=MESH)

        @pl.when(p.b < nb - 1)
        def _():
            pl.semaphore_signal(bar, inc=1, device_id=p.R, device_id_type=MESH)
        count = count + jnp.where(p.b > 0, 1, 0) + jnp.where(p.b < nb - 1, 1, 0)
    if line == "all":
        for j in range(nb):
            @pl.when(p.b != j)
            def _():
                pl.semaphore_signal(bar, inc=1, device_id=p.z(j), device_id_type=MESH)
        count = count + nb - 1
    return lambda: pl.semaphore_wait(bar, count)


def enter(p, nb, plane, line):
    greet(p, nb, plane, line)()


def rcopy(src, dst, ss, rs, dev):
    return pltpu.make_async_remote_copy(
        src_ref=src, dst_ref=dst, send_sem=ss, recv_sem=rs, device_id=dev, device_id_type=MESH
    )


class LineGather:
    def __init__(self, p, nb, own, out, ssem, rsem):
        self.p, self.nb, self.own, self.out, self.ssem, self.rsem = p, nb, own, out, ssem, rsem

    def _copies(self, t):
        p, nb = self.p, self.nb
        rb = p.b - t
        lb = p.b + t
        src_r = self.own if t == 0 else self.out.at[jnp.maximum(rb, 0)]
        src_l = self.own if t == 0 else self.out.at[jnp.minimum(lb, nb - 1)]
        right = rcopy(src_r, self.out.at[jnp.maximum(rb, 0)], self.ssem.at[0, t], self.rsem.at[0, t], p.R)
        left = rcopy(src_l, self.out.at[jnp.minimum(lb, nb - 1)], self.ssem.at[1, t], self.rsem.at[1, t], p.L)
        return right, left, (rb >= 0) & (p.b < nb - 1), (lb <= nb - 1) & (p.b > 0)

    def start(self, t):
        right, left, cr, cl = self._copies(t)
        pl.when(cr)(right.start)
        pl.when(cl)(left.start)

    def wait_recv(self, t):
        p, nb = self.p, self.nb
        right, left, _, _ = self._copies(t)
        pl.when(p.b - 1 - t >= 0)(right.wait_recv)
        pl.when(p.b + 1 + t <= nb - 1)(left.wait_recv)

    def wait_send(self, t):
        right, left, cr, cl = self._copies(t)
        pl.when(cr)(right.wait_send)
        pl.when(cl)(left.wait_send)


class PlaneGather:
    def __init__(self, p, own, out, ssem, rsem, lsem):
        rows = own.shape[0]
        half = rows // 2

        def whole(i):
            return out.at[pl.ds(pl.multiple_of(i * rows, rows), rows)]

        def low(i):
            return out.at[pl.ds(pl.multiple_of(i * rows, rows), half)]

        def high(i):
            return out.at[pl.ds(pl.multiple_of(i * rows + half, half), half)]

        def send(k, src, dst, dev):
            return rcopy(src, dst, ssem.at[k], rsem.at[k], dev)

        self.x = send(0, own, whole(p.me), p.X)
        self.y = send(1, own, whole(p.me), p.Y)
        self.c = send(2, own, whole(p.me), p.C)
        self.local = pltpu.make_async_copy(own, whole(p.me), lsem)
        self.fx = send(3, high(p.yi), high(p.yi), p.X)
        self.fy = send(4, low(p.xi), low(p.xi), p.Y)
        self.cx = send(5, whole(p.xi), whole(p.xi), p.C)
        self.cy = send(6, whole(p.yi), whole(p.yi), p.C)
        self.cd0 = send(7, low(p.di), low(p.di), p.C)
        self.cd1 = send(8, high(p.di), high(p.di), p.C)

    def start(self):
        for k in (self.x, self.y, self.c, self.local):
            k.start()

    def forward(self):
        self.x.wait_recv()
        self.fy.start()
        self.cx.start()
        self.y.wait_recv()
        self.fx.start()
        self.cy.start()

    def diag(self):
        self.fy.wait_recv()
        self.cd0.start()
        self.fx.wait_recv()
        self.cd1.start()

    def finish(self):
        self.local.wait()
        for k in (self.c, self.cx, self.cy, self.cd0, self.cd1):
            k.wait_recv()

    def drain(self):
        for k in (self.x, self.y, self.c, self.fx, self.fy, self.cx, self.cy, self.cd0, self.cd1):
            k.wait_send()


def staged(count, steps, body):
    def once(i, _):
        for at, todo in steps.items():
            @pl.when(i == at)
            def _():
                for f in todo:
                    f()
        body(i)
        return 0
    lax.fori_loop(0, count, once, 0)


def code_tables(seg, live, rows, col, place):
    nb, _, n = rows.shape
    ids = jnp.where(live[...] > 0, seg[...], -1 - lax.broadcasted_iota(jnp.int32, seg.shape, 1)).astype(jnp.float32)
    for j in range(nb):
        rows[j] = ids[:, j * n:(j + 1) * n]
    col[...] = jnp.broadcast_to(rows[place], (128, n)).T[:, :1]


def turn(b, nb, i):
    far = (i + 1) // 2
    j = jnp.where(i % 2 == 1, b - far, b + far)
    return (j >= 0) & (j <= nb - 1), jnp.clip(j, 0, nb - 1)


def row_loop(rows, chunk, body):
    if rows == chunk:
        body(0)
    else:
        def step(i, _):
            body(pl.multiple_of(i * chunk, chunk))
            return 0
        lax.fori_loop(0, rows // chunk, step, 0)


def add_low(a, b):
    return (a.astype(jnp.float32) + b.astype(jnp.float32)).astype(a.dtype)


def add_into(dst, src):
    def body(r):
        rows = pl.ds(r, 48)
        dst[rows] = add_low(dst[rows], src[rows])
    row_loop(dst.shape[0], 48, body)


class PlaneSum:
    def __init__(self, p, g, buf, stage, ss, rs, ls):
        self.p = p
        self.P, self.BX, self.BY, self.CX, self.CY = buf
        self.R, self.C = g.shape[-2:]
        h = self.R // 2
        self.h = h
        lo, hi = pl.ds(0, h), pl.ds(h, h)
        self.g = g
        self.stage = stage
        self.ss, self.rs = ss, rs
        self.own = None if stage is None else pltpu.make_async_copy(g.at[:, :, p.c], stage, ls)
        self.cBX = rcopy(self.P.at[:, 1 - p.x, lo], self.BX, ss.at[1], rs.at[1], p.X)
        self.cBY = rcopy(self.P.at[1 - p.s, :, hi], self.BY, ss.at[2], rs.at[2], p.Y)
        self.cCX = rcopy(self.P.at[p.s, 1 - p.x, hi], self.CX, ss.at[3], rs.at[3], p.X)
        self.cCY = rcopy(self.P.at[1 - p.s, p.x, lo], self.CY, ss.at[4], rs.at[4], p.Y)
        self.total = self.P.at[p.s, p.x]

    def piece(self, t):
        s, x = t // 2, t % 2
        return rcopy(self.g.at[s, x, 1 - self.p.c], self.P.at[s, x], self.ss.at[5 + t], self.rs.at[5 + t], self.p.C)

    def _core(self):
        return rcopy(self.g.at[:, :, 1 - self.p.c], self.P, self.ss.at[0], self.rs.at[0], self.p.C)

    def a_start(self):
        self._core().start()

    def own_start(self):
        self.own.start()

    def b_start(self, pieces=False):
        if self.own is not None:
            self.own.wait()
        if not pieces:
            self._core().wait_recv()

        def block(i, _):
            s, x = i // 2, i % 2
            if pieces:
                self.piece(i).wait_recv()

            def body(r):
                rows = pl.ds(r, 48)
                mine = self.g[s, x, self.p.c, rows] if self.stage is None else self.stage[s, x, rows]
                self.P[s, x, rows] = add_low(mine, self.P[s, x, rows])
            row_loop(self.R, 48, body)
            return 0
        lax.fori_loop(0, 4, block, 0)
        self.cBX.start()
        self.cBY.start()

    def c_start(self):
        p, h = self.p, self.h
        lo, hi = pl.ds(0, h), pl.ds(h, h)
        self.cBX.wait_recv()
        add_into(self.P.at[1 - p.s, p.x, lo], self.BX.at[1 - p.s])
        self.cCY.start()
        self.cBY.wait_recv()
        add_into(self.P.at[p.s, 1 - p.x, hi], self.BY.at[1 - p.x])
        self.cCX.start()
        add_into(self.P.at[p.s, p.x, lo], self.BX.at[p.s])
        add_into(self.P.at[p.s, p.x, hi], self.BY.at[p.x])

    def end(self):
        h = self.h
        self.cCY.wait_recv()
        add_into(self.total.at[pl.ds(0, h)], self.CY)
        self.cCX.wait_recv()
        add_into(self.total.at[pl.ds(h, h)], self.CX)

    def drain(self, pieces=False):
        for k in (self.cBX, self.cBY, self.cCX, self.cCY):
            k.wait_send()
        if pieces:
            for t in range(4):
                self.piece(t).wait_send()
        else:
            self._core().wait_send()


class LineSum:
    def __init__(self, p, nb, part, out, Z, ss, rs):
        self.p, self.nb, self.F, self.O, self.Z, self.ss, self.rs = p, nb, part, out, Z, ss, rs
        self.R, self.C = part.shape
        self.h = self.R // 2

    def quarter(self, ref, j):
        R, C = self.R, self.C
        r, c = (j // 2) * (R // 2), (j % 2) * (C // 2)
        if not isinstance(j, int):
            r, c = pl.multiple_of(r, R // 2), pl.multiple_of(c, C // 2)
        return ref.at[pl.ds(r, R // 2), pl.ds(c, C // 2)]

    def _send(self, j, slot):
        return rcopy(self.quarter(self.F, j), self.Z.at[slot], self.ss.at[j], self.rs.at[slot], self.p.z(j))

    def start(self):
        for j in range(self.nb):
            pl.when(self.p.b != j)(self._send(j, self.p.b).start)

    def _spread(self, t):
        p, nb = self.p, self.nb
        k = nb + 2 * t
        r, l = p.b - t, p.b + t
        qr = self.quarter(self.O, jnp.maximum(r, 0))
        ql = self.quarter(self.O, jnp.minimum(l, nb - 1))
        right = rcopy(qr, qr, self.ss.at[k], self.rs.at[k], p.R)
        left = rcopy(ql, ql, self.ss.at[k + 1], self.rs.at[k + 1], p.L)
        return right, left, (r >= 0) & (p.b < nb - 1), (l <= nb - 1) & (p.b > 0)

    def _spread_recv(self, t, forwarded):
        right, left, _, _ = self._spread(t)
        p, nb = self.p, self.nb
        hands_right, hands_left = p.b < nb - 1, p.b > 0
        if t == nb - 2:
            hands_right, hands_left = False, False
        if forwarded:
            pl.when((p.b - 1 - t >= 0) & hands_right)(right.wait_recv)
            pl.when((p.b + 1 + t <= nb - 1) & hands_left)(left.wait_recv)
        else:
            pl.when((p.b - 1 - t >= 0) & jnp.logical_not(hands_right))(right.wait_recv)
            pl.when((p.b + 1 + t <= nb - 1) & jnp.logical_not(hands_left))(left.wait_recv)

    def _sum(self):
        p, nb = self.p, self.nb
        mine = self.quarter(self.F, p.b)
        total = self.quarter(self.O, p.b)
        for j in range(nb):
            pl.when(p.b != j)(self._send(j, j).wait_recv)

        def body(r):
            rows = pl.ds(r, 48)
            acc = mine[rows].astype(jnp.float32)
            for d in range(1, nb):
                acc = acc + self.Z[(p.b + d) % nb, rows].astype(jnp.float32)
            total[rows] = acc.astype(mine.dtype)
        row_loop(self.h, 48, body)

    def spread(self, t):
        if t == 0:
            self._sum()
        else:
            self._spread_recv(t - 1, True)
        right, left, cr, cl = self._spread(t)
        pl.when(cr)(right.start)
        pl.when(cl)(left.start)

    def finish(self):
        for t in range(self.nb - 1):
            self._spread_recv(t, False)

    def drain(self):
        for j in range(self.nb):
            pl.when(self.p.b != j)(self._send(j, self.p.b).wait_send)
        for t in range(self.nb - 1):
            right, left, cr, cl = self._spread(t)
            pl.when(cr)(right.wait_send)
            pl.when(cl)(left.wait_send)


class DirectSum(LineSum):
    def _share(self, j, slot):
        q = self.quarter(self.O, slot)
        return rcopy(q, q, self.ss.at[self.nb + j], self.rs.at[self.nb + slot], self.p.z(j))

    def share(self):
        self._sum()
        for j in range(self.nb):
            pl.when(self.p.b != j)(self._share(j, self.p.b).start)

    def finish(self):
        for j in range(self.nb):
            pl.when(self.p.b != j)(self._share(j, j).wait_recv)

    def drain(self):
        for j in range(self.nb):
            @pl.when(self.p.b != j)
            def _():
                self._send(j, self.p.b).wait_send()
                self._share(j, self.p.b).wait_send()


class ChainSum(LineSum):
    def _right(self, j):
        return rcopy(self.quarter(self.F, j), self.Z.at[j], self.ss.at[j], self.rs.at[j], self.p.R)

    def _left(self, j, last):
        slot = self.nb if last else j
        k = 3 * self.nb - 2 + j
        return rcopy(self.quarter(self.F, j), self.Z.at[slot], self.ss.at[k], self.rs.at[k], self.p.L)

    def start(self):
        self.hop(0)

    def hop(self, t):
        nb, p = self.nb, self.p

        @pl.when(p.b == t)
        def _():
            for j in range(nb - 1, t, -1):
                if t > 0:
                    self._right(j).wait_recv()
                    add_into(self.quarter(self.F, j), self.Z.at[j])
                self._right(j).start()

        @pl.when(p.b == nb - 1 - t)
        def _():
            for j in range(nb - 1 - t):
                if t > 0:
                    self._left(j, False).wait_recv()
                    add_into(self.quarter(self.F, j), self.Z.at[j])
                self._left(j, j == nb - 2 - t).start()

    def _sum(self):
        p, nb = self.p, self.nb
        mine = self.quarter(self.F, p.b)
        total = self.quarter(self.O, p.b)
        for j in range(nb):
            @pl.when(p.b == j)
            def _():
                if j > 0:
                    self._right(j).wait_recv()
                if j < nb - 1:
                    self._left(j, True).wait_recv()

        @pl.when(p.b > 0)
        def _():
            add_into(mine, self.Z.at[p.b])

        @pl.when(p.b < nb - 1)
        def _():
            add_into(mine, self.Z.at[nb])

        def body(r):
            rows = pl.ds(r, 48)
            total[rows] = mine[rows]
        row_loop(self.h, 48, body)

    def drain(self):
        nb, p = self.nb, self.p
        for t in range(nb - 1):
            @pl.when(p.b == t)
            def _():
                for j in range(nb - 1, t, -1):
                    self._right(j).wait_send()

            @pl.when(p.b == nb - 1 - t)
            def _():
                for j in range(nb - 1 - t):
                    self._left(j, j == nb - 2 - t).wait_send()
            right, left, cr, cl = self._spread(t)
            pl.when(cr)(right.wait_send)
            pl.when(cl)(left.wait_send)


def plane_scratch(shape):
    R, C = shape
    h = R // 2
    sizes = ((2, 2, R, C), (2, h, C), (2, h, C), (h, C), (h, C))
    return [pltpu.VMEM(s, jnp.bfloat16) for s in sizes]


def line_scratch(shape, nb):
    return pltpu.VMEM((nb + 1, shape[0] // 2, shape[1] // 2), jnp.bfloat16)


PLANE_BUFS = 5
PLANE_SEMS = 9


def line_sems(nb):
    return 2 * nb + 2 * (nb - 1)


class TableSum:
    def __init__(self, p, nb, t, bufs, line, ss, rs):
        self.p, self.nb, self.t, self.bufs, self.line = p, nb, t, bufs, line
        self.steps = [
            rcopy(t if i == 0 else bufs.at[i - 1], bufs.at[3 + i], ss.at[i], rs.at[i], dev)
            for i, dev in enumerate((p.C, p.X, p.Y))
        ]
        self.ss, self.rs = ss, rs

    def start(self):
        self.steps[0].start()

    def step(self, i):
        self.steps[i].wait_recv()
        self.bufs[i] = (self.t[...] if i == 0 else self.bufs[i - 1]) + self.bufs[3 + i]
        if i < 2:
            self.steps[i + 1].start()
        else:
            self.line[self.p.b] = self.bufs[2]
            for j in range(self.nb):
                pl.when(self.p.b != j)(self._z(j, self.p.b).start)

    def _z(self, j, slot):
        return rcopy(
            self.bufs.at[2], self.line.at[slot], self.ss.at[3 + j], self.rs.at[3 + slot], self.p.z(j)
        )

    def finish(self, out):
        for j in range(self.nb):
            pl.when(self.p.b != j)(self._z(j, j).wait_recv)
        total = self.line[0]
        for j in range(1, self.nb):
            total = total + self.line[j]
        out[...] = total

    def drain(self):
        for k in self.steps:
            k.wait_send()
        for j in range(self.nb):
            pl.when(self.p.b != j)(self._z(j, self.p.b).wait_send)


HEAD_DIM = 64
PAIR = 128
MASKED = -1e30
TILE = 512


def dot(a, b, ca, cb):
    return lax.dot_general(a, b, (((ca,), (cb,)), ((), ())), preferred_element_type=jnp.float32)


def left_lanes(shape):
    return lax.broadcasted_iota(jnp.int32, shape, 1) < HEAD_DIM


def one_head(pair, left, first):
    keep = left if first else jnp.logical_not(left)
    return jnp.where(keep, pair, jnp.zeros_like(pair))


def lane_groups(op, a):
    out = a[:, :PAIR]
    for g in range(1, a.shape[1] // PAIR):
        out = op(out, a[:, g * PAIR:(g + 1) * PAIR])
    return out


def attn_fwd_kernel(span, col_ref, row_ref, q_ref, k_ref, v_ref, o_ref, ob_ref, lse_ref, s_ref, m_ref, l_ref, acc_ref):
    rows = q_ref.shape[0]
    left = left_lanes((rows, PAIR))
    m_ref[...] = jnp.full_like(m_ref, MASKED)
    l_ref[...] = jnp.zeros_like(l_ref)
    acc_ref[...] = jnp.zeros_like(acc_ref)
    q = q_ref[...]
    heads = [one_head(q, left, i == 0) for i in range(2)]
    codes = col_ref[...]

    def score(t, _):
        at = pl.multiple_of(t * TILE, TILE)
        k = k_ref[pl.ds(at, TILE), :]
        mask = codes == row_ref[:, pl.ds(at, TILE)]
        for i in range(2):
            s = jnp.where(mask, dot(heads[i], k, 1, 1), MASKED)
            s_ref[i, t] = s
            m_ref[i] = jnp.maximum(m_ref[i], lane_groups(jnp.maximum, s))
        return 0

    lax.fori_loop(span[0], span[1], score, 0)
    tops = [jnp.max(m_ref[i], axis=1, keepdims=True) for i in range(2)]

    def mix(t, _):
        v = v_ref[pl.ds(pl.multiple_of(t * TILE, TILE), TILE), :]
        parts = []
        for i in range(2):
            p = jnp.exp(s_ref[i, t] - tops[i])
            l_ref[i] += lane_groups(jnp.add, p)
            parts.append(dot(p.astype(jnp.bfloat16), v, 1, 0))
        acc_ref[...] += jnp.where(left, parts[0], parts[1])
        return 0

    lax.fori_loop(span[0], span[1], mix, 0)
    sums = [jnp.sum(l_ref[i], axis=1, keepdims=True) for i in range(2)]
    total = jnp.where(left, sums[0], sums[1])
    o = acc_ref[...] / total
    o_ref[...] = o
    ob_ref[...] = o.astype(jnp.bfloat16)
    lse_ref[...] = jnp.where(left, tops[0], tops[1]) + jnp.log(total)


def attention(q, k_all, v_all, codes, own_codes, span):
    rows, width = q.shape
    total = k_all.shape[0]
    pairs = width // PAIR
    own = pl.BlockSpec((rows, PAIR), lambda h, s: (0, h))
    every = pl.BlockSpec((total, PAIR), lambda h, s: (0, h))
    return pl.pallas_call(
        attn_fwd_kernel,
        grid_spec=pltpu.PrefetchScalarGridSpec(
            num_scalar_prefetch=1,
            grid=(pairs,),
            in_specs=[
                pl.BlockSpec((rows, 1), lambda h, s: (0, 0)),
                pl.BlockSpec((1, total), lambda h, s: (0, 0)),
                own, every, every,
            ],
            out_specs=[own, own, own],
            scratch_shapes=[
                pltpu.VMEM((2, total // TILE, rows, TILE), jnp.float32),
                pltpu.VMEM((2, rows, PAIR), jnp.float32),
                pltpu.VMEM((2, rows, PAIR), jnp.float32),
                pltpu.VMEM((rows, PAIR), jnp.float32),
            ],
        ),
        out_shape=[
            jax.ShapeDtypeStruct((rows, width), jnp.float32),
            jax.ShapeDtypeStruct((rows, width), jnp.bfloat16),
            jax.ShapeDtypeStruct((rows, width), jnp.float32),
        ],
        compiler_params=pltpu.CompilerParams(vmem_limit_bytes=48 << 20),
        name="attention",
    )(span, own_codes.reshape(rows, 1), codes.reshape(1, total), q, k_all, v_all)


def stats_kernel(g_ref, o_ref, lse_ref, out_ref, delta_ref):
    rows = g_ref.shape[0]
    left = left_lanes((rows, PAIR))
    t = g_ref[...].astype(jnp.float32) * o_ref[...]
    d0 = jnp.sum(jnp.where(left, t, 0.0), axis=1, keepdims=True)
    d1 = jnp.sum(jnp.where(left, 0.0, t), axis=1, keepdims=True)
    delta_ref[...] = jnp.where(left, d0, d1)
    lane = lax.broadcasted_iota(jnp.int32, (rows, PAIR), 1)
    lse = lse_ref[...]
    packed = jnp.where(lane == 0, lse[:, :1], jnp.where(lane == 1, lse[:, HEAD_DIM:HEAD_DIM + 1], jnp.where(lane == 2, d0, d1)))
    out_ref[0] = packed.T[:8]


def row_stats(grad, o, lse):
    rows, width = grad.shape
    pairs = width // PAIR
    own = pl.BlockSpec((rows, PAIR), lambda h: (0, h))
    return pl.pallas_call(
        stats_kernel,
        grid=(pairs,),
        in_specs=[own, own, own],
        out_specs=[pl.BlockSpec((1, 8, rows), lambda h: (h, 0, 0)), own],
        out_shape=[
            jax.ShapeDtypeStruct((pairs, 8, rows), jnp.float32),
            jax.ShapeDtypeStruct((rows, width), jnp.float32),
        ],
        name="row_stats",
    )(grad, o, lse)


def attn_bwd_kernel(span, col_ref, row_ref, q_ref, k_ref, v_ref, g_ref, lse_ref, delta_ref,
                    qa_ref, ka_ref, va_ref, ga_ref, st_ref, dq_ref, dk_ref, dv_ref):
    rows = q_ref.shape[0]
    left = left_lanes((rows, PAIR))
    dq_ref[...] = jnp.zeros_like(dq_ref)
    dk_ref[...] = jnp.zeros_like(dk_ref)
    dv_ref[...] = jnp.zeros_like(dv_ref)
    codes = col_ref[...]
    qs = [one_head(q_ref[...], left, i == 0) for i in range(2)]
    ks = [one_head(k_ref[...], left, i == 0) for i in range(2)]
    vs = [one_head(v_ref[...], left, i == 0) for i in range(2)]
    gs = [one_head(g_ref[...], left, i == 0) for i in range(2)]
    lses = [lse_ref[:, i * HEAD_DIM:i * HEAD_DIM + 1] for i in range(2)]
    deltas = [delta_ref[:, i * HEAD_DIM:i * HEAD_DIM + 1] for i in range(2)]

    def step(t, _):
        at = pl.multiple_of(t * TILE, TILE)
        tile = pl.ds(at, TILE)
        mask = codes == row_ref[:, tile]
        k, v, q, g = ka_ref[tile, :], va_ref[tile, :], qa_ref[tile, :], ga_ref[tile, :]
        dqs, dks, dvs = [], [], []
        for i in range(2):
            s = jnp.where(mask, dot(qs[i], k, 1, 1), MASKED)
            p = jnp.exp(s - lses[i])
            dp = dot(gs[i], v, 1, 1)
            ds = (p * (dp - deltas[i])).astype(jnp.bfloat16)
            dqs.append(dot(ds, k, 1, 0))
            st = jnp.where(mask, dot(ks[i], q, 1, 1), MASKED)
            pt = jnp.exp(st - st_ref[0, i:i + 1, tile])
            dvs.append(dot(pt.astype(jnp.bfloat16), g, 1, 0))
            dpt = dot(vs[i], g, 1, 1)
            dst = (pt * (dpt - st_ref[0, 2 + i:3 + i, tile])).astype(jnp.bfloat16)
            dks.append(dot(dst, q, 1, 0))
        dq_ref[...] += jnp.where(left, dqs[0], dqs[1])
        dk_ref[...] += jnp.where(left, dks[0], dks[1])
        dv_ref[...] += jnp.where(left, dvs[0], dvs[1])
        return 0

    lax.fori_loop(span[0], span[1], step, 0)


def attention_grad(q, k, v, g, lse, delta, q_all, k_all, v_all, g_all, stats, codes, own_codes, span):
    rows, width = q.shape
    total = k_all.shape[0]
    pairs = width // PAIR
    own = pl.BlockSpec((rows, PAIR), lambda h, s: (0, h))
    every = pl.BlockSpec((total, PAIR), lambda h, s: (0, h))
    return pl.pallas_call(
        attn_bwd_kernel,
        grid_spec=pltpu.PrefetchScalarGridSpec(
            num_scalar_prefetch=1,
            grid=(pairs,),
            in_specs=[
                pl.BlockSpec((rows, 1), lambda h, s: (0, 0)),
                pl.BlockSpec((1, total), lambda h, s: (0, 0)),
                own, own, own, own, own, own, every, every, every, every,
                pl.BlockSpec((1, 8, total), lambda h, s: (h, 0, 0)),
            ],
            out_specs=[own, own, own],
        ),
        out_shape=[
            jax.ShapeDtypeStruct((rows, width), jnp.float32),
            jax.ShapeDtypeStruct((rows, width), jnp.float32),
            jax.ShapeDtypeStruct((rows, width), jnp.float32),
        ],
        compiler_params=pltpu.CompilerParams(vmem_limit_bytes=48 << 20),
        name="attention_grad",
    )(span, own_codes.reshape(rows, 1), codes.reshape(1, total), q, k, v, g, lse, delta, q_all, k_all, v_all, g_all, stats)


VEC_ROWS = 8


def forward_kernel(nb, *refs):
    x_ref, seg, live = refs[:3]
    shards_in = refs[3:9]
    vecs_in = refs[9:18]
    wq_o, wk_o, wv_o, wo_o, wup_o, wdn_o = refs[18:24]
    q_o, k_o, v_o = refs[24:27]
    o_ref, ob_ref, lse_ref, vec_ref, bup_ref = refs[27:32]
    rest = refs[32:]
    x_all, wq, wk, wv, pack, packs, q, k, v, m_ref, l_ref, codes, rows = rest[:13]
    zs, zr, gs, gr, gl, ws, es = rest[13:]
    n, width = x_ref.shape
    pairs = width // PAIR
    p = Place()
    own = pltpu.make_async_copy(x_ref, x_all.at[p.b], ws.at[3])
    own.start()
    pack[...] = jnp.zeros_like(pack)
    for i in range(VEC_ROWS):
        pack[i:i + 1, :vecs_in[i].shape[1]] = vecs_in[i][...].astype(jnp.float32)
    for i in range(vecs_in[8].shape[1] // PAIR):
        pack[VEC_ROWS + i:VEC_ROWS + i + 1, :] = vecs_in[8][:, i * PAIR:(i + 1) * PAIR].astype(jnp.float32)
    enter(p, nb, True, "near")
    line = LineGather(p, nb, x_ref, x_all, zs, zr)
    targets = (packs, wq, wk, wv, wo_o, wup_o, wdn_o)
    sources = (pack,) + tuple(shards_in)
    g = [PlaneGather(p, sources[i], targets[i], gs.at[i], gr.at[i], gl.at[i]) for i in range(7)]
    line.start(0)
    for c in g[:5]:
        c.start()
    code_tables(seg, live, rows, codes, p.b)
    for c in g[:4]:
        c.forward()
    g[5].start()
    g[6].start()
    line.wait_recv(0)
    line.start(1)
    for c in g[:4]:
        c.diag()
    for c in g[:4]:
        c.finish()
    own.wait()
    keep = [
        pltpu.make_async_copy(a, b, ws.at[i]) for i, (a, b) in enumerate(((wq, wq_o), (wk, wk_o), (wv, wv_o)))
    ]
    for c in keep:
        c.start()

    piece = width // 8
    r = lax.broadcasted_iota(jnp.int32, (PAIR, width), 0)
    c = lax.broadcasted_iota(jnp.int32, (PAIR, width), 1)
    total = jnp.zeros((2 * VEC_ROWS, width), jnp.float32)
    for i in range(8):
        pick = ((c == r + i * piece) & (r < piece)).astype(jnp.bfloat16)
        total += dot(packs[2 * VEC_ROWS * i:2 * VEC_ROWS * (i + 1), :].astype(jnp.bfloat16), pick, 1, 0)
    vec_ref[...] = total[:VEC_ROWS]
    up_piece = bup_ref.shape[1] // 8
    for i in range(8):
        for t in range(up_piece // PAIR):
            at = i * up_piece + t * PAIR
            row = 2 * VEC_ROWS * i + VEC_ROWS + t
            bup_ref[:, at:at + PAIR] = packs[row:row + 1, :]

    scale = HEAD_DIM ** (-0.5)
    step = 256

    def outs(j, e):
        return [
            pltpu.make_async_copy(a.at[j], b.at[j], es.at[i, e])
            for i, (a, b) in enumerate(((q, q_o), (k, k_o), (v, v_o)))
        ]

    def project(j):
        def columns(t, _):
            at = pl.ds(pl.multiple_of(t * step, step), step)
            xs = x_all[j]
            q[j, :, at] = ((dot(xs, wq[:, at], 1, 0) + vec_ref[0:1, at]) * scale).astype(jnp.bfloat16)
            k[j, :, at] = dot(xs, wk[:, at], 1, 0).astype(jnp.bfloat16)
            v[j, :, at] = (dot(xs, wv[:, at], 1, 0) + vec_ref[1:2, at]).astype(jnp.bfloat16)
            return 0
        lax.fori_loop(0, width // step, columns, 0, unroll=True)

    def attend(j):
        def pair(h, _):
            left = left_lanes((n, PAIR))
            lanes = pl.ds(pl.multiple_of(h * PAIR, PAIR), PAIR)
            mask = codes[...] == rows[j]
            qs, ks, vs = q[p.b, :, lanes], k[j, :, lanes], v[j, :, lanes]
            parts, alphas = [], []
            for i in range(2):
                s = jnp.where(mask, dot(one_head(qs, left, i == 0), ks, 1, 1), MASKED)
                top = jnp.max(lane_groups(jnp.maximum, s), axis=1, keepdims=True)
                old = m_ref[2 * h + i]
                new = jnp.maximum(old, top)
                alpha = jnp.exp(old - new)
                e = jnp.exp(s - jnp.concatenate([new] * (n // PAIR), axis=1))
                m_ref[2 * h + i] = new
                l_ref[2 * h + i] = l_ref[2 * h + i] * alpha + lane_groups(jnp.add, e)
                alphas.append(alpha)
                parts.append(dot(e.astype(jnp.bfloat16), vs, 1, 0))
            got = jnp.where(left, parts[0], parts[1])
            o_ref[:, lanes] = o_ref[:, lanes] * jnp.where(left, alphas[0], alphas[1]) + got
            return 0
        lax.fori_loop(0, pairs, pair, 0, unroll=2)

    def block(i):
        ok, j = turn(p.b, nb, i)

        @pl.when(ok)
        def _():
            project(j)
            for c in outs(j, i):
                c.start()
            attend(j)

    def hop(t, last=False):
        line.wait_recv(t)
        if not last:
            line.start(t + 1)

    m_ref[...] = jnp.full_like(m_ref, MASKED)
    l_ref[...] = jnp.zeros_like(l_ref)
    o_ref[...] = jnp.zeros_like(o_ref)
    staged(
        2 * nb - 1,
        {
            1: [g[4].forward, g[5].forward],
            2: [lambda: hop(1)],
            3: [g[6].forward, g[4].diag],
            5: [g[5].diag, g[6].diag, lambda: hop(2, True)],
        },
        block,
    )

    def close(h, _):
        left = left_lanes((n, PAIR))
        lanes = pl.ds(pl.multiple_of(h * PAIR, PAIR), PAIR)
        sums = [jnp.sum(l_ref[2 * h + i], axis=1, keepdims=True) for i in range(2)]
        mass = jnp.where(left, sums[0], sums[1])
        out = o_ref[:, lanes] / mass
        o_ref[:, lanes] = out
        ob_ref[:, lanes] = out.astype(jnp.bfloat16)
        lse_ref[:, lanes] = jnp.where(left, m_ref[2 * h], m_ref[2 * h + 1]) + jnp.log(mass)
        return 0
    lax.fori_loop(0, pairs, close, 0)
    for c in g[4:]:
        c.finish()
    for c in keep:
        c.wait()
    for i in range(2 * nb - 1):
        ok, j = turn(p.b, nb, i)

        @pl.when(ok)
        def _():
            for c in outs(j, i):
                c.wait()
    for t in range(nb - 1):
        line.wait_send(t)
    for c in g:
        c.drain()


def forward(x, seg, live, weights, vecs, nb):
    n, width = x.shape
    hidden = weights[4].shape[1]
    bf, f32 = jnp.bfloat16, jnp.float32
    every = jax.ShapeDtypeStruct((nb, n, width), bf)
    block = jax.ShapeDtypeStruct((n, width), f32)
    mats = [jax.ShapeDtypeStruct((8 * w.shape[0], w.shape[1]), w.dtype) for w in weights]
    dma = pltpu.SemaphoreType.DMA
    return pl.pallas_call(
        functools.partial(forward_kernel, nb),
        out_shape=(
            *mats, every, every, every, block, jax.ShapeDtypeStruct((n, width), bf), block,
            jax.ShapeDtypeStruct((VEC_ROWS, width), f32), jax.ShapeDtypeStruct((1, hidden), f32),
        ),
        in_specs=[VM] * 18,
        out_specs=(ANY,) * 9 + (VM,) * 5,
        scratch_shapes=[
            pltpu.VMEM((nb, n, width), bf),
            pltpu.VMEM((width, width), bf), pltpu.VMEM((width, width), bf), pltpu.VMEM((width, width), bf),
            pltpu.VMEM((2 * VEC_ROWS, PAIR), f32), pltpu.VMEM((16 * VEC_ROWS, PAIR), f32),
            pltpu.VMEM((nb, n, width), bf), pltpu.VMEM((nb, n, width), bf), pltpu.VMEM((nb, n, width), bf),
            pltpu.VMEM((width // HEAD_DIM, n, PAIR), f32), pltpu.VMEM((width // HEAD_DIM, n, PAIR), f32),
            pltpu.VMEM((n, 1), f32), pltpu.VMEM((nb, 1, n), f32),
            dma((2, nb - 1)), dma((2, nb - 1)), dma((7, 9)), dma((7, 9)), dma((7,)), dma((4,)), dma((3, 2 * nb)),
        ],
        compiler_params=pltpu.CompilerParams(
            collective_id=1, has_side_effects=True, vmem_limit_bytes=60 << 20
        ),
        name="forward",
    )(
        x, seg, live, *weights, *[v.reshape(1, -1) for v in vecs]
    )


ROOT_HALF = 0.7071067811865476
ROOT_TWO_PI = 0.3989422804014327
CHUNK = 768
PART = 256


def erf_parts(x):
    x = jnp.clip(x, -3.832506856900711, 3.832506856900711)
    y = x * x
    top = jnp.full_like(y, 0.00022905065861350646)
    for a in (0.0034082910107109506, 0.050955695062380861, 0.18520832239976145, 1.128379143519084):
        top = top * y + a
    low = jnp.full_like(y, -1.1791602954361697e-7)
    for a in (
        0.000023547966471313185, 0.0010179625278914885, 0.014070470171167667,
        0.11098505178285362, 0.49746925110067538, 1.0,
    ):
        low = low * y + a
    return x * top / low


def middle_kernel(
    att_ref, x_ref, cot_ref, o_ref, lse_ref, vec_ref, bup_ref, wo_hbm, wup_hbm, wdn_hbm,
    out_ref, rest_ref, do_ref, stats_ref, delta_ref, table_ref, gdn_hbm, gup_hbm, gwo_ref,
    wo, wup, wdn, u_ref, slope_ref, y_ref, dh_ref, low_ref, gdn, gup, sems, osems,
):
    n, width = x_ref.shape
    hidden = wup.shape[1]
    chunks = hidden // CHUNK
    f32, bf = jnp.float32, jnp.bfloat16
    loads = [
        pltpu.make_async_copy(a, b, sems.at[i])
        for i, (a, b) in enumerate(((wo_hbm, wo), (wup_hbm, wup), (wdn_hbm, wdn)))
    ]
    for c in loads:
        c.start()
    table_ref[...] = jnp.zeros_like(table_ref)

    def vec(i):
        return vec_ref[i:i + 1, :]

    def mean(a):
        return jnp.sum(a, axis=1, keepdims=True) * (1.0 / width)

    def centred(h):
        c = h - mean(h)
        inv = lax.rsqrt(mean(c * c) + EPSILON)
        return c * inv, inv

    def pull(grad, hat, inv, gain):
        d = grad * gain
        return inv * (d - mean(d) - hat * mean(d * hat))

    def column_sum(a):
        return jnp.sum(a, axis=0, keepdims=True)

    blocks = 2
    m = n // blocks

    def rows_of(i):
        return pl.ds(pl.multiple_of(i * m, m), m)

    loads[0].wait()

    def first(i, _):
        r = rows_of(i)
        h = x_ref[r, :].astype(f32) + dot(att_ref[r, :], wo[...], 1, 0) + vec(2)
        hat, _ = centred(h)
        y = hat * vec(3) + vec(4)
        rest_ref[r, :] = h
        dh_ref[r, :] = y + vec(5)
        low_ref[r, :] = y.astype(bf)
        return 0
    lax.fori_loop(0, blocks, first, 0)
    for c in loads[1:]:
        c.wait()

    def up(t, _):
        total = dh_ref[...]
        for s in range(CHUNK // PART):
            at = pl.ds(pl.multiple_of(t * CHUNK + s * PART, PART), PART)
            z = dot(low_ref[...], wup[:, at], 1, 0) + bup_ref[:, at]
            cdf = 0.5 + 0.5 * erf_parts(z * ROOT_HALF)
            low = (z * cdf).astype(bf)
            u_ref[:, at] = low
            slope_ref[:, at] = cdf + z * (jnp.exp(-0.5 * z * z) * ROOT_TWO_PI)
            total = total + dot(low, wdn[at, :], 1, 0)
        dh_ref[...] = total
        return 0
    lax.fori_loop(0, chunks, up, 0)

    def second(i, _):
        r = rows_of(i)
        hat, inv = centred(dh_ref[r, :])
        out_ref[r, :] = (hat * vec(6) + vec(7)).astype(bf)
        g = cot_ref[r, :].astype(f32)
        table_ref[6:7, :] += column_sum(g * hat)
        table_ref[7:8, :] += column_sum(g)
        dh = pull(g, hat, inv, vec(6))
        table_ref[5:6, :] += column_sum(dh)
        dh_ref[r, :] = dh
        y_ref[r, :] = dh.astype(bf)
        return 0
    lax.fori_loop(0, blocks, second, 0)

    def down(t, _):
        at = pl.ds(pl.multiple_of(t * CHUNK, CHUNK), CHUNK)
        parts = []
        total = dh_ref[...]
        for s in range(CHUNK // PART):
            cols = pl.ds(pl.multiple_of(t * CHUNK + s * PART, PART), PART)
            dz = dot(y_ref[...], wdn[cols, :], 1, 1) * slope_ref[:, cols]
            table_ref[pl.ds(8 + t, 1), s * PART:(s + 1) * PART] = column_sum(dz)
            c = dz.astype(bf)
            parts.append(c)
            total = total + dot(c, wup[:, cols], 1, 1)
            gdn[cols, :] = dot(u_ref[:, cols], y_ref[...], 0, 0).astype(bf)
        dh_ref[...] = total
        c = jnp.concatenate(parts, axis=1)
        r = width // 8
        for i in range(2):
            half = width // 2
            g = dot(low_ref[:, i * half:(i + 1) * half], c, 0, 0).astype(bf)
            for k in range(4):
                gup[4 * i + k, t] = g[k * r:(k + 1) * r]
        pltpu.make_async_copy(gdn.at[at], gdn_hbm.at[at], osems.at[0, t]).start()
        pltpu.make_async_copy(gup.at[:, t], gup_hbm.at[:, t], osems.at[1, t]).start()
        return 0
    lax.fori_loop(0, chunks, down, 0)

    def third(i, _):
        r = rows_of(i)
        hat, inv = centred(rest_ref[r, :])
        g = dh_ref[r, :]
        table_ref[3:4, :] += column_sum(g * hat)
        table_ref[4:5, :] += column_sum(g)
        dh = pull(g, hat, inv, vec(3))
        table_ref[2:3, :] += column_sum(dh)
        rest_ref[r, :] = dh
        low = dh.astype(bf)
        low_ref[r, :] = low
        do = dot(low, wo[...], 1, 1).astype(bf)
        do_ref[r, :] = do
        table_ref[1:2, :] += column_sum(do.astype(f32))
        return 0
    lax.fori_loop(0, blocks, third, 0)

    def heads(h, _):
        lanes = pl.ds(pl.multiple_of(h * PAIR, PAIR), PAIR)
        left = left_lanes((n, PAIR))
        t = do_ref[:, lanes].astype(f32) * o_ref[:, lanes]
        d0 = jnp.sum(jnp.where(left, t, 0.0), axis=1, keepdims=True)
        d1 = jnp.sum(jnp.where(left, 0.0, t), axis=1, keepdims=True)
        delta_ref[:, lanes] = jnp.where(left, d0, d1)
        lane = lax.broadcasted_iota(jnp.int32, (n, PAIR), 1)
        lse = lse_ref[:, lanes]
        packed = jnp.where(lane == 0, lse[:, :1], jnp.where(
            lane == 1, lse[:, HEAD_DIM:HEAD_DIM + 1], jnp.where(lane == 2, d0, d1)))
        stats_ref[h] = packed.T[:8]
        gwo_ref[lanes, :] = dot(att_ref[:, lanes], low_ref[...], 0, 0).astype(bf)
        return 0
    lax.fori_loop(0, width // PAIR, heads, 0)
    for t in range(chunks):
        at = pl.ds(t * CHUNK, CHUNK)
        pltpu.make_async_copy(gdn.at[at], gdn_hbm.at[at], osems.at[0, t]).wait()
        pltpu.make_async_copy(gup.at[:, t], gup_hbm.at[:, t], osems.at[1, t]).wait()


def middle(att, x, cot, o, lse, vecs, bup, wo, wup, wdn):
    n, width = x.shape
    hidden = wup.shape[1]
    chunks = hidden // CHUNK
    bf, f32 = jnp.bfloat16, jnp.float32
    S = jax.ShapeDtypeStruct
    dma = pltpu.SemaphoreType.DMA
    return pl.pallas_call(
        middle_kernel,
        out_shape=(
            S((n, width), bf), S((n, width), f32), S((n, width), bf), S((width // PAIR, 8, n), f32),
            S((n, width), f32), S((16, width), f32), S((hidden, width), bf),
            S((8, chunks, width // 8, CHUNK), bf), S((width, width), bf),
        ),
        in_specs=[VM] * 7 + [ANY] * 3,
        out_specs=(VM,) * 6 + (ANY, ANY, VM),
        scratch_shapes=[
            pltpu.VMEM((width, width), bf), pltpu.VMEM((width, hidden), bf), pltpu.VMEM((hidden, width), bf),
            pltpu.VMEM((n, hidden), bf), pltpu.VMEM((n, hidden), f32), pltpu.VMEM((n, width), bf),
            pltpu.VMEM((n, width), f32), pltpu.VMEM((n, width), bf),
            pltpu.VMEM((hidden, width), bf), pltpu.VMEM((8, chunks, width // 8, CHUNK), bf),
            dma((3,)), dma((2, chunks)),
        ],
        compiler_params=pltpu.CompilerParams(vmem_limit_bytes=60 << 20),
        name="middle",
    )(att, x, cot, o, lse, vecs, bup, wo, wup, wdn)


PAIR_GROUP = 2


class AttentionGrad:
    def __init__(self, codes, rows, q, k, v, g, lse, delta, stats, own, dq, dk, dv):
        self.codes, self.rows = codes, rows
        self.q, self.k, self.v, self.g = q, k, v, g
        self.lse, self.delta, self.stats = lse, delta, stats
        self.own = own
        self.dq, self.dk, self.dv = dq, dk, dv
        self.n = dq.shape[0]
        self.pairs = dq.shape[1] // PAIR

    def queries(self, j, group):
        own = self.own

        def pair(h):
            left = left_lanes((self.n, PAIR))
            lanes = pl.ds(pl.multiple_of(h * PAIR, PAIR), PAIR)
            mask = self.codes[...] == self.rows[j]
            q, g = self.q[own, :, lanes], self.g[own, :, lanes]
            k, v = self.k[j, :, lanes], self.v[j, :, lanes]
            lse, delta = self.lse[:, lanes], self.delta[:, lanes]
            parts = []
            for i in range(2):
                at = slice(i * HEAD_DIM, i * HEAD_DIM + 1)
                s = jnp.where(mask, dot(one_head(q, left, i == 0), k, 1, 1), MASKED)
                p = jnp.exp(s - lse[:, at])
                dp = dot(one_head(g, left, i == 0), v, 1, 1)
                ds = (p * (dp - delta[:, at])).astype(jnp.bfloat16)
                parts.append(dot(ds, k, 1, 0))
            self.dq[:, lanes] += jnp.where(left, parts[0], parts[1])

        for i in range(PAIR_GROUP):
            pair(group * PAIR_GROUP + i)

    def keys(self, j, group):
        own = self.own

        def pair(h):
            left = left_lanes((self.n, PAIR))
            lanes = pl.ds(pl.multiple_of(h * PAIR, PAIR), PAIR)
            mask = self.codes[...] == self.rows[j]
            k, v = self.k[own, :, lanes], self.v[own, :, lanes]
            q, g = self.q[j, :, lanes], self.g[j, :, lanes]
            dks, dvs = [], []
            for i in range(2):
                st = jnp.where(mask, dot(one_head(k, left, i == 0), q, 1, 1), MASKED)
                pt = jnp.exp(st - self.stats[j, h, i:i + 1])
                dvs.append(dot(pt.astype(jnp.bfloat16), g, 1, 0))
                dpt = dot(one_head(v, left, i == 0), g, 1, 1)
                dst = (pt * (dpt - self.stats[j, h, 2 + i:3 + i])).astype(jnp.bfloat16)
                dks.append(dot(dst, q, 1, 0))
            self.dk[:, lanes] += jnp.where(left, dks[0], dks[1])
            self.dv[:, lanes] += jnp.where(left, dvs[0], dvs[1])

        for i in range(PAIR_GROUP):
            pair(group * PAIR_GROUP + i)


TABLE = 16


def backward_kernel(nb, *refs):
    seg, live, g_own, st_own, lse, delta, x_hbm, rest_hbm, table = refs[:9]
    q_hbm, k_hbm, v_hbm, wq_hbm, wk_hbm, wv_hbm = refs[9:15]
    early = refs[15:18]
    token_ref, table_out = refs[18:20]
    outs = refs[20:24]
    rest = refs[24:]
    q, k, v, g, stats, dq, dk, dv, wq, wk, wv, gw, stage_dn, stage_up, tab, tsum, tline, x_ref, rest_ref, codes, rows = rest[:21]
    zbufs = rest[21:25]
    bufs = rest[25:25 + 4 * PLANE_BUFS]
    zs, zr, ls, ps, pr, ds, dr, rls, ts, tr = rest[25 + 4 * PLANE_BUFS:]
    n, width = g_own.shape
    p = Place()
    loads = [
        pltpu.make_async_copy(a, b, ls.at[i])
        for i, (a, b) in enumerate((
            (k_hbm, k), (v_hbm, v), (q_hbm, q), (g_own, g.at[p.b]), (st_own, stats.at[p.b]),
            (wq_hbm, wq), (wk_hbm, wk), (wv_hbm, wv), (x_hbm, x_ref), (rest_hbm, rest_ref),
            (early[2], gw.at[0, :, :, :, pl.ds(gw.shape[4] // 2, gw.shape[4] // 2)]),
        ))
    ]
    for c in loads:
        c.start()
    enter(p, nb, True, "all")
    lines = [
        LineGather(p, nb, g_own, g, zs.at[0], zr.at[0]),
        LineGather(p, nb, st_own, stats, zs.at[1], zr.at[1]),
    ]
    sources = (early[0], early[1], gw.at[0], gw.at[1])
    stages = (stage_dn, stage_up, None, None)
    planes = [
        PlaneSum(
            p, sources[i], bufs[PLANE_BUFS * i:PLANE_BUFS * (i + 1)], stages[i], ps.at[i], pr.at[i], rls.at[min(i, 1)]
        )
        for i in range(4)
    ]
    dn, up, qo, kv = planes
    chains = [
        (DirectSum if i == 3 else ChainSum)(p, nb, planes[i].total, outs[i], zbufs[i], ds.at[i], dr.at[i])
        for i in range(4)
    ]
    ldn, lup, lqo, lkv = chains
    vec = TableSum(p, nb, tab, tsum, tline, ts, tr)
    for c in lines:
        c.start(0)
    for c in (dn, up):
        c.a_start()
        c.own_start()
    work = AttentionGrad(codes, rows, q, k, v, g, lse, delta, stats, p.b, dq, dk, dv)
    code_tables(seg, live, rows, codes, p.b)
    for c in (dq, dk, dv):
        c[...] = jnp.zeros_like(c)
    for c in loads[:4]:
        c.wait()
    dn.b_start()

    low = k
    def slot(i):
        return (p.b + 1 + i) % nb

    def settle(i, src, scale, row):
        value = src[...] if scale is None else src[...] * scale
        if row is not None:
            tab[row:row + 1, :] = jnp.sum(value, axis=0, keepdims=True)
        low[slot(i)] = value.astype(jnp.bfloat16)

    def weight_grad(i, item, base):
        half = width // 2
        r = width // 8
        for m in range(2):
            part = dot(x_ref[:, m * half:(m + 1) * half], low[slot(i)], 0, 0).astype(jnp.bfloat16)
            for a in range(2):
                for b in range(2):
                    at = (2 * a + b) * r
                    gw[item, m, a, b, base:base + r] = part[at:at + r]

    def hop(t, last=False):
        for c in lines:
            c.wait_recv(t)
            if not last:
                c.start(t + 1)

    groups = work.pairs // PAIR_GROUP
    staged(
        nb * groups,
        {
            2: [up.b_start],
            5: [lambda: hop(0)],
            6: [dn.c_start],
        },
        lambda i: work.queries((p.b + i // groups) % nb, i % groups),
    )
    for c in loads[4:]:
        c.wait()
    tab[...] = table[...]
    settle(0, dq, HEAD_DIM ** (-0.5), 0)
    vec.start()
    weight_grad(0, 0, 0)
    qo.a_start()
    hop(1)
    up.c_start()

    def keys(i):
        ok, j = turn(p.b, nb, i // groups)
        pl.when(ok)(lambda: work.keys(j, i % groups))

    def across(a, c):
        a.end()
        c.start()

    staged(
        (2 * nb - 1) * groups,
        {
            2: [lambda: across(dn, ldn), qo.b_start],
            5: [lambda: across(up, lup)],
            6: [lambda: ldn.hop(1)],
            8: [qo.c_start],
            9: [lambda: lup.hop(1), lambda: ldn.hop(2)],
            12: [lambda: across(qo, lqo), lambda: lup.hop(2), lambda: ldn.spread(0)],
            15: [lambda: hop(2, True), lambda: lqo.hop(1), lambda: lup.spread(0), lambda: ldn.spread(1)],
            18: [lambda: lqo.hop(2), lambda: lup.spread(1), lambda: ldn.spread(2)],
        },
        keys,
    )
    settle(1, dk, None, None)
    weight_grad(1, 1, 0)
    settle(2, dv, None, None)
    weight_grad(2, 1, width // 8)
    kv.a_start()
    vec.step(0)
    kv.b_start()

    part = 256

    def columns(t, _):
        at = pl.ds(pl.multiple_of(t * part, part), part)
        total = rest_ref[:, at]
        for i, w in enumerate((wq, wk, wv)):
            total = total + dot(low[slot(i)], w[at, :], 1, 1)
        token_ref[:, at] = total.astype(jnp.bfloat16)
        return 0
    lax.fori_loop(0, width // part, columns, 0)

    lqo.spread(0)
    lup.spread(2)
    vec.step(1)
    kv.c_start()
    lqo.spread(1)
    vec.step(2)
    across(kv, lkv)
    lqo.spread(2)
    lkv.share()
    vec.finish(table_out)
    for c in chains:
        c.finish()
    for t in range(nb - 1):
        for c in lines:
            c.wait_send(t)
    for c in planes:
        c.drain()
    for c in chains:
        c.drain()
    vec.drain()


def backward(seg, live, do, stats, lse, delta, x, rest, table, q_all, k_all, v_all, weights, early, nb):
    n, width = do.shape
    bf, f32 = jnp.bfloat16, jnp.float32
    pair = (2, 2, 2, width // 4, width)
    sources = [early[0].shape, early[1].shape, pair, pair]
    sums = [s[-2:] for s in sources]
    scratch = []
    for s in sources:
        scratch += plane_scratch(s[-2:])
    ns = line_sems(nb)
    every = pltpu.VMEM((nb, n, width), bf)
    total = pltpu.VMEM((n, width), f32)
    square = pltpu.VMEM((width, width), bf)
    dma = pltpu.SemaphoreType.DMA
    return pl.pallas_call(
        functools.partial(backward_kernel, nb),
        out_shape=(
            jax.ShapeDtypeStruct((n, width), bf), jax.ShapeDtypeStruct((TABLE, width), f32),
            *[jax.ShapeDtypeStruct(s, bf) for s in sums],
        ),
        in_specs=[VM] * 6 + [ANY] * 2 + [VM] + [ANY] * 9,
        out_specs=(VM,) * 6,
        scratch_shapes=[
            every, every, every, every, pltpu.VMEM((nb,) + stats.shape, f32), total, total, total,
            square, square, square, pltpu.VMEM((2,) + pair, bf),
            *[pltpu.VMEM(s[:2] + s[3:], bf) for s in sources[:2]],
            pltpu.VMEM((TABLE, width), f32), pltpu.VMEM((6, TABLE, width), f32), pltpu.VMEM((nb, TABLE, width), f32),
            pltpu.VMEM((n, width), bf), total, pltpu.VMEM((n, 1), f32), pltpu.VMEM((nb, 1, n), f32),
            *[line_scratch(s, nb) for s in sums], *scratch,
            dma((2, 2, nb - 1)), dma((2, 2, nb - 1)), dma((12,)), dma((4, PLANE_SEMS)), dma((4, PLANE_SEMS)),
            dma((4, ns)), dma((4, ns)), dma((2,)), dma((3 + nb,)), dma((3 + nb,)),
        ],
        compiler_params=pltpu.CompilerParams(
            collective_id=4, has_side_effects=True, vmem_limit_bytes=63 << 20
        ),
        name="backward",
    )(
        seg, live, do, stats, lse, delta, x, rest, table,
        q_all, k_all, v_all, *weights, *early,
    )


def finish_kernel(dn, up, qo, kv, table, token, *outs):
    f32 = jnp.float32
    outs[15][...] = token[...]
    n = outs[0].shape[0]
    for i, (a, at) in enumerate(((qo, 0), (kv, 0), (kv, n), (qo, n))):
        outs[i][...] = a[at:at + n, :].astype(f32)
    outs[4][...] = dn[...].astype(f32)
    rows = outs[5].shape[0]
    width = up.shape[1]
    for t in range(outs[5].shape[1] // width):
        outs[5][:, t * width:(t + 1) * width] = up[t * rows:(t + 1) * rows, :].astype(f32)
    shard = lax.axis_index("seq") * 4 + lax.axis_index("shard")
    piece = outs[6].shape[1]
    r = lax.broadcasted_iota(jnp.int32, (width, PAIR), 0)
    c = lax.broadcasted_iota(jnp.int32, (width, PAIR), 1)
    pick = ((r == c + shard * piece) & (c < piece)).astype(f32)
    small = lax.dot_general(
        table[:8, :], pick, (((1,), (0,)), ((), ())), precision=lax.Precision.HIGHEST,
        preferred_element_type=f32,
    )
    for i in range(8):
        outs[6 + i][...] = small[i:i + 1, :piece]
    wide = outs[14].shape[1]
    per = width // wide
    at = pl.multiple_of((shard % per) * wide, wide)
    outs[14][...] = table[pl.ds(8 + shard // per, 1), pl.ds(at, wide)]


def finish(dn, up, qo, kv, table, token, wide):
    width = table.shape[1]
    f32 = jnp.float32
    S = jax.ShapeDtypeStruct
    piece = width // 8
    chunks = up.shape[0] // piece
    out = pl.pallas_call(
        finish_kernel,
        out_shape=(
            *[S((piece, width), f32)] * 4, S(dn.shape, f32), S((piece, chunks * width), f32),
            *[S((1, piece), f32)] * 8, S((1, wide), f32), S(token.shape, token.dtype),
        ),
        in_specs=[VM] * 6,
        out_specs=(VM,) * 16,
        compiler_params=pltpu.CompilerParams(vmem_limit_bytes=60 << 20),
        name="finish",
    )(dn, up, qo, kv, table, token)
    return out[15], list(out[:6]) + [a.reshape(-1) for a in out[6:15]]


EPSILON = 1e-06
PLANE = ("seq", "shard")


def normalize(hidden, gain, shift):
    center = hidden - jnp.mean(hidden, axis=-1, keepdims=True)
    spread = jnp.mean(center * center, axis=-1, keepdims=True)
    return center * lax.rsqrt(spread + EPSILON) * gain + shift


def smooth_gate(hidden):
    return jax.nn.gelu(hidden, approximate=False)


def mm(left, right):
    return jnp.dot(left, right, preferred_element_type=jnp.float32)


def contract_rows(left, right):
    return dot(left, right, 0, 0)


def times_transpose(left, right):
    return dot(left, right, 1, 1)


def tuned_plane():
    return lax.axis_size("seq") == 2 and lax.axis_size("shard") == 4 and lax.axis_size("blk") == 4


def total(g):
    part = lax.psum_scatter(g.astype(jnp.bfloat16), PLANE, scatter_dimension=0, tiled=True)
    return lax.psum(part, "blk").astype(jnp.float32)


def whole_line(
    inputs, seg, live, mats, vecs, cotangent, codes, own_codes, start,
):
    rows, width = inputs.shape
    length = seg.shape[0]
    scale = HEAD_DIM ** (-0.5)
    xs = lax.all_gather(inputs, "blk", axis=0, tiled=True)
    wq, wk, wv, wo, wup, wdn = [lax.all_gather(w, PLANE, axis=0, tiled=True) for w in mats]
    whole = [lax.all_gather(v, PLANE, axis=0, tiled=True).astype(jnp.float32) for v in vecs]
    bq, bv, bo, g1, s1, bdn, g2, s2, bup = whole
    own_seg = lax.dynamic_slice_in_dim(seg, start, rows)
    low = jnp.sum((seg < own_seg[0]).astype(jnp.int32))
    high = jnp.sum((seg <= own_seg[rows - 1]).astype(jnp.int32))
    span = jnp.stack([low // TILE, (high + TILE - 1) // TILE])
    q_all = ((mm(xs, wq) + bq) * scale).astype(jnp.bfloat16)
    k_all = mm(xs, wk).astype(jnp.bfloat16)
    v_all = (mm(xs, wv) + bv).astype(jnp.bfloat16)
    q, k, v = [lax.dynamic_slice_in_dim(a, start, rows) for a in (q_all, k_all, v_all)]
    summed, attended, lse = attention(q, k_all, v_all, codes, own_codes, span)

    first_sum = inputs.astype(jnp.float32) + (mm(attended, wo) + bo)
    first_norm, first_pull = jax.vjp(normalize, first_sum, g1, s1)
    first_low = first_norm.astype(jnp.bfloat16)
    hidden = mm(first_low, wup) + bup
    gated, gate_pull = jax.vjp(smooth_gate, hidden)
    gated_low = gated.astype(jnp.bfloat16)
    second_sum = first_norm + (mm(gated_low, wdn) + bdn)
    result, second_pull = jax.vjp(normalize, second_sum, g2, s2)
    second_grad, g2_grad, s2_grad = second_pull(cotangent.astype(jnp.float32))
    bdn_grad = jnp.sum(second_grad, axis=0)
    second_low = second_grad.astype(jnp.bfloat16)
    wdn_grad = contract_rows(gated_low, second_low)
    (hidden_grad,) = gate_pull(times_transpose(second_low, wdn))
    bup_grad = jnp.sum(hidden_grad, axis=0)
    hidden_low = hidden_grad.astype(jnp.bfloat16)
    wup_grad = contract_rows(first_low, hidden_low)
    norm_grad = second_grad + times_transpose(hidden_low, wup)
    first_grad, g1_grad, s1_grad = first_pull(norm_grad)
    bo_grad = jnp.sum(first_grad, axis=0)
    first_grad_low = first_grad.astype(jnp.bfloat16)
    wo_grad = contract_rows(attended, first_grad_low)
    do = times_transpose(first_grad_low, wo).astype(jnp.bfloat16)

    stats, delta = row_stats(do, summed, lse)
    do_all, stats_all = [lax.all_gather(a, "blk", axis=0) for a in (do, stats)]
    stats_all = jnp.transpose(stats_all, (1, 2, 0, 3)).reshape(stats.shape[0], 8, length)
    dq, dk, dv = attention_grad(
        q, k, v, do, lse, delta, q_all, k_all, v_all, do_all.reshape(length, width), stats_all,
        codes, own_codes, span,
    )
    r = dq * scale
    rq, rk, rv = [a.astype(jnp.bfloat16) for a in (r, dk, dv)]
    token_grad = first_grad + times_transpose(rq, wq) + times_transpose(rk, wk) + times_transpose(rv, wv)
    grads = [contract_rows(inputs, a) for a in (rq, rk, rv)] + [wo_grad, wdn_grad, wup_grad]
    vectors = [
        jnp.sum(r, axis=0), jnp.sum(dv, axis=0), bo_grad, g1_grad, s1_grad, bdn_grad, g2_grad, s2_grad, bup_grad,
    ]
    return result.astype(jnp.bfloat16), token_grad.astype(jnp.bfloat16), [total(g) for g in grads + vectors]


def tuned_line(inputs, mats, vecs, cotangent, seg, live, nb):
    out = forward(inputs, seg, live, mats, vecs, nb)
    wq, wk, wv, wo, wup, wdn, q_all, k_all, v_all, summed, attended, lse, table, bup = out
    out = middle(attended, inputs, cotangent, summed, lse, table, bup, wo, wup, wdn)
    result, rest, do, stats, delta, table, gdn, gup, gwo = out
    width = inputs.shape[1]
    early = [g.reshape(2, 2, 2, -1, width) for g in (gdn, gup, gwo)]
    token_grad, table, rdn, rup, rqo, rkv = backward(
        seg, live, do, stats, lse, delta, inputs, rest, table, q_all, k_all, v_all, [wq, wk, wv], early, nb,
    )
    token_grad, sums = finish(rdn, rup, rqo, rkv, table, token_grad, vecs[8].shape[0])
    return result, token_grad, sums


def per_device(
    tokens, segments, live_mask, query_weight, key_weight, value_weight, out_weight,
    query_bias, value_bias, out_bias, first_gain, first_shift, up_weight, up_bias,
    down_weight, down_bias, second_gain, second_shift, cotangent,
):
    inputs = tokens[0]
    rows = inputs.shape[0]
    nb = lax.axis_size("blk")
    seg, live = segments[0], live_mask[0]
    start = lax.axis_index("blk") * rows
    codes = jnp.where(live > 0, seg, -1 - jnp.arange(seg.shape[0], dtype=jnp.int32))
    own_codes = lax.dynamic_slice_in_dim(codes, start, rows)
    mats = [query_weight, key_weight, value_weight, out_weight, up_weight, down_weight]
    vecs = [query_bias, value_bias, out_bias, first_gain, first_shift, down_bias, second_gain, second_shift, up_bias]
    if tuned_plane():
        result, token_grad, sums = tuned_line(inputs, mats, vecs, cotangent[0], segments, live_mask, nb)
    else:
        result, token_grad, sums = whole_line(
            inputs, seg, live, mats, vecs, cotangent[0], codes, own_codes, start
        )
    rwq, rwk, rwv, ro, rdn, rup, rbq, rbv, rbo, rg1, rs1, rbdn, rg2, rs2, rbup = sums
    return (
        result[None], token_grad[None],
        rwq, rwk, rwv, ro, rbq, rbv, rbo, rg1, rs1, rup, rbup, rdn, rbdn, rg2, rs2,
    )


def solution(mesh):
    flat = P(PLANE, "blk", None)
    mat = P(PLANE, None)
    vec = P(PLANE)
    return jax.shard_map(
        per_device,
        mesh=mesh,
        in_specs=(
            flat, mat, mat, mat, mat, mat, mat, vec, vec, vec, vec, vec, mat, vec, mat, vec, vec, vec, flat,
        ),
        out_specs=(flat, flat, mat, mat, mat, mat, vec, vec, vec, vec, vec, mat, vec, mat, vec, vec, vec),
        check_vma=False,
    )
```

```python
import functools
import jax
import jax.numpy as jnp
from jax import lax
from jax.experimental import pallas as pl
from jax.experimental.pallas import tpu as pltpu
from jax.sharding import PartitionSpec as P

MESH = pl.DeviceIdType.MESH
ANY = pl.BlockSpec(memory_space=pl.ANY)
VMEM_LIMIT = 56 << 20
VM = pl.BlockSpec(memory_space=pltpu.VMEM)


class Place:
    def __init__(self):
        b = lax.axis_index("blk")
        s = lax.axis_index("seq")
        h = lax.axis_index("shard")
        x = h // 2
        c = h % 2
        self.b, self.s, self.h, self.x, self.c = b, s, h, x, c
        self.X = (b, s, (1 - x) * 2 + c)
        self.Y = (b, 1 - s, h)
        self.C = (b, s, x * 2 + 1 - c)
        self.L = (b - 1, s, h)
        self.R = (b + 1, s, h)
        self.me = s * 4 + h
        self.xi = s * 4 + (1 - x) * 2 + c
        self.yi = (1 - s) * 4 + h
        self.di = (1 - s) * 4 + (1 - x) * 2 + c

    def z(self, j):
        return (j, self.s, self.h)


def greet(p, nb, plane, line):
    bar = pltpu.get_barrier_semaphore()
    count = 0
    if plane:
        for peer in (p.X, p.Y, p.C):
            pl.semaphore_signal(bar, inc=1, device_id=peer, device_id_type=MESH)
        count = count + 3
    if line == "near":
        @pl.when(p.b > 0)
        def _():
            pl.semaphore_signal(bar, inc=1, device_id=p.L, device_id_type=MESH)

        @pl.when(p.b < nb - 1)
        def _():
            pl.semaphore_signal(bar, inc=1, device_id=p.R, device_id_type=MESH)
        count = count + jnp.where(p.b > 0, 1, 0) + jnp.where(p.b < nb - 1, 1, 0)
    if line == "all":
        for j in range(nb):
            @pl.when(p.b != j)
            def _():
                pl.semaphore_signal(bar, inc=1, device_id=p.z(j), device_id_type=MESH)
        count = count + nb - 1
    return lambda: pl.semaphore_wait(bar, count)


def enter(p, nb, plane, line):
    greet(p, nb, plane, line)()


def rcopy(src, dst, ss, rs, dev):
    return pltpu.make_async_remote_copy(
        src_ref=src, dst_ref=dst, send_sem=ss, recv_sem=rs, device_id=dev, device_id_type=MESH
    )


class LineGather:
    def __init__(self, p, nb, own, out, ssem, rsem):
        self.p, self.nb, self.own, self.out, self.ssem, self.rsem = p, nb, own, out, ssem, rsem

    def _copies(self, t):
        p, nb = self.p, self.nb
        rb = p.b - t
        lb = p.b + t
        src_r = self.own if t == 0 else self.out.at[jnp.maximum(rb, 0)]
        src_l = self.own if t == 0 else self.out.at[jnp.minimum(lb, nb - 1)]
        right = rcopy(src_r, self.out.at[jnp.maximum(rb, 0)], self.ssem.at[0, t], self.rsem.at[0, t], p.R)
        left = rcopy(src_l, self.out.at[jnp.minimum(lb, nb - 1)], self.ssem.at[1, t], self.rsem.at[1, t], p.L)
        return right, left, (rb >= 0) & (p.b < nb - 1), (lb <= nb - 1) & (p.b > 0)

    def start(self, t):
        right, left, cr, cl = self._copies(t)
        pl.when(cr)(right.start)
        pl.when(cl)(left.start)

    def wait_recv(self, t):
        p, nb = self.p, self.nb
        right, left, _, _ = self._copies(t)
        pl.when(p.b - 1 - t >= 0)(right.wait_recv)
        pl.when(p.b + 1 + t <= nb - 1)(left.wait_recv)

    def wait_send(self, t):
        right, left, cr, cl = self._copies(t)
        pl.when(cr)(right.wait_send)
        pl.when(cl)(left.wait_send)


class PlaneGather:
    def __init__(self, p, own, out, ssem, rsem, lsem):
        rows = own.shape[0]
        half = rows // 2

        def whole(i):
            return out.at[pl.ds(pl.multiple_of(i * rows, rows), rows)]

        def low(i):
            return out.at[pl.ds(pl.multiple_of(i * rows, rows), half)]

        def high(i):
            return out.at[pl.ds(pl.multiple_of(i * rows + half, half), half)]

        def send(k, src, dst, dev):
            return rcopy(src, dst, ssem.at[k], rsem.at[k], dev)

        self.x = send(0, own, whole(p.me), p.X)
        self.y = send(1, own, whole(p.me), p.Y)
        self.c = send(2, own, whole(p.me), p.C)
        self.local = pltpu.make_async_copy(own, whole(p.me), lsem)
        self.fx = send(3, high(p.yi), high(p.yi), p.X)
        self.fy = send(4, low(p.xi), low(p.xi), p.Y)
        self.cx = send(5, whole(p.xi), whole(p.xi), p.C)
        self.cy = send(6, whole(p.yi), whole(p.yi), p.C)
        self.cd0 = send(7, low(p.di), low(p.di), p.C)
        self.cd1 = send(8, high(p.di), high(p.di), p.C)

    def start(self):
        for k in (self.x, self.y, self.c, self.local):
            k.start()

    def forward(self):
        self.x.wait_recv()
        self.fy.start()
        self.cx.start()
        self.y.wait_recv()
        self.fx.start()
        self.cy.start()

    def diag(self):
        self.fy.wait_recv()
        self.cd0.start()
        self.fx.wait_recv()
        self.cd1.start()

    def finish(self):
        self.local.wait()
        for k in (self.c, self.cx, self.cy, self.cd0, self.cd1):
            k.wait_recv()

    def drain(self):
        for k in (self.x, self.y, self.c, self.fx, self.fy, self.cx, self.cy, self.cd0, self.cd1):
            k.wait_send()


def staged(count, steps, body):
    def once(i, _):
        for at, todo in steps.items():
            @pl.when(i == at)
            def _():
                for f in todo:
                    f()
        body(i)
        return 0
    lax.fori_loop(0, count, once, 0)


def code_tables(seg, live, rows, col, place):
    nb, _, n = rows.shape
    ids = jnp.where(live[...] > 0, seg[...], -1 - lax.broadcasted_iota(jnp.int32, seg.shape, 1)).astype(jnp.float32)
    for j in range(nb):
        rows[j] = ids[:, j * n:(j + 1) * n]
    col[...] = jnp.broadcast_to(rows[place], (128, n)).T[:, :1]


def turn(b, nb, i):
    far = (i + 1) // 2
    j = jnp.where(i % 2 == 1, b - far, b + far)
    return (j >= 0) & (j <= nb - 1), jnp.clip(j, 0, nb - 1)


def row_loop(rows, chunk, body):
    if rows == chunk:
        body(0)
    else:
        def step(i, _):
            body(pl.multiple_of(i * chunk, chunk))
            return 0
        lax.fori_loop(0, rows // chunk, step, 0)


def add_low(a, b):
    return (a.astype(jnp.float32) + b.astype(jnp.float32)).astype(a.dtype)


def add_into(dst, src):
    def body(r):
        rows = pl.ds(r, 48)
        dst[rows] = add_low(dst[rows], src[rows])
    row_loop(dst.shape[0], 48, body)


class PlaneSum:
    def __init__(self, p, g, buf, stage, ss, rs, ls):
        self.p = p
        self.P, self.BX, self.BY, self.CX, self.CY = buf
        self.R, self.C = g.shape[-2:]
        h = self.R // 2
        self.h = h
        lo, hi = pl.ds(0, h), pl.ds(h, h)
        self.g = g
        self.stage = stage
        self.ss, self.rs = ss, rs
        self.own = None if stage is None else pltpu.make_async_copy(g.at[:, :, p.c], stage, ls)
        self.cBX = rcopy(self.P.at[:, 1 - p.x, lo], self.BX, ss.at[1], rs.at[1], p.X)
        self.cBY = rcopy(self.P.at[1 - p.s, :, hi], self.BY, ss.at[2], rs.at[2], p.Y)
        self.cCX = rcopy(self.P.at[p.s, 1 - p.x, hi], self.CX, ss.at[3], rs.at[3], p.X)
        self.cCY = rcopy(self.P.at[1 - p.s, p.x, lo], self.CY, ss.at[4], rs.at[4], p.Y)
        self.total = self.P.at[p.s, p.x]

    def piece(self, t):
        s, x = t // 2, t % 2
        return rcopy(self.g.at[s, x, 1 - self.p.c], self.P.at[s, x], self.ss.at[5 + t], self.rs.at[5 + t], self.p.C)

    def _core(self):
        return rcopy(self.g.at[:, :, 1 - self.p.c], self.P, self.ss.at[0], self.rs.at[0], self.p.C)

    def a_start(self):
        self._core().start()

    def own_start(self):
        self.own.start()

    def b_start(self, pieces=False):
        if self.own is not None:
            self.own.wait()
        if not pieces:
            self._core().wait_recv()

        def block(i, _):
            s, x = i // 2, i % 2
            if pieces:
                self.piece(i).wait_recv()

            def body(r):
                rows = pl.ds(r, 48)
                mine = self.g[s, x, self.p.c, rows] if self.stage is None else self.stage[s, x, rows]
                self.P[s, x, rows] = add_low(mine, self.P[s, x, rows])
            row_loop(self.R, 48, body)
            return 0
        lax.fori_loop(0, 4, block, 0)
        self.cBX.start()
        self.cBY.start()

    def c_start(self):
        p, h = self.p, self.h
        lo, hi = pl.ds(0, h), pl.ds(h, h)
        self.cBX.wait_recv()
        add_into(self.P.at[1 - p.s, p.x, lo], self.BX.at[1 - p.s])
        self.cCY.start()
        self.cBY.wait_recv()
        add_into(self.P.at[p.s, 1 - p.x, hi], self.BY.at[1 - p.x])
        self.cCX.start()
        add_into(self.P.at[p.s, p.x, lo], self.BX.at[p.s])
        add_into(self.P.at[p.s, p.x, hi], self.BY.at[p.x])

    def end(self):
        h = self.h
        self.cCY.wait_recv()
        add_into(self.total.at[pl.ds(0, h)], self.CY)
        self.cCX.wait_recv()
        add_into(self.total.at[pl.ds(h, h)], self.CX)

    def drain(self, pieces=False):
        for k in (self.cBX, self.cBY, self.cCX, self.cCY):
            k.wait_send()
        if pieces:
            for t in range(4):
                self.piece(t).wait_send()
        else:
            self._core().wait_send()


class LineSum:
    def __init__(self, p, nb, part, out, Z, ss, rs):
        self.p, self.nb, self.F, self.O, self.Z, self.ss, self.rs = p, nb, part, out, Z, ss, rs
        self.R, self.C = part.shape
        self.h = self.R // 2

    def quarter(self, ref, j):
        R, C = self.R, self.C
        r, c = (j // 2) * (R // 2), (j % 2) * (C // 2)
        if not isinstance(j, int):
            r, c = pl.multiple_of(r, R // 2), pl.multiple_of(c, C // 2)
        return ref.at[pl.ds(r, R // 2), pl.ds(c, C // 2)]

    def _send(self, j, slot):
        return rcopy(self.quarter(self.F, j), self.Z.at[slot], self.ss.at[j], self.rs.at[slot], self.p.z(j))

    def start(self):
        for j in range(self.nb):
            pl.when(self.p.b != j)(self._send(j, self.p.b).start)

    def _spread(self, t):
        p, nb = self.p, self.nb
        k = nb + 2 * t
        r, l = p.b - t, p.b + t
        qr = self.quarter(self.O, jnp.maximum(r, 0))
        ql = self.quarter(self.O, jnp.minimum(l, nb - 1))
        right = rcopy(qr, qr, self.ss.at[k], self.rs.at[k], p.R)
        left = rcopy(ql, ql, self.ss.at[k + 1], self.rs.at[k + 1], p.L)
        return right, left, (r >= 0) & (p.b < nb - 1), (l <= nb - 1) & (p.b > 0)

    def _spread_recv(self, t, forwarded):
        right, left, _, _ = self._spread(t)
        p, nb = self.p, self.nb
        hands_right, hands_left = p.b < nb - 1, p.b > 0
        if t == nb - 2:
            hands_right, hands_left = False, False
        if forwarded:
            pl.when((p.b - 1 - t >= 0) & hands_right)(right.wait_recv)
            pl.when((p.b + 1 + t <= nb - 1) & hands_left)(left.wait_recv)
        else:
            pl.when((p.b - 1 - t >= 0) & jnp.logical_not(hands_right))(right.wait_recv)
            pl.when((p.b + 1 + t <= nb - 1) & jnp.logical_not(hands_left))(left.wait_recv)

    def _sum(self):
        p, nb = self.p, self.nb
        mine = self.quarter(self.F, p.b)
        total = self.quarter(self.O, p.b)
        for j in range(nb):
            pl.when(p.b != j)(self._send(j, j).wait_recv)

        def body(r):
            rows = pl.ds(r, 48)
            acc = mine[rows].astype(jnp.float32)
            for d in range(1, nb):
                acc = acc + self.Z[(p.b + d) % nb, rows].astype(jnp.float32)
            total[rows] = acc.astype(mine.dtype)
        row_loop(self.h, 48, body)

    def spread(self, t):
        if t == 0:
            self._sum()
        else:
            self._spread_recv(t - 1, True)
        right, left, cr, cl = self._spread(t)
        pl.when(cr)(right.start)
        pl.when(cl)(left.start)

    def finish(self):
        for t in range(self.nb - 1):
            self._spread_recv(t, False)

    def drain(self):
        for j in range(self.nb):
            pl.when(self.p.b != j)(self._send(j, self.p.b).wait_send)
        for t in range(self.nb - 1):
            right, left, cr, cl = self._spread(t)
            pl.when(cr)(right.wait_send)
            pl.when(cl)(left.wait_send)


class DirectSum(LineSum):
    def _share(self, j, slot):
        q = self.quarter(self.O, slot)
        return rcopy(q, q, self.ss.at[self.nb + j], self.rs.at[self.nb + slot], self.p.z(j))

    def share(self):
        self._sum()
        for j in range(self.nb):
            pl.when(self.p.b != j)(self._share(j, self.p.b).start)

    def finish(self):
        for j in range(self.nb):
            pl.when(self.p.b != j)(self._share(j, j).wait_recv)

    def drain(self):
        for j in range(self.nb):
            @pl.when(self.p.b != j)
            def _():
                self._send(j, self.p.b).wait_send()
                self._share(j, self.p.b).wait_send()


class ChainSum(LineSum):
    def _right(self, j):
        return rcopy(self.quarter(self.F, j), self.Z.at[j], self.ss.at[j], self.rs.at[j], self.p.R)

    def _left(self, j, last):
        slot = self.nb if last else j
        k = 3 * self.nb - 2 + j
        return rcopy(self.quarter(self.F, j), self.Z.at[slot], self.ss.at[k], self.rs.at[k], self.p.L)

    def start(self):
        self.hop(0)

    def hop(self, t):
        nb, p = self.nb, self.p

        @pl.when(p.b == t)
        def _():
            for j in range(nb - 1, t, -1):
                if t > 0:
                    self._right(j).wait_recv()
                    add_into(self.quarter(self.F, j), self.Z.at[j])
                self._right(j).start()

        @pl.when(p.b == nb - 1 - t)
        def _():
            for j in range(nb - 1 - t):
                if t > 0:
                    self._left(j, False).wait_recv()
                    add_into(self.quarter(self.F, j), self.Z.at[j])
                self._left(j, j == nb - 2 - t).start()

    def _sum(self):
        p, nb = self.p, self.nb
        mine = self.quarter(self.F, p.b)
        total = self.quarter(self.O, p.b)
        for j in range(nb):
            @pl.when(p.b == j)
            def _():
                if j > 0:
                    self._right(j).wait_recv()
                if j < nb - 1:
                    self._left(j, True).wait_recv()

        @pl.when(p.b > 0)
        def _():
            add_into(mine, self.Z.at[p.b])

        @pl.when(p.b < nb - 1)
        def _():
            add_into(mine, self.Z.at[nb])

        def body(r):
            rows = pl.ds(r, 48)
            total[rows] = mine[rows]
        row_loop(self.h, 48, body)

    def drain(self):
        nb, p = self.nb, self.p
        for t in range(nb - 1):
            @pl.when(p.b == t)
            def _():
                for j in range(nb - 1, t, -1):
                    self._right(j).wait_send()

            @pl.when(p.b == nb - 1 - t)
            def _():
                for j in range(nb - 1 - t):
                    self._left(j, j == nb - 2 - t).wait_send()
            right, left, cr, cl = self._spread(t)
            pl.when(cr)(right.wait_send)
            pl.when(cl)(left.wait_send)


def plane_scratch(shape):
    R, C = shape
    h = R // 2
    sizes = ((2, 2, R, C), (2, h, C), (2, h, C), (h, C), (h, C))
    return [pltpu.VMEM(s, jnp.bfloat16) for s in sizes]


def line_scratch(shape, nb):
    return pltpu.VMEM((nb + 1, shape[0] // 2, shape[1] // 2), jnp.bfloat16)


PLANE_BUFS = 5
PLANE_SEMS = 9


def line_sems(nb):
    return 2 * nb + 2 * (nb - 1)


class TableSum:
    def __init__(self, p, nb, t, bufs, line, ss, rs):
        self.p, self.nb, self.t, self.bufs, self.line = p, nb, t, bufs, line
        self.steps = [
            rcopy(t if i == 0 else bufs.at[i - 1], bufs.at[3 + i], ss.at[i], rs.at[i], dev)
            for i, dev in enumerate((p.C, p.X, p.Y))
        ]
        self.ss, self.rs = ss, rs

    def start(self):
        self.steps[0].start()

    def step(self, i):
        self.steps[i].wait_recv()
        self.bufs[i] = (self.t[...] if i == 0 else self.bufs[i - 1]) + self.bufs[3 + i]
        if i < 2:
            self.steps[i + 1].start()
        else:
            self.line[self.p.b] = self.bufs[2]
            for j in range(self.nb):
                pl.when(self.p.b != j)(self._z(j, self.p.b).start)

    def _z(self, j, slot):
        return rcopy(
            self.bufs.at[2], self.line.at[slot], self.ss.at[3 + j], self.rs.at[3 + slot], self.p.z(j)
        )

    def finish(self, out):
        for j in range(self.nb):
            pl.when(self.p.b != j)(self._z(j, j).wait_recv)
        total = self.line[0]
        for j in range(1, self.nb):
            total = total + self.line[j]
        out[...] = total

    def drain(self):
        for k in self.steps:
            k.wait_send()
        for j in range(self.nb):
            pl.when(self.p.b != j)(self._z(j, self.p.b).wait_send)


HEAD_DIM = 64
PAIR = 128
MASKED = -1e30
TILE = 512


def dot(a, b, ca, cb):
    return lax.dot_general(a, b, (((ca,), (cb,)), ((), ())), preferred_element_type=jnp.float32)


def left_lanes(shape):
    return lax.broadcasted_iota(jnp.int32, shape, 1) < HEAD_DIM


def one_head(pair, left, first):
    keep = left if first else jnp.logical_not(left)
    return jnp.where(keep, pair, jnp.zeros_like(pair))


def lane_groups(op, a):
    out = a[:, :PAIR]
    for g in range(1, a.shape[1] // PAIR):
        out = op(out, a[:, g * PAIR:(g + 1) * PAIR])
    return out


def attn_fwd_kernel(span, col_ref, row_ref, q_ref, k_ref, v_ref, o_ref, ob_ref, lse_ref, s_ref, m_ref, l_ref, acc_ref):
    rows = q_ref.shape[0]
    left = left_lanes((rows, PAIR))
    m_ref[...] = jnp.full_like(m_ref, MASKED)
    l_ref[...] = jnp.zeros_like(l_ref)
    acc_ref[...] = jnp.zeros_like(acc_ref)
    q = q_ref[...]
    heads = [one_head(q, left, i == 0) for i in range(2)]
    codes = col_ref[...]

    def score(t, _):
        at = pl.multiple_of(t * TILE, TILE)
        k = k_ref[pl.ds(at, TILE), :]
        mask = codes == row_ref[:, pl.ds(at, TILE)]
        for i in range(2):
            s = jnp.where(mask, dot(heads[i], k, 1, 1), MASKED)
            s_ref[i, t] = s
            m_ref[i] = jnp.maximum(m_ref[i], lane_groups(jnp.maximum, s))
        return 0

    lax.fori_loop(span[0], span[1], score, 0)
    tops = [jnp.max(m_ref[i], axis=1, keepdims=True) for i in range(2)]

    def mix(t, _):
        v = v_ref[pl.ds(pl.multiple_of(t * TILE, TILE), TILE), :]
        parts = []
        for i in range(2):
            p = jnp.exp(s_ref[i, t] - tops[i])
            l_ref[i] += lane_groups(jnp.add, p)
            parts.append(dot(p.astype(jnp.bfloat16), v, 1, 0))
        acc_ref[...] += jnp.where(left, parts[0], parts[1])
        return 0

    lax.fori_loop(span[0], span[1], mix, 0)
    sums = [jnp.sum(l_ref[i], axis=1, keepdims=True) for i in range(2)]
    total = jnp.where(left, sums[0], sums[1])
    o = acc_ref[...] / total
    o_ref[...] = o
    ob_ref[...] = o.astype(jnp.bfloat16)
    lse_ref[...] = jnp.where(left, tops[0], tops[1]) + jnp.log(total)


def attention(q, k_all, v_all, codes, own_codes, span):
    rows, width = q.shape
    total = k_all.shape[0]
    pairs = width // PAIR
    own = pl.BlockSpec((rows, PAIR), lambda h, s: (0, h))
    every = pl.BlockSpec((total, PAIR), lambda h, s: (0, h))
    return pl.pallas_call(
        attn_fwd_kernel,
        grid_spec=pltpu.PrefetchScalarGridSpec(
            num_scalar_prefetch=1,
            grid=(pairs,),
            in_specs=[
                pl.BlockSpec((rows, 1), lambda h, s: (0, 0)),
                pl.BlockSpec((1, total), lambda h, s: (0, 0)),
                own, every, every,
            ],
            out_specs=[own, own, own],
            scratch_shapes=[
                pltpu.VMEM((2, total // TILE, rows, TILE), jnp.float32),
                pltpu.VMEM((2, rows, PAIR), jnp.float32),
                pltpu.VMEM((2, rows, PAIR), jnp.float32),
                pltpu.VMEM((rows, PAIR), jnp.float32),
            ],
        ),
        out_shape=[
            jax.ShapeDtypeStruct((rows, width), jnp.float32),
            jax.ShapeDtypeStruct((rows, width), jnp.bfloat16),
            jax.ShapeDtypeStruct((rows, width), jnp.float32),
        ],
        compiler_params=pltpu.CompilerParams(vmem_limit_bytes=48 << 20),
        name="attention",
    )(span, own_codes.reshape(rows, 1), codes.reshape(1, total), q, k_all, v_all)


def stats_kernel(g_ref, o_ref, lse_ref, out_ref, delta_ref):
    rows = g_ref.shape[0]
    left = left_lanes((rows, PAIR))
    t = g_ref[...].astype(jnp.float32) * o_ref[...]
    d0 = jnp.sum(jnp.where(left, t, 0.0), axis=1, keepdims=True)
    d1 = jnp.sum(jnp.where(left, 0.0, t), axis=1, keepdims=True)
    delta_ref[...] = jnp.where(left, d0, d1)
    lane = lax.broadcasted_iota(jnp.int32, (rows, PAIR), 1)
    lse = lse_ref[...]
    packed = jnp.where(lane == 0, lse[:, :1], jnp.where(lane == 1, lse[:, HEAD_DIM:HEAD_DIM + 1], jnp.where(lane == 2, d0, d1)))
    out_ref[0] = packed.T[:8]


def row_stats(grad, o, lse):
    rows, width = grad.shape
    pairs = width // PAIR
    own = pl.BlockSpec((rows, PAIR), lambda h: (0, h))
    return pl.pallas_call(
        stats_kernel,
        grid=(pairs,),
        in_specs=[own, own, own],
        out_specs=[pl.BlockSpec((1, 8, rows), lambda h: (h, 0, 0)), own],
        out_shape=[
            jax.ShapeDtypeStruct((pairs, 8, rows), jnp.float32),
            jax.ShapeDtypeStruct((rows, width), jnp.float32),
        ],
        name="row_stats",
    )(grad, o, lse)


def attn_bwd_kernel(span, col_ref, row_ref, q_ref, k_ref, v_ref, g_ref, lse_ref, delta_ref,
                    qa_ref, ka_ref, va_ref, ga_ref, st_ref, dq_ref, dk_ref, dv_ref):
    rows = q_ref.shape[0]
    left = left_lanes((rows, PAIR))
    dq_ref[...] = jnp.zeros_like(dq_ref)
    dk_ref[...] = jnp.zeros_like(dk_ref)
    dv_ref[...] = jnp.zeros_like(dv_ref)
    codes = col_ref[...]
    qs = [one_head(q_ref[...], left, i == 0) for i in range(2)]
    ks = [one_head(k_ref[...], left, i == 0) for i in range(2)]
    vs = [one_head(v_ref[...], left, i == 0) for i in range(2)]
    gs = [one_head(g_ref[...], left, i == 0) for i in range(2)]
    lses = [lse_ref[:, i * HEAD_DIM:i * HEAD_DIM + 1] for i in range(2)]
    deltas = [delta_ref[:, i * HEAD_DIM:i * HEAD_DIM + 1] for i in range(2)]

    def step(t, _):
        at = pl.multiple_of(t * TILE, TILE)
        tile = pl.ds(at, TILE)
        mask = codes == row_ref[:, tile]
        k, v, q, g = ka_ref[tile, :], va_ref[tile, :], qa_ref[tile, :], ga_ref[tile, :]
        dqs, dks, dvs = [], [], []
        for i in range(2):
            s = jnp.where(mask, dot(qs[i], k, 1, 1), MASKED)
            p = jnp.exp(s - lses[i])
            dp = dot(gs[i], v, 1, 1)
            ds = (p * (dp - deltas[i])).astype(jnp.bfloat16)
            dqs.append(dot(ds, k, 1, 0))
            st = jnp.where(mask, dot(ks[i], q, 1, 1), MASKED)
            pt = jnp.exp(st - st_ref[0, i:i + 1, tile])
            dvs.append(dot(pt.astype(jnp.bfloat16), g, 1, 0))
            dpt = dot(vs[i], g, 1, 1)
            dst = (pt * (dpt - st_ref[0, 2 + i:3 + i, tile])).astype(jnp.bfloat16)
            dks.append(dot(dst, q, 1, 0))
        dq_ref[...] += jnp.where(left, dqs[0], dqs[1])
        dk_ref[...] += jnp.where(left, dks[0], dks[1])
        dv_ref[...] += jnp.where(left, dvs[0], dvs[1])
        return 0

    lax.fori_loop(span[0], span[1], step, 0)


def attention_grad(q, k, v, g, lse, delta, q_all, k_all, v_all, g_all, stats, codes, own_codes, span):
    rows, width = q.shape
    total = k_all.shape[0]
    pairs = width // PAIR
    own = pl.BlockSpec((rows, PAIR), lambda h, s: (0, h))
    every = pl.BlockSpec((total, PAIR), lambda h, s: (0, h))
    return pl.pallas_call(
        attn_bwd_kernel,
        grid_spec=pltpu.PrefetchScalarGridSpec(
            num_scalar_prefetch=1,
            grid=(pairs,),
            in_specs=[
                pl.BlockSpec((rows, 1), lambda h, s: (0, 0)),
                pl.BlockSpec((1, total), lambda h, s: (0, 0)),
                own, own, own, own, own, own, every, every, every, every,
                pl.BlockSpec((1, 8, total), lambda h, s: (h, 0, 0)),
            ],
            out_specs=[own, own, own],
        ),
        out_shape=[
            jax.ShapeDtypeStruct((rows, width), jnp.float32),
            jax.ShapeDtypeStruct((rows, width), jnp.float32),
            jax.ShapeDtypeStruct((rows, width), jnp.float32),
        ],
        compiler_params=pltpu.CompilerParams(vmem_limit_bytes=48 << 20),
        name="attention_grad",
    )(span, own_codes.reshape(rows, 1), codes.reshape(1, total), q, k, v, g, lse, delta, q_all, k_all, v_all, g_all, stats)


VEC_ROWS = 8


def forward_kernel(nb, *refs):
    x_ref, seg, live = refs[:3]
    shards_in = refs[3:9]
    vecs_in = refs[9:18]
    wq_o, wk_o, wv_o, wo_o, wup_o, wdn_o = refs[18:24]
    q_o, k_o, v_o = refs[24:27]
    o_ref, ob_ref, lse_ref, vec_ref, bup_ref = refs[27:32]
    rest = refs[32:]
    x_all, wq, wk, wv, pack, packs, q, k, v, m_ref, l_ref, codes, rows = rest[:13]
    zs, zr, gs, gr, gl, ws, es = rest[13:]
    n, width = x_ref.shape
    pairs = width // PAIR
    p = Place()
    own = pltpu.make_async_copy(x_ref, x_all.at[p.b], ws.at[3])
    own.start()
    pack[...] = jnp.zeros_like(pack)
    for i in range(VEC_ROWS):
        pack[i:i + 1, :vecs_in[i].shape[1]] = vecs_in[i][...].astype(jnp.float32)
    for i in range(vecs_in[8].shape[1] // PAIR):
        pack[VEC_ROWS + i:VEC_ROWS + i + 1, :] = vecs_in[8][:, i * PAIR:(i + 1) * PAIR].astype(jnp.float32)
    enter(p, nb, True, "near")
    line = LineGather(p, nb, x_ref, x_all, zs, zr)
    targets = (packs, wq, wk, wv, wo_o, wup_o, wdn_o)
    sources = (pack,) + tuple(shards_in)
    g = [PlaneGather(p, sources[i], targets[i], gs.at[i], gr.at[i], gl.at[i]) for i in range(7)]
    line.start(0)
    for c in g[:5]:
        c.start()
    code_tables(seg, live, rows, codes, p.b)
    for c in g[:4]:
        c.forward()
    g[5].start()
    g[6].start()
    line.wait_recv(0)
    line.start(1)
    for c in g[:4]:
        c.diag()
    for c in g[:4]:
        c.finish()
    own.wait()
    keep = [
        pltpu.make_async_copy(a, b, ws.at[i]) for i, (a, b) in enumerate(((wq, wq_o), (wk, wk_o), (wv, wv_o)))
    ]
    for c in keep:
        c.start()

    piece = width // 8
    r = lax.broadcasted_iota(jnp.int32, (PAIR, width), 0)
    c = lax.broadcasted_iota(jnp.int32, (PAIR, width), 1)
    total = jnp.zeros((2 * VEC_ROWS, width), jnp.float32)
    for i in range(8):
        pick = ((c == r + i * piece) & (r < piece)).astype(jnp.bfloat16)
        total += dot(packs[2 * VEC_ROWS * i:2 * VEC_ROWS * (i + 1), :].astype(jnp.bfloat16), pick, 1, 0)
    vec_ref[...] = total[:VEC_ROWS]
    up_piece = bup_ref.shape[1] // 8
    for i in range(8):
        for t in range(up_piece // PAIR):
            at = i * up_piece + t * PAIR
            row = 2 * VEC_ROWS * i + VEC_ROWS + t
            bup_ref[:, at:at + PAIR] = packs[row:row + 1, :]

    scale = HEAD_DIM ** (-0.5)
    step = 256

    def outs(j, e):
        return [
            pltpu.make_async_copy(a.at[j], b.at[j], es.at[i, e])
            for i, (a, b) in enumerate(((q, q_o), (k, k_o), (v, v_o)))
        ]

    def project(j):
        def columns(t, _):
            at = pl.ds(pl.multiple_of(t * step, step), step)
            xs = x_all[j]
            q[j, :, at] = ((dot(xs, wq[:, at], 1, 0) + vec_ref[0:1, at]) * scale).astype(jnp.bfloat16)
            k[j, :, at] = dot(xs, wk[:, at], 1, 0).astype(jnp.bfloat16)
            v[j, :, at] = (dot(xs, wv[:, at], 1, 0) + vec_ref[1:2, at]).astype(jnp.bfloat16)
            return 0
        lax.fori_loop(0, width // step, columns, 0, unroll=True)

    def attend(j):
        def pair(h, _):
            left = left_lanes((n, PAIR))
            lanes = pl.ds(pl.multiple_of(h * PAIR, PAIR), PAIR)
            mask = codes[...] == rows[j]
            qs, ks, vs = q[p.b, :, lanes], k[j, :, lanes], v[j, :, lanes]
            parts, alphas = [], []
            for i in range(2):
                s = jnp.where(mask, dot(one_head(qs, left, i == 0), ks, 1, 1), MASKED)
                top = jnp.max(lane_groups(jnp.maximum, s), axis=1, keepdims=True)
                old = m_ref[2 * h + i]
                new = jnp.maximum(old, top)
                alpha = jnp.exp(old - new)
                e = jnp.exp(s - jnp.concatenate([new] * (n // PAIR), axis=1))
                m_ref[2 * h + i] = new
                l_ref[2 * h + i] = l_ref[2 * h + i] * alpha + lane_groups(jnp.add, e)
                alphas.append(alpha)
                parts.append(dot(e.astype(jnp.bfloat16), vs, 1, 0))
            got = jnp.where(left, parts[0], parts[1])
            o_ref[:, lanes] = o_ref[:, lanes] * jnp.where(left, alphas[0], alphas[1]) + got
            return 0
        lax.fori_loop(0, pairs, pair, 0, unroll=2)

    def block(i):
        ok, j = turn(p.b, nb, i)

        @pl.when(ok)
        def _():
            project(j)
            for c in outs(j, i):
                c.start()
            attend(j)

    def hop(t, last=False):
        line.wait_recv(t)
        if not last:
            line.start(t + 1)

    m_ref[...] = jnp.full_like(m_ref, MASKED)
    l_ref[...] = jnp.zeros_like(l_ref)
    o_ref[...] = jnp.zeros_like(o_ref)
    staged(
        2 * nb - 1,
        {
            1: [g[4].forward, g[5].forward],
            2: [lambda: hop(1)],
            3: [g[6].forward, g[4].diag],
            5: [g[5].diag, g[6].diag, lambda: hop(2, True)],
        },
        block,
    )

    def close(h, _):
        left = left_lanes((n, PAIR))
        lanes = pl.ds(pl.multiple_of(h * PAIR, PAIR), PAIR)
        sums = [jnp.sum(l_ref[2 * h + i], axis=1, keepdims=True) for i in range(2)]
        mass = jnp.where(left, sums[0], sums[1])
        out = o_ref[:, lanes] / mass
        o_ref[:, lanes] = out
        ob_ref[:, lanes] = out.astype(jnp.bfloat16)
        lse_ref[:, lanes] = jnp.where(left, m_ref[2 * h], m_ref[2 * h + 1]) + jnp.log(mass)
        return 0
    lax.fori_loop(0, pairs, close, 0)
    for c in g[4:]:
        c.finish()
    for c in keep:
        c.wait()
    for i in range(2 * nb - 1):
        ok, j = turn(p.b, nb, i)

        @pl.when(ok)
        def _():
            for c in outs(j, i):
                c.wait()
    for t in range(nb - 1):
        line.wait_send(t)
    for c in g:
        c.drain()


def forward(x, seg, live, weights, vecs, nb):
    n, width = x.shape
    hidden = weights[4].shape[1]
    bf, f32 = jnp.bfloat16, jnp.float32
    every = jax.ShapeDtypeStruct((nb, n, width), bf)
    block = jax.ShapeDtypeStruct((n, width), f32)
    mats = [jax.ShapeDtypeStruct((8 * w.shape[0], w.shape[1]), w.dtype) for w in weights]
    dma = pltpu.SemaphoreType.DMA
    return pl.pallas_call(
        functools.partial(forward_kernel, nb),
        out_shape=(
            *mats, every, every, every, block, jax.ShapeDtypeStruct((n, width), bf), block,
            jax.ShapeDtypeStruct((VEC_ROWS, width), f32), jax.ShapeDtypeStruct((1, hidden), f32),
        ),
        in_specs=[VM] * 18,
        out_specs=(ANY,) * 9 + (VM,) * 5,
        scratch_shapes=[
            pltpu.VMEM((nb, n, width), bf),
            pltpu.VMEM((width, width), bf), pltpu.VMEM((width, width), bf), pltpu.VMEM((width, width), bf),
            pltpu.VMEM((2 * VEC_ROWS, PAIR), f32), pltpu.VMEM((16 * VEC_ROWS, PAIR), f32),
            pltpu.VMEM((nb, n, width), bf), pltpu.VMEM((nb, n, width), bf), pltpu.VMEM((nb, n, width), bf),
            pltpu.VMEM((width // HEAD_DIM, n, PAIR), f32), pltpu.VMEM((width // HEAD_DIM, n, PAIR), f32),
            pltpu.VMEM((n, 1), f32), pltpu.VMEM((nb, 1, n), f32),
            dma((2, nb - 1)), dma((2, nb - 1)), dma((7, 9)), dma((7, 9)), dma((7,)), dma((4,)), dma((3, 2 * nb)),
        ],
        compiler_params=pltpu.CompilerParams(
            collective_id=1, has_side_effects=True, vmem_limit_bytes=60 << 20
        ),
        name="forward",
    )(
        x, seg, live, *weights, *[v.reshape(1, -1) for v in vecs]
    )


ROOT_HALF = 0.7071067811865476
ROOT_TWO_PI = 0.3989422804014327
CHUNK = 768
PART = 256


def erf_parts(x):
    x = jnp.clip(x, -3.832506856900711, 3.832506856900711)
    y = x * x
    top = jnp.full_like(y, 0.00022905065861350646)
    for a in (0.0034082910107109506, 0.050955695062380861, 0.18520832239976145, 1.128379143519084):
        top = top * y + a
    low = jnp.full_like(y, -1.1791602954361697e-7)
    for a in (
        0.000023547966471313185, 0.0010179625278914885, 0.014070470171167667,
        0.11098505178285362, 0.49746925110067538, 1.0,
    ):
        low = low * y + a
    return x * top / low


def middle_kernel(
    att_ref, x_ref, cot_ref, o_ref, lse_ref, vec_ref, bup_ref, wo_hbm, wup_hbm, wdn_hbm,
    out_ref, rest_ref, do_ref, stats_ref, delta_ref, table_ref, gdn_hbm, gup_hbm, gwo_ref,
    wo, wup, wdn, u_ref, slope_ref, y_ref, dh_ref, low_ref, gdn, gup, sems, osems,
):
    n, width = x_ref.shape
    hidden = wup.shape[1]
    chunks = hidden // CHUNK
    f32, bf = jnp.float32, jnp.bfloat16
    loads = [
        pltpu.make_async_copy(a, b, sems.at[i])
        for i, (a, b) in enumerate(((wo_hbm, wo), (wup_hbm, wup), (wdn_hbm, wdn)))
    ]
    for c in loads:
        c.start()
    table_ref[...] = jnp.zeros_like(table_ref)

    def vec(i):
        return vec_ref[i:i + 1, :]

    def mean(a):
        return jnp.sum(a, axis=1, keepdims=True) * (1.0 / width)

    def centred(h):
        c = h - mean(h)
        inv = lax.rsqrt(mean(c * c) + EPSILON)
        return c * inv, inv

    def pull(grad, hat, inv, gain):
        d = grad * gain
        return inv * (d - mean(d) - hat * mean(d * hat))

    def column_sum(a):
        return jnp.sum(a, axis=0, keepdims=True)

    blocks = 2
    m = n // blocks

    def rows_of(i):
        return pl.ds(pl.multiple_of(i * m, m), m)

    loads[0].wait()

    def first(i, _):
        r = rows_of(i)
        h = x_ref[r, :].astype(f32) + dot(att_ref[r, :], wo[...], 1, 0) + vec(2)
        hat, _ = centred(h)
        y = hat * vec(3) + vec(4)
        rest_ref[r, :] = h
        dh_ref[r, :] = y + vec(5)
        low_ref[r, :] = y.astype(bf)
        return 0
    lax.fori_loop(0, blocks, first, 0)
    for c in loads[1:]:
        c.wait()

    def up(t, _):
        total = dh_ref[...]
        for s in range(CHUNK // PART):
            at = pl.ds(pl.multiple_of(t * CHUNK + s * PART, PART), PART)
            z = dot(low_ref[...], wup[:, at], 1, 0) + bup_ref[:, at]
            cdf = 0.5 + 0.5 * erf_parts(z * ROOT_HALF)
            low = (z * cdf).astype(bf)
            u_ref[:, at] = low
            slope_ref[:, at] = cdf + z * (jnp.exp(-0.5 * z * z) * ROOT_TWO_PI)
            total = total + dot(low, wdn[at, :], 1, 0)
        dh_ref[...] = total
        return 0
    lax.fori_loop(0, chunks, up, 0, unroll=True)

    def second(i, _):
        r = rows_of(i)
        hat, inv = centred(dh_ref[r, :])
        out_ref[r, :] = (hat * vec(6) + vec(7)).astype(bf)
        g = cot_ref[r, :].astype(f32)
        table_ref[6:7, :] += column_sum(g * hat)
        table_ref[7:8, :] += column_sum(g)
        dh = pull(g, hat, inv, vec(6))
        table_ref[5:6, :] += column_sum(dh)
        dh_ref[r, :] = dh
        y_ref[r, :] = dh.astype(bf)
        return 0
    lax.fori_loop(0, blocks, second, 0)

    def down(t, _):
        at = pl.ds(pl.multiple_of(t * CHUNK, CHUNK), CHUNK)
        parts = []
        total = dh_ref[...]
        for s in range(CHUNK // PART):
            cols = pl.ds(pl.multiple_of(t * CHUNK + s * PART, PART), PART)
            dz = dot(y_ref[...], wdn[cols, :], 1, 1) * slope_ref[:, cols]
            table_ref[pl.ds(8 + t, 1), s * PART:(s + 1) * PART] = column_sum(dz)
            c = dz.astype(bf)
            parts.append(c)
            total = total + dot(c, wup[:, cols], 1, 1)
            gdn[cols, :] = dot(u_ref[:, cols], y_ref[...], 0, 0).astype(bf)
        dh_ref[...] = total
        c = jnp.concatenate(parts, axis=1)
        r = width // 8
        for i in range(2):
            half = width // 2
            g = dot(low_ref[:, i * half:(i + 1) * half], c, 0, 0).astype(bf)
            for k in range(4):
                gup[4 * i + k, t] = g[k * r:(k + 1) * r]
        pltpu.make_async_copy(gdn.at[at], gdn_hbm.at[at], osems.at[0, t]).start()
        pltpu.make_async_copy(gup.at[:, t], gup_hbm.at[:, t], osems.at[1, t]).start()
        return 0
    lax.fori_loop(0, chunks, down, 0, unroll=True)

    def third(i, _):
        r = rows_of(i)
        hat, inv = centred(rest_ref[r, :])
        g = dh_ref[r, :]
        table_ref[3:4, :] += column_sum(g * hat)
        table_ref[4:5, :] += column_sum(g)
        dh = pull(g, hat, inv, vec(3))
        table_ref[2:3, :] += column_sum(dh)
        rest_ref[r, :] = dh
        low = dh.astype(bf)
        low_ref[r, :] = low
        do = dot(low, wo[...], 1, 1).astype(bf)
        do_ref[r, :] = do
        table_ref[1:2, :] += column_sum(do.astype(f32))
        return 0
    lax.fori_loop(0, blocks, third, 0)

    def heads(h, _):
        lanes = pl.ds(pl.multiple_of(h * PAIR, PAIR), PAIR)
        left = left_lanes((n, PAIR))
        t = do_ref[:, lanes].astype(f32) * o_ref[:, lanes]
        d0 = jnp.sum(jnp.where(left, t, 0.0), axis=1, keepdims=True)
        d1 = jnp.sum(jnp.where(left, 0.0, t), axis=1, keepdims=True)
        delta_ref[:, lanes] = jnp.where(left, d0, d1)
        lane = lax.broadcasted_iota(jnp.int32, (n, PAIR), 1)
        lse = lse_ref[:, lanes]
        packed = jnp.where(lane == 0, lse[:, :1], jnp.where(
            lane == 1, lse[:, HEAD_DIM:HEAD_DIM + 1], jnp.where(lane == 2, d0, d1)))
        stats_ref[h] = packed.T[:8]
        gwo_ref[lanes, :] = dot(att_ref[:, lanes], low_ref[...], 0, 0).astype(bf)
        return 0
    lax.fori_loop(0, width // PAIR, heads, 0)
    for t in range(chunks):
        at = pl.ds(t * CHUNK, CHUNK)
        pltpu.make_async_copy(gdn.at[at], gdn_hbm.at[at], osems.at[0, t]).wait()
        pltpu.make_async_copy(gup.at[:, t], gup_hbm.at[:, t], osems.at[1, t]).wait()


def middle(att, x, cot, o, lse, vecs, bup, wo, wup, wdn):
    n, width = x.shape
    hidden = wup.shape[1]
    chunks = hidden // CHUNK
    bf, f32 = jnp.bfloat16, jnp.float32
    S = jax.ShapeDtypeStruct
    dma = pltpu.SemaphoreType.DMA
    return pl.pallas_call(
        middle_kernel,
        out_shape=(
            S((n, width), bf), S((n, width), f32), S((n, width), bf), S((width // PAIR, 8, n), f32),
            S((n, width), f32), S((16, width), f32), S((hidden, width), bf),
            S((8, chunks, width // 8, CHUNK), bf), S((width, width), bf),
        ),
        in_specs=[VM] * 7 + [ANY] * 3,
        out_specs=(VM,) * 6 + (ANY, ANY, VM),
        scratch_shapes=[
            pltpu.VMEM((width, width), bf), pltpu.VMEM((width, hidden), bf), pltpu.VMEM((hidden, width), bf),
            pltpu.VMEM((n, hidden), bf), pltpu.VMEM((n, hidden), f32), pltpu.VMEM((n, width), bf),
            pltpu.VMEM((n, width), f32), pltpu.VMEM((n, width), bf),
            pltpu.VMEM((hidden, width), bf), pltpu.VMEM((8, chunks, width // 8, CHUNK), bf),
            dma((3,)), dma((2, chunks)),
        ],
        compiler_params=pltpu.CompilerParams(vmem_limit_bytes=60 << 20),
        name="middle",
    )(att, x, cot, o, lse, vecs, bup, wo, wup, wdn)


PAIR_GROUP = 2


class AttentionGrad:
    def __init__(self, codes, rows, q, k, v, g, lse, delta, stats, own, dq, dk, dv):
        self.codes, self.rows = codes, rows
        self.q, self.k, self.v, self.g = q, k, v, g
        self.lse, self.delta, self.stats = lse, delta, stats
        self.own = own
        self.dq, self.dk, self.dv = dq, dk, dv
        self.n = dq.shape[0]
        self.pairs = dq.shape[1] // PAIR

    def queries(self, j, group):
        own = self.own

        def pair(h):
            left = left_lanes((self.n, PAIR))
            lanes = pl.ds(pl.multiple_of(h * PAIR, PAIR), PAIR)
            mask = self.codes[...] == self.rows[j]
            q, g = self.q[own, :, lanes], self.g[own, :, lanes]
            k, v = self.k[j, :, lanes], self.v[j, :, lanes]
            lse, delta = self.lse[:, lanes], self.delta[:, lanes]
            parts = []
            for i in range(2):
                at = slice(i * HEAD_DIM, i * HEAD_DIM + 1)
                s = jnp.where(mask, dot(one_head(q, left, i == 0), k, 1, 1), MASKED)
                p = jnp.exp(s - lse[:, at])
                dp = dot(one_head(g, left, i == 0), v, 1, 1)
                ds = (p * (dp - delta[:, at])).astype(jnp.bfloat16)
                parts.append(dot(ds, k, 1, 0))
            self.dq[:, lanes] += jnp.where(left, parts[0], parts[1])

        for i in range(PAIR_GROUP):
            pair(group * PAIR_GROUP + i)

    def keys(self, j, group):
        own = self.own

        def pair(h):
            left = left_lanes((self.n, PAIR))
            lanes = pl.ds(pl.multiple_of(h * PAIR, PAIR), PAIR)
            mask = self.codes[...] == self.rows[j]
            k, v = self.k[own, :, lanes], self.v[own, :, lanes]
            q, g = self.q[j, :, lanes], self.g[j, :, lanes]
            dks, dvs = [], []
            for i in range(2):
                st = jnp.where(mask, dot(one_head(k, left, i == 0), q, 1, 1), MASKED)
                pt = jnp.exp(st - self.stats[j, h, i:i + 1])
                dvs.append(dot(pt.astype(jnp.bfloat16), g, 1, 0))
                dpt = dot(one_head(v, left, i == 0), g, 1, 1)
                dst = (pt * (dpt - self.stats[j, h, 2 + i:3 + i])).astype(jnp.bfloat16)
                dks.append(dot(dst, q, 1, 0))
            self.dk[:, lanes] += jnp.where(left, dks[0], dks[1])
            self.dv[:, lanes] += jnp.where(left, dvs[0], dvs[1])

        for i in range(PAIR_GROUP):
            pair(group * PAIR_GROUP + i)


TABLE = 16


def backward_kernel(nb, *refs):
    seg, live, g_own, st_own, lse, delta, x_hbm, rest_hbm, table = refs[:9]
    q_hbm, k_hbm, v_hbm, wq_hbm, wk_hbm, wv_hbm = refs[9:15]
    early = refs[15:18]
    token_ref, table_out = refs[18:20]
    outs = refs[20:24]
    rest = refs[24:]
    q, k, v, g, stats, dq, dk, dv, wq, wk, wv, gw, stage_dn, stage_up, tab, tsum, tline, x_ref, rest_ref, codes, rows = rest[:21]
    zbufs = rest[21:25]
    bufs = rest[25:25 + 4 * PLANE_BUFS]
    zs, zr, ls, ps, pr, ds, dr, rls, ts, tr = rest[25 + 4 * PLANE_BUFS:]
    n, width = g_own.shape
    p = Place()
    loads = [
        pltpu.make_async_copy(a, b, ls.at[i])
        for i, (a, b) in enumerate((
            (k_hbm, k), (v_hbm, v), (q_hbm, q), (g_own, g.at[p.b]), (st_own, stats.at[p.b]),
            (wq_hbm, wq), (wk_hbm, wk), (wv_hbm, wv), (x_hbm, x_ref), (rest_hbm, rest_ref),
            (early[2], gw.at[0, :, :, :, pl.ds(gw.shape[4] // 2, gw.shape[4] // 2)]),
        ))
    ]
    for c in loads:
        c.start()
    enter(p, nb, True, "all")
    lines = [
        LineGather(p, nb, g_own, g, zs.at[0], zr.at[0]),
        LineGather(p, nb, st_own, stats, zs.at[1], zr.at[1]),
    ]
    sources = (early[0], early[1], gw.at[0], gw.at[1])
    stages = (stage_dn, stage_up, None, None)
    planes = [
        PlaneSum(
            p, sources[i], bufs[PLANE_BUFS * i:PLANE_BUFS * (i + 1)], stages[i], ps.at[i], pr.at[i], rls.at[min(i, 1)]
        )
        for i in range(4)
    ]
    dn, up, qo, kv = planes
    chains = [
        (DirectSum if i == 3 else ChainSum)(p, nb, planes[i].total, outs[i], zbufs[i], ds.at[i], dr.at[i])
        for i in range(4)
    ]
    ldn, lup, lqo, lkv = chains
    vec = TableSum(p, nb, tab, tsum, tline, ts, tr)
    for c in lines:
        c.start(0)
    for c in (dn, up):
        c.a_start()
        c.own_start()
    work = AttentionGrad(codes, rows, q, k, v, g, lse, delta, stats, p.b, dq, dk, dv)
    code_tables(seg, live, rows, codes, p.b)
    for c in (dq, dk, dv):
        c[...] = jnp.zeros_like(c)
    for c in loads[:4]:
        c.wait()
    dn.b_start()

    low = k
    def slot(i):
        return (p.b + 1 + i) % nb

    def settle(i, src, scale, row):
        value = src[...] if scale is None else src[...] * scale
        if row is not None:
            tab[row:row + 1, :] = jnp.sum(value, axis=0, keepdims=True)
        low[slot(i)] = value.astype(jnp.bfloat16)

    def weight_grad(i, item, base):
        half = width // 2
        r = width // 8
        for m in range(2):
            part = dot(x_ref[:, m * half:(m + 1) * half], low[slot(i)], 0, 0).astype(jnp.bfloat16)
            for a in range(2):
                for b in range(2):
                    at = (2 * a + b) * r
                    gw[item, m, a, b, base:base + r] = part[at:at + r]

    def hop(t, last=False):
        for c in lines:
            c.wait_recv(t)
            if not last:
                c.start(t + 1)

    groups = work.pairs // PAIR_GROUP
    staged(
        nb * groups,
        {
            2: [up.b_start],
            5: [lambda: hop(0)],
            6: [dn.c_start],
        },
        lambda i: work.queries((p.b + i // groups) % nb, i % groups),
    )
    for c in loads[4:]:
        c.wait()
    tab[...] = table[...]
    settle(0, dq, HEAD_DIM ** (-0.5), 0)
    vec.start()
    weight_grad(0, 0, 0)
    qo.a_start()
    hop(1)
    up.c_start()

    def keys(i):
        ok, j = turn(p.b, nb, i // groups)
        pl.when(ok)(lambda: work.keys(j, i % groups))

    def across(a, c):
        a.end()
        c.start()

    staged(
        (2 * nb - 1) * groups,
        {
            2: [lambda: across(dn, ldn), qo.b_start],
            5: [lambda: across(up, lup)],
            6: [lambda: ldn.hop(1)],
            8: [qo.c_start],
            9: [lambda: lup.hop(1), lambda: ldn.hop(2)],
            12: [lambda: across(qo, lqo), lambda: lup.hop(2), lambda: ldn.spread(0)],
            15: [lambda: hop(2, True), lambda: lqo.hop(1), lambda: lup.spread(0), lambda: ldn.spread(1)],
            18: [lambda: lqo.hop(2), lambda: lup.spread(1), lambda: ldn.spread(2)],
        },
        keys,
    )
    settle(1, dk, None, None)
    weight_grad(1, 1, 0)
    settle(2, dv, None, None)
    weight_grad(2, 1, width // 8)
    kv.a_start()
    vec.step(0)
    kv.b_start()

    part = 256

    def columns(t, _):
        at = pl.ds(pl.multiple_of(t * part, part), part)
        total = rest_ref[:, at]
        for i, w in enumerate((wq, wk, wv)):
            total = total + dot(low[slot(i)], w[at, :], 1, 1)
        token_ref[:, at] = total.astype(jnp.bfloat16)
        return 0
    lax.fori_loop(0, width // part, columns, 0)

    lqo.spread(0)
    lup.spread(2)
    vec.step(1)
    kv.c_start()
    lqo.spread(1)
    vec.step(2)
    across(kv, lkv)
    lqo.spread(2)
    lkv.share()
    vec.finish(table_out)
    for c in chains:
        c.finish()
    for t in range(nb - 1):
        for c in lines:
            c.wait_send(t)
    for c in planes:
        c.drain()
    for c in chains:
        c.drain()
    vec.drain()


def backward(seg, live, do, stats, lse, delta, x, rest, table, q_all, k_all, v_all, weights, early, nb):
    n, width = do.shape
    bf, f32 = jnp.bfloat16, jnp.float32
    pair = (2, 2, 2, width // 4, width)
    sources = [early[0].shape, early[1].shape, pair, pair]
    sums = [s[-2:] for s in sources]
    scratch = []
    for s in sources:
        scratch += plane_scratch(s[-2:])
    ns = line_sems(nb)
    every = pltpu.VMEM((nb, n, width), bf)
    total = pltpu.VMEM((n, width), f32)
    square = pltpu.VMEM((width, width), bf)
    dma = pltpu.SemaphoreType.DMA
    return pl.pallas_call(
        functools.partial(backward_kernel, nb),
        out_shape=(
            jax.ShapeDtypeStruct((n, width), bf), jax.ShapeDtypeStruct((TABLE, width), f32),
            *[jax.ShapeDtypeStruct(s, bf) for s in sums],
        ),
        in_specs=[VM] * 6 + [ANY] * 2 + [VM] + [ANY] * 9,
        out_specs=(VM,) * 6,
        scratch_shapes=[
            every, every, every, every, pltpu.VMEM((nb,) + stats.shape, f32), total, total, total,
            square, square, square, pltpu.VMEM((2,) + pair, bf),
            *[pltpu.VMEM(s[:2] + s[3:], bf) for s in sources[:2]],
            pltpu.VMEM((TABLE, width), f32), pltpu.VMEM((6, TABLE, width), f32), pltpu.VMEM((nb, TABLE, width), f32),
            pltpu.VMEM((n, width), bf), total, pltpu.VMEM((n, 1), f32), pltpu.VMEM((nb, 1, n), f32),
            *[line_scratch(s, nb) for s in sums], *scratch,
            dma((2, 2, nb - 1)), dma((2, 2, nb - 1)), dma((12,)), dma((4, PLANE_SEMS)), dma((4, PLANE_SEMS)),
            dma((4, ns)), dma((4, ns)), dma((2,)), dma((3 + nb,)), dma((3 + nb,)),
        ],
        compiler_params=pltpu.CompilerParams(
            collective_id=4, has_side_effects=True, vmem_limit_bytes=63 << 20
        ),
        name="backward",
    )(
        seg, live, do, stats, lse, delta, x, rest, table,
        q_all, k_all, v_all, *weights, *early,
    )


def finish_kernel(dn, up, qo, kv, table, token, *outs):
    f32 = jnp.float32
    outs[15][...] = token[...]
    n = outs[0].shape[0]
    for i, (a, at) in enumerate(((qo, 0), (kv, 0), (kv, n), (qo, n))):
        outs[i][...] = a[at:at + n, :].astype(f32)
    outs[4][...] = dn[...].astype(f32)
    rows = outs[5].shape[0]
    width = up.shape[1]
    for t in range(outs[5].shape[1] // width):
        outs[5][:, t * width:(t + 1) * width] = up[t * rows:(t + 1) * rows, :].astype(f32)
    shard = lax.axis_index("seq") * 4 + lax.axis_index("shard")
    piece = outs[6].shape[1]
    r = lax.broadcasted_iota(jnp.int32, (width, PAIR), 0)
    c = lax.broadcasted_iota(jnp.int32, (width, PAIR), 1)
    pick = ((r == c + shard * piece) & (c < piece)).astype(f32)
    small = lax.dot_general(
        table[:8, :], pick, (((1,), (0,)), ((), ())), precision=lax.Precision.HIGHEST,
        preferred_element_type=f32,
    )
    for i in range(8):
        outs[6 + i][...] = small[i:i + 1, :piece]
    wide = outs[14].shape[1]
    per = width // wide
    at = pl.multiple_of((shard % per) * wide, wide)
    outs[14][...] = table[pl.ds(8 + shard // per, 1), pl.ds(at, wide)]


def finish(dn, up, qo, kv, table, token, wide):
    width = table.shape[1]
    f32 = jnp.float32
    S = jax.ShapeDtypeStruct
    piece = width // 8
    chunks = up.shape[0] // piece
    out = pl.pallas_call(
        finish_kernel,
        out_shape=(
            *[S((piece, width), f32)] * 4, S(dn.shape, f32), S((piece, chunks * width), f32),
            *[S((1, piece), f32)] * 8, S((1, wide), f32), S(token.shape, token.dtype),
        ),
        in_specs=[VM] * 6,
        out_specs=(VM,) * 16,
        compiler_params=pltpu.CompilerParams(vmem_limit_bytes=60 << 20),
        name="finish",
    )(dn, up, qo, kv, table, token)
    return out[15], list(out[:6]) + [a.reshape(-1) for a in out[6:15]]


EPSILON = 1e-06
PLANE = ("seq", "shard")


def normalize(hidden, gain, shift):
    center = hidden - jnp.mean(hidden, axis=-1, keepdims=True)
    spread = jnp.mean(center * center, axis=-1, keepdims=True)
    return center * lax.rsqrt(spread + EPSILON) * gain + shift


def smooth_gate(hidden):
    return jax.nn.gelu(hidden, approximate=False)


def mm(left, right):
    return jnp.dot(left, right, preferred_element_type=jnp.float32)


def contract_rows(left, right):
    return dot(left, right, 0, 0)


def times_transpose(left, right):
    return dot(left, right, 1, 1)


def tuned_plane():
    return lax.axis_size("seq") == 2 and lax.axis_size("shard") == 4 and lax.axis_size("blk") == 4


def total(g):
    part = lax.psum_scatter(g.astype(jnp.bfloat16), PLANE, scatter_dimension=0, tiled=True)
    return lax.psum(part, "blk").astype(jnp.float32)


def whole_line(
    inputs, seg, live, mats, vecs, cotangent, codes, own_codes, start,
):
    rows, width = inputs.shape
    length = seg.shape[0]
    scale = HEAD_DIM ** (-0.5)
    xs = lax.all_gather(inputs, "blk", axis=0, tiled=True)
    wq, wk, wv, wo, wup, wdn = [lax.all_gather(w, PLANE, axis=0, tiled=True) for w in mats]
    whole = [lax.all_gather(v, PLANE, axis=0, tiled=True).astype(jnp.float32) for v in vecs]
    bq, bv, bo, g1, s1, bdn, g2, s2, bup = whole
    own_seg = lax.dynamic_slice_in_dim(seg, start, rows)
    low = jnp.sum((seg < own_seg[0]).astype(jnp.int32))
    high = jnp.sum((seg <= own_seg[rows - 1]).astype(jnp.int32))
    span = jnp.stack([low // TILE, (high + TILE - 1) // TILE])
    q_all = ((mm(xs, wq) + bq) * scale).astype(jnp.bfloat16)
    k_all = mm(xs, wk).astype(jnp.bfloat16)
    v_all = (mm(xs, wv) + bv).astype(jnp.bfloat16)
    q, k, v = [lax.dynamic_slice_in_dim(a, start, rows) for a in (q_all, k_all, v_all)]
    summed, attended, lse = attention(q, k_all, v_all, codes, own_codes, span)

    first_sum = inputs.astype(jnp.float32) + (mm(attended, wo) + bo)
    first_norm, first_pull = jax.vjp(normalize, first_sum, g1, s1)
    first_low = first_norm.astype(jnp.bfloat16)
    hidden = mm(first_low, wup) + bup
    gated, gate_pull = jax.vjp(smooth_gate, hidden)
    gated_low = gated.astype(jnp.bfloat16)
    second_sum = first_norm + (mm(gated_low, wdn) + bdn)
    result, second_pull = jax.vjp(normalize, second_sum, g2, s2)
    second_grad, g2_grad, s2_grad = second_pull(cotangent.astype(jnp.float32))
    bdn_grad = jnp.sum(second_grad, axis=0)
    second_low = second_grad.astype(jnp.bfloat16)
    wdn_grad = contract_rows(gated_low, second_low)
    (hidden_grad,) = gate_pull(times_transpose(second_low, wdn))
    bup_grad = jnp.sum(hidden_grad, axis=0)
    hidden_low = hidden_grad.astype(jnp.bfloat16)
    wup_grad = contract_rows(first_low, hidden_low)
    norm_grad = second_grad + times_transpose(hidden_low, wup)
    first_grad, g1_grad, s1_grad = first_pull(norm_grad)
    bo_grad = jnp.sum(first_grad, axis=0)
    first_grad_low = first_grad.astype(jnp.bfloat16)
    wo_grad = contract_rows(attended, first_grad_low)
    do = times_transpose(first_grad_low, wo).astype(jnp.bfloat16)

    stats, delta = row_stats(do, summed, lse)
    do_all, stats_all = [lax.all_gather(a, "blk", axis=0) for a in (do, stats)]
    stats_all = jnp.transpose(stats_all, (1, 2, 0, 3)).reshape(stats.shape[0], 8, length)
    dq, dk, dv = attention_grad(
        q, k, v, do, lse, delta, q_all, k_all, v_all, do_all.reshape(length, width), stats_all,
        codes, own_codes, span,
    )
    r = dq * scale
    rq, rk, rv = [a.astype(jnp.bfloat16) for a in (r, dk, dv)]
    token_grad = first_grad + times_transpose(rq, wq) + times_transpose(rk, wk) + times_transpose(rv, wv)
    grads = [contract_rows(inputs, a) for a in (rq, rk, rv)] + [wo_grad, wdn_grad, wup_grad]
    vectors = [
        jnp.sum(r, axis=0), jnp.sum(dv, axis=0), bo_grad, g1_grad, s1_grad, bdn_grad, g2_grad, s2_grad, bup_grad,
    ]
    return result.astype(jnp.bfloat16), token_grad.astype(jnp.bfloat16), [total(g) for g in grads + vectors]


def tuned_line(inputs, mats, vecs, cotangent, seg, live, nb):
    out = forward(inputs, seg, live, mats, vecs, nb)
    wq, wk, wv, wo, wup, wdn, q_all, k_all, v_all, summed, attended, lse, table, bup = out
    out = middle(attended, inputs, cotangent, summed, lse, table, bup, wo, wup, wdn)
    result, rest, do, stats, delta, table, gdn, gup, gwo = out
    width = inputs.shape[1]
    early = [g.reshape(2, 2, 2, -1, width) for g in (gdn, gup, gwo)]
    token_grad, table, rdn, rup, rqo, rkv = backward(
        seg, live, do, stats, lse, delta, inputs, rest, table, q_all, k_all, v_all, [wq, wk, wv], early, nb,
    )
    token_grad, sums = finish(rdn, rup, rqo, rkv, table, token_grad, vecs[8].shape[0])
    return result, token_grad, sums


def per_device(
    tokens, segments, live_mask, query_weight, key_weight, value_weight, out_weight,
    query_bias, value_bias, out_bias, first_gain, first_shift, up_weight, up_bias,
    down_weight, down_bias, second_gain, second_shift, cotangent,
):
    inputs = tokens[0]
    rows = inputs.shape[0]
    nb = lax.axis_size("blk")
    seg, live = segments[0], live_mask[0]
    start = lax.axis_index("blk") * rows
    codes = jnp.where(live > 0, seg, -1 - jnp.arange(seg.shape[0], dtype=jnp.int32))
    own_codes = lax.dynamic_slice_in_dim(codes, start, rows)
    mats = [query_weight, key_weight, value_weight, out_weight, up_weight, down_weight]
    vecs = [query_bias, value_bias, out_bias, first_gain, first_shift, down_bias, second_gain, second_shift, up_bias]
    if tuned_plane():
        result, token_grad, sums = tuned_line(inputs, mats, vecs, cotangent[0], segments, live_mask, nb)
    else:
        result, token_grad, sums = whole_line(
            inputs, seg, live, mats, vecs, cotangent[0], codes, own_codes, start
        )
    rwq, rwk, rwv, ro, rdn, rup, rbq, rbv, rbo, rg1, rs1, rbdn, rg2, rs2, rbup = sums
    return (
        result[None], token_grad[None],
        rwq, rwk, rwv, ro, rbq, rbv, rbo, rg1, rs1, rup, rbup, rdn, rbdn, rg2, rs2,
    )


def solution(mesh):
    flat = P(PLANE, "blk", None)
    mat = P(PLANE, None)
    vec = P(PLANE)
    return jax.shard_map(
        per_device,
        mesh=mesh,
        in_specs=(
            flat, mat, mat, mat, mat, mat, mat, vec, vec, vec, vec, vec, mat, vec, mat, vec, vec, vec, flat,
        ),
        out_specs=(flat, flat, mat, mat, mat, mat, vec, vec, vec, vec, vec, mat, vec, mat, vec, vec, vec),
        check_vma=False,
    )
```

```python
import functools
import jax
import jax.numpy as jnp
from jax import lax
from jax.experimental import pallas as pl
from jax.experimental.pallas import tpu as pltpu
from jax.sharding import PartitionSpec as P

MESH = pl.DeviceIdType.MESH
ANY = pl.BlockSpec(memory_space=pl.ANY)
VMEM_LIMIT = 56 << 20
VM = pl.BlockSpec(memory_space=pltpu.VMEM)


class Place:
    def __init__(self):
        b = lax.axis_index("blk")
        s = lax.axis_index("seq")
        h = lax.axis_index("shard")
        x = h // 2
        c = h % 2
        self.b, self.s, self.h, self.x, self.c = b, s, h, x, c
        self.X = (b, s, (1 - x) * 2 + c)
        self.Y = (b, 1 - s, h)
        self.C = (b, s, x * 2 + 1 - c)
        self.L = (b - 1, s, h)
        self.R = (b + 1, s, h)
        self.me = s * 4 + h
        self.xi = s * 4 + (1 - x) * 2 + c
        self.yi = (1 - s) * 4 + h
        self.di = (1 - s) * 4 + (1 - x) * 2 + c

    def z(self, j):
        return (j, self.s, self.h)


def greet(p, nb, plane, line):
    bar = pltpu.get_barrier_semaphore()
    count = 0
    if plane:
        for peer in (p.X, p.Y, p.C):
            pl.semaphore_signal(bar, inc=1, device_id=peer, device_id_type=MESH)
        count = count + 3
    if line == "near":
        @pl.when(p.b > 0)
        def _():
            pl.semaphore_signal(bar, inc=1, device_id=p.L, device_id_type=MESH)

        @pl.when(p.b < nb - 1)
        def _():
            pl.semaphore_signal(bar, inc=1, device_id=p.R, device_id_type=MESH)
        count = count + jnp.where(p.b > 0, 1, 0) + jnp.where(p.b < nb - 1, 1, 0)
    if line == "all":
        for j in range(nb):
            @pl.when(p.b != j)
            def _():
                pl.semaphore_signal(bar, inc=1, device_id=p.z(j), device_id_type=MESH)
        count = count + nb - 1
    return lambda: pl.semaphore_wait(bar, count)


def enter(p, nb, plane, line):
    greet(p, nb, plane, line)()


def rcopy(src, dst, ss, rs, dev):
    return pltpu.make_async_remote_copy(
        src_ref=src, dst_ref=dst, send_sem=ss, recv_sem=rs, device_id=dev, device_id_type=MESH
    )


class LineGather:
    def __init__(self, p, nb, own, out, ssem, rsem):
        self.p, self.nb, self.own, self.out, self.ssem, self.rsem = p, nb, own, out, ssem, rsem

    def _copies(self, t):
        p, nb = self.p, self.nb
        rb = p.b - t
        lb = p.b + t
        src_r = self.own if t == 0 else self.out.at[jnp.maximum(rb, 0)]
        src_l = self.own if t == 0 else self.out.at[jnp.minimum(lb, nb - 1)]
        right = rcopy(src_r, self.out.at[jnp.maximum(rb, 0)], self.ssem.at[0, t], self.rsem.at[0, t], p.R)
        left = rcopy(src_l, self.out.at[jnp.minimum(lb, nb - 1)], self.ssem.at[1, t], self.rsem.at[1, t], p.L)
        return right, left, (rb >= 0) & (p.b < nb - 1), (lb <= nb - 1) & (p.b > 0)

    def start(self, t):
        right, left, cr, cl = self._copies(t)
        pl.when(cr)(right.start)
        pl.when(cl)(left.start)

    def wait_recv(self, t):
        p, nb = self.p, self.nb
        right, left, _, _ = self._copies(t)
        pl.when(p.b - 1 - t >= 0)(right.wait_recv)
        pl.when(p.b + 1 + t <= nb - 1)(left.wait_recv)

    def wait_send(self, t):
        right, left, cr, cl = self._copies(t)
        pl.when(cr)(right.wait_send)
        pl.when(cl)(left.wait_send)


class PlaneGather:
    def __init__(self, p, own, out, ssem, rsem, lsem):
        rows = own.shape[0]
        half = rows // 2

        def whole(i):
            return out.at[pl.ds(pl.multiple_of(i * rows, rows), rows)]

        def low(i):
            return out.at[pl.ds(pl.multiple_of(i * rows, rows), half)]

        def high(i):
            return out.at[pl.ds(pl.multiple_of(i * rows + half, half), half)]

        def send(k, src, dst, dev):
            return rcopy(src, dst, ssem.at[k], rsem.at[k], dev)

        self.x = send(0, own, whole(p.me), p.X)
        self.y = send(1, own, whole(p.me), p.Y)
        self.c = send(2, own, whole(p.me), p.C)
        self.local = pltpu.make_async_copy(own, whole(p.me), lsem)
        self.fx = send(3, high(p.yi), high(p.yi), p.X)
        self.fy = send(4, low(p.xi), low(p.xi), p.Y)
        self.cx = send(5, whole(p.xi), whole(p.xi), p.C)
        self.cy = send(6, whole(p.yi), whole(p.yi), p.C)
        self.cd0 = send(7, low(p.di), low(p.di), p.C)
        self.cd1 = send(8, high(p.di), high(p.di), p.C)

    def start(self):
        for k in (self.x, self.y, self.c, self.local):
            k.start()

    def forward(self):
        self.x.wait_recv()
        self.fy.start()
        self.cx.start()
        self.y.wait_recv()
        self.fx.start()
        self.cy.start()

    def diag(self):
        self.fy.wait_recv()
        self.cd0.start()
        self.fx.wait_recv()
        self.cd1.start()

    def finish(self):
        self.local.wait()
        for k in (self.c, self.cx, self.cy, self.cd0, self.cd1):
            k.wait_recv()

    def drain(self):
        for k in (self.x, self.y, self.c, self.fx, self.fy, self.cx, self.cy, self.cd0, self.cd1):
            k.wait_send()


def staged(count, steps, body):
    def once(i, _):
        for at, todo in steps.items():
            @pl.when(i == at)
            def _():
                for f in todo:
                    f()
        body(i)
        return 0
    lax.fori_loop(0, count, once, 0)


def code_tables(seg, live, rows, col, place):
    nb, _, n = rows.shape
    ids = jnp.where(live[...] > 0, seg[...], -1 - lax.broadcasted_iota(jnp.int32, seg.shape, 1)).astype(jnp.float32)
    for j in range(nb):
        rows[j] = ids[:, j * n:(j + 1) * n]
    col[...] = jnp.broadcast_to(rows[place], (128, n)).T[:, :1]


def turn(b, nb, i):
    far = (i + 1) // 2
    j = jnp.where(i % 2 == 1, b - far, b + far)
    return (j >= 0) & (j <= nb - 1), jnp.clip(j, 0, nb - 1)


def row_loop(rows, chunk, body):
    if rows == chunk:
        body(0)
    else:
        def step(i, _):
            body(pl.multiple_of(i * chunk, chunk))
            return 0
        lax.fori_loop(0, rows // chunk, step, 0)


def add_low(a, b):
    return (a.astype(jnp.float32) + b.astype(jnp.float32)).astype(a.dtype)


def add_into(dst, src):
    def body(r):
        rows = pl.ds(r, 48)
        dst[rows] = add_low(dst[rows], src[rows])
    row_loop(dst.shape[0], 48, body)


class PlaneSum:
    def __init__(self, p, g, buf, stage, ss, rs, ls):
        self.p = p
        self.P, self.BX, self.BY, self.CX, self.CY = buf
        self.R, self.C = g.shape[-2:]
        h = self.R // 2
        self.h = h
        lo, hi = pl.ds(0, h), pl.ds(h, h)
        self.g = g
        self.stage = stage
        self.ss, self.rs = ss, rs
        self.own = None if stage is None else pltpu.make_async_copy(g.at[:, :, p.c], stage, ls)
        self.cBX = rcopy(self.P.at[:, 1 - p.x, lo], self.BX, ss.at[1], rs.at[1], p.X)
        self.cBY = rcopy(self.P.at[1 - p.s, :, hi], self.BY, ss.at[2], rs.at[2], p.Y)
        self.cCX = rcopy(self.P.at[p.s, 1 - p.x, hi], self.CX, ss.at[3], rs.at[3], p.X)
        self.cCY = rcopy(self.P.at[1 - p.s, p.x, lo], self.CY, ss.at[4], rs.at[4], p.Y)
        self.total = self.P.at[p.s, p.x]

    def piece(self, t):
        s, x = t // 2, t % 2
        return rcopy(self.g.at[s, x, 1 - self.p.c], self.P.at[s, x], self.ss.at[5 + t], self.rs.at[5 + t], self.p.C)

    def _core(self):
        return rcopy(self.g.at[:, :, 1 - self.p.c], self.P, self.ss.at[0], self.rs.at[0], self.p.C)

    def a_start(self):
        self._core().start()

    def own_start(self):
        self.own.start()

    def b_start(self, pieces=False):
        if self.own is not None:
            self.own.wait()
        if not pieces:
            self._core().wait_recv()

        def block(i, _):
            s, x = i // 2, i % 2
            if pieces:
                self.piece(i).wait_recv()

            def body(r):
                rows = pl.ds(r, 48)
                mine = self.g[s, x, self.p.c, rows] if self.stage is None else self.stage[s, x, rows]
                self.P[s, x, rows] = add_low(mine, self.P[s, x, rows])
            row_loop(self.R, 48, body)
            return 0
        lax.fori_loop(0, 4, block, 0)
        self.cBX.start()
        self.cBY.start()

    def c_start(self):
        p, h = self.p, self.h
        lo, hi = pl.ds(0, h), pl.ds(h, h)
        self.cBX.wait_recv()
        add_into(self.P.at[1 - p.s, p.x, lo], self.BX.at[1 - p.s])
        self.cCY.start()
        self.cBY.wait_recv()
        add_into(self.P.at[p.s, 1 - p.x, hi], self.BY.at[1 - p.x])
        self.cCX.start()
        add_into(self.P.at[p.s, p.x, lo], self.BX.at[p.s])
        add_into(self.P.at[p.s, p.x, hi], self.BY.at[p.x])

    def end(self):
        h = self.h
        self.cCY.wait_recv()
        add_into(self.total.at[pl.ds(0, h)], self.CY)
        self.cCX.wait_recv()
        add_into(self.total.at[pl.ds(h, h)], self.CX)

    def drain(self, pieces=False):
        for k in (self.cBX, self.cBY, self.cCX, self.cCY):
            k.wait_send()
        if pieces:
            for t in range(4):
                self.piece(t).wait_send()
        else:
            self._core().wait_send()


class LineSum:
    def __init__(self, p, nb, part, out, Z, ss, rs):
        self.p, self.nb, self.F, self.O, self.Z, self.ss, self.rs = p, nb, part, out, Z, ss, rs
        self.R, self.C = part.shape
        self.h = self.R // 2

    def quarter(self, ref, j):
        R, C = self.R, self.C
        r, c = (j // 2) * (R // 2), (j % 2) * (C // 2)
        if not isinstance(j, int):
            r, c = pl.multiple_of(r, R // 2), pl.multiple_of(c, C // 2)
        return ref.at[pl.ds(r, R // 2), pl.ds(c, C // 2)]

    def _send(self, j, slot):
        return rcopy(self.quarter(self.F, j), self.Z.at[slot], self.ss.at[j], self.rs.at[slot], self.p.z(j))

    def start(self):
        for j in range(self.nb):
            pl.when(self.p.b != j)(self._send(j, self.p.b).start)

    def _spread(self, t):
        p, nb = self.p, self.nb
        k = nb + 2 * t
        r, l = p.b - t, p.b + t
        qr = self.quarter(self.O, jnp.maximum(r, 0))
        ql = self.quarter(self.O, jnp.minimum(l, nb - 1))
        right = rcopy(qr, qr, self.ss.at[k], self.rs.at[k], p.R)
        left = rcopy(ql, ql, self.ss.at[k + 1], self.rs.at[k + 1], p.L)
        return right, left, (r >= 0) & (p.b < nb - 1), (l <= nb - 1) & (p.b > 0)

    def _spread_recv(self, t, forwarded):
        right, left, _, _ = self._spread(t)
        p, nb = self.p, self.nb
        hands_right, hands_left = p.b < nb - 1, p.b > 0
        if t == nb - 2:
            hands_right, hands_left = False, False
        if forwarded:
            pl.when((p.b - 1 - t >= 0) & hands_right)(right.wait_recv)
            pl.when((p.b + 1 + t <= nb - 1) & hands_left)(left.wait_recv)
        else:
            pl.when((p.b - 1 - t >= 0) & jnp.logical_not(hands_right))(right.wait_recv)
            pl.when((p.b + 1 + t <= nb - 1) & jnp.logical_not(hands_left))(left.wait_recv)

    def _sum(self):
        p, nb = self.p, self.nb
        mine = self.quarter(self.F, p.b)
        total = self.quarter(self.O, p.b)
        for j in range(nb):
            pl.when(p.b != j)(self._send(j, j).wait_recv)

        def body(r):
            rows = pl.ds(r, 48)
            acc = mine[rows].astype(jnp.float32)
            for d in range(1, nb):
                acc = acc + self.Z[(p.b + d) % nb, rows].astype(jnp.float32)
            total[rows] = acc.astype(mine.dtype)
        row_loop(self.h, 48, body)

    def spread(self, t):
        if t == 0:
            self._sum()
        else:
            self._spread_recv(t - 1, True)
        right, left, cr, cl = self._spread(t)
        pl.when(cr)(right.start)
        pl.when(cl)(left.start)

    def finish(self):
        for t in range(self.nb - 1):
            self._spread_recv(t, False)

    def drain(self):
        for j in range(self.nb):
            pl.when(self.p.b != j)(self._send(j, self.p.b).wait_send)
        for t in range(self.nb - 1):
            right, left, cr, cl = self._spread(t)
            pl.when(cr)(right.wait_send)
            pl.when(cl)(left.wait_send)


class DirectSum(LineSum):
    def _share(self, j, slot):
        q = self.quarter(self.O, slot)
        return rcopy(q, q, self.ss.at[self.nb + j], self.rs.at[self.nb + slot], self.p.z(j))

    def share(self):
        self._sum()
        for j in range(self.nb):
            pl.when(self.p.b != j)(self._share(j, self.p.b).start)

    def finish(self):
        for j in range(self.nb):
            pl.when(self.p.b != j)(self._share(j, j).wait_recv)

    def drain(self):
        for j in range(self.nb):
            @pl.when(self.p.b != j)
            def _():
                self._send(j, self.p.b).wait_send()
                self._share(j, self.p.b).wait_send()


class ChainSum(LineSum):
    def _right(self, j):
        return rcopy(self.quarter(self.F, j), self.Z.at[j], self.ss.at[j], self.rs.at[j], self.p.R)

    def _left(self, j, last):
        slot = self.nb if last else j
        k = 3 * self.nb - 2 + j
        return rcopy(self.quarter(self.F, j), self.Z.at[slot], self.ss.at[k], self.rs.at[k], self.p.L)

    def start(self):
        self.hop(0)

    def hop(self, t):
        nb, p = self.nb, self.p

        @pl.when(p.b == t)
        def _():
            for j in range(nb - 1, t, -1):
                if t > 0:
                    self._right(j).wait_recv()
                    add_into(self.quarter(self.F, j), self.Z.at[j])
                self._right(j).start()

        @pl.when(p.b == nb - 1 - t)
        def _():
            for j in range(nb - 1 - t):
                if t > 0:
                    self._left(j, False).wait_recv()
                    add_into(self.quarter(self.F, j), self.Z.at[j])
                self._left(j, j == nb - 2 - t).start()

    def _sum(self):
        p, nb = self.p, self.nb
        mine = self.quarter(self.F, p.b)
        total = self.quarter(self.O, p.b)
        for j in range(nb):
            @pl.when(p.b == j)
            def _():
                if j > 0:
                    self._right(j).wait_recv()
                if j < nb - 1:
                    self._left(j, True).wait_recv()

        @pl.when(p.b > 0)
        def _():
            add_into(mine, self.Z.at[p.b])

        @pl.when(p.b < nb - 1)
        def _():
            add_into(mine, self.Z.at[nb])

        def body(r):
            rows = pl.ds(r, 48)
            total[rows] = mine[rows]
        row_loop(self.h, 48, body)

    def drain(self):
        nb, p = self.nb, self.p
        for t in range(nb - 1):
            @pl.when(p.b == t)
            def _():
                for j in range(nb - 1, t, -1):
                    self._right(j).wait_send()

            @pl.when(p.b == nb - 1 - t)
            def _():
                for j in range(nb - 1 - t):
                    self._left(j, j == nb - 2 - t).wait_send()
            right, left, cr, cl = self._spread(t)
            pl.when(cr)(right.wait_send)
            pl.when(cl)(left.wait_send)


def plane_scratch(shape):
    R, C = shape
    h = R // 2
    sizes = ((2, 2, R, C), (2, h, C), (2, h, C), (h, C), (h, C))
    return [pltpu.VMEM(s, jnp.bfloat16) for s in sizes]


def line_scratch(shape, nb):
    return pltpu.VMEM((nb + 1, shape[0] // 2, shape[1] // 2), jnp.bfloat16)


PLANE_BUFS = 5
PLANE_SEMS = 9


def line_sems(nb):
    return 2 * nb + 2 * (nb - 1)


class TableSum:
    def __init__(self, p, nb, t, bufs, line, ss, rs):
        self.p, self.nb, self.t, self.bufs, self.line = p, nb, t, bufs, line
        self.steps = [
            rcopy(t if i == 0 else bufs.at[i - 1], bufs.at[3 + i], ss.at[i], rs.at[i], dev)
            for i, dev in enumerate((p.C, p.X, p.Y))
        ]
        self.ss, self.rs = ss, rs

    def start(self):
        self.steps[0].start()

    def step(self, i):
        self.steps[i].wait_recv()
        self.bufs[i] = (self.t[...] if i == 0 else self.bufs[i - 1]) + self.bufs[3 + i]
        if i < 2:
            self.steps[i + 1].start()
        else:
            self.line[self.p.b] = self.bufs[2]
            for j in range(self.nb):
                pl.when(self.p.b != j)(self._z(j, self.p.b).start)

    def _z(self, j, slot):
        return rcopy(
            self.bufs.at[2], self.line.at[slot], self.ss.at[3 + j], self.rs.at[3 + slot], self.p.z(j)
        )

    def finish(self, out):
        for j in range(self.nb):
            pl.when(self.p.b != j)(self._z(j, j).wait_recv)
        total = self.line[0]
        for j in range(1, self.nb):
            total = total + self.line[j]
        out[...] = total

    def drain(self):
        for k in self.steps:
            k.wait_send()
        for j in range(self.nb):
            pl.when(self.p.b != j)(self._z(j, self.p.b).wait_send)


HEAD_DIM = 64
PAIR = 128
MASKED = -1e30
TILE = 512


def dot(a, b, ca, cb):
    return lax.dot_general(a, b, (((ca,), (cb,)), ((), ())), preferred_element_type=jnp.float32)


def left_lanes(shape):
    return lax.broadcasted_iota(jnp.int32, shape, 1) < HEAD_DIM


def one_head(pair, left, first):
    keep = left if first else jnp.logical_not(left)
    return jnp.where(keep, pair, jnp.zeros_like(pair))


def lane_groups(op, a):
    out = a[:, :PAIR]
    for g in range(1, a.shape[1] // PAIR):
        out = op(out, a[:, g * PAIR:(g + 1) * PAIR])
    return out


def attn_fwd_kernel(span, col_ref, row_ref, q_ref, k_ref, v_ref, o_ref, ob_ref, lse_ref, s_ref, m_ref, l_ref, acc_ref):
    rows = q_ref.shape[0]
    left = left_lanes((rows, PAIR))
    m_ref[...] = jnp.full_like(m_ref, MASKED)
    l_ref[...] = jnp.zeros_like(l_ref)
    acc_ref[...] = jnp.zeros_like(acc_ref)
    q = q_ref[...]
    heads = [one_head(q, left, i == 0) for i in range(2)]
    codes = col_ref[...]

    def score(t, _):
        at = pl.multiple_of(t * TILE, TILE)
        k = k_ref[pl.ds(at, TILE), :]
        mask = codes == row_ref[:, pl.ds(at, TILE)]
        for i in range(2):
            s = jnp.where(mask, dot(heads[i], k, 1, 1), MASKED)
            s_ref[i, t] = s
            m_ref[i] = jnp.maximum(m_ref[i], lane_groups(jnp.maximum, s))
        return 0

    lax.fori_loop(span[0], span[1], score, 0)
    tops = [jnp.max(m_ref[i], axis=1, keepdims=True) for i in range(2)]

    def mix(t, _):
        v = v_ref[pl.ds(pl.multiple_of(t * TILE, TILE), TILE), :]
        parts = []
        for i in range(2):
            p = jnp.exp(s_ref[i, t] - tops[i])
            l_ref[i] += lane_groups(jnp.add, p)
            parts.append(dot(p.astype(jnp.bfloat16), v, 1, 0))
        acc_ref[...] += jnp.where(left, parts[0], parts[1])
        return 0

    lax.fori_loop(span[0], span[1], mix, 0)
    sums = [jnp.sum(l_ref[i], axis=1, keepdims=True) for i in range(2)]
    total = jnp.where(left, sums[0], sums[1])
    o = acc_ref[...] / total
    o_ref[...] = o
    ob_ref[...] = o.astype(jnp.bfloat16)
    lse_ref[...] = jnp.where(left, tops[0], tops[1]) + jnp.log(total)


def attention(q, k_all, v_all, codes, own_codes, span):
    rows, width = q.shape
    total = k_all.shape[0]
    pairs = width // PAIR
    own = pl.BlockSpec((rows, PAIR), lambda h, s: (0, h))
    every = pl.BlockSpec((total, PAIR), lambda h, s: (0, h))
    return pl.pallas_call(
        attn_fwd_kernel,
        grid_spec=pltpu.PrefetchScalarGridSpec(
            num_scalar_prefetch=1,
            grid=(pairs,),
            in_specs=[
                pl.BlockSpec((rows, 1), lambda h, s: (0, 0)),
                pl.BlockSpec((1, total), lambda h, s: (0, 0)),
                own, every, every,
            ],
            out_specs=[own, own, own],
            scratch_shapes=[
                pltpu.VMEM((2, total // TILE, rows, TILE), jnp.float32),
                pltpu.VMEM((2, rows, PAIR), jnp.float32),
                pltpu.VMEM((2, rows, PAIR), jnp.float32),
                pltpu.VMEM((rows, PAIR), jnp.float32),
            ],
        ),
        out_shape=[
            jax.ShapeDtypeStruct((rows, width), jnp.float32),
            jax.ShapeDtypeStruct((rows, width), jnp.bfloat16),
            jax.ShapeDtypeStruct((rows, width), jnp.float32),
        ],
        compiler_params=pltpu.CompilerParams(vmem_limit_bytes=48 << 20),
        name="attention",
    )(span, own_codes.reshape(rows, 1), codes.reshape(1, total), q, k_all, v_all)


def stats_kernel(g_ref, o_ref, lse_ref, out_ref, delta_ref):
    rows = g_ref.shape[0]
    left = left_lanes((rows, PAIR))
    t = g_ref[...].astype(jnp.float32) * o_ref[...]
    d0 = jnp.sum(jnp.where(left, t, 0.0), axis=1, keepdims=True)
    d1 = jnp.sum(jnp.where(left, 0.0, t), axis=1, keepdims=True)
    delta_ref[...] = jnp.where(left, d0, d1)
    lane = lax.broadcasted_iota(jnp.int32, (rows, PAIR), 1)
    lse = lse_ref[...]
    packed = jnp.where(lane == 0, lse[:, :1], jnp.where(lane == 1, lse[:, HEAD_DIM:HEAD_DIM + 1], jnp.where(lane == 2, d0, d1)))
    out_ref[0] = packed.T[:8]


def row_stats(grad, o, lse):
    rows, width = grad.shape
    pairs = width // PAIR
    own = pl.BlockSpec((rows, PAIR), lambda h: (0, h))
    return pl.pallas_call(
        stats_kernel,
        grid=(pairs,),
        in_specs=[own, own, own],
        out_specs=[pl.BlockSpec((1, 8, rows), lambda h: (h, 0, 0)), own],
        out_shape=[
            jax.ShapeDtypeStruct((pairs, 8, rows), jnp.float32),
            jax.ShapeDtypeStruct((rows, width), jnp.float32),
        ],
        name="row_stats",
    )(grad, o, lse)


def attn_bwd_kernel(span, col_ref, row_ref, q_ref, k_ref, v_ref, g_ref, lse_ref, delta_ref,
                    qa_ref, ka_ref, va_ref, ga_ref, st_ref, dq_ref, dk_ref, dv_ref):
    rows = q_ref.shape[0]
    left = left_lanes((rows, PAIR))
    dq_ref[...] = jnp.zeros_like(dq_ref)
    dk_ref[...] = jnp.zeros_like(dk_ref)
    dv_ref[...] = jnp.zeros_like(dv_ref)
    codes = col_ref[...]
    qs = [one_head(q_ref[...], left, i == 0) for i in range(2)]
    ks = [one_head(k_ref[...], left, i == 0) for i in range(2)]
    vs = [one_head(v_ref[...], left, i == 0) for i in range(2)]
    gs = [one_head(g_ref[...], left, i == 0) for i in range(2)]
    lses = [lse_ref[:, i * HEAD_DIM:i * HEAD_DIM + 1] for i in range(2)]
    deltas = [delta_ref[:, i * HEAD_DIM:i * HEAD_DIM + 1] for i in range(2)]

    def step(t, _):
        at = pl.multiple_of(t * TILE, TILE)
        tile = pl.ds(at, TILE)
        mask = codes == row_ref[:, tile]
        k, v, q, g = ka_ref[tile, :], va_ref[tile, :], qa_ref[tile, :], ga_ref[tile, :]
        dqs, dks, dvs = [], [], []
        for i in range(2):
            s = jnp.where(mask, dot(qs[i], k, 1, 1), MASKED)
            p = jnp.exp(s - lses[i])
            dp = dot(gs[i], v, 1, 1)
            ds = (p * (dp - deltas[i])).astype(jnp.bfloat16)
            dqs.append(dot(ds, k, 1, 0))
            st = jnp.where(mask, dot(ks[i], q, 1, 1), MASKED)
            pt = jnp.exp(st - st_ref[0, i:i + 1, tile])
            dvs.append(dot(pt.astype(jnp.bfloat16), g, 1, 0))
            dpt = dot(vs[i], g, 1, 1)
            dst = (pt * (dpt - st_ref[0, 2 + i:3 + i, tile])).astype(jnp.bfloat16)
            dks.append(dot(dst, q, 1, 0))
        dq_ref[...] += jnp.where(left, dqs[0], dqs[1])
        dk_ref[...] += jnp.where(left, dks[0], dks[1])
        dv_ref[...] += jnp.where(left, dvs[0], dvs[1])
        return 0

    lax.fori_loop(span[0], span[1], step, 0)


def attention_grad(q, k, v, g, lse, delta, q_all, k_all, v_all, g_all, stats, codes, own_codes, span):
    rows, width = q.shape
    total = k_all.shape[0]
    pairs = width // PAIR
    own = pl.BlockSpec((rows, PAIR), lambda h, s: (0, h))
    every = pl.BlockSpec((total, PAIR), lambda h, s: (0, h))
    return pl.pallas_call(
        attn_bwd_kernel,
        grid_spec=pltpu.PrefetchScalarGridSpec(
            num_scalar_prefetch=1,
            grid=(pairs,),
            in_specs=[
                pl.BlockSpec((rows, 1), lambda h, s: (0, 0)),
                pl.BlockSpec((1, total), lambda h, s: (0, 0)),
                own, own, own, own, own, own, every, every, every, every,
                pl.BlockSpec((1, 8, total), lambda h, s: (h, 0, 0)),
            ],
            out_specs=[own, own, own],
        ),
        out_shape=[
            jax.ShapeDtypeStruct((rows, width), jnp.float32),
            jax.ShapeDtypeStruct((rows, width), jnp.float32),
            jax.ShapeDtypeStruct((rows, width), jnp.float32),
        ],
        compiler_params=pltpu.CompilerParams(vmem_limit_bytes=48 << 20),
        name="attention_grad",
    )(span, own_codes.reshape(rows, 1), codes.reshape(1, total), q, k, v, g, lse, delta, q_all, k_all, v_all, g_all, stats)


VEC_ROWS = 8


def forward_kernel(nb, *refs):
    x_ref, seg, live = refs[:3]
    shards_in = refs[3:9]
    vecs_in = refs[9:18]
    wq_o, wk_o, wv_o, wo_o, wup_o, wdn_o = refs[18:24]
    q_o, k_o, v_o = refs[24:27]
    o_ref, ob_ref, lse_ref, vec_ref, bup_ref = refs[27:32]
    rest = refs[32:]
    x_all, wq, wk, wv, pack, packs, q, k, v, m_ref, l_ref, codes, rows = rest[:13]
    zs, zr, gs, gr, gl, ws, es = rest[13:]
    n, width = x_ref.shape
    pairs = width // PAIR
    p = Place()
    own = pltpu.make_async_copy(x_ref, x_all.at[p.b], ws.at[3])
    own.start()
    pack[...] = jnp.zeros_like(pack)
    for i in range(VEC_ROWS):
        pack[i:i + 1, :vecs_in[i].shape[1]] = vecs_in[i][...].astype(jnp.float32)
    for i in range(vecs_in[8].shape[1] // PAIR):
        pack[VEC_ROWS + i:VEC_ROWS + i + 1, :] = vecs_in[8][:, i * PAIR:(i + 1) * PAIR].astype(jnp.float32)
    enter(p, nb, True, "near")
    line = LineGather(p, nb, x_ref, x_all, zs, zr)
    targets = (packs, wq, wk, wv, wo_o, wup_o, wdn_o)
    sources = (pack,) + tuple(shards_in)
    g = [PlaneGather(p, sources[i], targets[i], gs.at[i], gr.at[i], gl.at[i]) for i in range(7)]
    line.start(0)
    for c in g[:5]:
        c.start()
    code_tables(seg, live, rows, codes, p.b)
    for c in g[:4]:
        c.forward()
    g[5].start()
    g[6].start()
    line.wait_recv(0)
    line.start(1)
    for c in g[:4]:
        c.diag()
    for c in g[:4]:
        c.finish()
    own.wait()
    keep = [
        pltpu.make_async_copy(a, b, ws.at[i]) for i, (a, b) in enumerate(((wq, wq_o), (wk, wk_o), (wv, wv_o)))
    ]
    for c in keep:
        c.start()

    piece = width // 8
    r = lax.broadcasted_iota(jnp.int32, (PAIR, width), 0)
    c = lax.broadcasted_iota(jnp.int32, (PAIR, width), 1)
    total = jnp.zeros((2 * VEC_ROWS, width), jnp.float32)
    for i in range(8):
        pick = ((c == r + i * piece) & (r < piece)).astype(jnp.bfloat16)
        total += dot(packs[2 * VEC_ROWS * i:2 * VEC_ROWS * (i + 1), :].astype(jnp.bfloat16), pick, 1, 0)
    vec_ref[...] = total[:VEC_ROWS]
    up_piece = bup_ref.shape[1] // 8
    for i in range(8):
        for t in range(up_piece // PAIR):
            at = i * up_piece + t * PAIR
            row = 2 * VEC_ROWS * i + VEC_ROWS + t
            bup_ref[:, at:at + PAIR] = packs[row:row + 1, :]

    scale = HEAD_DIM ** (-0.5)
    step = 256

    def outs(j, e):
        return [
            pltpu.make_async_copy(a.at[j], b.at[j], es.at[i, e])
            for i, (a, b) in enumerate(((q, q_o), (k, k_o), (v, v_o)))
        ]

    def project(j):
        def columns(t, _):
            at = pl.ds(pl.multiple_of(t * step, step), step)
            xs = x_all[j]
            q[j, :, at] = ((dot(xs, wq[:, at], 1, 0) + vec_ref[0:1, at]) * scale).astype(jnp.bfloat16)
            k[j, :, at] = dot(xs, wk[:, at], 1, 0).astype(jnp.bfloat16)
            v[j, :, at] = (dot(xs, wv[:, at], 1, 0) + vec_ref[1:2, at]).astype(jnp.bfloat16)
            return 0
        lax.fori_loop(0, width // step, columns, 0, unroll=True)

    def attend(j):
        def pair(h, _):
            left = left_lanes((n, PAIR))
            lanes = pl.ds(pl.multiple_of(h * PAIR, PAIR), PAIR)
            mask = codes[...] == rows[j]
            qs, ks, vs = q[p.b, :, lanes], k[j, :, lanes], v[j, :, lanes]
            parts, alphas = [], []
            for i in range(2):
                s = jnp.where(mask, dot(one_head(qs, left, i == 0), ks, 1, 1), MASKED)
                top = jnp.max(lane_groups(jnp.maximum, s), axis=1, keepdims=True)
                old = m_ref[2 * h + i]
                new = jnp.maximum(old, top)
                alpha = jnp.exp(old - new)
                e = jnp.exp(s - jnp.concatenate([new] * (n // PAIR), axis=1))
                m_ref[2 * h + i] = new
                l_ref[2 * h + i] = l_ref[2 * h + i] * alpha + lane_groups(jnp.add, e)
                alphas.append(alpha)
                parts.append(dot(e.astype(jnp.bfloat16), vs, 1, 0))
            got = jnp.where(left, parts[0], parts[1])
            o_ref[:, lanes] = o_ref[:, lanes] * jnp.where(left, alphas[0], alphas[1]) + got
            return 0
        lax.fori_loop(0, pairs, pair, 0, unroll=2)

    def block(i):
        ok, j = turn(p.b, nb, i)

        @pl.when(ok)
        def _():
            project(j)
            for c in outs(j, i):
                c.start()
            attend(j)

    def hop(t, last=False):
        line.wait_recv(t)
        if not last:
            line.start(t + 1)

    m_ref[...] = jnp.full_like(m_ref, MASKED)
    l_ref[...] = jnp.zeros_like(l_ref)
    o_ref[...] = jnp.zeros_like(o_ref)
    staged(
        2 * nb - 1,
        {
            1: [g[4].forward, g[5].forward],
            2: [lambda: hop(1)],
            3: [g[6].forward, g[4].diag],
            5: [g[5].diag, g[6].diag, lambda: hop(2, True)],
        },
        block,
    )

    def close(h, _):
        left = left_lanes((n, PAIR))
        lanes = pl.ds(pl.multiple_of(h * PAIR, PAIR), PAIR)
        sums = [jnp.sum(l_ref[2 * h + i], axis=1, keepdims=True) for i in range(2)]
        mass = jnp.where(left, sums[0], sums[1])
        out = o_ref[:, lanes] / mass
        o_ref[:, lanes] = out
        ob_ref[:, lanes] = out.astype(jnp.bfloat16)
        lse_ref[:, lanes] = jnp.where(left, m_ref[2 * h], m_ref[2 * h + 1]) + jnp.log(mass)
        return 0
    lax.fori_loop(0, pairs, close, 0)
    for c in g[4:]:
        c.finish()
    for c in keep:
        c.wait()
    for i in range(2 * nb - 1):
        ok, j = turn(p.b, nb, i)

        @pl.when(ok)
        def _():
            for c in outs(j, i):
                c.wait()
    for t in range(nb - 1):
        line.wait_send(t)
    for c in g:
        c.drain()


def forward(x, seg, live, weights, vecs, nb):
    n, width = x.shape
    hidden = weights[4].shape[1]
    bf, f32 = jnp.bfloat16, jnp.float32
    every = jax.ShapeDtypeStruct((nb, n, width), bf)
    block = jax.ShapeDtypeStruct((n, width), f32)
    mats = [jax.ShapeDtypeStruct((8 * w.shape[0], w.shape[1]), w.dtype) for w in weights]
    dma = pltpu.SemaphoreType.DMA
    return pl.pallas_call(
        functools.partial(forward_kernel, nb),
        out_shape=(
            *mats, every, every, every, block, jax.ShapeDtypeStruct((n, width), bf), block,
            jax.ShapeDtypeStruct((VEC_ROWS, width), f32), jax.ShapeDtypeStruct((1, hidden), f32),
        ),
        in_specs=[VM] * 18,
        out_specs=(ANY,) * 9 + (VM,) * 5,
        scratch_shapes=[
            pltpu.VMEM((nb, n, width), bf),
            pltpu.VMEM((width, width), bf), pltpu.VMEM((width, width), bf), pltpu.VMEM((width, width), bf),
            pltpu.VMEM((2 * VEC_ROWS, PAIR), f32), pltpu.VMEM((16 * VEC_ROWS, PAIR), f32),
            pltpu.VMEM((nb, n, width), bf), pltpu.VMEM((nb, n, width), bf), pltpu.VMEM((nb, n, width), bf),
            pltpu.VMEM((width // HEAD_DIM, n, PAIR), f32), pltpu.VMEM((width // HEAD_DIM, n, PAIR), f32),
            pltpu.VMEM((n, 1), f32), pltpu.VMEM((nb, 1, n), f32),
            dma((2, nb - 1)), dma((2, nb - 1)), dma((7, 9)), dma((7, 9)), dma((7,)), dma((4,)), dma((3, 2 * nb)),
        ],
        compiler_params=pltpu.CompilerParams(
            collective_id=1, has_side_effects=True, vmem_limit_bytes=60 << 20
        ),
        name="forward",
    )(
        x, seg, live, *weights, *[v.reshape(1, -1) for v in vecs]
    )


ROOT_HALF = 0.7071067811865476
ROOT_TWO_PI = 0.3989422804014327
CHUNK = 768
PART = 256


def erf_parts(x):
    x = jnp.clip(x, -3.832506856900711, 3.832506856900711)
    y = x * x
    top = jnp.full_like(y, 0.00022905065861350646)
    for a in (0.0034082910107109506, 0.050955695062380861, 0.18520832239976145, 1.128379143519084):
        top = top * y + a
    low = jnp.full_like(y, -1.1791602954361697e-7)
    for a in (
        0.000023547966471313185, 0.0010179625278914885, 0.014070470171167667,
        0.11098505178285362, 0.49746925110067538, 1.0,
    ):
        low = low * y + a
    return x * top / low


def middle_kernel(
    att_ref, x_ref, cot_ref, o_ref, lse_ref, vec_ref, bup_ref, wo_hbm, wup_hbm, wdn_hbm,
    out_ref, rest_ref, do_ref, stats_ref, delta_ref, table_ref, gdn_hbm, gup_hbm, gwo_ref,
    wo, wup, wdn, u_ref, slope_ref, y_ref, dh_ref, low_ref, gdn, gup, sems, osems,
):
    n, width = x_ref.shape
    hidden = wup.shape[1]
    chunks = hidden // CHUNK
    f32, bf = jnp.float32, jnp.bfloat16
    loads = [
        pltpu.make_async_copy(a, b, sems.at[i])
        for i, (a, b) in enumerate(((wo_hbm, wo), (wup_hbm, wup), (wdn_hbm, wdn)))
    ]
    for c in loads:
        c.start()
    table_ref[...] = jnp.zeros_like(table_ref)

    def vec(i):
        return vec_ref[i:i + 1, :]

    def mean(a):
        return jnp.sum(a, axis=1, keepdims=True) * (1.0 / width)

    def centred(h):
        c = h - mean(h)
        inv = lax.rsqrt(mean(c * c) + EPSILON)
        return c * inv, inv

    def pull(grad, hat, inv, gain):
        d = grad * gain
        return inv * (d - mean(d) - hat * mean(d * hat))

    def column_sum(a):
        return jnp.sum(a, axis=0, keepdims=True)

    blocks = 2
    m = n // blocks

    def rows_of(i):
        return pl.ds(pl.multiple_of(i * m, m), m)

    loads[0].wait()

    def first(i, _):
        r = rows_of(i)
        h = x_ref[r, :].astype(f32) + dot(att_ref[r, :], wo[...], 1, 0) + vec(2)
        hat, _ = centred(h)
        y = hat * vec(3) + vec(4)
        rest_ref[r, :] = h
        dh_ref[r, :] = y + vec(5)
        low_ref[r, :] = y.astype(bf)
        return 0
    lax.fori_loop(0, blocks, first, 0)
    for c in loads[1:]:
        c.wait()

    def up(t, _):
        total = dh_ref[...]
        for s in range(CHUNK // PART):
            at = pl.ds(pl.multiple_of(t * CHUNK + s * PART, PART), PART)
            z = dot(low_ref[...], wup[:, at], 1, 0) + bup_ref[:, at]
            cdf = 0.5 + 0.5 * erf_parts(z * ROOT_HALF)
            low = (z * cdf).astype(bf)
            u_ref[:, at] = low
            slope_ref[:, at] = cdf + z * (jnp.exp(-0.5 * z * z) * ROOT_TWO_PI)
            total = total + dot(low, wdn[at, :], 1, 0)
        dh_ref[...] = total
        return 0
    lax.fori_loop(0, chunks, up, 0, unroll=2)

    def second(i, _):
        r = rows_of(i)
        hat, inv = centred(dh_ref[r, :])
        out_ref[r, :] = (hat * vec(6) + vec(7)).astype(bf)
        g = cot_ref[r, :].astype(f32)
        table_ref[6:7, :] += column_sum(g * hat)
        table_ref[7:8, :] += column_sum(g)
        dh = pull(g, hat, inv, vec(6))
        table_ref[5:6, :] += column_sum(dh)
        dh_ref[r, :] = dh
        y_ref[r, :] = dh.astype(bf)
        return 0
    lax.fori_loop(0, blocks, second, 0)

    def down(t, _):
        at = pl.ds(pl.multiple_of(t * CHUNK, CHUNK), CHUNK)
        parts = []
        total = dh_ref[...]
        for s in range(CHUNK // PART):
            cols = pl.ds(pl.multiple_of(t * CHUNK + s * PART, PART), PART)
            dz = dot(y_ref[...], wdn[cols, :], 1, 1) * slope_ref[:, cols]
            table_ref[pl.ds(8 + t, 1), s * PART:(s + 1) * PART] = column_sum(dz)
            c = dz.astype(bf)
            parts.append(c)
            total = total + dot(c, wup[:, cols], 1, 1)
            gdn[cols, :] = dot(u_ref[:, cols], y_ref[...], 0, 0).astype(bf)
        dh_ref[...] = total
        c = jnp.concatenate(parts, axis=1)
        r = width // 8
        for i in range(2):
            half = width // 2
            g = dot(low_ref[:, i * half:(i + 1) * half], c, 0, 0).astype(bf)
            for k in range(4):
                gup[4 * i + k, t] = g[k * r:(k + 1) * r]
        pltpu.make_async_copy(gdn.at[at], gdn_hbm.at[at], osems.at[0, t]).start()
        pltpu.make_async_copy(gup.at[:, t], gup_hbm.at[:, t], osems.at[1, t]).start()
        return 0
    lax.fori_loop(0, chunks, down, 0, unroll=2)

    def third(i, _):
        r = rows_of(i)
        hat, inv = centred(rest_ref[r, :])
        g = dh_ref[r, :]
        table_ref[3:4, :] += column_sum(g * hat)
        table_ref[4:5, :] += column_sum(g)
        dh = pull(g, hat, inv, vec(3))
        table_ref[2:3, :] += column_sum(dh)
        rest_ref[r, :] = dh
        low = dh.astype(bf)
        low_ref[r, :] = low
        do = dot(low, wo[...], 1, 1).astype(bf)
        do_ref[r, :] = do
        table_ref[1:2, :] += column_sum(do.astype(f32))
        return 0
    lax.fori_loop(0, blocks, third, 0)

    def heads(h, _):
        lanes = pl.ds(pl.multiple_of(h * PAIR, PAIR), PAIR)
        left = left_lanes((n, PAIR))
        t = do_ref[:, lanes].astype(f32) * o_ref[:, lanes]
        d0 = jnp.sum(jnp.where(left, t, 0.0), axis=1, keepdims=True)
        d1 = jnp.sum(jnp.where(left, 0.0, t), axis=1, keepdims=True)
        delta_ref[:, lanes] = jnp.where(left, d0, d1)
        lane = lax.broadcasted_iota(jnp.int32, (n, PAIR), 1)
        lse = lse_ref[:, lanes]
        packed = jnp.where(lane == 0, lse[:, :1], jnp.where(
            lane == 1, lse[:, HEAD_DIM:HEAD_DIM + 1], jnp.where(lane == 2, d0, d1)))
        stats_ref[h] = packed.T[:8]
        gwo_ref[lanes, :] = dot(att_ref[:, lanes], low_ref[...], 0, 0).astype(bf)
        return 0
    lax.fori_loop(0, width // PAIR, heads, 0)
    for t in range(chunks):
        at = pl.ds(t * CHUNK, CHUNK)
        pltpu.make_async_copy(gdn.at[at], gdn_hbm.at[at], osems.at[0, t]).wait()
        pltpu.make_async_copy(gup.at[:, t], gup_hbm.at[:, t], osems.at[1, t]).wait()


def middle(att, x, cot, o, lse, vecs, bup, wo, wup, wdn):
    n, width = x.shape
    hidden = wup.shape[1]
    chunks = hidden // CHUNK
    bf, f32 = jnp.bfloat16, jnp.float32
    S = jax.ShapeDtypeStruct
    dma = pltpu.SemaphoreType.DMA
    return pl.pallas_call(
        middle_kernel,
        out_shape=(
            S((n, width), bf), S((n, width), f32), S((n, width), bf), S((width // PAIR, 8, n), f32),
            S((n, width), f32), S((16, width), f32), S((hidden, width), bf),
            S((8, chunks, width // 8, CHUNK), bf), S((width, width), bf),
        ),
        in_specs=[VM] * 7 + [ANY] * 3,
        out_specs=(VM,) * 6 + (ANY, ANY, VM),
        scratch_shapes=[
            pltpu.VMEM((width, width), bf), pltpu.VMEM((width, hidden), bf), pltpu.VMEM((hidden, width), bf),
            pltpu.VMEM((n, hidden), bf), pltpu.VMEM((n, hidden), f32), pltpu.VMEM((n, width), bf),
            pltpu.VMEM((n, width), f32), pltpu.VMEM((n, width), bf),
            pltpu.VMEM((hidden, width), bf), pltpu.VMEM((8, chunks, width // 8, CHUNK), bf),
            dma((3,)), dma((2, chunks)),
        ],
        compiler_params=pltpu.CompilerParams(vmem_limit_bytes=60 << 20),
        name="middle",
    )(att, x, cot, o, lse, vecs, bup, wo, wup, wdn)


PAIR_GROUP = 2


class AttentionGrad:
    def __init__(self, codes, rows, q, k, v, g, lse, delta, stats, own, dq, dk, dv):
        self.codes, self.rows = codes, rows
        self.q, self.k, self.v, self.g = q, k, v, g
        self.lse, self.delta, self.stats = lse, delta, stats
        self.own = own
        self.dq, self.dk, self.dv = dq, dk, dv
        self.n = dq.shape[0]
        self.pairs = dq.shape[1] // PAIR

    def queries(self, j, group):
        own = self.own

        def pair(h):
            left = left_lanes((self.n, PAIR))
            lanes = pl.ds(pl.multiple_of(h * PAIR, PAIR), PAIR)
            mask = self.codes[...] == self.rows[j]
            q, g = self.q[own, :, lanes], self.g[own, :, lanes]
            k, v = self.k[j, :, lanes], self.v[j, :, lanes]
            lse, delta = self.lse[:, lanes], self.delta[:, lanes]
            parts = []
            for i in range(2):
                at = slice(i * HEAD_DIM, i * HEAD_DIM + 1)
                s = jnp.where(mask, dot(one_head(q, left, i == 0), k, 1, 1), MASKED)
                p = jnp.exp(s - lse[:, at])
                dp = dot(one_head(g, left, i == 0), v, 1, 1)
                ds = (p * (dp - delta[:, at])).astype(jnp.bfloat16)
                parts.append(dot(ds, k, 1, 0))
            self.dq[:, lanes] += jnp.where(left, parts[0], parts[1])

        for i in range(PAIR_GROUP):
            pair(group * PAIR_GROUP + i)

    def keys(self, j, group):
        own = self.own

        def pair(h):
            left = left_lanes((self.n, PAIR))
            lanes = pl.ds(pl.multiple_of(h * PAIR, PAIR), PAIR)
            mask = self.codes[...] == self.rows[j]
            k, v = self.k[own, :, lanes], self.v[own, :, lanes]
            q, g = self.q[j, :, lanes], self.g[j, :, lanes]
            dks, dvs = [], []
            for i in range(2):
                st = jnp.where(mask, dot(one_head(k, left, i == 0), q, 1, 1), MASKED)
                pt = jnp.exp(st - self.stats[j, h, i:i + 1])
                dvs.append(dot(pt.astype(jnp.bfloat16), g, 1, 0))
                dpt = dot(one_head(v, left, i == 0), g, 1, 1)
                dst = (pt * (dpt - self.stats[j, h, 2 + i:3 + i])).astype(jnp.bfloat16)
                dks.append(dot(dst, q, 1, 0))
            self.dk[:, lanes] += jnp.where(left, dks[0], dks[1])
            self.dv[:, lanes] += jnp.where(left, dvs[0], dvs[1])

        for i in range(PAIR_GROUP):
            pair(group * PAIR_GROUP + i)


TABLE = 16


def backward_kernel(nb, *refs):
    seg, live, g_own, st_own, lse, delta, x_hbm, rest_hbm, table = refs[:9]
    q_hbm, k_hbm, v_hbm, wq_hbm, wk_hbm, wv_hbm = refs[9:15]
    early = refs[15:18]
    token_ref, table_out = refs[18:20]
    outs = refs[20:24]
    rest = refs[24:]
    q, k, v, g, stats, dq, dk, dv, wq, wk, wv, gw, stage_dn, stage_up, tab, tsum, tline, x_ref, rest_ref, codes, rows = rest[:21]
    zbufs = rest[21:25]
    bufs = rest[25:25 + 4 * PLANE_BUFS]
    zs, zr, ls, ps, pr, ds, dr, rls, ts, tr = rest[25 + 4 * PLANE_BUFS:]
    n, width = g_own.shape
    p = Place()
    loads = [
        pltpu.make_async_copy(a, b, ls.at[i])
        for i, (a, b) in enumerate((
            (k_hbm, k), (v_hbm, v), (q_hbm, q), (g_own, g.at[p.b]), (st_own, stats.at[p.b]),
            (wq_hbm, wq), (wk_hbm, wk), (wv_hbm, wv), (x_hbm, x_ref), (rest_hbm, rest_ref),
            (early[2], gw.at[0, :, :, :, pl.ds(gw.shape[4] // 2, gw.shape[4] // 2)]),
        ))
    ]
    for c in loads:
        c.start()
    enter(p, nb, True, "all")
    lines = [
        LineGather(p, nb, g_own, g, zs.at[0], zr.at[0]),
        LineGather(p, nb, st_own, stats, zs.at[1], zr.at[1]),
    ]
    sources = (early[0], early[1], gw.at[0], gw.at[1])
    stages = (stage_dn, stage_up, None, None)
    planes = [
        PlaneSum(
            p, sources[i], bufs[PLANE_BUFS * i:PLANE_BUFS * (i + 1)], stages[i], ps.at[i], pr.at[i], rls.at[min(i, 1)]
        )
        for i in range(4)
    ]
    dn, up, qo, kv = planes
    chains = [
        (DirectSum if i == 3 else ChainSum)(p, nb, planes[i].total, outs[i], zbufs[i], ds.at[i], dr.at[i])
        for i in range(4)
    ]
    ldn, lup, lqo, lkv = chains
    vec = TableSum(p, nb, tab, tsum, tline, ts, tr)
    for c in lines:
        c.start(0)
    for c in (dn, up):
        c.a_start()
        c.own_start()
    work = AttentionGrad(codes, rows, q, k, v, g, lse, delta, stats, p.b, dq, dk, dv)
    code_tables(seg, live, rows, codes, p.b)
    for c in (dq, dk, dv):
        c[...] = jnp.zeros_like(c)
    for c in loads[:4]:
        c.wait()
    dn.b_start()

    low = k
    def slot(i):
        return (p.b + 1 + i) % nb

    def settle(i, src, scale, row):
        value = src[...] if scale is None else src[...] * scale
        if row is not None:
            tab[row:row + 1, :] = jnp.sum(value, axis=0, keepdims=True)
        low[slot(i)] = value.astype(jnp.bfloat16)

    def weight_grad(i, item, base):
        half = width // 2
        r = width // 8
        for m in range(2):
            part = dot(x_ref[:, m * half:(m + 1) * half], low[slot(i)], 0, 0).astype(jnp.bfloat16)
            for a in range(2):
                for b in range(2):
                    at = (2 * a + b) * r
                    gw[item, m, a, b, base:base + r] = part[at:at + r]

    def hop(t, last=False):
        for c in lines:
            c.wait_recv(t)
            if not last:
                c.start(t + 1)

    groups = work.pairs // PAIR_GROUP
    staged(
        nb * groups,
        {
            2: [up.b_start],
            5: [lambda: hop(0)],
            6: [dn.c_start],
        },
        lambda i: work.queries((p.b + i // groups) % nb, i % groups),
    )
    for c in loads[4:]:
        c.wait()
    tab[...] = table[...]
    settle(0, dq, HEAD_DIM ** (-0.5), 0)
    vec.start()
    weight_grad(0, 0, 0)
    qo.a_start()
    hop(1)
    up.c_start()

    def keys(i):
        ok, j = turn(p.b, nb, i // groups)
        pl.when(ok)(lambda: work.keys(j, i % groups))

    def across(a, c):
        a.end()
        c.start()

    staged(
        (2 * nb - 1) * groups,
        {
            2: [lambda: across(dn, ldn), qo.b_start],
            5: [lambda: across(up, lup)],
            6: [lambda: ldn.hop(1)],
            8: [qo.c_start],
            9: [lambda: lup.hop(1), lambda: ldn.hop(2)],
            12: [lambda: across(qo, lqo), lambda: lup.hop(2), lambda: ldn.spread(0)],
            15: [lambda: hop(2, True), lambda: lqo.hop(1), lambda: lup.spread(0), lambda: ldn.spread(1)],
            18: [lambda: lqo.hop(2), lambda: lup.spread(1), lambda: ldn.spread(2)],
        },
        keys,
    )
    settle(1, dk, None, None)
    weight_grad(1, 1, 0)
    settle(2, dv, None, None)
    weight_grad(2, 1, width // 8)
    kv.a_start()
    vec.step(0)
    kv.b_start()

    part = 256

    def columns(t, _):
        at = pl.ds(pl.multiple_of(t * part, part), part)
        total = rest_ref[:, at]
        for i, w in enumerate((wq, wk, wv)):
            total = total + dot(low[slot(i)], w[at, :], 1, 1)
        token_ref[:, at] = total.astype(jnp.bfloat16)
        return 0
    lax.fori_loop(0, width // part, columns, 0)

    lqo.spread(0)
    lup.spread(2)
    vec.step(1)
    kv.c_start()
    lqo.spread(1)
    vec.step(2)
    across(kv, lkv)
    lqo.spread(2)
    lkv.share()
    vec.finish(table_out)
    for c in chains:
        c.finish()
    for t in range(nb - 1):
        for c in lines:
            c.wait_send(t)
    for c in planes:
        c.drain()
    for c in chains:
        c.drain()
    vec.drain()


def backward(seg, live, do, stats, lse, delta, x, rest, table, q_all, k_all, v_all, weights, early, nb):
    n, width = do.shape
    bf, f32 = jnp.bfloat16, jnp.float32
    pair = (2, 2, 2, width // 4, width)
    sources = [early[0].shape, early[1].shape, pair, pair]
    sums = [s[-2:] for s in sources]
    scratch = []
    for s in sources:
        scratch += plane_scratch(s[-2:])
    ns = line_sems(nb)
    every = pltpu.VMEM((nb, n, width), bf)
    total = pltpu.VMEM((n, width), f32)
    square = pltpu.VMEM((width, width), bf)
    dma = pltpu.SemaphoreType.DMA
    return pl.pallas_call(
        functools.partial(backward_kernel, nb),
        out_shape=(
            jax.ShapeDtypeStruct((n, width), bf), jax.ShapeDtypeStruct((TABLE, width), f32),
            *[jax.ShapeDtypeStruct(s, bf) for s in sums],
        ),
        in_specs=[VM] * 6 + [ANY] * 2 + [VM] + [ANY] * 9,
        out_specs=(VM,) * 6,
        scratch_shapes=[
            every, every, every, every, pltpu.VMEM((nb,) + stats.shape, f32), total, total, total,
            square, square, square, pltpu.VMEM((2,) + pair, bf),
            *[pltpu.VMEM(s[:2] + s[3:], bf) for s in sources[:2]],
            pltpu.VMEM((TABLE, width), f32), pltpu.VMEM((6, TABLE, width), f32), pltpu.VMEM((nb, TABLE, width), f32),
            pltpu.VMEM((n, width), bf), total, pltpu.VMEM((n, 1), f32), pltpu.VMEM((nb, 1, n), f32),
            *[line_scratch(s, nb) for s in sums], *scratch,
            dma((2, 2, nb - 1)), dma((2, 2, nb - 1)), dma((12,)), dma((4, PLANE_SEMS)), dma((4, PLANE_SEMS)),
            dma((4, ns)), dma((4, ns)), dma((2,)), dma((3 + nb,)), dma((3 + nb,)),
        ],
        compiler_params=pltpu.CompilerParams(
            collective_id=4, has_side_effects=True, vmem_limit_bytes=63 << 20
        ),
        name="backward",
    )(
        seg, live, do, stats, lse, delta, x, rest, table,
        q_all, k_all, v_all, *weights, *early,
    )


def finish_kernel(dn, up, qo, kv, table, token, *outs):
    f32 = jnp.float32
    outs[15][...] = token[...]
    n = outs[0].shape[0]
    for i, (a, at) in enumerate(((qo, 0), (kv, 0), (kv, n), (qo, n))):
        outs[i][...] = a[at:at + n, :].astype(f32)
    outs[4][...] = dn[...].astype(f32)
    rows = outs[5].shape[0]
    width = up.shape[1]
    for t in range(outs[5].shape[1] // width):
        outs[5][:, t * width:(t + 1) * width] = up[t * rows:(t + 1) * rows, :].astype(f32)
    shard = lax.axis_index("seq") * 4 + lax.axis_index("shard")
    piece = outs[6].shape[1]
    r = lax.broadcasted_iota(jnp.int32, (width, PAIR), 0)
    c = lax.broadcasted_iota(jnp.int32, (width, PAIR), 1)
    pick = ((r == c + shard * piece) & (c < piece)).astype(f32)
    small = lax.dot_general(
        table[:8, :], pick, (((1,), (0,)), ((), ())), precision=lax.Precision.HIGHEST,
        preferred_element_type=f32,
    )
    for i in range(8):
        outs[6 + i][...] = small[i:i + 1, :piece]
    wide = outs[14].shape[1]
    per = width // wide
    at = pl.multiple_of((shard % per) * wide, wide)
    outs[14][...] = table[pl.ds(8 + shard // per, 1), pl.ds(at, wide)]


def finish(dn, up, qo, kv, table, token, wide):
    width = table.shape[1]
    f32 = jnp.float32
    S = jax.ShapeDtypeStruct
    piece = width // 8
    chunks = up.shape[0] // piece
    out = pl.pallas_call(
        finish_kernel,
        out_shape=(
            *[S((piece, width), f32)] * 4, S(dn.shape, f32), S((piece, chunks * width), f32),
            *[S((1, piece), f32)] * 8, S((1, wide), f32), S(token.shape, token.dtype),
        ),
        in_specs=[VM] * 6,
        out_specs=(VM,) * 16,
        compiler_params=pltpu.CompilerParams(vmem_limit_bytes=60 << 20),
        name="finish",
    )(dn, up, qo, kv, table, token)
    return out[15], list(out[:6]) + [a.reshape(-1) for a in out[6:15]]


EPSILON = 1e-06
PLANE = ("seq", "shard")


def normalize(hidden, gain, shift):
    center = hidden - jnp.mean(hidden, axis=-1, keepdims=True)
    spread = jnp.mean(center * center, axis=-1, keepdims=True)
    return center * lax.rsqrt(spread + EPSILON) * gain + shift


def smooth_gate(hidden):
    return jax.nn.gelu(hidden, approximate=False)


def mm(left, right):
    return jnp.dot(left, right, preferred_element_type=jnp.float32)


def contract_rows(left, right):
    return dot(left, right, 0, 0)


def times_transpose(left, right):
    return dot(left, right, 1, 1)


def tuned_plane():
    return lax.axis_size("seq") == 2 and lax.axis_size("shard") == 4 and lax.axis_size("blk") == 4


def total(g):
    part = lax.psum_scatter(g.astype(jnp.bfloat16), PLANE, scatter_dimension=0, tiled=True)
    return lax.psum(part, "blk").astype(jnp.float32)


def whole_line(
    inputs, seg, live, mats, vecs, cotangent, codes, own_codes, start,
):
    rows, width = inputs.shape
    length = seg.shape[0]
    scale = HEAD_DIM ** (-0.5)
    xs = lax.all_gather(inputs, "blk", axis=0, tiled=True)
    wq, wk, wv, wo, wup, wdn = [lax.all_gather(w, PLANE, axis=0, tiled=True) for w in mats]
    whole = [lax.all_gather(v, PLANE, axis=0, tiled=True).astype(jnp.float32) for v in vecs]
    bq, bv, bo, g1, s1, bdn, g2, s2, bup = whole
    own_seg = lax.dynamic_slice_in_dim(seg, start, rows)
    low = jnp.sum((seg < own_seg[0]).astype(jnp.int32))
    high = jnp.sum((seg <= own_seg[rows - 1]).astype(jnp.int32))
    span = jnp.stack([low // TILE, (high + TILE - 1) // TILE])
    q_all = ((mm(xs, wq) + bq) * scale).astype(jnp.bfloat16)
    k_all = mm(xs, wk).astype(jnp.bfloat16)
    v_all = (mm(xs, wv) + bv).astype(jnp.bfloat16)
    q, k, v = [lax.dynamic_slice_in_dim(a, start, rows) for a in (q_all, k_all, v_all)]
    summed, attended, lse = attention(q, k_all, v_all, codes, own_codes, span)

    first_sum = inputs.astype(jnp.float32) + (mm(attended, wo) + bo)
    first_norm, first_pull = jax.vjp(normalize, first_sum, g1, s1)
    first_low = first_norm.astype(jnp.bfloat16)
    hidden = mm(first_low, wup) + bup
    gated, gate_pull = jax.vjp(smooth_gate, hidden)
    gated_low = gated.astype(jnp.bfloat16)
    second_sum = first_norm + (mm(gated_low, wdn) + bdn)
    result, second_pull = jax.vjp(normalize, second_sum, g2, s2)
    second_grad, g2_grad, s2_grad = second_pull(cotangent.astype(jnp.float32))
    bdn_grad = jnp.sum(second_grad, axis=0)
    second_low = second_grad.astype(jnp.bfloat16)
    wdn_grad = contract_rows(gated_low, second_low)
    (hidden_grad,) = gate_pull(times_transpose(second_low, wdn))
    bup_grad = jnp.sum(hidden_grad, axis=0)
    hidden_low = hidden_grad.astype(jnp.bfloat16)
    wup_grad = contract_rows(first_low, hidden_low)
    norm_grad = second_grad + times_transpose(hidden_low, wup)
    first_grad, g1_grad, s1_grad = first_pull(norm_grad)
    bo_grad = jnp.sum(first_grad, axis=0)
    first_grad_low = first_grad.astype(jnp.bfloat16)
    wo_grad = contract_rows(attended, first_grad_low)
    do = times_transpose(first_grad_low, wo).astype(jnp.bfloat16)

    stats, delta = row_stats(do, summed, lse)
    do_all, stats_all = [lax.all_gather(a, "blk", axis=0) for a in (do, stats)]
    stats_all = jnp.transpose(stats_all, (1, 2, 0, 3)).reshape(stats.shape[0], 8, length)
    dq, dk, dv = attention_grad(
        q, k, v, do, lse, delta, q_all, k_all, v_all, do_all.reshape(length, width), stats_all,
        codes, own_codes, span,
    )
    r = dq * scale
    rq, rk, rv = [a.astype(jnp.bfloat16) for a in (r, dk, dv)]
    token_grad = first_grad + times_transpose(rq, wq) + times_transpose(rk, wk) + times_transpose(rv, wv)
    grads = [contract_rows(inputs, a) for a in (rq, rk, rv)] + [wo_grad, wdn_grad, wup_grad]
    vectors = [
        jnp.sum(r, axis=0), jnp.sum(dv, axis=0), bo_grad, g1_grad, s1_grad, bdn_grad, g2_grad, s2_grad, bup_grad,
    ]
    return result.astype(jnp.bfloat16), token_grad.astype(jnp.bfloat16), [total(g) for g in grads + vectors]


def tuned_line(inputs, mats, vecs, cotangent, seg, live, nb):
    out = forward(inputs, seg, live, mats, vecs, nb)
    wq, wk, wv, wo, wup, wdn, q_all, k_all, v_all, summed, attended, lse, table, bup = out
    out = middle(attended, inputs, cotangent, summed, lse, table, bup, wo, wup, wdn)
    result, rest, do, stats, delta, table, gdn, gup, gwo = out
    width = inputs.shape[1]
    early = [g.reshape(2, 2, 2, -1, width) for g in (gdn, gup, gwo)]
    token_grad, table, rdn, rup, rqo, rkv = backward(
        seg, live, do, stats, lse, delta, inputs, rest, table, q_all, k_all, v_all, [wq, wk, wv], early, nb,
    )
    token_grad, sums = finish(rdn, rup, rqo, rkv, table, token_grad, vecs[8].shape[0])
    return result, token_grad, sums


def per_device(
    tokens, segments, live_mask, query_weight, key_weight, value_weight, out_weight,
    query_bias, value_bias, out_bias, first_gain, first_shift, up_weight, up_bias,
    down_weight, down_bias, second_gain, second_shift, cotangent,
):
    inputs = tokens[0]
    rows = inputs.shape[0]
    nb = lax.axis_size("blk")
    seg, live = segments[0], live_mask[0]
    start = lax.axis_index("blk") * rows
    codes = jnp.where(live > 0, seg, -1 - jnp.arange(seg.shape[0], dtype=jnp.int32))
    own_codes = lax.dynamic_slice_in_dim(codes, start, rows)
    mats = [query_weight, key_weight, value_weight, out_weight, up_weight, down_weight]
    vecs = [query_bias, value_bias, out_bias, first_gain, first_shift, down_bias, second_gain, second_shift, up_bias]
    if tuned_plane():
        result, token_grad, sums = tuned_line(inputs, mats, vecs, cotangent[0], segments, live_mask, nb)
    else:
        result, token_grad, sums = whole_line(
            inputs, seg, live, mats, vecs, cotangent[0], codes, own_codes, start
        )
    rwq, rwk, rwv, ro, rdn, rup, rbq, rbv, rbo, rg1, rs1, rbdn, rg2, rs2, rbup = sums
    return (
        result[None], token_grad[None],
        rwq, rwk, rwv, ro, rbq, rbv, rbo, rg1, rs1, rup, rbup, rdn, rbdn, rg2, rs2,
    )


def solution(mesh):
    flat = P(PLANE, "blk", None)
    mat = P(PLANE, None)
    vec = P(PLANE)
    return jax.shard_map(
        per_device,
        mesh=mesh,
        in_specs=(
            flat, mat, mat, mat, mat, mat, mat, vec, vec, vec, vec, vec, mat, vec, mat, vec, vec, vec, flat,
        ),
        out_specs=(flat, flat, mat, mat, mat, mat, vec, vec, vec, vec, vec, mat, vec, mat, vec, vec, vec),
        check_vma=False,
    )
```
